32 devices in a mesh: dp: 4 (over y, x), expert: 8 (over z, core).
Axes of the slice: x: 2, y: 2, z: 4, core: 2. Of those that a mesh axis runs over, the one named last changes fastest.
Arguments:
- layer_input: bfloat16 [6144, 2048], P(('dp', 'expert')), may hold values from -6 to 6
- out_cotangent: bfloat16 [6144, 2048], P(('dp', 'expert')), may hold values from -6 to 6
- segments: int32 [32, 192], P(('dp', 'expert')), may hold values from 0 to 2, never falling along the last dimension, each value on 1 to 96 neighbouring positions
- routes: int32 [6144, 8], P(('dp', 'expert')), may hold values from 0 to 23, all different within a row; in each aligned block of 192 rows (0 to 191, 192 to 383, ...) at most 72 rows name the same one
- w_qkv: bfloat16 [2048, 6144], P(('dp', 'expert')), may hold values from -0.125 to 0.125
- w_out: bfloat16 [2048, 2048], P(('dp', 'expert')), may hold values from -0.5 to 0.5
- w_router: bfloat16 [2048, 24], P(('dp', 'expert')), may hold values from -0.0625 to 0.0625
- attn_gain: bfloat16 [2048], P(('dp', 'expert')), may hold values from 0.5 to 1.5
- mlp_gain: bfloat16 [2048], P(('dp', 'expert')), may hold values from 0.5 to 1.5
- query_gain: bfloat16 [2048], P(('dp', 'expert')), may hold values from 0.099609375 to 1.8984375
- key_gain: bfloat16 [2048], P(('dp', 'expert')), may hold values from 0.099609375 to 1.8984375
- w_gate_up: bfloat16 [24, 2048, 2048], P('expert'), may hold values from -0.125 to 0.125
- w_down: bfloat16 [24, 1024, 2048], P('expert'), may hold values from -0.75 to 0.75
Outputs:
- out: bfloat16 [6144, 2048], P(('dp', 'expert'))
- grad_input: float32 [6144, 2048], P(('dp', 'expert'))
- grad_qkv: float32 [2048, 3, 2048], P('dp', None, 'expert')
- grad_out: float32 [2048, 2048], P('expert', 'dp')
- grad_router: float32 [2048, 24], P(('dp', 'expert'))
- grad_attn_gain: float32 [2048], P(('dp', 'expert'))
- grad_mlp_gain: float32 [2048], P(('dp', 'expert'))
- grad_query_gain: float32 [2048], P('expert')
- grad_key_gain: float32 [2048], P('expert')
- grad_gate_up: float32 [24, 2048, 2048], P('expert', 'dp')
- grad_down: float32 [24, 1024, 2048], P('expert', 'dp')
The draws below stay inside these ranges and needn't reach their ends.
Inputs may be any that keep to these rules, and one draw needn't show every extreme that they name: `routes`: each row names 8 different experts. Among the rows of one device no expert is named more than 72 times, a bound that some block reaches. `segments`: within a sequence the numbers never fall; a document has at most 96 tokens and one has exactly that many.
All inputs are finite; a program needn't handle non-finite values.
Results may differ from the reference program's by a relative error of at most 0.02.
Values may be sent and summed in bfloat16 or wider, within the bound.
A program may use at most 320 MiB of HBM per device.

```python
import math
import jax
import jax.numpy as jnp
import numpy as np
from jax import lax

D = 2048
FF = 1024
HEADS = 16
HEAD_DIM = 128
TOPK = 8
TOK_DEV = 192
EXPERTS = 24
SEQS = 32
TOKENS = 6144
CAP = 72
DOCS = 3
DOC_MOST = 96


def strengthened(array, stream_key, source, target, shards_of, factor):
    owner, partner = [(jnp.arange(array.shape[dim]) // (array.shape[dim] // shards_of)).reshape([-1 if axis == dim else 1 for axis in range(array.ndim)]) for dim in (source, target)]
    chosen = jax.random.permutation(stream_key, shards_of)[partner]
    strong = (owner == chosen) | (owner == (partner + shards_of // 2) % shards_of)
    return jnp.where(strong, factor * array, array)


def level_of(rng, shape, shards, low, top_value):
    def one(dim, parts):
        steps = jax.random.uniform(jax.random.fold_in(jax.random.fold_in(rng, 6), dim), (parts,), jnp.float32, low / len(shards), top_value / len(shards))
        return jnp.repeat(jnp.exp(steps), shape[dim] // parts).reshape((-1,) + (1,) * (len(shape) - dim - 1))

    gain = one(*shards[0])
    for cut in shards[1:]:
        gain = gain * one(*cut)
    return gain


def profile(amount, total, most, skew):
    weights = [(1 << 20) // math.isqrt(rank ** skew) + 1 for rank in range(2, amount + 1)]
    spare, given = total - most - (amount - 1), [1] * (amount - 1)
    while spare > 0:
        candidates = [i for i in range(amount - 1) if given[i] < most]
        mass, remaining = sum([weights[i] for i in candidates]), spare
        for i in candidates:
            extra = min(most - given[i], max(1, remaining * weights[i] // mass), spare)
            given[i] = given[i] + extra
            spare = spare - extra
    return np.array([most] + given)


def ragged_sizes(key, count, total, reach, lean):
    if count == 2:
        one = jax.random.randint(key, (), max(1, total - reach), min(reach, total - 1) + 1)
        return jnp.stack([one, total - one])
    tallies = jnp.asarray(profile(count, total, reach, lean), jnp.int32)
    couples = (count - 1) // 2
    source_of, sink = tallies[1:1 + 2 * couples:2], tallies[2:2 + 2 * couples:2]
    slack = jnp.minimum(source_of - 1, reach - sink)
    shifted = jax.random.randint(jax.random.fold_in(key, 1), (couples,), 0, 1 << 20) % (slack + 1)
    tallies = tallies.at[1:1 + 2 * couples:2].set(source_of - shifted).at[2:2 + 2 * couples:2].set(sink + shifted)
    return tallies[jax.random.permutation(jax.random.fold_in(key, 2), count)]


def deal_out(own_key, own, number, rows, count, top, bound, skew):
    sequence = jax.random.permutation(own_key, count)
    crowded, common = load_shares(count, rows * top, bound, skew, True), load_shares(count, rows * top, bound, skew, False)
    places = jnp.arange(count)

    def named(tallies, rotation):
        used = int((tallies > 0).sum())
        fixed = max(1, used // 4)
        shifted = fixed + (places - fixed + rotation * (used - fixed)) % max(1, count - fixed)
        return jnp.zeros((count,), jnp.int32).at[sequence[jnp.where(places < fixed, places, shifted)]].set(jnp.asarray(tallies, jnp.int32))

    tallies = jnp.where(number % 4 == 0, named(crowded, number // 4), named(common, number - number // 4 - 1))
    mixed = jax.random.permutation(jax.random.fold_in(own, 3), count)
    giver, sink = mixed[0:count // 2 * 2:2], mixed[1:count // 2 * 2:2]
    margin = jnp.minimum(tallies[giver] - 1, bound - tallies[sink]) // 2
    margin = jnp.where((giver == sequence[0]) | (sink == sequence[0]) | (tallies[sink] == 0), 0, jnp.maximum(margin, 0))
    shifted = jax.random.randint(jax.random.fold_in(own, 4), (count // 2,), 0, 1 << 20) % (margin + 1)
    tallies = tallies.at[giver].add(-shifted).at[sink].add(shifted)
    members = jnp.searchsorted(jnp.cumsum(tallies), jnp.arange(rows * top), side="right").astype(jnp.int32)
    table = members.reshape(top, rows).T
    table = table[jax.random.permutation(jax.random.fold_in(own, 1), rows)]
    rotation = jax.random.randint(jax.random.fold_in(own, 2), (rows, 1), 0, top)
    return jnp.take_along_axis(table, (jnp.arange(top)[None, :] + rotation) % top, axis=1)


def load_shares(number_of, total, bound, slope, full):
    portions = [(1 << 20) // math.isqrt(standing ** slope) + 1 for standing in range(1, number_of + 1)]
    largest = bound if full else min(bound, max(-(-total // number_of), total * portions[0] // sum(portions)))
    least = 1 if total - largest >= number_of - 1 else 0
    given, surplus = [largest] + [least] * (number_of - 1), total - largest - least * (number_of - 1)
    while surplus > 0:
        movable = [i for i in range(1, number_of) if given[i] < largest] or [i for i in range(1, number_of) if given[i] < bound]
        pool, left = sum([portions[i] for i in movable]), surplus
        for i in movable:
            more = min(bound - given[i], max(1, left * portions[i] // pool), surplus)
            given[i] = given[i] + more
            surplus = surplus - more
    return np.array(given)


def centred(stream_key, shape, width, most, shards=(), held_as=jnp.bfloat16):
    factor_of = level_of(stream_key, shape, shards, -0.22, 0.18) if shards else 1.0
    array = jax.random.normal(stream_key, shape, jnp.float32) * width * factor_of
    return jnp.minimum(jnp.maximum(array, -most), most).astype(held_as)


def bell_draw_with(rng, extent, spread, reach, shards, heavy, kind=jnp.bfloat16):
    array = spread * jax.random.normal(rng, extent, jnp.float32)
    if shards:
        array = array * level_of(rng, extent, shards, -0.22, 0.18)
    return jnp.clip(strengthened(array, jax.random.fold_in(rng, 3), *heavy), -reach, reach).astype(kind)


def setup_inputs(seed: int = 0) -> dict:
    streams_of = jax.random.split(jax.random.key(seed), 14)
    layer_input = bell_draw_with(streams_of[0], (TOKENS, D), 1.0, 6.0, ((0, 32),), (0, 1, 32, 2.75))
    out_cotangent = centred(streams_of[1], (TOKENS, D), 1.0, 6.0, ((0, 32),))
    segments = jax.vmap(lambda own: jnp.searchsorted(jnp.cumsum(ragged_sizes(own, DOCS, TOK_DEV, DOC_MOST, 2)), jnp.arange(TOK_DEV), side="right"))(jax.random.split(streams_of[2], SEQS)).reshape((SEQS, TOK_DEV)).astype(jnp.int32)
    routes_keys = jax.random.split(jax.random.fold_in(streams_of[3], 1), TOKENS // TOK_DEV)
    routes_turns = jax.random.permutation(jax.random.fold_in(streams_of[3], 3), TOKENS // TOK_DEV)
    routes = jax.vmap(lambda own, number: deal_out(jax.random.fold_in(streams_of[3], 2), own, number, TOK_DEV, EXPERTS, TOPK, CAP, 1))(routes_keys, routes_turns).reshape((TOKENS, TOPK))
    w_qkv = centred(streams_of[4], (D, 3 * D), D ** -0.5, 0.125, ((0, 32),))
    w_out = centred(streams_of[5], (D, D), (D // 16) ** -0.5, 0.5, ((0, 32),))
    w_router = centred(streams_of[6], (D, EXPERTS), (4 * D) ** -0.5, 0.0625, ((0, 32),))
    attn_gain = jnp.clip(1.0 + 0.1 * jax.random.normal(streams_of[7], (D,), jnp.float32), 0.5, 1.5).astype(jnp.bfloat16)
    mlp_gain = jnp.clip(1.0 + 0.1 * jax.random.normal(streams_of[8], (D,), jnp.float32), 0.5, 1.5).astype(jnp.bfloat16)
    query_gain = jnp.clip(1.0 + 0.18 * jax.random.normal(streams_of[9], (D,), jnp.float32), 0.099609375, 1.8984375).astype(jnp.bfloat16)
    key_gain = jnp.clip(1.0 + 0.18 * jax.random.normal(streams_of[10], (D,), jnp.float32), 0.099609375, 1.8984375).astype(jnp.bfloat16)
    w_gate_up = centred(streams_of[11], (EXPERTS, D, 2 * FF), D ** -0.5, 0.125, ((0, 8),))
    w_down = centred(streams_of[12], (EXPERTS, FF, D), (FF // 16) ** -0.5, 0.75, ((0, 8),))
    return dict(layer_input=layer_input, out_cotangent=out_cotangent, segments=segments, routes=routes, w_qkv=w_qkv, w_out=w_out, w_router=w_router, attn_gain=attn_gain, mlp_gain=mlp_gain, query_gain=query_gain, key_gain=key_gain, w_gate_up=w_gate_up, w_down=w_down)


NORM_EPS = 1e-05
PRECISE = lax.Precision.HIGHEST

@jax.custom_vjp
def low(v):
    return lax.optimization_barrier(v.astype(jnp.bfloat16)).astype(jnp.float32)

@jax.custom_vjp
def low_back(v):
    return v

def low_keep(v):
    return (low(v), None)

def low_pass(kept, grad):
    return (grad,)

def back_keep(v):
    return (v, None)

def back_low(kept, grad):
    return (low(grad),)
low.defvjp(low_keep, low_pass)
low_back.defvjp(back_keep, back_low)

def rms_scale(values):
    return lax.rsqrt(lax.optimization_barrier(jnp.mean(values * values, axis=-1, keepdims=True)) + NORM_EPS)

def rotary(values, length):
    half_size = values.shape[-1] // 2
    index_half = jnp.arange(half_size, dtype=jnp.float32)
    frequency = jnp.exp(index_half * (-2.0 * math.log(10000.0) / values.shape[-1]))
    angles = jnp.arange(length, dtype=jnp.float32)[:, None] * frequency[None, :]
    cosine = jnp.cos(angles)[:, None, :]
    sine_table = jnp.sin(angles)[:, None, :]
    first_half = values[..., :half_size]
    second = values[..., half_size:]
    return jnp.concatenate([first_half * cosine - second * sine_table, second * cosine + first_half * sine_table], axis=-1)

def attend(query_rows, key_rows, value_rows, segment):
    length = query_rows.shape[1]
    scores = low_back(jnp.einsum('gqhd,gkhd->ghqk', query_rows, key_rows, precision=PRECISE) * (1.0 / math.sqrt(query_rows.shape[-1])))
    position = jnp.arange(length)
    allowed = (position[:, None] >= position[None, :])[None, None] & (segment[:, None, :, None] == segment[:, None, None, :])
    attn_weights = low(jax.nn.softmax(jnp.where(allowed, scores, -1e+30), axis=-1))
    return jnp.einsum('ghqk,gkhd->gqhd', attn_weights, value_rows, precision=PRECISE)

def reference(layer_input, out_cotangent, segments, routes, w_qkv, w_out, w_router, attn_gain, mlp_gain, query_gain, key_gain, w_gate_up, w_down):
    per_block = math.gcd(SEQS, max(1, 4096 // TOK_DEV))
    block_count = SEQS // per_block
    chooser = (routes[:, :, None] == jnp.arange(EXPERTS)[None, None, :]).astype(jnp.float32)
    seg_blocks = segments.reshape(block_count, per_block, TOK_DEV)

    def forward(inputs, qkv_weight, out_weight, router_weight, gain_attn, gain_mlp, gain_query, gain_key, gate_up_weight, down_weight):
        hidden_one = low(inputs * rms_scale(inputs) * gain_attn)
        projected = low_back(jnp.dot(hidden_one, qkv_weight, precision=PRECISE))
        query_rows = projected[:, :D]
        key_rows = projected[:, D:2 * D]
        value_rows = projected[:, 2 * D:]
        query_rows = query_rows * rms_scale(query_rows) * gain_query
        key_rows = key_rows * rms_scale(key_rows) * gain_key
        block_shape = (block_count, per_block, TOK_DEV, HEADS, HEAD_DIM)
        query_rows = low(rotary(query_rows.reshape(block_shape), TOK_DEV))
        key_rows = low(rotary(key_rows.reshape(block_shape), TOK_DEV))
        value_rows = low(value_rows.reshape(block_shape))
        attended = lax.map(jax.checkpoint(lambda blocks: attend(*blocks)), (query_rows, key_rows, value_rows, seg_blocks))
        attended = low(low_back(attended.reshape(TOKENS, D)))
        residual = inputs + low_back(jnp.dot(attended, out_weight, precision=PRECISE))
        hidden_two = low(residual * rms_scale(residual) * gain_mlp)
        logits = low_back(jnp.dot(hidden_two, router_weight, precision=PRECISE))
        chosen = lax.optimization_barrier(jnp.sum(chooser * logits[:, None, :], axis=-1))
        gate_values = jax.nn.softmax(chosen, axis=-1)
        gate_table = lax.optimization_barrier(jnp.sum(chooser * gate_values[:, :, None], axis=1))

        def expert_step(running, packed):
            gate_up_one, down_one, gate_column = packed
            rows_in = low_back(hidden_two)
            hidden = low_back(jnp.dot(rows_in, gate_up_one, precision=PRECISE))
            activated = low(jax.nn.silu(hidden[:, :FF]) * hidden[:, FF:])
            expert_out = low(low_back(jnp.dot(activated, down_one, precision=PRECISE)))
            return (running + gate_column[:, None] * expert_out, None)
        mixture, unused = lax.scan(jax.checkpoint(expert_step), jnp.zeros_like(residual), (gate_up_weight, down_weight, gate_table.T))
        return residual + mixture
    floats = [array_in.astype(jnp.float32) for array_in in (layer_input, w_qkv, w_out, w_router, attn_gain, mlp_gain, query_gain, key_gain, w_gate_up, w_down)]
    output, pullback = jax.vjp(forward, *floats)
    gradients = pullback(out_cotangent.astype(jnp.float32))
    return (output.astype(jnp.bfloat16), gradients[0], gradients[1].reshape(D, 3, D), gradients[2], gradients[3], gradients[4], gradients[5], gradients[6], gradients[7], gradients[8], gradients[9])
```

```python
import functools
import math

import jax
import jax.numpy as jnp
from jax import lax
from jax.experimental import pallas as pl
from jax.experimental.pallas import tpu as pltpu
from jax.sharding import PartitionSpec as P

HEADS = 16
NORM_EPS = 1e-05
MESH = pl.DeviceIdType.MESH
ANY = pl.BlockSpec(memory_space=pl.ANY)
LOW = jnp.bfloat16
FULL = jnp.float32


def line_place():
    place = lax.axis_index("expert")
    level, side = lax.div(place, 2), lax.rem(place, 2)
    return place, level, side, place + 1 - 2 * side


def line_barrier(place, other, has_up, has_down):
    barrier = pltpu.get_barrier_semaphore()
    pl.semaphore_signal(barrier, inc=1, device_id={"expert": other}, device_id_type=MESH)

    @pl.when(has_up)
    def _():
        pl.semaphore_signal(barrier, inc=1, device_id={"expert": place + 2}, device_id_type=MESH)

    @pl.when(has_down)
    def _():
        pl.semaphore_signal(barrier, inc=1, device_id={"expert": place - 2}, device_id_type=MESH)

    pl.semaphore_wait(barrier, 1 + has_up.astype(jnp.int32) + has_down.astype(jnp.int32))


def line_gather_kernel(levels, cuts, *refs):
    count = len(cuts)
    ins, outs = refs[:count], refs[count : 2 * count]
    up_sem, down_sem, side_sem, recv_sem, own_sem = refs[2 * count :]
    pieces = [(i, k) for i in range(count) for k in range(cuts[i])]
    place, level, side, other = line_place()
    has_up, has_down = level < levels - 1, level > 0

    def part(ref, i, k):
        rows = ins[i].shape[0] // cuts[i]
        return ref.at[pl.ds(k * rows, rows)]

    def sending(q, block, own, sem, target):
        i, k = pieces[q]
        landing = part(outs[i].at[block], i, k)
        return pltpu.make_async_remote_copy(
            src_ref=part(ins[i], i, k) if own else landing,
            dst_ref=landing,
            send_sem=sem,
            recv_sem=recv_sem.at[block, q],
            device_id={"expert": target},
            device_id_type=MESH,
        )

    def up(q, step):
        return sending(q, place - 2 * step, step == 0, up_sem.at[step, q], place + 2)

    def down(q, step):
        return sending(q, place + 2 * step, step == 0, down_sem.at[step, q], place - 2)

    def across(q, step):
        return sending(q, place - 2 * step, step == 0, side_sem.at[step + levels - 1, q], other)

    own_copies = [
        pltpu.make_async_copy(ins[i], outs[i].at[place], own_sem.at[i]) for i in range(count)
    ]
    line_barrier(place, other, has_up, has_down)
    for q in range(len(pieces)):
        pl.when(has_up)(up(q, 0).start)
        pl.when(has_down)(down(q, 0).start)
    for q in range(len(pieces)):
        across(q, 0).start()
    for copy in own_copies:
        copy.start()
    for step in range(1, levels):
        for q in range(len(pieces)):

            @pl.when(level >= step)
            def _():
                across(q, step).wait_recv()
                pl.when(has_up)(up(q, step).start)
                across(q, step).start()

            @pl.when(level + step < levels)
            def _():
                across(q, -step).wait_recv()
                pl.when(has_down)(down(q, step).start)
                across(q, -step).start()

    for q in range(len(pieces)):
        for far in range(levels):
            sending(q, 2 * far + 1 - side, False, side_sem.at[0, q], other).wait_recv()
        across(q, 0).wait_send()
        for step in range(levels):
            pl.when(has_up & (level >= step))(up(q, step).wait_send)
            pl.when(has_down & (level + step < levels))(down(q, step).wait_send)
            if step:
                pl.when(level >= step)(across(q, step).wait_send)
                pl.when(level + step < levels)(across(q, -step).wait_send)
    for copy in own_copies:
        copy.wait()


def line_gather(size, arrays, cuts, number):
    levels, total = size // 2, sum(cuts)
    sems = pltpu.SemaphoreType.DMA
    return pl.pallas_call(
        functools.partial(line_gather_kernel, levels, tuple(cuts)),
        out_shape=[jax.ShapeDtypeStruct((size,) + a.shape, a.dtype) for a in arrays],
        in_specs=[ANY] * len(arrays),
        out_specs=[ANY] * len(arrays),
        scratch_shapes=[
            sems((levels, total)),
            sems((levels, total)),
            sems((2 * levels - 1, total)),
            sems((size, total)),
            sems((len(arrays),)),
        ],
        compiler_params=pltpu.CompilerParams(collective_id=number, has_side_effects=True),
        cost_estimate=pl.CostEstimate(flops=0, transcendentals=0, bytes_accessed=150_000_000),
        name="line_gather",
    )(*arrays)


def line_reduce_kernel(levels, cuts, part_ref, sum_ref, own, beside, rising, falling, *sems):
    load_sem, side_send, side_recv, up_send, up_recv, down_send, down_recv, out_sem = sems
    place, level, side, other = line_place()
    has_up, has_down = level < levels - 1, level > 0
    rows = part_ref.shape[1] // cuts

    def cut(ref, block, k):
        return ref.at[block, pl.ds(k * rows, rows)]

    def moving(source, target_ref, block, k, send, recv, target):
        return pltpu.make_async_remote_copy(
            src_ref=source,
            dst_ref=cut(target_ref, block, k),
            send_sem=send.at[block, k],
            recv_sem=recv.at[block, k],
            device_id={"expert": target},
            device_id_type=MESH,
        )

    def loading(far, k):
        return pltpu.make_async_copy(
            cut(part_ref, 2 * far + side, k), cut(own, far, k), load_sem.at[far, k]
        )

    def across(far, k):
        source = cut(part_ref, 2 * far + 1 - side, k)
        return moving(source, beside, far, k, side_send, side_recv, other)

    def up(far, k):
        return moving(cut(own, far, k), rising, far, k, up_send, up_recv, place + 2)

    def down(far, k):
        return moving(cut(own, far, k), falling, far, k, down_send, down_recv, place - 2)

    def value(ref, block, k):
        return cut(ref, block, k)[...].astype(jnp.float32)

    order = []
    for step in range(levels):
        for far in (levels - 1 - step, step):
            if far not in order:
                order.append(far)
    for far in order:
        for k in range(cuts):
            loading(far, k).start()
    line_barrier(place, other, has_up, has_down)
    for far in order:
        for k in range(cuts):
            across(far, k).start()

    def pair(far, k):
        loading(far, k).wait()
        across(far, k).wait_recv()
        return value(own, far, k) + value(beside, far, k)

    for step in range(levels - 1):
        for k in range(cuts):
            high, low = levels - 1 - step, step

            @pl.when((level < high) & has_down)
            def _():
                both = pair(high, k)
                up(high, k).wait_recv()
                cut(own, high, k)[...] = (both + value(rising, high, k)).astype(own.dtype)

            @pl.when((level < high) & jnp.logical_not(has_down))
            def _():
                cut(own, high, k)[...] = pair(high, k).astype(own.dtype)

            pl.when(level < high)(up(high, k).start)

            @pl.when((level > low) & has_up)
            def _():
                both = pair(low, k)
                down(low, k).wait_recv()
                cut(own, low, k)[...] = (both + value(falling, low, k)).astype(own.dtype)

            @pl.when((level > low) & jnp.logical_not(has_up))
            def _():
                cut(own, low, k)[...] = pair(low, k).astype(own.dtype)

            pl.when(level > low)(down(low, k).start)

    for k in range(cuts):
        cut(own, level, k)[...] = pair(level, k).astype(own.dtype)

        @pl.when(has_down)
        def _():
            up(level, k).wait_recv()
            total = value(own, level, k) + value(rising, level, k)
            cut(own, level, k)[...] = total.astype(own.dtype)

        @pl.when(has_up)
        def _():
            down(level, k).wait_recv()
            total = value(own, level, k) + value(falling, level, k)
            cut(own, level, k)[...] = total.astype(own.dtype)

        pltpu.make_async_copy(
            cut(own, level, k), sum_ref.at[pl.ds(k * rows, rows)], out_sem.at[k]
        ).start()
    for k in range(cuts):
        pltpu.make_async_copy(
            cut(own, level, k), sum_ref.at[pl.ds(k * rows, rows)], out_sem.at[k]
        ).wait()
        for far in range(levels):
            across(far, k).wait_send()
            pl.when(level < far)(up(far, k).wait_send)
            pl.when(level > far)(down(far, k).wait_send)


def line_reduce(size, parts, cuts, number):
    levels = size // 2
    block = parts.shape[1:]
    sems = pltpu.SemaphoreType.DMA((levels, cuts))
    return pl.pallas_call(
        functools.partial(line_reduce_kernel, levels, cuts),
        out_shape=jax.ShapeDtypeStruct(block, parts.dtype),
        in_specs=[ANY],
        out_specs=ANY,
        scratch_shapes=[pltpu.VMEM((levels,) + block, parts.dtype)] * 4
        + [sems] * 7
        + [pltpu.SemaphoreType.DMA((cuts,))],
        compiler_params=pltpu.CompilerParams(
            collective_id=number, has_side_effects=True, vmem_limit_bytes=40 << 20
        ),
        cost_estimate=pl.CostEstimate(flops=0, transcendentals=0, bytes_accessed=150_000_000),
        name="line_reduce",
    )(parts)


def exchange_kernel(axis, size, spread, *refs):
    count = len(spread)
    ins, outs = refs[:count], refs[count : 2 * count]
    send_sem, recv_sem, own_sem = refs[2 * count :]
    place = lax.axis_index(axis)
    barrier = pltpu.get_barrier_semaphore()
    peers = [lax.rem(place + shift, size) for shift in range(1, size)]
    for peer in peers:
        pl.semaphore_signal(barrier, inc=1, device_id={axis: peer}, device_id_type=MESH)
    pl.semaphore_wait(barrier, size - 1)

    def source(i, block):
        return ins[i] if spread[i] else ins[i].at[block]

    def sending(i, shift, peer, landing):
        return pltpu.make_async_remote_copy(
            src_ref=source(i, peer),
            dst_ref=outs[i].at[landing],
            send_sem=send_sem.at[i, shift],
            recv_sem=recv_sem.at[i, landing],
            device_id={axis: peer},
            device_id_type=MESH,
        )

    own = [
        pltpu.make_async_copy(source(i, place), outs[i].at[place], own_sem.at[i])
        for i in range(count)
    ]
    for shift, peer in enumerate(peers):
        for i in range(count):
            sending(i, shift, peer, place).start()
    for copy in own:
        copy.start()
    for shift, peer in enumerate(peers):
        for i in range(count):
            sending(i, shift, peer, peer).wait_recv()
            sending(i, shift, peer, place).wait_send()
    for copy in own:
        copy.wait()


def exchange(axis, size, arrays, spread, number):
    sems = pltpu.SemaphoreType.DMA
    outs = [
        jax.ShapeDtypeStruct((size,) + a.shape if flat else a.shape, a.dtype)
        for a, flat in zip(arrays, spread)
    ]
    return pl.pallas_call(
        functools.partial(exchange_kernel, axis, size, tuple(spread)),
        out_shape=outs,
        in_specs=[ANY] * len(arrays),
        out_specs=[ANY] * len(arrays),
        scratch_shapes=[
            sems((len(arrays), size)),
            sems((len(arrays), size)),
            sems((len(arrays),)),
        ],
        compiler_params=pltpu.CompilerParams(collective_id=number, has_side_effects=True),
        cost_estimate=pl.CostEstimate(flops=0, transcendentals=0, bytes_accessed=30_000_000),
        name="exchange_" + axis,
    )(*arrays)


def rms_scale(values):
    return lax.rsqrt(jnp.mean(values * values, axis=-1, keepdims=True) + NORM_EPS)


def rotary(values, direction):
    length = values.shape[-3]
    half_size = values.shape[-1] // 2
    index_half = jnp.arange(half_size, dtype=FULL)
    frequency = jnp.exp(index_half * (-2.0 * math.log(10000.0) / values.shape[-1]))
    angles = jnp.arange(length, dtype=FULL)[:, None] * frequency[None, :]
    cosine = jnp.cos(angles)[:, None, :]
    sine_table = direction * jnp.sin(angles)[:, None, :]
    first_half = values[..., :half_size]
    second = values[..., half_size:]
    return jnp.concatenate(
        [first_half * cosine - second * sine_table, second * cosine + first_half * sine_table],
        axis=-1,
    )


def norm_back(grad_normed, normed, scale_rows):
    return scale_rows * (
        grad_normed - normed * jnp.mean(grad_normed * normed, axis=-1, keepdims=True)
    )


def contract_rows(left_side, right_side):
    return lax.dot_general(
        left_side, right_side, (((0,), (0,)), ((), ())), preferred_element_type=FULL
    )


def contract_cols(left_side, right_side):
    return lax.dot_general(
        left_side, right_side, (((1,), (1,)), ((), ())), preferred_element_type=FULL
    )


def einsum(spec, left_side, right_side):
    return jnp.einsum(spec, left_side, right_side, preferred_element_type=FULL)


def on_device(
    dp_count,
    line_count,
    layer_input,
    out_cotangent,
    segments,
    routes,
    w_qkv,
    w_out,
    w_router,
    attn_gain,
    mlp_gain,
    query_gain,
    key_gain,
    w_gate_up,
    w_down,
):
    row_count, model_dim = layer_input.shape
    top_count = routes.shape[1]
    expert_count = w_router.shape[1]
    local_count = w_gate_up.shape[0]
    head_size = model_dim // HEADS
    head_cols = model_dim // line_count
    heads_here = head_cols // head_size
    capacity = (row_count * top_count * 9 // 8 + expert_count - 1) // expert_count
    scaling = 1.0 / math.sqrt(head_size)
    place = lax.axis_index("expert")
    all_rows = line_count * row_count
    shard = w_qkv.shape[0]

    out_full = lax.all_gather(w_out, ("dp", "expert"), axis=0, tiled=True)
    small = jnp.concatenate(
        [w_router] + [g[:, None] for g in (attn_gain, mlp_gain, query_gain, key_gain)], axis=1
    )
    small = jnp.pad(small, ((0, 0), (0, 128 - small.shape[1])))
    columns = w_qkv.reshape(shard, 3, line_count, head_cols).transpose(2, 0, 1, 3)
    columns = columns.reshape(line_count, shard, 3 * head_cols)
    packed = jnp.concatenate(
        [columns, jnp.broadcast_to(small[None], (line_count,) + small.shape)], axis=2
    )
    (packed,) = exchange("expert", line_count, [packed], [False], 1)
    packed = packed.reshape(line_count * shard, packed.shape[2])
    (packed,) = exchange("dp", dp_count, [packed], [True], 2)
    packed = packed.reshape(model_dim, packed.shape[2])
    qkv_here = packed[:, : 3 * head_cols]
    router_full = packed[:, 3 * head_cols : 3 * head_cols + expert_count]
    gains = packed[:, 3 * head_cols + expert_count : 3 * head_cols + expert_count + 4].astype(FULL)
    gain_attn, gain_mlp = gains[:, 0], gains[:, 1]
    own_gains = lax.dynamic_slice_in_dim(gains, place * head_cols, head_cols, axis=0)
    gain_query, gain_key = own_gains[:, 2], own_gains[:, 3]

    numbers = jnp.concatenate([routes.T, segments, jnp.zeros((7, row_count), jnp.int32)], axis=0)
    x_all, numbers_all = line_gather(line_count, [layer_input, numbers], [4, 1], 3)
    routes_all = numbers_all[:, :top_count]
    segments_all = numbers_all[:, top_count]
    (x_all,) = (x_all.reshape(all_rows, model_dim),)
    inputs_all = x_all.astype(FULL)
    hidden_one = (inputs_all * rms_scale(inputs_all) * gain_attn).astype(LOW)
    projected = jnp.dot(hidden_one, qkv_here, preferred_element_type=FULL)
    query_rows = projected[:, :head_cols]
    key_rows = projected[:, head_cols : 2 * head_cols]
    value_rows = projected[:, 2 * head_cols :]
    squares = jnp.stack(
        [jnp.sum(query_rows * query_rows, axis=-1), jnp.sum(key_rows * key_rows, axis=-1)]
    ).reshape(2 * line_count, row_count)
    (squares,) = exchange("expert", line_count, [squares], [True], 4)
    squares = jnp.sum(squares, axis=0).reshape(2, all_rows, 1)
    scale_query = lax.rsqrt(squares[0] / model_dim + NORM_EPS)
    scale_key = lax.rsqrt(squares[1] / model_dim + NORM_EPS)
    normed_query = query_rows * scale_query
    normed_key = key_rows * scale_key
    head_shape = (line_count, row_count, heads_here, head_size)
    query_rot = rotary((normed_query * gain_query).reshape(head_shape), 1.0).astype(LOW)
    key_rot = rotary((normed_key * gain_key).reshape(head_shape), 1.0).astype(LOW)
    value_low = value_rows.reshape(head_shape).astype(LOW)
    position = jnp.arange(row_count)
    allowed = (position[:, None] >= position[None, :])[None] & (
        segments_all[:, :, None] == segments_all[:, None, :]
    )
    scores = einsum("gqhd,gkhd->ghqk", query_rot, key_rot) * scaling
    scores = jnp.where(allowed[:, None], scores, -1e30)
    expanded = jnp.exp(scores - jnp.max(scores, axis=-1, keepdims=True))
    attn = expanded / jnp.sum(expanded, axis=-1, keepdims=True)
    attn_low = attn.astype(LOW)
    attended = einsum("ghqk,gkhd->gqhd", attn_low, value_low).astype(LOW)
    attended = attended.reshape(line_count, row_count, head_cols)
    (own_attended,) = exchange("expert", line_count, [attended], [False], 5)
    own_attended = own_attended.transpose(1, 0, 2).reshape(row_count, model_dim)
    inputs = layer_input.astype(FULL)
    scale_attn = rms_scale(inputs)
    normed_attn = inputs * scale_attn
    residual = inputs + jnp.dot(own_attended, out_full, preferred_element_type=FULL)
    scale_mlp = rms_scale(residual)
    normed_mlp = residual * scale_mlp
    hidden_two = (normed_mlp * gain_mlp).astype(LOW)

    logits = jnp.dot(hidden_two, router_full, preferred_element_type=FULL)
    chosen = jnp.any(routes[:, :, None] == jnp.arange(expert_count)[None, None, :], axis=1)
    masked = jnp.where(chosen, logits, -1e30)
    powers = jnp.where(chosen, jnp.exp(masked - jnp.max(masked, axis=-1, keepdims=True)), 0.0)
    gates = powers / jnp.sum(powers, axis=-1, keepdims=True)

    h_all, gates_all = line_gather(line_count, [hidden_two, gates.T], [4, 1], 6)
    (dy_all,) = line_gather(line_count, [out_cotangent], [4], 7)
    local = place * local_count + jnp.arange(local_count)
    used = jnp.any(routes_all[:, None] == local[None, :, None, None], axis=2)
    lower = (position[:, None] < position[None, :]).astype(LOW)
    rank = einsum("gju,ut->gjt", used.astype(LOW), lower).astype(jnp.int32)
    rank = jnp.where(used, rank, -1)
    table = (rank[:, :, None, :] == jnp.arange(capacity)[None, None, :, None]).astype(LOW)
    local_gates = lax.dynamic_slice_in_dim(gates_all, place * local_count, local_count, axis=1)
    slot_gates = jnp.sum(table.astype(FULL) * local_gates[:, :, None, :], axis=-1)
    slots = line_count * capacity
    slot_gates = slot_gates.transpose(1, 0, 2).reshape(local_count, slots, 1)

    def place_rows(rows):
        return jnp.stack(
            [
                einsum("gst,gtd->gsd", table[:, j], rows).astype(LOW).reshape(slots, model_dim)
                for j in range(local_count)
            ]
        )

    def collect(rows, weights):
        return sum(
            einsum(
                "gst,gsd->gtd", weights[:, j], rows[j].reshape(line_count, capacity, model_dim)
            )
            for j in range(local_count)
        ).astype(LOW)

    expert_rows = place_rows(h_all)
    dy_rows = place_rows(dy_all).astype(FULL)
    hidden = einsum("erd,edf->erf", expert_rows, w_gate_up)
    hidden_size = hidden.shape[2] // 2
    gate_part = hidden[..., :hidden_size]
    up_part = hidden[..., hidden_size:]
    sigmoid_gate = jax.nn.sigmoid(gate_part)
    silu_gate = gate_part * sigmoid_gate
    activated = (silu_gate * up_part).astype(LOW)
    expert_out = einsum("erf,efd->erd", activated, w_down).astype(LOW)
    grad_expert_out = (slot_gates * dy_rows).astype(LOW)
    grad_w_down = einsum("erf,erd->efd", activated, grad_expert_out).astype(LOW)
    sum_down = lax.psum_scatter(grad_w_down, "dp", scatter_dimension=1, tiled=True)
    grad_act = einsum("erd,efd->erf", grad_expert_out, w_down)
    grad_gate = grad_act * up_part * sigmoid_gate * (1.0 + gate_part * (1.0 - sigmoid_gate))
    grad_hidden = jnp.concatenate([grad_gate, grad_act * silu_gate], axis=-1).astype(LOW)
    grad_w_gate_up = einsum("erd,erf->edf", expert_rows, grad_hidden).astype(LOW)
    sum_gate_up = lax.psum_scatter(grad_w_gate_up, "dp", scatter_dimension=1, tiled=True)
    grad_rows = einsum("erf,edf->erd", grad_hidden, w_gate_up).astype(LOW)
    slot_grads = jnp.sum(expert_out.astype(FULL) * dy_rows, axis=-1)
    slot_grads = slot_grads.reshape(local_count, line_count, capacity)
    grad_gates = jnp.sum(
        table.astype(FULL) * slot_grads.transpose(1, 0, 2)[:, :, :, None], axis=2
    )
    (grad_gates,) = exchange("expert", line_count, [grad_gates], [False], 8)
    grad_gates = grad_gates.reshape(expert_count, row_count).T
    grad_two = line_reduce(line_count, collect(grad_rows, table), 4, 9).astype(FULL)
    weighted_table = table * local_gates[:, :, None, :].astype(LOW)
    mixture = line_reduce(line_count, collect(expert_out, weighted_table), 4, 10).astype(FULL)
    output = (residual + mixture).astype(LOW)

    grad_out_rows = out_cotangent.astype(FULL)
    grad_logits = gates * (grad_gates - jnp.sum(gates * grad_gates, axis=-1, keepdims=True))
    grad_logits = grad_logits.astype(LOW)
    grad_router = contract_rows(grad_logits, hidden_two)
    grad_two = grad_two + contract_cols(grad_logits, router_full)
    grad_gain_mlp = jnp.sum(grad_two * normed_mlp, axis=0)
    grad_resid = grad_out_rows + norm_back(grad_two * gain_mlp, normed_mlp, scale_mlp)
    grad_attn = grad_resid.astype(LOW)

    (grad_attn_all,) = line_gather(line_count, [grad_attn], [4], 11)
    grad_attn_all = grad_attn_all.reshape(all_rows, model_dim)
    out_here = lax.dynamic_slice_in_dim(out_full, place * head_cols, head_cols, axis=0)
    grad_w_out = contract_rows(attended.reshape(all_rows, head_cols), grad_attn_all)
    grad_attended = contract_cols(grad_attn_all, out_here).astype(LOW).reshape(head_shape)
    grad_value = einsum("ghqk,gqhd->gkhd", attn_low, grad_attended)
    grad_weights = einsum("gqhd,gkhd->ghqk", grad_attended, value_low)
    row_delta = jnp.sum(grad_weights * attn, axis=-1, keepdims=True)
    grad_scores = (attn * (grad_weights - row_delta)).astype(LOW)
    grad_query_rot = einsum("ghqk,gkhd->gqhd", grad_scores, key_rot) * scaling
    grad_key_rot = einsum("ghqk,gqhd->gkhd", grad_scores, query_rot) * scaling
    grad_query_normed = rotary(grad_query_rot, -1.0).reshape(all_rows, head_cols)
    grad_key_normed = rotary(grad_key_rot, -1.0).reshape(all_rows, head_cols)
    gain_pair = jnp.stack(
        [
            jnp.sum(grad_query_normed * normed_query, axis=0),
            jnp.sum(grad_key_normed * normed_key, axis=0),
        ]
    )
    weighted_query = grad_query_normed * gain_query
    weighted_key = grad_key_normed * gain_key
    dots = jnp.stack(
        [
            jnp.sum(weighted_query * normed_query, axis=-1),
            jnp.sum(weighted_key * normed_key, axis=-1),
        ]
    ).reshape(2 * line_count, row_count)
    (dots,) = exchange("expert", line_count, [dots], [True], 12)
    dots = jnp.sum(dots, axis=0).reshape(2, all_rows, 1) / model_dim
    grad_query = scale_query * (weighted_query - normed_query * dots[0])
    grad_key = scale_key * (weighted_key - normed_key * dots[1])
    grad_proj = jnp.concatenate(
        [grad_query, grad_key, grad_value.reshape(all_rows, head_cols)], axis=-1
    ).astype(LOW)
    grad_one = contract_cols(grad_proj, qkv_here).astype(LOW)
    grad_one = line_reduce(
        line_count, grad_one.reshape(line_count, row_count, model_dim), 4, 13
    ).astype(FULL)
    grad_w_qkv = contract_rows(hidden_one, grad_proj)
    grad_gain_attn = jnp.sum(grad_one * normed_attn, axis=0)
    grad_inputs = grad_resid + norm_back(grad_one * gain_attn, normed_attn, scale_attn)

    out_cols = model_dim // dp_count
    qkv_parts = grad_w_qkv.astype(LOW).reshape(dp_count, out_cols, 3 * head_cols)
    out_parts = grad_w_out.astype(LOW).reshape(head_cols, dp_count, out_cols).transpose(1, 0, 2)
    qkv_parts, out_parts, gain_pair = exchange(
        "dp", dp_count, [qkv_parts, out_parts, gain_pair], [False, False, True], 14
    )
    sum_qkv = jnp.sum(qkv_parts.astype(FULL), axis=0).reshape(out_cols, 3, head_cols)
    sum_out = jnp.sum(out_parts.astype(FULL), axis=0)
    gain_pair = jnp.sum(gain_pair, axis=0)
    shared = jnp.concatenate([grad_router, grad_gain_attn[None], grad_gain_mlp[None]], axis=0)
    kinds = shared.shape[0]
    shared = jnp.pad(shared, ((0, -kinds % 8), (0, 0)))
    tall = shared.shape[0]
    shared = shared.reshape(tall, dp_count, line_count, shard).transpose(2, 0, 1, 3)
    shared = shared.reshape(line_count, tall, dp_count * shard)
    (shared,) = exchange("expert", line_count, [shared], [False], 15)
    shared = jnp.sum(shared, axis=0).reshape(tall, dp_count, shard).transpose(1, 0, 2)
    (shared,) = exchange("dp", dp_count, [shared], [False], 16)
    shared = jnp.sum(shared, axis=0)
    return (
        output,
        grad_inputs,
        sum_qkv,
        sum_out,
        shared[:expert_count].T,
        shared[expert_count],
        shared[expert_count + 1],
        gain_pair[0],
        gain_pair[1],
        sum_gate_up.astype(FULL),
        sum_down.astype(FULL),
    )


def solution(mesh):
    both = ("dp", "expert")
    rows, flat = P(both, None), P(both)
    placed = (rows,) * 7 + (flat,) * 4 + (P("expert", None, None),) * 2
    return jax.shard_map(
        functools.partial(on_device, mesh.shape["dp"], mesh.shape["expert"]),
        mesh=mesh,
        in_specs=placed,
        out_specs=(
            rows,
            rows,
            P("dp", None, "expert"),
            P("expert", "dp"),
            rows,
            flat,
            flat,
            P("expert"),
            P("expert"),
            P("expert", "dp", None),
            P("expert", "dp", None),
        ),
        check_vma=False,
    )
```

```python
import functools
import math

import jax
import jax.numpy as jnp
from jax import lax
from jax.experimental import pallas as pl
from jax.experimental.pallas import tpu as pltpu
from jax.sharding import PartitionSpec as P

HEADS = 16
NORM_EPS = 1e-05
MESH = pl.DeviceIdType.MESH
ANY = pl.BlockSpec(memory_space=pl.ANY)
LOW = jnp.bfloat16
FULL = jnp.float32


def line_place():
    place = lax.axis_index("expert")
    level, side = lax.div(place, 2), lax.rem(place, 2)
    return place, level, side, place + 1 - 2 * side


def greet(axis, targets):
    barrier = pltpu.get_barrier_semaphore()
    for target, there in targets:

        def signal(target=target):
            pl.semaphore_signal(barrier, inc=1, device_id={axis: target}, device_id_type=MESH)

        if there is None:
            signal()
        else:
            pl.when(there)(signal)


def line_barrier(levels):
    place, level, _, other = line_place()
    has_up, has_down = level < levels - 1, level > 0
    greet("expert", [(other, None), (place + 2, has_up), (place - 2, has_down)])
    count = 1 + has_up.astype(jnp.int32) + has_down.astype(jnp.int32)
    pl.semaphore_wait(pltpu.get_barrier_semaphore(), count)


def around(axis, size):
    place = lax.axis_index(axis)
    return [lax.rem(place + shift, size) for shift in range(1, size)]


def remote(source, target, send, recv, device):
    return pltpu.make_async_remote_copy(
        src_ref=source,
        dst_ref=target,
        send_sem=send,
        recv_sem=recv,
        device_id=device,
        device_id_type=MESH,
    )


class LineGather:
    def __init__(self, levels, cuts, ins, outs, up_sem, down_sem, side_sem, recv_sem, own_sem):
        self.levels, self.cuts, self.ins, self.outs = levels, cuts, ins, outs
        self.up_sem, self.down_sem, self.side_sem = up_sem, down_sem, side_sem
        self.recv_sem = recv_sem
        self.pieces = [(i, k) for i in range(len(cuts)) for k in range(cuts[i])]
        self.place, self.level, self.side, self.other = line_place()
        self.has_up, self.has_down = self.level < levels - 1, self.level > 0
        self.own = [
            pltpu.make_async_copy(ins[i], outs[i].at[self.place], own_sem.at[i])
            for i in range(len(cuts))
        ]

    @staticmethod
    def scratch(size, cuts):
        levels, total = size // 2, sum(cuts)
        shapes = ((levels, total), (levels, total), (2 * levels - 1, total), (size, total))
        return [pltpu.SemaphoreType.DMA(shape) for shape in shapes + ((len(cuts),),)]

    def part(self, ref, i, k):
        rows = self.ins[i].shape[0] // self.cuts[i]
        return ref.at[pl.ds(k * rows, rows)]

    def sending(self, q, block, own, sem, target):
        i, k = self.pieces[q]
        landing = self.part(self.outs[i].at[block], i, k)
        source = self.part(self.ins[i], i, k) if own else landing
        return remote(source, landing, sem, self.recv_sem.at[block, q], {"expert": target})

    def up(self, q, step):
        block = self.place - 2 * step
        return self.sending(q, block, step == 0, self.up_sem.at[step, q], self.place + 2)

    def down(self, q, step):
        block = self.place + 2 * step
        return self.sending(q, block, step == 0, self.down_sem.at[step, q], self.place - 2)

    def across(self, q, step):
        sem = self.side_sem.at[step + self.levels - 1, q]
        return self.sending(q, self.place - 2 * step, step == 0, sem, self.other)

    def begin(self):
        for q in range(len(self.pieces)):
            pl.when(self.has_up)(self.up(q, 0).start)
            pl.when(self.has_down)(self.down(q, 0).start)
        for q in range(len(self.pieces)):
            self.across(q, 0).start()
        for copy in self.own:
            copy.start()

    def forward(self, step, q):
        @pl.when(self.level >= step)
        def _():
            self.across(q, step).wait_recv()
            pl.when(self.has_up)(self.up(q, step).start)
            self.across(q, step).start()

        @pl.when(self.level + step < self.levels)
        def _():
            self.across(q, -step).wait_recv()
            pl.when(self.has_down)(self.down(q, step).start)
            self.across(q, -step).start()

    def finish(self):
        for q in range(len(self.pieces)):
            for far in range(self.levels):
                block = 2 * far + 1 - self.side
                self.sending(q, block, False, self.side_sem.at[0, q], self.other).wait_recv()
            self.across(q, 0).wait_send()
            for step in range(self.levels):
                above, below = self.level >= step, self.level + step < self.levels
                pl.when(self.has_up & above)(self.up(q, step).wait_send)
                pl.when(self.has_down & below)(self.down(q, step).wait_send)
                if step:
                    pl.when(above)(self.across(q, step).wait_send)
                    pl.when(below)(self.across(q, -step).wait_send)
        for copy in self.own:
            copy.wait()

    def run(self):
        self.begin()
        for step in range(1, self.levels):
            for q in range(len(self.pieces)):
                self.forward(step, q)
        self.finish()


def line_gather_kernel(levels, cuts, *refs):
    count = len(cuts)
    line = LineGather(levels, cuts, refs[:count], refs[count : 2 * count], *refs[2 * count :])
    line_barrier(levels)
    line.run()


def call(kernel, name, number, outs, scratch, arrays, moved):
    return pl.pallas_call(
        kernel,
        out_shape=outs,
        in_specs=[ANY] * len(arrays),
        out_specs=[ANY] * len(outs),
        scratch_shapes=scratch,
        compiler_params=pltpu.CompilerParams(
            collective_id=number, has_side_effects=True, vmem_limit_bytes=48 << 20
        ),
        cost_estimate=pl.CostEstimate(flops=0, transcendentals=0, bytes_accessed=moved),
        name=name,
    )(*arrays)


def line_gather(size, arrays, cuts, number):
    return call(
        functools.partial(line_gather_kernel, size // 2, tuple(cuts)),
        "line_gather",
        number,
        [jax.ShapeDtypeStruct((size,) + a.shape, a.dtype) for a in arrays],
        LineGather.scratch(size, cuts),
        arrays,
        150_000_000,
    )


class LineReduce:
    def __init__(self, levels, cuts, parts, total, own, beside, rising, falling, *sems):
        self.levels, self.cuts, self.parts, self.total = levels, cuts, parts, total
        self.own, self.beside, self.rising, self.falling = own, beside, rising, falling
        self.load_sem, self.side_send, self.side_recv = sems[:3]
        self.up_send, self.up_recv, self.down_send, self.down_recv, self.out_sem = sems[3:]
        self.place, self.level, self.side, self.other = line_place()
        self.has_up, self.has_down = self.level < levels - 1, self.level > 0
        self.rows = parts.shape[1] // cuts
        self.order = []
        for step in range(levels):
            for far in (levels - 1 - step, step):
                if far not in self.order:
                    self.order.append(far)

    @staticmethod
    def scratch(size, block, dtype, cuts):
        levels = size // 2
        return (
            [pltpu.VMEM((levels,) + block, dtype)] * 4
            + [pltpu.SemaphoreType.DMA((levels, cuts))] * 7
            + [pltpu.SemaphoreType.DMA((cuts,))]
        )

    def cut(self, ref, block, k):
        return ref.at[block, pl.ds(k * self.rows, self.rows)]

    def loading(self, far, k):
        source = self.cut(self.parts, 2 * far + self.side, k)
        return pltpu.make_async_copy(source, self.cut(self.own, far, k), self.load_sem.at[far, k])

    def across(self, far, k):
        source = self.cut(self.parts, 2 * far + 1 - self.side, k)
        sems = self.side_send.at[far, k], self.side_recv.at[far, k]
        return remote(source, self.cut(self.beside, far, k), *sems, {"expert": self.other})

    def up(self, far, k):
        sems = self.up_send.at[far, k], self.up_recv.at[far, k]
        target = {"expert": self.place + 2}
        return remote(self.cut(self.own, far, k), self.cut(self.rising, far, k), *sems, target)

    def down(self, far, k):
        sems = self.down_send.at[far, k], self.down_recv.at[far, k]
        target = {"expert": self.place - 2}
        return remote(self.cut(self.own, far, k), self.cut(self.falling, far, k), *sems, target)

    def value(self, ref, block, k):
        return self.cut(ref, block, k)[...].astype(FULL)

    def load(self):
        for far in self.order:
            for k in range(self.cuts):
                self.loading(far, k).start()

    def begin(self):
        for far in self.order:
            for k in range(self.cuts):
                self.across(far, k).start()

    def pair(self, far, k):
        self.loading(far, k).wait()
        self.across(far, k).wait_recv()
        return self.value(self.own, far, k) + self.value(self.beside, far, k)

    def store(self, far, k, total):
        self.cut(self.own, far, k)[...] = total.astype(self.own.dtype)

    def toward(self, far, k, ahead, behind, move, arrived):
        @pl.when(ahead & behind)
        def _():
            both = self.pair(far, k)
            move(far, k).wait_recv()
            self.store(far, k, both + self.value(arrived, far, k))

        @pl.when(ahead & jnp.logical_not(behind))
        def _():
            self.store(far, k, self.pair(far, k))

        pl.when(ahead)(move(far, k).start)

    def main(self, beside=None):
        for step in range(self.levels - 1):
            high, low = self.levels - 1 - step, step
            for k in range(self.cuts):
                if beside:
                    beside(step * self.cuts + k)
                self.toward(high, k, self.level < high, self.has_down, self.up, self.rising)
                self.toward(low, k, self.level > low, self.has_up, self.down, self.falling)
        for k in range(self.cuts):
            self.store(self.level, k, self.pair(self.level, k))
            for there, move, arrived in (
                (self.has_down, self.up, self.rising),
                (self.has_up, self.down, self.falling),
            ):

                @pl.when(there)
                def _():
                    move(self.level, k).wait_recv()
                    total = self.value(self.own, self.level, k) + self.value(arrived, self.level, k)
                    self.store(self.level, k, total)

            self.leaving(k).start()

    def leaving(self, k):
        target = self.total.at[pl.ds(k * self.rows, self.rows)]
        return pltpu.make_async_copy(self.cut(self.own, self.level, k), target, self.out_sem.at[k])

    def finish(self):
        for k in range(self.cuts):
            self.leaving(k).wait()
            for far in range(self.levels):
                self.across(far, k).wait_send()
                pl.when(self.level < far)(self.up(far, k).wait_send)
                pl.when(self.level > far)(self.down(far, k).wait_send)


def line_reduce_kernel(levels, cuts, *refs):
    line = LineReduce(levels, cuts, *refs)
    line.load()
    line_barrier(levels)
    line.begin()
    line.main()
    line.finish()


def line_reduce(size, parts, cuts, number):
    block = parts.shape[1:]
    return call(
        functools.partial(line_reduce_kernel, size // 2, cuts),
        "line_reduce",
        number,
        [jax.ShapeDtypeStruct(block, parts.dtype)],
        LineReduce.scratch(size, block, parts.dtype, cuts),
        [parts],
        150_000_000,
    )[0]


class Exchange:
    def __init__(self, axis, size, spread, cuts, ins, outs, send_sem, recv_sem, own_sem):
        self.axis, self.spread, self.ins, self.outs = axis, spread, ins, outs
        self.send_sem, self.recv_sem, self.own_sem = send_sem, recv_sem, own_sem
        self.cuts = cuts
        self.firsts = [sum(cuts[:i]) for i in range(len(cuts))]
        self.pieces = [(i, k) for i in range(len(cuts)) for k in range(cuts[i])]
        self.place, self.peers = lax.axis_index(axis), around(axis, size)

    @staticmethod
    def scratch(size, cuts):
        sems = pltpu.SemaphoreType.DMA
        return [sems((sum(cuts), size)), sems((sum(cuts), size)), sems((len(cuts),))]

    def source(self, i, block):
        return self.ins[i] if self.spread[i] else self.ins[i].at[block]

    def staying(self, i):
        target = self.outs[i].at[self.place]
        return pltpu.make_async_copy(self.source(i, self.place), target, self.own_sem.at[i])

    def sending(self, i, k, shift, landing):
        peer = self.peers[shift]
        source, target, q = self.source(i, peer), self.outs[i].at[landing], self.firsts[i] + k
        if self.cuts[i] > 1:
            rows = target.shape[0] // self.cuts[i]
            source, target = source.at[pl.ds(k * rows, rows)], target.at[pl.ds(k * rows, rows)]
        sems = self.send_sem.at[q, shift], self.recv_sem.at[q, landing]
        return remote(source, target, *sems, {self.axis: peer})

    def send(self, i, k):
        for shift in range(len(self.peers)):
            self.sending(i, k, shift, self.place).start()

    def stay(self):
        for i in range(len(self.spread)):
            self.staying(i).start()

    def begin(self):
        for i, k in self.pieces:
            self.send(i, k)
        self.stay()

    def land(self):
        for shift, peer in enumerate(self.peers):
            for i, k in self.pieces:
                self.sending(i, k, shift, peer).wait_recv()

    def arrive(self):
        self.land()
        for i in range(len(self.spread)):
            self.staying(i).wait()

    def finish(self):
        for shift in range(len(self.peers)):
            for i, k in self.pieces:
                self.sending(i, k, shift, self.place).wait_send()


def exchange_kernel(axis, size, spread, *refs):
    count = len(spread)
    ins, outs, sems = refs[:count], refs[count : 2 * count], refs[2 * count :]
    moves = Exchange(axis, size, spread, (1,) * count, ins, outs, *sems)
    greet(axis, [(peer, None) for peer in moves.peers])
    pl.semaphore_wait(pltpu.get_barrier_semaphore(), size - 1)
    moves.begin()
    moves.arrive()
    moves.finish()


def exchange_outs(size, arrays, spread):
    return [
        jax.ShapeDtypeStruct((size,) + a.shape if flat else a.shape, a.dtype)
        for a, flat in zip(arrays, spread)
    ]


def exchange(axis, size, arrays, spread, number):
    return call(
        functools.partial(exchange_kernel, axis, size, tuple(spread)),
        "exchange_" + axis,
        number,
        exchange_outs(size, arrays, spread),
        Exchange.scratch(size, (1,) * len(arrays)),
        arrays,
        30_000_000,
    )


def opening_kernel(size, dp_count, cuts, *refs):
    count = len(cuts)
    ins, w_ref, small_ref = refs[:count], refs[count], refs[count + 1]
    outs, w_out, small_out = refs[count + 2 : 2 * count + 2], refs[2 * count + 2], refs[2 * count + 3]
    line_sems, rest = refs[2 * count + 4 : 2 * count + 9], refs[2 * count + 9 :]
    send_sem, recv_sem, own_sem = rest[:3]
    line = LineGather(size // 2, cuts, ins, outs, *line_sems)
    place, mine = line.place, lax.axis_index("dp")
    peers = around("expert", size)
    width = w_out.shape[3] // 3
    mine_refs = [w_out.at[mine], small_out.at[mine]]
    across = Exchange("dp", dp_count, (True,) * 2, (size,) * 2, mine_refs, [w_out, small_out], *rest[3:])
    greet("expert", [(peer, None) for peer in peers])
    greet("dp", [(peer, None) for peer in across.peers])
    pl.semaphore_wait(pltpu.get_barrier_semaphore(), size + dp_count - 2)

    def ends(peer, landing, j):
        if j == 3:
            return small_ref, small_out.at[mine, landing]
        start = pl.multiple_of(j * width * size + peer * width, 128)
        target = w_out.at[mine, landing, :, pl.ds(j * width, width)]
        return w_ref.at[:, pl.ds(start, width)], target

    def sending(shift, landing, j):
        source, target = ends(peers[shift], landing, j)
        sems = send_sem.at[shift, j], recv_sem.at[landing, j]
        return remote(source, target, *sems, {"expert": peers[shift]})

    own = [pltpu.make_async_copy(*ends(place, place, j), own_sem.at[j]) for j in range(4)]
    for shift in range(size - 1):
        for j in range(4):
            sending(shift, place, j).start()
    for copy in own:
        copy.start()
    line.begin()
    for copy in own:
        copy.wait()
    across.send(0, place)
    across.send(1, place)
    for shift, peer in enumerate(peers):
        for j in range(4):
            sending(shift, peer, j).wait_recv()
        across.send(0, peer)
        across.send(1, peer)
    for step in range(1, size // 2):
        for q in range(len(line.pieces)):
            line.forward(step, q)
    line.finish()
    for shift in range(size - 1):
        for j in range(4):
            sending(shift, place, j).wait_send()
    across.land()
    across.finish()


def opening(size, dp_count, arrays, cuts, weights, small, number):
    sems = pltpu.SemaphoreType.DMA
    outs = [jax.ShapeDtypeStruct((size,) + a.shape, a.dtype) for a in arrays]
    rows, columns = weights.shape
    whole = (dp_count, size, rows)
    outs.append(jax.ShapeDtypeStruct(whole + (columns // size,), weights.dtype))
    outs.append(jax.ShapeDtypeStruct(whole + (small.shape[1],), small.dtype))
    return call(
        functools.partial(opening_kernel, size, dp_count, tuple(cuts)),
        "opening",
        number,
        outs,
        LineGather.scratch(size, cuts)
        + [sems((size, 4)), sems((size, 4)), sems((4,))]
        + Exchange.scratch(dp_count, (size, size)),
        list(arrays) + [weights, small],
        200_000_000,
    )


def closing_kernel(size, dp_count, cuts, sum_cuts, *refs):
    ins, outs, rest = refs[:5], refs[5:10], refs[10:]
    line = LineReduce(size // 2, cuts, ins[0], outs[0], *rest[:12])
    sums = Exchange("dp", dp_count, (False, False, True), sum_cuts, ins[1:4], outs[1:4], *rest[12:15])
    got, half, last = rest[15:18]
    first = Exchange("expert", size, (False,), (1,), ins[4:5], [got], *rest[18:21])
    second = Exchange("dp", dp_count, (False,), (1,), [half], [last], *rest[21:24])
    line.load()
    greet("expert", [(peer, None) for peer in first.peers])
    greet("dp", [(peer, None) for peer in sums.peers])
    pl.semaphore_wait(pltpu.get_barrier_semaphore(), size + dp_count - 2)
    first.begin()
    line.begin()
    sums.stay()
    turns = (size // 2 - 1) * cuts
    tall = half.shape[1]

    def beside(turn):
        for q in range(len(sums.pieces)):
            if q * turns // len(sums.pieces) == turn:
                sums.send(*sums.pieces[q])
        if turn == turns // 2:
            first.arrive()
            for copy in range(dp_count):
                rows = pl.ds(copy * tall, tall)
                half[copy] = sum(got[i, rows, :] for i in range(size))
            second.begin()

    line.main(beside)
    second.arrive()
    outs[4][...] = sum(last[i] for i in range(dp_count))
    sums.arrive()
    for moves in (line, first, second, sums):
        moves.finish()


def closing(size, dp_count, parts, cuts, sums, shared, number):
    block = parts.shape[1:]
    tall = shared.shape[1] // dp_count
    wide = shared.shape[2]
    vmem = pl.BlockSpec(memory_space=pltpu.VMEM)
    sum_cuts = (8, 2, 1)
    outs = [jax.ShapeDtypeStruct(block, parts.dtype)]
    outs += exchange_outs(dp_count, sums, (False, False, True))
    outs.append(jax.ShapeDtypeStruct((tall, wide), FULL))
    return pl.pallas_call(
        functools.partial(closing_kernel, size, dp_count, cuts, sum_cuts),
        out_shape=outs,
        in_specs=[ANY] * 5,
        out_specs=[ANY] * 4 + [vmem],
        scratch_shapes=LineReduce.scratch(size, block, parts.dtype, cuts)
        + Exchange.scratch(dp_count, sum_cuts)
        + [pltpu.VMEM((size,) + shared.shape[1:], FULL)]
        + [pltpu.VMEM((dp_count, tall, wide), FULL)] * 2
        + Exchange.scratch(size, (1,))
        + Exchange.scratch(dp_count, (1,)),
        compiler_params=pltpu.CompilerParams(
            collective_id=number, has_side_effects=True, vmem_limit_bytes=48 << 20
        ),
        cost_estimate=pl.CostEstimate(flops=0, transcendentals=0, bytes_accessed=200_000_000),
        name="closing",
    )(parts, *sums, shared)


def rows_kernel(local_count, table_ref, rows_ref, out_ref):
    capacity = out_ref.shape[1]
    placed = jnp.dot(table_ref[0], rows_ref[0], preferred_element_type=FULL)
    for j in range(local_count):
        out_ref[j] = placed[j * capacity : (j + 1) * capacity].astype(LOW)


def place_rows(table, rows, local_count):
    groups, slots, tokens = table.shape
    width = rows.shape[2]
    capacity = slots // local_count
    return pl.pallas_call(
        functools.partial(rows_kernel, local_count),
        out_shape=jax.ShapeDtypeStruct((local_count, groups * capacity, width), LOW),
        grid=(groups,),
        in_specs=[
            pl.BlockSpec((1, slots, tokens), lambda g: (g, 0, 0)),
            pl.BlockSpec((1, tokens, width), lambda g: (g, 0, 0)),
        ],
        out_specs=pl.BlockSpec((local_count, capacity, width), lambda g: (0, g, 0)),
        cost_estimate=pl.CostEstimate(
            flops=2 * table.size * width, transcendentals=0, bytes_accessed=4 * rows.size
        ),
        name="place_rows",
    )(table, rows)


def collect_kernel(*refs):
    tables, rows_refs, out_ref = refs[: len(refs) // 2], refs[len(refs) // 2 : -1], refs[-1]
    total = 0.0
    for table_ref, rows_ref in zip(tables, rows_refs):
        total += jnp.dot(table_ref[0], rows_ref[0], preferred_element_type=FULL)
    out_ref[0] = total.astype(LOW)


def collect(tables, rows):
    groups, tokens, capacity = tables[0].shape
    width = rows[0].shape[2]
    return pl.pallas_call(
        collect_kernel,
        out_shape=jax.ShapeDtypeStruct((groups, tokens, width), LOW),
        grid=(groups,),
        in_specs=[pl.BlockSpec((1, tokens, capacity), lambda g: (g, 0, 0))] * len(rows)
        + [pl.BlockSpec((1, capacity, width), lambda g: (0, g, 0))] * len(rows),
        out_specs=pl.BlockSpec((1, tokens, width), lambda g: (g, 0, 0)),
        cost_estimate=pl.CostEstimate(
            flops=2 * len(rows) * tables[0].size * width,
            transcendentals=0,
            bytes_accessed=4 * groups * tokens * width,
        ),
        name="collect",
    )(*tables, *rows)


def across_cols(left_side, right_side):
    return lax.dot_general(
        left_side, right_side, (((1,), (1,)), ((), ())), preferred_element_type=FULL
    )


def expert_kernel(
    tiles,
    x_ref,
    dy_ref,
    scale_ref,
    gate_ref,
    up_ref,
    down_ref,
    grads_ref,
    out_ref,
    back_ref,
    dots_ref,
    turned,
    weighted,
    out_sum,
    back_sum,
    side_buf,
    down_buf,
    sems,
):
    tile = pl.program_id(0)
    slot = lax.rem(tile, 2)
    width = gate_ref.shape[2]
    copies, high = side_buf.shape[2], side_buf.shape[3]
    some, low = down_buf.shape[1], down_buf.shape[2]
    hidden = tiles * width

    def leaving(at, half, slot):
        columns = pl.ds(pl.multiple_of(half * hidden + at * width, 128), width)
        target = grads_ref.at[:, pl.ds(0, high), columns]
        return pltpu.make_async_copy(side_buf.at[slot, half], target, sems.at[slot, half])

    def leaving_down(at, slot):
        target = grads_ref.at[pl.ds(at * some, some), pl.ds(high, low), :]
        return pltpu.make_async_copy(down_buf.at[slot], target, sems.at[slot, 2])

    def settle(at, slot):
        leaving(at, 0, slot).wait()
        leaving(at, 1, slot).wait()
        leaving_down(at, slot).wait()

    @pl.when(tile == 0)
    def _():
        turned[...] = x_ref[0].T
        weighted[...] = (scale_ref[0] * dy_ref[0].astype(FULL)).astype(LOW)
        out_sum[...] = jnp.zeros_like(out_sum)
        back_sum[...] = jnp.zeros_like(back_sum)

    @pl.when(tile >= 2)
    def _():
        settle(tile - 2, slot)

    rows, grads = x_ref[0], weighted[...]
    w_gate, w_up, w_down = gate_ref[0], up_ref[0], down_ref[0]
    gate = jnp.dot(rows, w_gate, preferred_element_type=FULL)
    up = jnp.dot(rows, w_up, preferred_element_type=FULL)
    sigmoid = jax.nn.sigmoid(gate)
    silu = gate * sigmoid
    act = (silu * up).astype(LOW)
    out_sum[...] += jnp.dot(act, w_down, preferred_element_type=FULL)
    grad_act = across_cols(grads, w_down)
    grad_gate = (grad_act * up * sigmoid * (1.0 + gate * (1.0 - sigmoid))).astype(LOW)
    grad_up = (grad_act * silu).astype(LOW)
    back_sum[...] += across_cols(grad_gate, w_gate) + across_cols(grad_up, w_up)
    turned_rows = turned[...]
    for half, grad in enumerate((grad_gate, grad_up)):
        total = jnp.dot(turned_rows, grad, preferred_element_type=FULL).astype(LOW)
        side_buf[slot, half] = total.reshape(copies, high, width)
        leaving(tile, half, slot).start()
    total = jnp.dot(act.T, grads, preferred_element_type=FULL).astype(LOW)
    down_buf[slot] = total.reshape(some, low, total.shape[1])
    leaving_down(tile, slot).start()

    @pl.when(tile == tiles - 1)
    def _():
        final = out_sum[...]
        dots_ref[0] = jnp.sum(final * dy_ref[0].astype(FULL), axis=-1, keepdims=True)
        out_ref[0] = (scale_ref[0] * final).astype(LOW)
        back_ref[0] = back_sum[...].astype(LOW)
        settle(tile - 1, 1 - slot)
        settle(tile, slot)


def expert(j, dp_count, x_rows, dy_rows, scales, w_gate_up, w_down, tiles=4):
    _, slots, width = x_rows.shape
    hidden = w_down.shape[1]
    tile = hidden // tiles
    high, low = width // dp_count, hidden // dp_count
    some = tile // low
    once = pl.Buffered(1)
    row_spec = pl.BlockSpec((1, slots, width), lambda f: (j, 0, 0), pipeline_mode=once)
    out_spec = pl.BlockSpec((1, slots, width), lambda f: (0, 0, 0), pipeline_mode=once)
    return pl.pallas_call(
        functools.partial(expert_kernel, tiles),
        out_shape=[
            jax.ShapeDtypeStruct((dp_count, high + low, width), LOW),
            jax.ShapeDtypeStruct((1, slots, width), LOW),
            jax.ShapeDtypeStruct((1, slots, width), LOW),
            jax.ShapeDtypeStruct((1, slots, 1), FULL),
        ],
        grid=(tiles,),
        in_specs=[
            row_spec,
            row_spec,
            pl.BlockSpec((1, slots, 1), lambda f: (j, 0, 0), pipeline_mode=once),
            pl.BlockSpec((1, width, tile), lambda f: (j, 0, f)),
            pl.BlockSpec((1, width, tile), lambda f: (j, 0, tiles + f)),
            pl.BlockSpec((1, tile, width), lambda f: (j, f, 0)),
        ],
        out_specs=[
            ANY,
            out_spec,
            out_spec,
            pl.BlockSpec((1, slots, 1), lambda f: (0, 0, 0), pipeline_mode=once),
        ],
        scratch_shapes=[
            pltpu.VMEM((width, slots), LOW),
            pltpu.VMEM((slots, width), LOW),
            pltpu.VMEM((slots, width), FULL),
            pltpu.VMEM((slots, width), FULL),
            pltpu.VMEM((2, 2, dp_count, high, tile), LOW),
            pltpu.VMEM((2, some, low, width), LOW),
            pltpu.SemaphoreType.DMA((2, 3)),
        ],
        compiler_params=pltpu.CompilerParams(vmem_limit_bytes=60 << 20),
        cost_estimate=pl.CostEstimate(
            flops=18 * slots * width * hidden,
            transcendentals=slots * hidden,
            bytes_accessed=12 * width * hidden,
        ),
        name="expert",
    )(x_rows, dy_rows, scales, w_gate_up, w_gate_up, w_down)


def rms_scale(values):
    return lax.rsqrt(jnp.mean(values * values, axis=-1, keepdims=True) + NORM_EPS)


def rotary_tables(length, size):
    index = jnp.arange(size // 2, dtype=FULL)
    frequency = jnp.exp(index * (-2.0 * math.log(10000.0) / size))
    angles = jnp.arange(length, dtype=FULL)[:, None] * frequency[None, :]
    cosine, sine = jnp.cos(angles), jnp.sin(angles)
    return jnp.stack(
        [jnp.concatenate([cosine, cosine], axis=1), jnp.concatenate([-sine, sine], axis=1)]
    )


def norm_back(grad_normed, normed, scale_rows):
    return scale_rows * (
        grad_normed - normed * jnp.mean(grad_normed * normed, axis=-1, keepdims=True)
    )


def contract_rows(left_side, right_side):
    return lax.dot_general(
        left_side, right_side, (((0,), (0,)), ((), ())), preferred_element_type=FULL
    )


def contract_cols(left_side, right_side):
    return lax.dot_general(
        left_side, right_side, (((1,), (1,)), ((), ())), preferred_element_type=FULL
    )


def einsum(spec, left_side, right_side):
    return jnp.einsum(spec, left_side, right_side, preferred_element_type=FULL)


def turn(values, cosine, sine):
    return values * cosine + pltpu.roll(values, values.shape[1] // 2, 1) * sine


def allowed_pairs(column_ref, row_ref):
    shape = (column_ref.shape[1], row_ref.shape[2])
    later = lax.broadcasted_iota(jnp.int32, shape, 0) >= lax.broadcasted_iota(jnp.int32, shape, 1)
    return later & (column_ref[0] == row_ref[0])


def softmax(query, key, allowed):
    scores = across_cols(query, key) * (1.0 / math.sqrt(query.shape[1]))
    scores = jnp.where(allowed, scores, -1e30)
    powers = jnp.exp(scores - jnp.max(scores, axis=-1, keepdims=True))
    return powers / jnp.sum(powers, axis=-1, keepdims=True)


def attend_kernel(
    heads, rows_ref, scale_ref, gain_ref, turn_ref, column_ref, row_ref, kept_ref, out_ref
):
    width = out_ref.shape[2]
    size = width // heads
    allowed = allowed_pairs(column_ref, row_ref)
    cosine, sine = turn_ref[0], turn_ref[1]
    for h in range(heads):
        parts = []
        for part in range(3):
            columns = pl.ds(part * width + h * size, size)
            values = rows_ref[0, :, columns]
            if part < 2:
                values = values * scale_ref[0, :, part : part + 1]
                values = values * gain_ref[part : part + 1, h * size : (h + 1) * size]
                values = turn(values, cosine, sine)
            parts.append(values.astype(LOW))
            kept_ref[0, :, columns] = parts[-1]
        query, key, value = parts
        probs = softmax(query, key, allowed).astype(LOW)
        out_ref[0, :, pl.ds(h * size, size)] = jnp.dot(
            probs, value, preferred_element_type=FULL
        ).astype(LOW)


def block_of(array):
    rest = array.shape[1:]
    return pl.BlockSpec((1,) + rest, lambda g: (g,) + (0,) * len(rest))


def whole_of(array):
    return pl.BlockSpec(array.shape, lambda g: (0,) * array.ndim, pipeline_mode=pl.Buffered(1))


def attend(heads, rows, scales, gains, turns, column, row):
    groups, length, width = rows.shape
    kept = jax.ShapeDtypeStruct((groups, length, width), LOW)
    out = jax.ShapeDtypeStruct((groups, length, width // 3), LOW)
    return pl.pallas_call(
        functools.partial(attend_kernel, heads),
        out_shape=[kept, out],
        grid=(groups,),
        in_specs=[
            block_of(rows),
            block_of(scales),
            whole_of(gains),
            whole_of(turns),
            block_of(column),
            block_of(row),
        ],
        out_specs=[block_of(kept), block_of(out)],
        cost_estimate=pl.CostEstimate(
            flops=4 * groups * length * length * width, transcendentals=0, bytes_accessed=8 * rows.size
        ),
        name="attend",
    )(rows, scales, gains, turns, column, row)


def attend_back_kernel(
    heads,
    grad_ref,
    w_ref,
    kept_ref,
    out_ref,
    rows_ref,
    scale_ref,
    gain_ref,
    turn_ref,
    column_ref,
    row_ref,
    back_ref,
    dots_ref,
    gains_ref,
    w_grad_ref,
    w_sum,
):
    step = pl.program_id(0)
    width = out_ref.shape[2]
    size = width // heads
    scaling = 1.0 / math.sqrt(size)
    allowed = allowed_pairs(column_ref, row_ref)
    cosine, sine = turn_ref[0], turn_ref[1]

    @pl.when(step == 0)
    def _():
        w_sum[...] = jnp.zeros_like(w_sum)
        gains_ref[...] = jnp.zeros_like(gains_ref)

    grad_rows = grad_ref[0]
    grad_out = across_cols(grad_rows, w_ref[...]).astype(LOW)
    w_sum[...] += contract_rows(out_ref[0], grad_rows)
    dots = [0.0, 0.0]
    for h in range(heads):
        mine = slice(h * size, (h + 1) * size)
        query, key, value = (kept_ref[0, :, pl.ds(p * width + h * size, size)] for p in range(3))
        probs = softmax(query, key, allowed)
        grad = grad_out[:, mine]
        grad_value = contract_rows(probs.astype(LOW), grad)
        grad_probs = across_cols(grad, value)
        delta = jnp.sum(grad_probs * probs, axis=-1, keepdims=True)
        grad_scores = (probs * (grad_probs - delta)).astype(LOW)
        grad_query = jnp.dot(grad_scores, key, preferred_element_type=FULL) * scaling
        grad_key = contract_rows(grad_scores, query) * scaling
        for part, grad_turned in enumerate((grad_query, grad_key)):
            columns = pl.ds(part * width + h * size, size)
            grad_normed = turn(grad_turned, cosine, -sine)
            normed = rows_ref[0, :, columns] * scale_ref[0, :, part : part + 1]
            gains_ref[part : part + 1, mine] += jnp.sum(grad_normed * normed, axis=0, keepdims=True)
            weighted = grad_normed * gain_ref[part : part + 1, mine]
            dots[part] += jnp.sum(weighted * normed, axis=-1, keepdims=True)
            back_ref[0, :, columns] = weighted
        back_ref[0, :, pl.ds(2 * width + h * size, size)] = grad_value
    dots_ref[0] = jnp.concatenate(dots, axis=1)

    @pl.when(step == pl.num_programs(0) - 1)
    def _():
        for copy in range(w_grad_ref.shape[0]):
            wide = w_grad_ref.shape[2]
            w_grad_ref[copy] = w_sum[:, copy * wide : (copy + 1) * wide].astype(LOW)


def attend_back(heads, dp_count, grad, w_here, kept, out, rows, scales, gains, turns, column, row):
    groups, length, model_dim = grad.shape
    width = out.shape[2]
    back = jax.ShapeDtypeStruct((groups, length, 3 * width), FULL)
    dots = jax.ShapeDtypeStruct((groups, length, 2), FULL)
    gain_sums = jax.ShapeDtypeStruct((2, width), FULL)
    w_grad = jax.ShapeDtypeStruct((dp_count, width, model_dim // dp_count), LOW)
    blocks = [block_of, whole_of, block_of, block_of, block_of, block_of, whole_of, whole_of]
    arrays = [grad, w_here, kept, out, rows, scales, gains, turns, column, row]
    return pl.pallas_call(
        functools.partial(attend_back_kernel, heads),
        out_shape=[back, dots, gain_sums, w_grad],
        grid=(groups,),
        in_specs=[f(a) for f, a in zip(blocks + [block_of] * 2, arrays)],
        out_specs=[block_of(back), block_of(dots), whole_of(gain_sums), whole_of(w_grad)],
        scratch_shapes=[pltpu.VMEM((width, model_dim), FULL)],
        compiler_params=pltpu.CompilerParams(vmem_limit_bytes=48 << 20),
        cost_estimate=pl.CostEstimate(
            flops=4 * grad.size * width, transcendentals=0, bytes_accessed=10 * grad.size
        ),
        name="attend_back",
    )(*arrays)


def on_device(
    dp_count,
    line_count,
    layer_input,
    out_cotangent,
    segments,
    routes,
    w_qkv,
    w_out,
    w_router,
    attn_gain,
    mlp_gain,
    query_gain,
    key_gain,
    w_gate_up,
    w_down,
):
    row_count, model_dim = layer_input.shape
    top_count = routes.shape[1]
    expert_count = w_router.shape[1]
    local_count = w_gate_up.shape[0]
    head_size = model_dim // HEADS
    head_cols = model_dim // line_count
    heads_here = head_cols // head_size
    capacity = (row_count * top_count * 9 // 8 + expert_count - 1) // expert_count
    scaling = 1.0 / math.sqrt(head_size)
    place = lax.axis_index("expert")
    all_rows = line_count * row_count
    shard = w_qkv.shape[0]

    small = jnp.concatenate(
        [w_router] + [g[:, None] for g in (attn_gain, mlp_gain, query_gain, key_gain)], axis=1
    )
    small = jnp.pad(small, ((0, 0), (0, 128 - small.shape[1])))
    numbers = jnp.concatenate([routes.T, segments, jnp.zeros((7, row_count), jnp.int32)], axis=0)
    x_all, numbers_all, qkv_here, small = opening(
        line_count, dp_count, [layer_input, numbers], [4, 1], w_qkv, small, 1
    )
    out_full = lax.all_gather(w_out, ("dp", "expert"), axis=0, tiled=True)
    late_cotangent, x_all = lax.optimization_barrier((out_cotangent, x_all))
    dy_all = lax.all_gather(late_cotangent, "expert", axis=0)
    qkv_here = qkv_here.reshape(model_dim, 3 * head_cols)
    small = small.reshape(model_dim, small.shape[3])
    router_full = small[:, :expert_count]
    gains = small[:, expert_count : expert_count + 4].astype(FULL)
    gain_attn, gain_mlp = gains[:, 0], gains[:, 1]
    own_gains = lax.dynamic_slice_in_dim(gains, place * head_cols, head_cols, axis=0)
    gain_query, gain_key = own_gains[:, 2], own_gains[:, 3]

    routes_all = numbers_all[:, :top_count]
    segments_all = numbers_all[:, top_count]
    inputs_all = x_all.reshape(all_rows, model_dim).astype(FULL)
    normed_all = inputs_all * rms_scale(inputs_all)
    hidden_one = (normed_all * gain_attn).astype(LOW)
    projected = jnp.dot(hidden_one, qkv_here, preferred_element_type=FULL)
    query_rows = projected[:, :head_cols]
    key_rows = projected[:, head_cols : 2 * head_cols]
    value_rows = projected[:, 2 * head_cols :]
    squares = jnp.stack(
        [jnp.sum(query_rows * query_rows, axis=-1), jnp.sum(key_rows * key_rows, axis=-1)]
    ).reshape(2 * line_count, row_count)
    (squares,) = exchange("expert", line_count, [squares], [True], 4)
    squares = jnp.sum(squares, axis=0).reshape(2, line_count, row_count)
    scales = lax.rsqrt(squares / model_dim + NORM_EPS).transpose(1, 2, 0)
    tables = rotary_tables(row_count, head_size)
    both_gains = jnp.stack([gain_query, gain_key])
    column, row = segments_all[:, :, None], segments_all[:, None, :]
    projected = projected.reshape(line_count, row_count, 3 * head_cols)
    kept, attended = attend(heads_here, projected, scales, both_gains, tables, column, row)
    (own_attended,) = exchange("expert", line_count, [attended], [False], 5)
    own_attended = own_attended.transpose(1, 0, 2).reshape(row_count, model_dim)
    inputs = layer_input.astype(FULL)
    scale_attn = rms_scale(inputs)
    normed_attn = inputs * scale_attn
    residual = inputs + jnp.dot(own_attended, out_full, preferred_element_type=FULL)
    scale_mlp = rms_scale(residual)
    normed_mlp = residual * scale_mlp
    hidden_two = (normed_mlp * gain_mlp).astype(LOW)

    logits = jnp.dot(hidden_two, router_full, preferred_element_type=FULL)
    chosen = jnp.any(routes[:, :, None] == jnp.arange(expert_count)[None, None, :], axis=1)
    masked = jnp.where(chosen, logits, -1e30)
    powers = jnp.where(chosen, jnp.exp(masked - jnp.max(masked, axis=-1, keepdims=True)), 0.0)
    gates = powers / jnp.sum(powers, axis=-1, keepdims=True)

    h_all, gates_all = line_gather(line_count, [hidden_two, gates.T], [4, 1], 6)
    local = place * local_count + jnp.arange(local_count)
    used = jnp.any(routes_all[:, None] == local[None, :, None, None], axis=2)
    position = jnp.arange(row_count)
    lower = (position[:, None] < position[None, :]).astype(LOW)
    rank = einsum("gju,ut->gjt", used.astype(LOW), lower).astype(jnp.int32)
    rank = jnp.where(used, rank, -1)
    spots = jnp.arange(capacity)
    table = (rank[:, :, None, :] == spots[None, None, :, None]).astype(LOW)
    returns = [(rank[:, j, :, None] == spots[None, None, :]).astype(LOW) for j in range(local_count)]
    slots = line_count * capacity
    flat_table = table.reshape(line_count, local_count * capacity, row_count)
    expert_rows = place_rows(flat_table, h_all, local_count)
    dy_all, _ = lax.optimization_barrier((dy_all, expert_rows))
    dy_rows = place_rows(flat_table, dy_all, local_count)
    local_gates = lax.dynamic_slice_in_dim(gates_all, place * local_count, local_count, axis=1)
    slot_gates = jnp.sum(table.astype(FULL) * local_gates[:, :, None, :], axis=-1)
    slot_gates = slot_gates.transpose(1, 0, 2).reshape(local_count, slots, 1)
    out_rows, back_rows, slot_grads, grad_sums = [], [], [], []
    for j in range(local_count):
        grads, out_row, back_row, dots = expert(
            j, dp_count, expert_rows, dy_rows, slot_gates, w_gate_up, w_down
        )
        grads = grads.reshape(-1, model_dim)
        grad_sums.append(lax.psum_scatter(grads, "dp", scatter_dimension=0, tiled=True))
        out_rows.append(out_row)
        back_rows.append(back_row)
        slot_grads.append(dots.reshape(line_count, capacity))
    gate_rows = model_dim // dp_count
    sum_gate_up = jnp.stack([both[:gate_rows] for both in grad_sums]).astype(FULL)
    sum_down = jnp.stack([both[gate_rows:] for both in grad_sums]).astype(FULL)
    slot_grads = jnp.stack(slot_grads, axis=1)
    grad_gates = jnp.sum(table.astype(FULL) * slot_grads[:, :, :, None], axis=2)
    (grad_gates,) = exchange("expert", line_count, [grad_gates], [False], 8)
    grad_gates = grad_gates.reshape(expert_count, row_count).T
    grad_two = line_reduce(line_count, collect(returns, back_rows), 4, 9).astype(FULL)
    grad_out_rows = out_cotangent.astype(FULL)
    grad_logits = gates * (grad_gates - jnp.sum(gates * grad_gates, axis=-1, keepdims=True))
    grad_logits = grad_logits.astype(LOW)
    grad_router = contract_rows(grad_logits, hidden_two)
    grad_two = grad_two + contract_cols(grad_logits, router_full)
    grad_gain_mlp = jnp.sum(grad_two * normed_mlp, axis=0)
    grad_resid = grad_out_rows + norm_back(grad_two * gain_mlp, normed_mlp, scale_mlp)
    grad_attn = grad_resid.astype(LOW)

    (grad_attn_all,) = line_gather(line_count, [grad_attn], [4], 11)
    out_here = lax.dynamic_slice_in_dim(out_full, place * head_cols, head_cols, axis=0)
    back, dots, gain_pair, out_parts = attend_back(
        heads_here,
        dp_count,
        grad_attn_all,
        out_here,
        kept,
        attended,
        projected,
        scales,
        both_gains,
        tables,
        column,
        row,
    )
    dots = dots.transpose(2, 0, 1).reshape(2 * line_count, row_count)
    (dots,) = exchange("expert", line_count, [dots], [True], 12)
    dots = jnp.sum(dots, axis=0).reshape(2, all_rows, 1) / model_dim
    flat_scales = scales.reshape(all_rows, 2)
    back = back.reshape(all_rows, 3 * head_cols)
    projected = projected.reshape(all_rows, 3 * head_cols)
    grads = []
    for part in range(2):
        columns = slice(part * head_cols, (part + 1) * head_cols)
        scale = flat_scales[:, part : part + 1]
        normed = projected[:, columns] * scale
        grads.append(scale * (back[:, columns] - normed * dots[part]))
    grad_proj = jnp.concatenate(grads + [back[:, 2 * head_cols :]], axis=-1).astype(LOW)
    grad_one = contract_cols(grad_proj, qkv_here)
    grad_gain_attn = jnp.sum(grad_one * normed_all, axis=0)
    grad_one = grad_one.astype(LOW).reshape(line_count, row_count, model_dim)
    grad_w_qkv = contract_rows(hidden_one, grad_proj)

    out_cols = model_dim // dp_count
    qkv_parts = grad_w_qkv.astype(LOW).reshape(dp_count, out_cols, 3 * head_cols)
    shared = jnp.concatenate([grad_router, grad_gain_attn[None], grad_gain_mlp[None]], axis=0)
    tall = shared.shape[0] + -shared.shape[0] % 8
    shared = jnp.pad(shared, ((0, tall - shared.shape[0]), (0, 0)))
    shared = shared.reshape(tall, dp_count, line_count, shard).transpose(2, 1, 0, 3)
    shared = shared.reshape(line_count, dp_count * tall, shard)
    shared = jnp.pad(shared, ((0, 0), (0, 0), (0, 128 - shard)))
    grad_one, qkv_parts, out_parts, gain_pair, shared = closing(
        line_count, dp_count, grad_one, 4, [qkv_parts, out_parts, gain_pair], shared, 14
    )
    out_rows = lax.optimization_barrier((out_rows, grad_one))[0]
    mixture = line_reduce(line_count, collect(returns, out_rows), 4, 10).astype(FULL)
    output = (residual + mixture).astype(LOW)
    sum_qkv = jnp.sum(qkv_parts.astype(FULL), axis=0).reshape(out_cols, 3, head_cols)
    sum_out = jnp.sum(out_parts.astype(FULL), axis=0)
    gain_pair = jnp.sum(gain_pair, axis=0)
    shared = shared[:, :shard]
    grad_one = grad_one.astype(FULL)
    grad_inputs = grad_resid + norm_back(grad_one * gain_attn, normed_attn, scale_attn)
    return (
        output,
        grad_inputs,
        sum_qkv,
        sum_out,
        shared[:expert_count].T,
        shared[expert_count],
        shared[expert_count + 1],
        gain_pair[0],
        gain_pair[1],
        sum_gate_up.astype(FULL),
        sum_down.astype(FULL),
    )


def solution(mesh):
    both = ("dp", "expert")
    rows, flat = P(both, None), P(both)
    placed = (rows,) * 7 + (flat,) * 4 + (P("expert", None, None),) * 2
    return jax.shard_map(
        functools.partial(on_device, mesh.shape["dp"], mesh.shape["expert"]),
        mesh=mesh,
        in_specs=placed,
        out_specs=(
            rows,
            rows,
            P("dp", None, "expert"),
            P("expert", "dp"),
            rows,
            flat,
            flat,
            P("expert"),
            P("expert"),
            P("expert", "dp", None),
            P("expert", "dp", None),
        ),
        check_vma=False,
    )
```

```python
import functools
import math

import jax
import jax.numpy as jnp
from jax import lax
from jax.experimental import pallas as pl
from jax.experimental.pallas import tpu as pltpu
from jax.sharding import PartitionSpec as P

HEADS = 16
NORM_EPS = 1e-05
MESH = pl.DeviceIdType.MESH
ANY = pl.BlockSpec(memory_space=pl.ANY)
LOW = jnp.bfloat16
FULL = jnp.float32


def line_place():
    place = lax.axis_index("expert")
    level, side = lax.div(place, 2), lax.rem(place, 2)
    return place, level, side, place + 1 - 2 * side


def greet(axis, targets):
    barrier = pltpu.get_barrier_semaphore()
    for target, there in targets:

        def signal(target=target):
            pl.semaphore_signal(barrier, inc=1, device_id={axis: target}, device_id_type=MESH)

        if there is None:
            signal()
        else:
            pl.when(there)(signal)


def line_barrier(levels):
    place, level, _, other = line_place()
    has_up, has_down = level < levels - 1, level > 0
    greet("expert", [(other, None), (place + 2, has_up), (place - 2, has_down)])
    count = 1 + has_up.astype(jnp.int32) + has_down.astype(jnp.int32)
    pl.semaphore_wait(pltpu.get_barrier_semaphore(), count)


def around(axis, size):
    place = lax.axis_index(axis)
    return [lax.rem(place + shift, size) for shift in range(1, size)]


def remote(source, target, send, recv, device):
    return pltpu.make_async_remote_copy(
        src_ref=source,
        dst_ref=target,
        send_sem=send,
        recv_sem=recv,
        device_id=device,
        device_id_type=MESH,
    )


class LineGather:
    def __init__(self, levels, cuts, ins, outs, up_sem, down_sem, side_sem, recv_sem, own_sem):
        self.levels, self.cuts, self.ins, self.outs = levels, cuts, ins, outs
        self.up_sem, self.down_sem, self.side_sem = up_sem, down_sem, side_sem
        self.recv_sem = recv_sem
        self.pieces = [(i, k) for i in range(len(cuts)) for k in range(cuts[i])]
        self.place, self.level, self.side, self.other = line_place()
        self.has_up, self.has_down = self.level < levels - 1, self.level > 0
        self.own = [
            pltpu.make_async_copy(ins[i], outs[i].at[self.place], own_sem.at[i])
            for i in range(len(cuts))
        ]

    @staticmethod
    def scratch(size, cuts):
        levels, total = size // 2, sum(cuts)
        shapes = ((levels, total), (levels, total), (2 * levels - 1, total), (size, total))
        return [pltpu.SemaphoreType.DMA(shape) for shape in shapes + ((len(cuts),),)]

    def part(self, ref, i, k):
        rows = self.ins[i].shape[0] // self.cuts[i]
        return ref.at[pl.ds(k * rows, rows)]

    def sending(self, q, block, own, sem, target):
        i, k = self.pieces[q]
        landing = self.part(self.outs[i].at[block], i, k)
        source = self.part(self.ins[i], i, k) if own else landing
        return remote(source, landing, sem, self.recv_sem.at[block, q], {"expert": target})

    def up(self, q, step):
        block = self.place - 2 * step
        return self.sending(q, block, step == 0, self.up_sem.at[step, q], self.place + 2)

    def down(self, q, step):
        block = self.place + 2 * step
        return self.sending(q, block, step == 0, self.down_sem.at[step, q], self.place - 2)

    def across(self, q, step):
        sem = self.side_sem.at[step + self.levels - 1, q]
        return self.sending(q, self.place - 2 * step, step == 0, sem, self.other)

    def begin(self):
        for q in range(len(self.pieces)):
            pl.when(self.has_up)(self.up(q, 0).start)
            pl.when(self.has_down)(self.down(q, 0).start)
        for q in range(len(self.pieces)):
            self.across(q, 0).start()
        for copy in self.own:
            copy.start()

    def forward(self, step, q):
        @pl.when(self.level >= step)
        def _():
            self.across(q, step).wait_recv()
            pl.when(self.has_up)(self.up(q, step).start)
            self.across(q, step).start()

        @pl.when(self.level + step < self.levels)
        def _():
            self.across(q, -step).wait_recv()
            pl.when(self.has_down)(self.down(q, step).start)
            self.across(q, -step).start()

    def land_across(self, block):
        for q in range(len(self.pieces)):
            self.sending(q, block, False, self.side_sem.at[0, q], self.other).wait_recv()

    def finish(self, landed=False, held=0):
        if not landed:
            for far in range(self.levels):
                self.land_across(2 * far + 1 - self.side)
        for q in range(len(self.pieces)):
            self.across(q, 0).wait_send()
            for step in range(self.levels):
                above, below = self.level >= step, self.level + step < self.levels
                pl.when(self.has_up & above)(self.up(q, step).wait_send)
                pl.when(self.has_down & below)(self.down(q, step).wait_send)
                if step:
                    pl.when(above)(self.across(q, step).wait_send)
                    pl.when(below)(self.across(q, -step).wait_send)
        for copy in self.own[held:]:
            copy.wait()

    def run(self):
        self.begin()
        for step in range(1, self.levels):
            for q in range(len(self.pieces)):
                self.forward(step, q)
        self.finish()


def line_gather_kernel(levels, cuts, *refs):
    count = len(cuts)
    line = LineGather(levels, cuts, refs[:count], refs[count : 2 * count], *refs[2 * count :])
    line_barrier(levels)
    line.run()


def call(kernel, name, number, outs, scratch, arrays, moved):
    return pl.pallas_call(
        kernel,
        out_shape=outs,
        in_specs=[ANY] * len(arrays),
        out_specs=[ANY] * len(outs),
        scratch_shapes=scratch,
        compiler_params=pltpu.CompilerParams(
            collective_id=number, has_side_effects=True, vmem_limit_bytes=48 << 20
        ),
        cost_estimate=pl.CostEstimate(flops=0, transcendentals=0, bytes_accessed=moved),
        name=name,
    )(*arrays)


def line_gather(size, arrays, cuts, number):
    return call(
        functools.partial(line_gather_kernel, size // 2, tuple(cuts)),
        "line_gather",
        number,
        [jax.ShapeDtypeStruct((size,) + a.shape, a.dtype) for a in arrays],
        LineGather.scratch(size, cuts),
        arrays,
        150_000_000,
    )


class LineReduce:
    def __init__(self, levels, cuts, parts, total, own, beside, rising, falling, *sems):
        self.levels, self.cuts, self.parts, self.total = levels, cuts, parts, total
        self.made = parts.shape[0] == levels
        self.own, self.beside, self.rising, self.falling = own, beside, rising, falling
        self.load_sem, self.side_send, self.side_recv = sems[:3]
        self.up_send, self.up_recv, self.down_send, self.down_recv, self.out_sem = sems[3:]
        self.place, self.level, self.side, self.other = line_place()
        self.has_up, self.has_down = self.level < levels - 1, self.level > 0
        self.rows = parts.shape[1] // cuts
        self.order = []
        for step in range(levels):
            for far in (levels - 1 - step, step):
                if far not in self.order:
                    self.order.append(far)

    @staticmethod
    def scratch(size, block, dtype, cuts):
        levels = size // 2
        return (
            [pltpu.VMEM((levels,) + block, dtype)] * 4
            + [pltpu.SemaphoreType.DMA((levels, cuts))] * 7
            + [pltpu.SemaphoreType.DMA((cuts,))]
        )

    def cut(self, ref, block, k):
        return ref.at[block, pl.ds(k * self.rows, self.rows)]

    def loading(self, far, k):
        source = self.cut(self.parts, 2 * far + self.side, k)
        return pltpu.make_async_copy(source, self.cut(self.own, far, k), self.load_sem.at[far, k])

    def across(self, far, k):
        source = self.cut(self.parts, far if self.made else 2 * far + 1 - self.side, k)
        sems = self.side_send.at[far, k], self.side_recv.at[far, k]
        return remote(source, self.cut(self.beside, far, k), *sems, {"expert": self.other})

    def up(self, far, k):
        sems = self.up_send.at[far, k], self.up_recv.at[far, k]
        target = {"expert": self.place + 2}
        return remote(self.cut(self.own, far, k), self.cut(self.rising, far, k), *sems, target)

    def down(self, far, k):
        sems = self.down_send.at[far, k], self.down_recv.at[far, k]
        target = {"expert": self.place - 2}
        return remote(self.cut(self.own, far, k), self.cut(self.falling, far, k), *sems, target)

    def value(self, ref, block, k):
        return self.cut(ref, block, k)[...].astype(FULL)

    def load(self):
        for far in self.order:
            for k in range(self.cuts):
                self.loading(far, k).start()

    def begin(self):
        for far in self.order:
            for k in range(self.cuts):
                self.across(far, k).start()

    def prepare(self, far, which, make):
        if which == 0:
            make(2 * far + 1 - self.side, self.parts.at[far])
            for k in range(self.cuts):
                self.across(far, k).start()
        else:
            make(2 * far + self.side, self.own.at[far])

    def pair(self, far, k):
        if not self.made:
            self.loading(far, k).wait()
        self.across(far, k).wait_recv()
        return self.value(self.own, far, k) + self.value(self.beside, far, k)

    def store(self, far, k, total):
        self.cut(self.own, far, k)[...] = total.astype(self.own.dtype)

    def toward(self, far, k, ahead, behind, move, arrived):
        @pl.when(ahead & behind)
        def _():
            both = self.pair(far, k)
            move(far, k).wait_recv()
            self.store(far, k, both + self.value(arrived, far, k))

        @pl.when(ahead & jnp.logical_not(behind))
        def _():
            self.store(far, k, self.pair(far, k))

        pl.when(ahead)(move(far, k).start)

    def main(self, beside=None):
        for step in range(self.levels - 1):
            high, low = self.levels - 1 - step, step
            for k in range(self.cuts):
                if beside:
                    beside(step * self.cuts + k)
                self.toward(high, k, self.level < high, self.has_down, self.up, self.rising)
                self.toward(low, k, self.level > low, self.has_up, self.down, self.falling)
        for k in range(self.cuts):
            self.store(self.level, k, self.pair(self.level, k))
            for there, move, arrived in (
                (self.has_down, self.up, self.rising),
                (self.has_up, self.down, self.falling),
            ):

                @pl.when(there)
                def _():
                    move(self.level, k).wait_recv()
                    total = self.value(self.own, self.level, k) + self.value(arrived, self.level, k)
                    self.store(self.level, k, total)

            self.leaving(k).start()

    def leaving(self, k):
        target = self.total.at[pl.ds(k * self.rows, self.rows)]
        return pltpu.make_async_copy(self.cut(self.own, self.level, k), target, self.out_sem.at[k])

    def finish(self):
        for k in range(self.cuts):
            self.leaving(k).wait()
            for far in range(self.levels):
                self.across(far, k).wait_send()
                pl.when(self.level < far)(self.up(far, k).wait_send)
                pl.when(self.level > far)(self.down(far, k).wait_send)


class Exchange:
    def __init__(self, axis, size, spread, cuts, ins, outs, send_sem, recv_sem, own_sem):
        self.axis, self.spread, self.ins, self.outs = axis, spread, ins, outs
        self.send_sem, self.recv_sem, self.own_sem = send_sem, recv_sem, own_sem
        self.cuts = cuts
        self.firsts = [sum(cuts[:i]) for i in range(len(cuts))]
        self.pieces = [(i, k) for i in range(len(cuts)) for k in range(cuts[i])]
        self.place, self.peers = lax.axis_index(axis), around(axis, size)

    @staticmethod
    def scratch(size, cuts):
        sems = pltpu.SemaphoreType.DMA
        return [sems((sum(cuts), size)), sems((sum(cuts), size)), sems((len(cuts),))]

    def source(self, i, block):
        return self.ins[i] if self.spread[i] else self.ins[i].at[block]

    def staying(self, i):
        target = self.outs[i].at[self.place]
        return pltpu.make_async_copy(self.source(i, self.place), target, self.own_sem.at[i])

    def sending(self, i, k, shift, landing):
        peer = self.peers[shift]
        source, target, q = self.source(i, peer), self.outs[i].at[landing], self.firsts[i] + k
        if self.cuts[i] > 1:
            rows = target.shape[0] // self.cuts[i]
            source, target = source.at[pl.ds(k * rows, rows)], target.at[pl.ds(k * rows, rows)]
        sems = self.send_sem.at[q, shift], self.recv_sem.at[q, landing]
        return remote(source, target, *sems, {self.axis: peer})

    def send(self, i, k):
        for shift in range(len(self.peers)):
            self.sending(i, k, shift, self.place).start()

    def stay(self):
        for i in range(len(self.spread)):
            self.staying(i).start()

    def begin(self):
        for i, k in self.pieces:
            self.send(i, k)
        self.stay()

    def land(self):
        for shift, peer in enumerate(self.peers):
            for i, k in self.pieces:
                self.sending(i, k, shift, peer).wait_recv()

    def arrive(self):
        self.land()
        for i in range(len(self.spread)):
            self.staying(i).wait()

    def finish(self):
        for shift in range(len(self.peers)):
            for i, k in self.pieces:
                self.sending(i, k, shift, self.place).wait_send()


def exchange_kernel(axis, size, spread, *refs):
    count = len(spread)
    ins, outs, sems = refs[:count], refs[count : 2 * count], refs[2 * count :]
    moves = Exchange(axis, size, spread, (1,) * count, ins, outs, *sems)
    greet(axis, [(peer, None) for peer in moves.peers])
    pl.semaphore_wait(pltpu.get_barrier_semaphore(), size - 1)
    moves.begin()
    moves.arrive()
    moves.finish()


def exchange_outs(size, arrays, spread):
    return [
        jax.ShapeDtypeStruct((size,) + a.shape if flat else a.shape, a.dtype)
        for a, flat in zip(arrays, spread)
    ]


def exchange(axis, size, arrays, spread, number):
    return call(
        functools.partial(exchange_kernel, axis, size, tuple(spread)),
        "exchange_" + axis,
        number,
        exchange_outs(size, arrays, spread),
        Exchange.scratch(size, (1,) * len(arrays)),
        arrays,
        30_000_000,
    )


def opening_kernel(size, dp_count, cuts, *refs):
    count, levels = len(cuts), size // 2
    ins, (w_ref, small_ref, sheet_ref) = refs[:count], refs[count : count + 3]
    outs, rest = refs[count + 3 : 2 * count + 3], refs[2 * count + 3 :]
    w_out, small_out, sheet_out = rest[:3]
    line = LineGather(levels, cuts, ins, outs, *rest[3:8])
    send_sem, recv_sem, own_sem = rest[8:11]
    level, side, other = line.level, line.side, line.other
    place, mine = line.place, lax.axis_index("dp")
    peers = around("expert", size)
    width = w_out.shape[3] // 3
    mine_refs = [w_out.at[mine], small_out.at[mine]]
    across = Exchange(
        "dp", dp_count, (True,) * 2, (size,) * 2, mine_refs, [w_out, small_out], *rest[11:14]
    )
    up_send, down_send, line_recv, dp_send, dp_recv, side_send, side_recv, sheet_own = rest[14:]
    greet("expert", [(peer, None) for peer in peers])
    greet("dp", [(peer, None) for peer in across.peers])
    pl.semaphore_wait(pltpu.get_barrier_semaphore(), size + dp_count - 2)

    def ends(peer, landing, j):
        if j == 3:
            return small_ref, small_out.at[mine, landing]
        start = pl.multiple_of(j * width * size + peer * width, 128)
        target = w_out.at[mine, landing, :, pl.ds(j * width, width)]
        return w_ref.at[:, pl.ds(start, width)], target

    def sending(shift, landing, j):
        source, target = ends(peers[shift], landing, j)
        sems = send_sem.at[shift, j], recv_sem.at[landing, j]
        return remote(source, target, *sems, {"expert": peers[shift]})

    def sheet_line(far, own, send, target):
        landing = sheet_out.at[mine, 2 * far + side]
        source = sheet_ref if own else landing
        return remote(source, landing, send.at[far], line_recv.at[far], {"expert": target})

    def sheet_up(far, own=False):
        return sheet_line(far, own, up_send, place + 2)

    def sheet_down(far, own=False):
        return sheet_line(far, own, down_send, place - 2)

    def sheet_dp(far, shift, copy, own=False):
        landing = sheet_out.at[copy, 2 * far + side]
        source = sheet_ref if own else landing
        sems = dp_send.at[shift, far], dp_recv.at[copy, far]
        return remote(source, landing, *sems, {"dp": across.peers[shift]})

    def sheet_side(far, copy, whose, own=False):
        landing = sheet_out.at[copy, 2 * far + whose]
        source = sheet_ref if own else landing
        sems = side_send.at[copy, far], side_recv.at[copy, far]
        return remote(source, landing, *sems, {"expert": other})

    def spread_sheet(far, own=False):
        for shift in range(dp_count - 1):
            sheet_dp(far, shift, mine, own).start()
        sheet_side(far, mine, side, own).start()

    own = [pltpu.make_async_copy(*ends(place, place, j), own_sem.at[j]) for j in range(4)]
    sheet_stays = pltpu.make_async_copy(sheet_ref, sheet_out.at[mine, place], sheet_own.at[0])
    for shift in range(size - 1):
        for j in range(4):
            sending(shift, place, j).start()
    for copy in own:
        copy.start()
    sheet_stays.start()
    pl.when(line.has_up)(sheet_up(level, True).start)
    pl.when(line.has_down)(sheet_down(level, True).start)
    spread_sheet(level, True)
    line.begin()
    for copy in own:
        copy.wait()
    across.send(0, place)
    across.send(1, place)
    for shift, peer in enumerate(peers):
        for j in range(4):
            sending(shift, peer, j).wait_recv()
        across.send(0, peer)
        across.send(1, peer)
    for step in range(1, levels):

        @pl.when(level >= step)
        def _():
            sheet_up(level - step).wait_recv()
            pl.when(line.has_up)(sheet_up(level - step).start)
            spread_sheet(level - step)

        @pl.when(level + step < levels)
        def _():
            sheet_down(level + step).wait_recv()
            pl.when(line.has_down)(sheet_down(level + step).start)
            spread_sheet(level + step)

        for q in range(len(line.pieces)):
            line.forward(step, q)
    for shift, peer in enumerate(across.peers):
        for far in range(levels):
            sheet_dp(far, shift, peer).wait_recv()
            sheet_side(far, peer, side).start()
    line.finish()
    for shift in range(size - 1):
        for j in range(4):
            sending(shift, place, j).wait_send()
    across.land()
    across.finish()
    for far in range(levels):
        pl.when(line.has_up & (level >= far))(sheet_up(far).wait_send)
        pl.when(line.has_down & (level <= far))(sheet_down(far).wait_send)
        for shift in range(dp_count - 1):
            sheet_dp(far, shift, mine).wait_send()
        for copy in range(dp_count):
            sheet_side(far, copy, 1 - side).wait_recv()
            sheet_side(far, copy, side).wait_send()
    sheet_stays.wait()


def opening(size, dp_count, arrays, cuts, weights, small, sheet, number):
    sems = pltpu.SemaphoreType.DMA
    levels = size // 2
    outs = [jax.ShapeDtypeStruct((size,) + a.shape, a.dtype) for a in arrays]
    rows, columns = weights.shape
    whole = (dp_count, size, rows)
    outs.append(jax.ShapeDtypeStruct(whole + (columns // size,), weights.dtype))
    outs.append(jax.ShapeDtypeStruct(whole + (small.shape[1],), small.dtype))
    outs.append(jax.ShapeDtypeStruct((dp_count, size) + sheet.shape, sheet.dtype))
    return call(
        functools.partial(opening_kernel, size, dp_count, tuple(cuts)),
        "opening",
        number,
        outs,
        LineGather.scratch(size, cuts)
        + [sems((size, 4)), sems((size, 4)), sems((4,))]
        + Exchange.scratch(dp_count, (size, size))
        + [sems((levels,))] * 3
        + [sems((dp_count, levels))] * 4
        + [sems((1,))],
        list(arrays) + [weights, small, sheet],
        200_000_000,
    )


VMEM = pl.BlockSpec(memory_space=pltpu.VMEM)
COLUMNS = 512


def gather_place_kernel(levels, cuts, *refs):
    rows_ref, gates_ref, table_ref, dy_ref, x_out, dy_out, gates_out = refs[:7]
    held, dy_held, x_stage, dy_stage = refs[7:11]
    line_sems, (dy_sem, x_sems, dy_sems) = refs[11:16], refs[16:]
    line = LineGather(levels, cuts, [rows_ref, gates_ref], [held, gates_out], *line_sems)
    size, width = 2 * levels, held.shape[2]
    _, local_count, capacity, _ = x_stage.shape

    def leaving(block, stage, out, sems):
        target = out.at[:, pl.ds(pl.multiple_of(block * capacity, 8), capacity)]
        return pltpu.make_async_copy(stage.at[block], target, sems.at[block])

    def place(block, rows, stage, out, sems):
        table = table_ref[block]

        @pl.loop(0, width // COLUMNS)
        def _(n):
            columns = pl.ds(pl.multiple_of(n * COLUMNS, COLUMNS), COLUMNS)
            placed = jnp.dot(table, rows[block, :, columns], preferred_element_type=FULL)
            for j in range(local_count):
                part = placed[j * capacity : (j + 1) * capacity]
                stage[block, j, :, columns] = part.astype(stage.dtype)

        leaving(block, stage, out, sems).start()

    def place_x(block):
        place(block, held, x_stage, x_out, x_sems)

    loading = pltpu.make_async_copy(dy_ref, dy_held, dy_sem.at[0])
    loading.start()
    line_barrier(levels)
    line.begin()
    loading.wait()

    @pl.loop(0, size)
    def _(block):
        place(block, dy_held, dy_stage, dy_out, dy_sems)

    line.own[0].wait()
    place_x(line.place)
    for step in range(1, levels + 1):
        if step < levels:
            for q in range(len(line.pieces)):
                line.forward(step, q)
        for sign in (-1, 1):
            far = line.level + sign * (step - 1)
            there = (far >= 0) & (far < levels)
            if step > 1 or sign > 0:

                @pl.when(there)
                def _():
                    line.land_across(2 * far + 1 - line.side)
                    place_x(2 * far + 1 - line.side)

            near = line.level + sign * step
            if step < levels:

                @pl.when((near >= 0) & (near < levels))
                def _():
                    place_x(2 * near + line.side)

    line.finish(landed=True, held=1)
    for block in range(size):
        leaving(block, x_stage, x_out, x_sems).wait()
        leaving(block, dy_stage, dy_out, dy_sems).wait()


def gather_place(size, rows, gates, table, dy, local_count, number):
    cuts = (4, 1)
    tokens, width = rows.shape
    capacity = table.shape[1] // local_count
    placed = jax.ShapeDtypeStruct((local_count, size * capacity, width), rows.dtype)
    sems = pltpu.SemaphoreType.DMA
    return pl.pallas_call(
        functools.partial(gather_place_kernel, size // 2, cuts),
        out_shape=[placed, placed, jax.ShapeDtypeStruct((size,) + gates.shape, gates.dtype)],
        in_specs=[ANY, ANY, VMEM, ANY],
        out_specs=[ANY] * 3,
        scratch_shapes=[pltpu.VMEM((size, tokens, width), rows.dtype)] * 2
        + [pltpu.VMEM((size, local_count, capacity, width), rows.dtype)] * 2
        + LineGather.scratch(size, cuts)
        + [sems((1,)), sems((size,)), sems((size,))],
        compiler_params=pltpu.CompilerParams(
            collective_id=number, has_side_effects=True, vmem_limit_bytes=48 << 20
        ),
        cost_estimate=pl.CostEstimate(
            flops=4 * table.size * width, transcendentals=0, bytes_accessed=150_000_000
        ),
        name="gather_place",
    )(rows, gates, table, dy)


def collect_reduce_kernel(levels, cuts, local_count, *refs):
    tables, slots, small_ref = refs[:local_count], refs[local_count : 2 * local_count], refs[2 * local_count]
    total_ref, small_out = refs[2 * local_count + 1 : 2 * local_count + 3]
    away, rest = refs[2 * local_count + 3], refs[2 * local_count + 4 :]
    line = LineReduce(levels, cuts, away, total_ref, *rest[:12])
    small = Exchange("expert", 2 * levels, (False,), (1,), [small_ref], [small_out], *rest[12:])
    width = away.shape[2]
    greet("expert", [(peer, None) for peer in small.peers])
    pl.semaphore_wait(pltpu.get_barrier_semaphore(), 2 * levels - 1)

    def make(block, target):
        @pl.loop(0, width // COLUMNS)
        def _(n):
            columns = pl.ds(pl.multiple_of(n * COLUMNS, COLUMNS), COLUMNS)
            total = 0.0
            for table, rows in zip(tables, slots):
                total += jnp.dot(table[block], rows[block, :, columns], preferred_element_type=FULL)
            target[:, columns] = total.astype(target.dtype)

    small.begin()
    for far in line.order[:2]:
        line.prepare(far, 0, make)
        line.prepare(far, 1, make)
    later = [(far, which) for far in line.order[2:] for which in (0, 1)]

    def beside(turn):
        if turn < len(later):
            line.prepare(*later[turn], make)

    line.main(beside)
    small.arrive()
    line.finish()
    small.finish()


def collect_reduce(size, tables, slots, small, number):
    levels, cuts = size // 2, 4
    block = (tables[0].shape[1], slots[0].shape[2])
    kind = slots[0].dtype
    return pl.pallas_call(
        functools.partial(collect_reduce_kernel, levels, cuts, len(tables)),
        out_shape=[
            jax.ShapeDtypeStruct(block, kind),
            jax.ShapeDtypeStruct(small.shape, small.dtype),
        ],
        in_specs=[VMEM] * (2 * len(tables)) + [ANY],
        out_specs=[ANY, ANY],
        scratch_shapes=[pltpu.VMEM((levels,) + block, kind)]
        + LineReduce.scratch(size, block, kind, cuts)
        + Exchange.scratch(size, (1,)),
        compiler_params=pltpu.CompilerParams(
            collective_id=number, has_side_effects=True, vmem_limit_bytes=48 << 20
        ),
        cost_estimate=pl.CostEstimate(flops=0, transcendentals=0, bytes_accessed=150_000_000),
        name="collect_reduce",
    )(*tables, *slots, small)


def closing_kernel(size, dp_count, cuts, sum_cuts, *refs):
    ins, outs, rest = refs[:6], refs[6:12], refs[12:]
    lines = [LineReduce(size // 2, cuts, ins[i], outs[i], *rest[12 * i : 12 * i + 12]) for i in (0, 1)]
    rest = rest[24:]
    sums = Exchange("dp", dp_count, (False, False, True), sum_cuts, ins[2:5], outs[2:5], *rest[:3])
    got, half, last = rest[3:6]
    first = Exchange("expert", size, (False,), (1,), ins[5:6], [got], *rest[6:9])
    second = Exchange("dp", dp_count, (False,), (1,), [half], [last], *rest[9:12])
    for line in lines:
        line.load()
    greet("expert", [(peer, None) for peer in first.peers])
    greet("dp", [(peer, None) for peer in sums.peers])
    pl.semaphore_wait(pltpu.get_barrier_semaphore(), size + dp_count - 2)
    first.begin()
    for line in lines:
        line.begin()
    sums.stay()
    turns = (size // 2 - 1) * cuts
    tall = half.shape[1]

    def beside(turn):
        for q in range(len(sums.pieces)):
            if q * turns // len(sums.pieces) == turn:
                sums.send(*sums.pieces[q])
        if turn == turns // 2:
            first.arrive()
            for copy in range(dp_count):
                rows = pl.ds(copy * tall, tall)
                half[copy] = sum(got[i, rows, :] for i in range(size))
            second.begin()

    lines[0].main(beside)
    lines[1].main()
    second.arrive()
    outs[5][...] = sum(last[i] for i in range(dp_count))
    sums.arrive()
    for moves in lines + [first, second, sums]:
        moves.finish()


def closing(size, dp_count, parts, cuts, sums, shared, number):
    block = parts[0].shape[1:]
    tall = shared.shape[1] // dp_count
    wide = shared.shape[2]
    sum_cuts = (8, 2, 1)
    outs = [jax.ShapeDtypeStruct(block, parts[0].dtype)] * 2
    outs += exchange_outs(dp_count, sums, (False, False, True))
    outs.append(jax.ShapeDtypeStruct((tall, wide), FULL))
    return pl.pallas_call(
        functools.partial(closing_kernel, size, dp_count, cuts, sum_cuts),
        out_shape=outs,
        in_specs=[ANY] * 6,
        out_specs=[ANY] * 5 + [VMEM],
        scratch_shapes=LineReduce.scratch(size, block, parts[0].dtype, cuts) * 2
        + Exchange.scratch(dp_count, sum_cuts)
        + [pltpu.VMEM((size,) + shared.shape[1:], FULL)]
        + [pltpu.VMEM((dp_count, tall, wide), FULL)] * 2
        + Exchange.scratch(size, (1,))
        + Exchange.scratch(dp_count, (1,)),
        compiler_params=pltpu.CompilerParams(
            collective_id=number, has_side_effects=True, vmem_limit_bytes=48 << 20
        ),
        cost_estimate=pl.CostEstimate(flops=0, transcendentals=0, bytes_accessed=200_000_000),
        name="closing",
    )(*parts, *sums, shared)


def collect_kernel(*refs):
    tables, rows_refs, out_ref = refs[: len(refs) // 2], refs[len(refs) // 2 : -1], refs[-1]
    total = 0.0
    for table_ref, rows_ref in zip(tables, rows_refs):
        total += jnp.dot(table_ref[0], rows_ref[0], preferred_element_type=FULL)
    out_ref[0] = total.astype(LOW)


def collect(tables, rows):
    groups, tokens, capacity = tables[0].shape
    width = rows[0].shape[2]
    return pl.pallas_call(
        collect_kernel,
        out_shape=jax.ShapeDtypeStruct((groups, tokens, width), LOW),
        grid=(groups,),
        in_specs=[pl.BlockSpec((1, tokens, capacity), lambda g: (g, 0, 0))] * len(rows)
        + [pl.BlockSpec((1, capacity, width), lambda g: (0, g, 0))] * len(rows),
        out_specs=pl.BlockSpec((1, tokens, width), lambda g: (g, 0, 0)),
        cost_estimate=pl.CostEstimate(
            flops=2 * len(rows) * tables[0].size * width,
            transcendentals=0,
            bytes_accessed=4 * groups * tokens * width,
        ),
        name="collect",
    )(*tables, *rows)


def across_cols(left_side, right_side):
    return lax.dot_general(
        left_side, right_side, (((1,), (1,)), ((), ())), preferred_element_type=FULL
    )


def expert_kernel(
    tiles,
    x_ref,
    dy_ref,
    scale_ref,
    gate_ref,
    up_ref,
    down_ref,
    grads_ref,
    out_ref,
    back_ref,
    dots_ref,
    turned,
    weighted,
    out_sum,
    back_sum,
    side_buf,
    down_buf,
    sems,
):
    tile = pl.program_id(0)
    slot = lax.rem(tile, 2)
    width = gate_ref.shape[2]
    copies, high = side_buf.shape[2], side_buf.shape[3]
    some, low = down_buf.shape[1], down_buf.shape[2]
    hidden = tiles * width

    def leaving(at, half, slot):
        columns = pl.ds(pl.multiple_of(half * hidden + at * width, 128), width)
        target = grads_ref.at[:, pl.ds(0, high), columns]
        return pltpu.make_async_copy(side_buf.at[slot, half], target, sems.at[slot, half])

    def leaving_down(at, slot):
        target = grads_ref.at[pl.ds(at * some, some), pl.ds(high, low), :]
        return pltpu.make_async_copy(down_buf.at[slot], target, sems.at[slot, 2])

    def settle(at, slot):
        leaving(at, 0, slot).wait()
        leaving(at, 1, slot).wait()
        leaving_down(at, slot).wait()

    @pl.when(tile == 0)
    def _():
        turned[...] = x_ref[0].T
        weighted[...] = (scale_ref[0] * dy_ref[0].astype(FULL)).astype(LOW)
        out_sum[...] = jnp.zeros_like(out_sum)
        back_sum[...] = jnp.zeros_like(back_sum)

    @pl.when(tile >= 2)
    def _():
        settle(tile - 2, slot)

    rows, grads = x_ref[0], weighted[...]
    w_gate, w_up, w_down = gate_ref[0], up_ref[0], down_ref[0]
    gate = jnp.dot(rows, w_gate, preferred_element_type=FULL)
    up = jnp.dot(rows, w_up, preferred_element_type=FULL)
    sigmoid = jax.nn.sigmoid(gate)
    silu = gate * sigmoid
    act = (silu * up).astype(LOW)
    out_sum[...] += jnp.dot(act, w_down, preferred_element_type=FULL)
    grad_act = across_cols(grads, w_down)
    grad_gate = (grad_act * up * sigmoid * (1.0 + gate * (1.0 - sigmoid))).astype(LOW)
    grad_up = (grad_act * silu).astype(LOW)
    back_sum[...] += across_cols(grad_gate, w_gate) + across_cols(grad_up, w_up)
    turned_rows = turned[...]
    for half, grad in enumerate((grad_gate, grad_up)):
        total = jnp.dot(turned_rows, grad, preferred_element_type=FULL).astype(LOW)
        side_buf[slot, half] = total.reshape(copies, high, width)
        leaving(tile, half, slot).start()
    total = jnp.dot(act.T, grads, preferred_element_type=FULL).astype(LOW)
    down_buf[slot] = total.reshape(some, low, total.shape[1])
    leaving_down(tile, slot).start()

    @pl.when(tile == tiles - 1)
    def _():
        final = out_sum[...]
        dots_ref[0] = jnp.sum(final * dy_ref[0].astype(FULL), axis=-1, keepdims=True)
        out_ref[0] = (scale_ref[0] * final).astype(LOW)
        back_ref[0] = back_sum[...].astype(LOW)
        settle(tile - 1, 1 - slot)
        settle(tile, slot)


def expert(j, dp_count, x_rows, dy_rows, scales, w_gate_up, w_down, tiles=4):
    _, slots, width = x_rows.shape
    hidden = w_down.shape[1]
    tile = hidden // tiles
    high, low = width // dp_count, hidden // dp_count
    some = tile // low
    once = pl.Buffered(1)
    row_spec = pl.BlockSpec((1, slots, width), lambda f: (j, 0, 0), pipeline_mode=once)
    out_spec = pl.BlockSpec((1, slots, width), lambda f: (0, 0, 0), pipeline_mode=once)
    return pl.pallas_call(
        functools.partial(expert_kernel, tiles),
        out_shape=[
            jax.ShapeDtypeStruct((dp_count, high + low, width), LOW),
            jax.ShapeDtypeStruct((1, slots, width), LOW),
            jax.ShapeDtypeStruct((1, slots, width), LOW),
            jax.ShapeDtypeStruct((1, slots, 1), FULL),
        ],
        grid=(tiles,),
        in_specs=[
            row_spec,
            row_spec,
            pl.BlockSpec((1, slots, 1), lambda f: (j, 0, 0), pipeline_mode=once),
            pl.BlockSpec((1, width, tile), lambda f: (j, 0, f)),
            pl.BlockSpec((1, width, tile), lambda f: (j, 0, tiles + f)),
            pl.BlockSpec((1, tile, width), lambda f: (j, f, 0)),
        ],
        out_specs=[
            ANY,
            out_spec,
            out_spec,
            pl.BlockSpec((1, slots, 1), lambda f: (0, 0, 0), pipeline_mode=once),
        ],
        scratch_shapes=[
            pltpu.VMEM((width, slots), LOW),
            pltpu.VMEM((slots, width), LOW),
            pltpu.VMEM((slots, width), FULL),
            pltpu.VMEM((slots, width), FULL),
            pltpu.VMEM((2, 2, dp_count, high, tile), LOW),
            pltpu.VMEM((2, some, low, width), LOW),
            pltpu.SemaphoreType.DMA((2, 3)),
        ],
        compiler_params=pltpu.CompilerParams(vmem_limit_bytes=60 << 20),
        cost_estimate=pl.CostEstimate(
            flops=18 * slots * width * hidden,
            transcendentals=slots * hidden,
            bytes_accessed=12 * width * hidden,
        ),
        name="expert",
    )(x_rows, dy_rows, scales, w_gate_up, w_gate_up, w_down)


def rms_scale(values):
    return lax.rsqrt(jnp.mean(values * values, axis=-1, keepdims=True) + NORM_EPS)


def rotary_tables(length, size):
    index = jnp.arange(size // 2, dtype=FULL)
    frequency = jnp.exp(index * (-2.0 * math.log(10000.0) / size))
    angles = jnp.arange(length, dtype=FULL)[:, None] * frequency[None, :]
    cosine, sine = jnp.cos(angles), jnp.sin(angles)
    return jnp.stack(
        [jnp.concatenate([cosine, cosine], axis=1), jnp.concatenate([-sine, sine], axis=1)]
    )


def norm_back(grad_normed, normed, scale_rows):
    return scale_rows * (
        grad_normed - normed * jnp.mean(grad_normed * normed, axis=-1, keepdims=True)
    )


def contract_rows(left_side, right_side):
    return lax.dot_general(
        left_side, right_side, (((0,), (0,)), ((), ())), preferred_element_type=FULL
    )


def contract_cols(left_side, right_side):
    return lax.dot_general(
        left_side, right_side, (((1,), (1,)), ((), ())), preferred_element_type=FULL
    )


def einsum(spec, left_side, right_side):
    return jnp.einsum(spec, left_side, right_side, preferred_element_type=FULL)


def turn(values, cosine, sine):
    return values * cosine + pltpu.roll(values, values.shape[1] // 2, 1) * sine


def allowed_pairs(column_ref, row_ref):
    shape = (column_ref.shape[1], row_ref.shape[2])
    later = lax.broadcasted_iota(jnp.int32, shape, 0) >= lax.broadcasted_iota(jnp.int32, shape, 1)
    return later & (column_ref[0] == row_ref[0])


def softmax(query, key, allowed):
    scores = across_cols(query, key) * (1.0 / math.sqrt(query.shape[1]))
    scores = jnp.where(allowed, scores, -1e30)
    powers = jnp.exp(scores - jnp.max(scores, axis=-1, keepdims=True))
    return powers / jnp.sum(powers, axis=-1, keepdims=True)


def attend_kernel(
    heads, rows_ref, scale_ref, gain_ref, turn_ref, column_ref, row_ref, kept_ref, out_ref
):
    width = out_ref.shape[2]
    size = width // heads
    allowed = allowed_pairs(column_ref, row_ref)
    cosine, sine = turn_ref[0], turn_ref[1]
    for h in range(heads):
        parts = []
        for part in range(3):
            columns = pl.ds(part * width + h * size, size)
            values = rows_ref[0, :, columns]
            if part < 2:
                values = values * scale_ref[0, :, part : part + 1]
                values = values * gain_ref[part : part + 1, h * size : (h + 1) * size]
                values = turn(values, cosine, sine)
            parts.append(values.astype(LOW))
            kept_ref[0, :, columns] = parts[-1]
        query, key, value = parts
        probs = softmax(query, key, allowed).astype(LOW)
        out_ref[0, :, pl.ds(h * size, size)] = jnp.dot(
            probs, value, preferred_element_type=FULL
        ).astype(LOW)


def block_of(array):
    rest = array.shape[1:]
    return pl.BlockSpec((1,) + rest, lambda g: (g,) + (0,) * len(rest))


def whole_of(array):
    return pl.BlockSpec(array.shape, lambda g: (0,) * array.ndim, pipeline_mode=pl.Buffered(1))


def attend(heads, rows, scales, gains, turns, column, row):
    groups, length, width = rows.shape
    kept = jax.ShapeDtypeStruct((groups, length, width), LOW)
    out = jax.ShapeDtypeStruct((groups, length, width // 3), LOW)
    return pl.pallas_call(
        functools.partial(attend_kernel, heads),
        out_shape=[kept, out],
        grid=(groups,),
        in_specs=[
            block_of(rows),
            block_of(scales),
            whole_of(gains),
            whole_of(turns),
            block_of(column),
            block_of(row),
        ],
        out_specs=[block_of(kept), block_of(out)],
        cost_estimate=pl.CostEstimate(
            flops=4 * groups * length * length * width, transcendentals=0, bytes_accessed=8 * rows.size
        ),
        name="attend",
    )(rows, scales, gains, turns, column, row)


def attend_back_kernel(
    heads,
    grad_ref,
    w_ref,
    kept_ref,
    out_ref,
    rows_ref,
    scale_ref,
    gain_ref,
    turn_ref,
    column_ref,
    row_ref,
    back_ref,
    dots_ref,
    gains_ref,
    w_grad_ref,
    w_sum,
):
    step = pl.program_id(0)
    width = out_ref.shape[2]
    size = width // heads
    scaling = 1.0 / math.sqrt(size)
    allowed = allowed_pairs(column_ref, row_ref)
    cosine, sine = turn_ref[0], turn_ref[1]

    @pl.when(step == 0)
    def _():
        w_sum[...] = jnp.zeros_like(w_sum)
        gains_ref[...] = jnp.zeros_like(gains_ref)

    grad_rows = grad_ref[0]
    grad_out = across_cols(grad_rows, w_ref[...]).astype(LOW)
    w_sum[...] += contract_rows(out_ref[0], grad_rows)
    dots = [0.0, 0.0]
    for h in range(heads):
        mine = slice(h * size, (h + 1) * size)
        query, key, value = (kept_ref[0, :, pl.ds(p * width + h * size, size)] for p in range(3))
        probs = softmax(query, key, allowed)
        grad = grad_out[:, mine]
        grad_value = contract_rows(probs.astype(LOW), grad)
        grad_probs = across_cols(grad, value)
        delta = jnp.sum(grad_probs * probs, axis=-1, keepdims=True)
        grad_scores = (probs * (grad_probs - delta)).astype(LOW)
        grad_query = jnp.dot(grad_scores, key, preferred_element_type=FULL) * scaling
        grad_key = contract_rows(grad_scores, query) * scaling
        for part, grad_turned in enumerate((grad_query, grad_key)):
            columns = pl.ds(part * width + h * size, size)
            grad_normed = turn(grad_turned, cosine, -sine)
            normed = rows_ref[0, :, columns] * scale_ref[0, :, part : part + 1]
            gains_ref[part : part + 1, mine] += jnp.sum(grad_normed * normed, axis=0, keepdims=True)
            weighted = grad_normed * gain_ref[part : part + 1, mine]
            dots[part] += jnp.sum(weighted * normed, axis=-1, keepdims=True)
            back_ref[0, :, columns] = weighted
        back_ref[0, :, pl.ds(2 * width + h * size, size)] = grad_value
    dots_ref[0] = jnp.concatenate(dots, axis=1)

    @pl.when(step == pl.num_programs(0) - 1)
    def _():
        for copy in range(w_grad_ref.shape[0]):
            wide = w_grad_ref.shape[2]
            w_grad_ref[copy] = w_sum[:, copy * wide : (copy + 1) * wide].astype(LOW)


def attend_back(heads, dp_count, grad, w_here, kept, out, rows, scales, gains, turns, column, row):
    groups, length, model_dim = grad.shape
    width = out.shape[2]
    back = jax.ShapeDtypeStruct((groups, length, 3 * width), FULL)
    dots = jax.ShapeDtypeStruct((groups, length, 2), FULL)
    gain_sums = jax.ShapeDtypeStruct((2, width), FULL)
    w_grad = jax.ShapeDtypeStruct((dp_count, width, model_dim // dp_count), LOW)
    blocks = [block_of, whole_of, block_of, block_of, block_of, block_of, whole_of, whole_of]
    arrays = [grad, w_here, kept, out, rows, scales, gains, turns, column, row]
    return pl.pallas_call(
        functools.partial(attend_back_kernel, heads),
        out_shape=[back, dots, gain_sums, w_grad],
        grid=(groups,),
        in_specs=[f(a) for f, a in zip(blocks + [block_of] * 2, arrays)],
        out_specs=[block_of(back), block_of(dots), whole_of(gain_sums), whole_of(w_grad)],
        scratch_shapes=[pltpu.VMEM((width, model_dim), FULL)],
        compiler_params=pltpu.CompilerParams(vmem_limit_bytes=48 << 20),
        cost_estimate=pl.CostEstimate(
            flops=4 * grad.size * width, transcendentals=0, bytes_accessed=10 * grad.size
        ),
        name="attend_back",
    )(*arrays)


def on_device(
    dp_count,
    line_count,
    layer_input,
    out_cotangent,
    segments,
    routes,
    w_qkv,
    w_out,
    w_router,
    attn_gain,
    mlp_gain,
    query_gain,
    key_gain,
    w_gate_up,
    w_down,
):
    row_count, model_dim = layer_input.shape
    top_count = routes.shape[1]
    expert_count = w_router.shape[1]
    local_count = w_gate_up.shape[0]
    head_size = model_dim // HEADS
    head_cols = model_dim // line_count
    heads_here = head_cols // head_size
    capacity = (row_count * top_count * 9 // 8 + expert_count - 1) // expert_count
    scaling = 1.0 / math.sqrt(head_size)
    place = lax.axis_index("expert")
    all_rows = line_count * row_count
    shard = w_qkv.shape[0]

    small = jnp.concatenate(
        [w_router] + [g[:, None] for g in (attn_gain, mlp_gain, query_gain, key_gain)], axis=1
    )
    small = jnp.pad(small, ((0, 0), (0, 128 - small.shape[1])))
    numbers = jnp.concatenate([routes.T, segments, jnp.zeros((7, row_count), jnp.int32)], axis=0)
    x_all, numbers_all, qkv_here, small, out_full = opening(
        line_count, dp_count, [layer_input, numbers], [4, 1], w_qkv, small, w_out, 1
    )
    out_full = out_full.reshape(model_dim, model_dim)
    late_cotangent, x_all = lax.optimization_barrier((out_cotangent, x_all))
    dy_all = lax.all_gather(late_cotangent, "expert", axis=0)
    qkv_here = qkv_here.reshape(model_dim, 3 * head_cols)
    small = small.reshape(model_dim, small.shape[3])
    router_full = small[:, :expert_count]
    gains = small[:, expert_count : expert_count + 4].astype(FULL)
    gain_attn, gain_mlp = gains[:, 0], gains[:, 1]
    own_gains = lax.dynamic_slice_in_dim(gains, place * head_cols, head_cols, axis=0)
    gain_query, gain_key = own_gains[:, 2], own_gains[:, 3]

    routes_all = numbers_all[:, :top_count]
    segments_all = numbers_all[:, top_count]
    inputs_all = x_all.reshape(all_rows, model_dim).astype(FULL)
    normed_all = inputs_all * rms_scale(inputs_all)
    hidden_one = (normed_all * gain_attn).astype(LOW)
    projected = jnp.dot(hidden_one, qkv_here, preferred_element_type=FULL)
    query_rows = projected[:, :head_cols]
    key_rows = projected[:, head_cols : 2 * head_cols]
    value_rows = projected[:, 2 * head_cols :]
    squares = jnp.stack(
        [jnp.sum(query_rows * query_rows, axis=-1), jnp.sum(key_rows * key_rows, axis=-1)]
    ).reshape(2 * line_count, row_count)
    (squares,) = exchange("expert", line_count, [squares], [True], 4)
    squares = jnp.sum(squares, axis=0).reshape(2, line_count, row_count)
    scales = lax.rsqrt(squares / model_dim + NORM_EPS).transpose(1, 2, 0)
    tables = rotary_tables(row_count, head_size)
    both_gains = jnp.stack([gain_query, gain_key])
    column, row = segments_all[:, :, None], segments_all[:, None, :]
    projected = projected.reshape(line_count, row_count, 3 * head_cols)
    kept, attended = attend(heads_here, projected, scales, both_gains, tables, column, row)
    (own_attended,) = exchange("expert", line_count, [attended], [False], 5)
    own_attended = own_attended.transpose(1, 0, 2).reshape(row_count, model_dim)
    inputs = layer_input.astype(FULL)
    scale_attn = rms_scale(inputs)
    normed_attn = inputs * scale_attn
    residual = inputs + jnp.dot(own_attended, out_full, preferred_element_type=FULL)
    scale_mlp = rms_scale(residual)
    normed_mlp = residual * scale_mlp
    hidden_two = (normed_mlp * gain_mlp).astype(LOW)

    logits = jnp.dot(hidden_two, router_full, preferred_element_type=FULL)
    chosen = jnp.any(routes[:, :, None] == jnp.arange(expert_count)[None, None, :], axis=1)
    masked = jnp.where(chosen, logits, -1e30)
    powers = jnp.where(chosen, jnp.exp(masked - jnp.max(masked, axis=-1, keepdims=True)), 0.0)
    gates = powers / jnp.sum(powers, axis=-1, keepdims=True)

    local = place * local_count + jnp.arange(local_count)
    used = jnp.any(routes_all[:, None] == local[None, :, None, None], axis=2)
    position = jnp.arange(row_count)
    lower = (position[:, None] < position[None, :]).astype(LOW)
    rank = einsum("gju,ut->gjt", used.astype(LOW), lower).astype(jnp.int32)
    rank = jnp.where(used, rank, -1)
    spots = jnp.arange(capacity)
    table = (rank[:, :, None, :] == spots[None, None, :, None]).astype(LOW)
    returns = [(rank[:, j, :, None] == spots[None, None, :]).astype(LOW) for j in range(local_count)]
    slots = line_count * capacity
    flat_table = table.reshape(line_count, local_count * capacity, row_count)
    expert_rows, dy_rows, gates_all = gather_place(
        line_count, hidden_two, gates.T, flat_table, dy_all, local_count, 6
    )
    local_gates = lax.dynamic_slice_in_dim(gates_all, place * local_count, local_count, axis=1)
    slot_gates = jnp.sum(table.astype(FULL) * local_gates[:, :, None, :], axis=-1)
    slot_gates = slot_gates.transpose(1, 0, 2).reshape(local_count, slots, 1)
    out_rows, back_rows, slot_grads, grad_sums = [], [], [], []
    for j in range(local_count):
        grads, out_row, back_row, dots = expert(
            j, dp_count, expert_rows, dy_rows, slot_gates, w_gate_up, w_down
        )
        grads = grads.reshape(-1, model_dim)
        grad_sums.append(lax.psum_scatter(grads, "dp", scatter_dimension=0, tiled=True))
        out_rows.append(out_row)
        back_rows.append(back_row.reshape(line_count, capacity, model_dim))
        slot_grads.append(dots.reshape(line_count, capacity))
    gate_rows = model_dim // dp_count
    sum_gate_up = jnp.stack([both[:gate_rows] for both in grad_sums]).astype(FULL)
    sum_down = jnp.stack([both[gate_rows:] for both in grad_sums]).astype(FULL)
    slot_grads = jnp.stack(slot_grads, axis=1)
    grad_gates = jnp.sum(table.astype(FULL) * slot_grads[:, :, :, None], axis=2)
    grad_two, grad_gates = collect_reduce(line_count, returns, back_rows, grad_gates, 8)
    grad_gates = grad_gates.reshape(expert_count, row_count).T
    grad_two = grad_two.astype(FULL)

    grad_out_rows = out_cotangent.astype(FULL)
    grad_logits = gates * (grad_gates - jnp.sum(gates * grad_gates, axis=-1, keepdims=True))
    grad_logits = grad_logits.astype(LOW)
    grad_router = contract_rows(grad_logits, hidden_two)
    grad_two = grad_two + contract_cols(grad_logits, router_full)
    grad_gain_mlp = jnp.sum(grad_two * normed_mlp, axis=0)
    grad_resid = grad_out_rows + norm_back(grad_two * gain_mlp, normed_mlp, scale_mlp)
    grad_attn = grad_resid.astype(LOW)

    (grad_attn_all,) = line_gather(line_count, [grad_attn], [4], 11)
    out_here = lax.dynamic_slice_in_dim(out_full, place * head_cols, head_cols, axis=0)
    back, dots, gain_pair, out_parts = attend_back(
        heads_here,
        dp_count,
        grad_attn_all,
        out_here,
        kept,
        attended,
        projected,
        scales,
        both_gains,
        tables,
        column,
        row,
    )
    dots = dots.transpose(2, 0, 1).reshape(2 * line_count, row_count)
    (dots,) = exchange("expert", line_count, [dots], [True], 12)
    dots = jnp.sum(dots, axis=0).reshape(2, all_rows, 1) / model_dim
    flat_scales = scales.reshape(all_rows, 2)
    back = back.reshape(all_rows, 3 * head_cols)
    projected = projected.reshape(all_rows, 3 * head_cols)
    grads = []
    for part in range(2):
        columns = slice(part * head_cols, (part + 1) * head_cols)
        scale = flat_scales[:, part : part + 1]
        normed = projected[:, columns] * scale
        grads.append(scale * (back[:, columns] - normed * dots[part]))
    grad_proj = jnp.concatenate(grads + [back[:, 2 * head_cols :]], axis=-1).astype(LOW)
    grad_one = contract_cols(grad_proj, qkv_here)
    grad_gain_attn = jnp.sum(grad_one * normed_all, axis=0)
    grad_one = grad_one.astype(LOW).reshape(line_count, row_count, model_dim)
    grad_w_qkv = contract_rows(hidden_one, grad_proj)

    out_cols = model_dim // dp_count
    qkv_parts = grad_w_qkv.astype(LOW).reshape(dp_count, out_cols, 3 * head_cols)
    shared = jnp.concatenate([grad_router, grad_gain_attn[None], grad_gain_mlp[None]], axis=0)
    tall = shared.shape[0] + -shared.shape[0] % 8
    shared = jnp.pad(shared, ((0, tall - shared.shape[0]), (0, 0)))
    shared = shared.reshape(tall, dp_count, line_count, shard).transpose(2, 1, 0, 3)
    shared = shared.reshape(line_count, dp_count * tall, shard)
    shared = jnp.pad(shared, ((0, 0), (0, 0), (0, 128 - shard)))
    out_rows = lax.optimization_barrier((out_rows, grad_one))[0]
    grad_one, mixture, qkv_parts, out_parts, gain_pair, shared = closing(
        line_count,
        dp_count,
        [grad_one, collect(returns, out_rows)],
        4,
        [qkv_parts, out_parts, gain_pair],
        shared,
        14,
    )
    output = (residual + mixture.astype(FULL)).astype(LOW)
    sum_qkv = jnp.sum(qkv_parts.astype(FULL), axis=0).reshape(out_cols, 3, head_cols)
    sum_out = jnp.sum(out_parts.astype(FULL), axis=0)
    gain_pair = jnp.sum(gain_pair, axis=0)
    shared = shared[:, :shard]
    grad_one = grad_one.astype(FULL)
    grad_inputs = grad_resid + norm_back(grad_one * gain_attn, normed_attn, scale_attn)
    return (
        output,
        grad_inputs,
        sum_qkv,
        sum_out,
        shared[:expert_count].T,
        shared[expert_count],
        shared[expert_count + 1],
        gain_pair[0],
        gain_pair[1],
        sum_gate_up.astype(FULL),
        sum_down.astype(FULL),
    )


def solution(mesh):
    both = ("dp", "expert")
    rows, flat = P(both, None), P(both)
    placed = (rows,) * 7 + (flat,) * 4 + (P("expert", None, None),) * 2
    return jax.shard_map(
        functools.partial(on_device, mesh.shape["dp"], mesh.shape["expert"]),
        mesh=mesh,
        in_specs=placed,
        out_specs=(
            rows,
            rows,
            P("dp", None, "expert"),
            P("expert", "dp"),
            rows,
            flat,
            flat,
            P("expert"),
            P("expert"),
            P("expert", "dp", None),
            P("expert", "dp", None),
        ),
        check_vma=False,
    )
```

```python
import functools
import math

import jax
import jax.numpy as jnp
from jax import lax
from jax.experimental import pallas as pl
from jax.experimental.pallas import tpu as pltpu
from jax.sharding import PartitionSpec as P

HEADS = 16
NORM_EPS = 1e-05
MESH = pl.DeviceIdType.MESH
ANY = pl.BlockSpec(memory_space=pl.ANY)
LOW = jnp.bfloat16
FULL = jnp.float32


def line_place():
    place = lax.axis_index("expert")
    level, side = lax.div(place, 2), lax.rem(place, 2)
    return place, level, side, place + 1 - 2 * side


def greet(axis, targets):
    barrier = pltpu.get_barrier_semaphore()
    for target, there in targets:

        def signal(target=target):
            pl.semaphore_signal(barrier, inc=1, device_id={axis: target}, device_id_type=MESH)

        if there is None:
            signal()
        else:
            pl.when(there)(signal)


def line_barrier(levels):
    place, level, _, other = line_place()
    has_up, has_down = level < levels - 1, level > 0
    greet("expert", [(other, None), (place + 2, has_up), (place - 2, has_down)])
    count = 1 + has_up.astype(jnp.int32) + has_down.astype(jnp.int32)
    pl.semaphore_wait(pltpu.get_barrier_semaphore(), count)


def around(axis, size):
    place = lax.axis_index(axis)
    return [lax.rem(place + shift, size) for shift in range(1, size)]


def remote(source, target, send, recv, device):
    return pltpu.make_async_remote_copy(
        src_ref=source,
        dst_ref=target,
        send_sem=send,
        recv_sem=recv,
        device_id=device,
        device_id_type=MESH,
    )


class LineGather:
    def __init__(self, levels, cuts, ins, outs, up_sem, down_sem, side_sem, recv_sem, own_sem):
        self.levels, self.cuts, self.ins, self.outs = levels, cuts, ins, outs
        self.up_sem, self.down_sem, self.side_sem = up_sem, down_sem, side_sem
        self.recv_sem, self.own_sem = recv_sem, own_sem
        self.place, self.level, self.side, self.other = line_place()
        self.has_up, self.has_down = self.level < levels - 1, self.level > 0

    @staticmethod
    def scratch(size, cuts, count):
        levels, total = size // 2, cuts + count - 1
        shapes = ((levels, total), (levels, total), (2 * levels - 1, total), (size, total))
        return [pltpu.SemaphoreType.DMA(shape) for shape in shapes + ((count,),)]

    def pieces(self):
        return [(0, k) for k in range(self.cuts)] + [(i, 0) for i in range(1, len(self.ins))]

    def staying(self, i):
        target = self.outs[i].at[self.place]
        return pltpu.make_async_copy(self.ins[i], target, self.own_sem.at[i])

    def sending(self, piece, block, own, sem, target):
        i, k = piece
        landing, source, q = self.outs[i].at[block], self.ins[i], k
        if i:
            q = self.cuts + i - 1
        else:
            rows = source.shape[0] // self.cuts
            landing, source = landing.at[pl.ds(k * rows, rows)], source.at[pl.ds(k * rows, rows)]
        sems = sem.at[q], self.recv_sem.at[block, q]
        return remote(source if own else landing, landing, *sems, {"expert": target})

    def up(self, piece, step, own=False):
        block = self.place - 2 * step
        return self.sending(piece, block, own, self.up_sem.at[step], self.place + 2)

    def down(self, piece, step, own=False):
        block = self.place + 2 * step
        return self.sending(piece, block, own, self.down_sem.at[step], self.place - 2)

    def across(self, piece, step, own=False):
        sem = self.side_sem.at[step + self.levels - 1]
        return self.sending(piece, self.place - 2 * step, own, sem, self.other)

    def begin(self):
        for piece in self.pieces():
            pl.when(self.has_up)(self.up(piece, 0, True).start)
            pl.when(self.has_down)(self.down(piece, 0, True).start)
        for piece in self.pieces():
            self.across(piece, 0, True).start()
        for i in range(len(self.ins)):
            self.staying(i).start()

    def forward(self, step, piece):
        @pl.when(self.level >= step)
        def _():
            self.across(piece, step).wait_recv()
            pl.when(self.has_up)(self.up(piece, step).start)
            self.across(piece, step).start()

        @pl.when(self.level + step < self.levels)
        def _():
            self.across(piece, -step).wait_recv()
            pl.when(self.has_down)(self.down(piece, step).start)
            self.across(piece, -step).start()

    def land_across(self, block):
        for piece in self.pieces():
            self.sending(piece, block, False, self.side_sem.at[0], self.other).wait_recv()

    def main(self, landed=None, before=None):
        levels, cuts = self.levels, self.cuts

        @pl.loop(0, levels * cuts)
        def _(turn):
            step, k = lax.div(turn, cuts) + 1, lax.rem(turn, cuts)

            @pl.when(step < levels)
            def _():
                if before:
                    pl.when(k == 0)(lambda: before(step))
                self.forward(step, (0, k))

                @pl.when(k == cuts - 1)
                def _():
                    for i in range(1, len(self.ins)):
                        self.forward(step, (i, 0))

            group, sign, crossed = step - 1, 2 * lax.rem(k, 2) - 1, lax.div(k, 2)
            crossed = jnp.where(group == 0, k, crossed)
            far = jnp.where(group == 0, self.level, self.level + sign * group)

            @pl.when((far >= 0) & (far < levels) & (k < 4) & ((group > 0) | (k < 2)))
            def _():
                block = 2 * far + self.side + crossed * (1 - 2 * self.side)

                @pl.when(crossed == 1)
                def _():
                    self.land_across(block)

                if landed:
                    landed(block)

    def finish(self, held=0):
        for piece in self.pieces():
            self.across(piece, 0).wait_send()
            for step in range(self.levels):
                above, below = self.level >= step, self.level + step < self.levels
                pl.when(self.has_up & above)(self.up(piece, step).wait_send)
                pl.when(self.has_down & below)(self.down(piece, step).wait_send)
                if step:
                    pl.when(above)(self.across(piece, step).wait_send)
                    pl.when(below)(self.across(piece, -step).wait_send)
        for i in range(held, len(self.ins)):
            self.staying(i).wait()


def call(kernel, name, number, outs, scratch, arrays, moved):
    return pl.pallas_call(
        kernel,
        out_shape=outs,
        in_specs=[ANY] * len(arrays),
        out_specs=[ANY] * len(outs),
        scratch_shapes=scratch,
        compiler_params=pltpu.CompilerParams(
            collective_id=number, has_side_effects=True, vmem_limit_bytes=48 << 20
        ),
        cost_estimate=pl.CostEstimate(flops=0, transcendentals=0, bytes_accessed=moved),
        name=name,
    )(*arrays)


class LineReduce:
    def __init__(self, levels, cuts, parts, total, own, beside, rising, falling, *sems):
        self.levels, self.cuts, self.parts, self.total = levels, cuts, parts, total
        self.made = parts.shape[0] == levels
        self.own, self.beside, self.rising, self.falling = own, beside, rising, falling
        self.load_sem, self.side_send, self.side_recv = sems[:3]
        self.up_send, self.up_recv, self.down_send, self.down_recv, self.out_sem = sems[3:]
        self.place, self.level, self.side, self.other = line_place()
        self.has_up, self.has_down = self.level < levels - 1, self.level > 0
        self.rows = parts.shape[1] // cuts

    @staticmethod
    def scratch(size, block, dtype, cuts):
        levels = size // 2
        return (
            [pltpu.VMEM((levels,) + block, dtype)] * 4
            + [pltpu.SemaphoreType.DMA((levels, cuts))] * 7
            + [pltpu.SemaphoreType.DMA((cuts,))]
        )

    def cut(self, ref, block, k):
        return ref.at[block, pl.ds(k * self.rows, self.rows)]

    def loading(self, far, k):
        source = self.cut(self.parts, 2 * far + self.side, k)
        return pltpu.make_async_copy(source, self.cut(self.own, far, k), self.load_sem.at[far, k])

    def across(self, far, k):
        source = self.cut(self.parts, far if self.made else 2 * far + 1 - self.side, k)
        sems = self.side_send.at[far, k], self.side_recv.at[far, k]
        return remote(source, self.cut(self.beside, far, k), *sems, {"expert": self.other})

    def up(self, far, k):
        sems = self.up_send.at[far, k], self.up_recv.at[far, k]
        target = {"expert": self.place + 2}
        return remote(self.cut(self.own, far, k), self.cut(self.rising, far, k), *sems, target)

    def down(self, far, k):
        sems = self.down_send.at[far, k], self.down_recv.at[far, k]
        target = {"expert": self.place - 2}
        return remote(self.cut(self.own, far, k), self.cut(self.falling, far, k), *sems, target)

    def value(self, ref, block, k):
        return self.cut(ref, block, k)[...].astype(FULL)

    def load(self):
        for i in range(self.levels):
            for k in range(self.cuts):
                self.loading(self.far(i), k).start()

    def begin(self):
        for i in range(self.levels):
            for k in range(self.cuts):
                self.across(self.far(i), k).start()

    def far(self, i):
        return jnp.where(lax.rem(i, 2) == 0, self.levels - 1 - lax.div(i, 2), lax.div(i, 2))

    def prepare(self, turn, make):
        far = self.far(lax.div(turn, 2))

        @pl.when(lax.rem(turn, 2) == 0)
        def _():
            make(2 * far + 1 - self.side, self.parts.at[far])
            for k in range(self.cuts):
                self.across(far, k).start()

        @pl.when(lax.rem(turn, 2) == 1)
        def _():
            make(2 * far + self.side, self.own.at[far])

    def pair(self, far, k):
        if not self.made:
            self.loading(far, k).wait()
        self.across(far, k).wait_recv()
        return self.value(self.own, far, k) + self.value(self.beside, far, k)

    def store(self, far, k, total):
        self.cut(self.own, far, k)[...] = total.astype(self.own.dtype)

    def toward(self, far, k, ahead, behind, move, arrived):
        @pl.when(ahead & behind)
        def _():
            both = self.pair(far, k)
            move(far, k).wait_recv()
            self.store(far, k, both + self.value(arrived, far, k))

        @pl.when(ahead & jnp.logical_not(behind))
        def _():
            self.store(far, k, self.pair(far, k))

        pl.when(ahead)(move(far, k).start)

    def main(self, beside=None):
        @pl.loop(0, (self.levels - 1) * self.cuts)
        def _(turn):
            step, k = lax.div(turn, self.cuts), lax.rem(turn, self.cuts)
            high, low = self.levels - 1 - step, step
            if beside:
                beside(turn)
            self.toward(high, k, self.level < high, self.has_down, self.up, self.rising)
            self.toward(low, k, self.level > low, self.has_up, self.down, self.falling)

        @pl.loop(0, self.cuts)
        def _(k):
            self.store(self.level, k, self.pair(self.level, k))
            for there, move, arrived in (
                (self.has_down, self.up, self.rising),
                (self.has_up, self.down, self.falling),
            ):

                @pl.when(there)
                def _():
                    move(self.level, k).wait_recv()
                    total = self.value(self.own, self.level, k) + self.value(arrived, self.level, k)
                    self.store(self.level, k, total)

            self.leaving(k).start()

    def leaving(self, k):
        target = self.total.at[pl.ds(k * self.rows, self.rows)]
        return pltpu.make_async_copy(self.cut(self.own, self.level, k), target, self.out_sem.at[k])

    def finish(self):
        for k in range(self.cuts):
            self.leaving(k).wait()
            for far in range(self.levels):
                self.across(far, k).wait_send()
                pl.when(self.level < far)(self.up(far, k).wait_send)
                pl.when(self.level > far)(self.down(far, k).wait_send)


class Exchange:
    def __init__(self, axis, size, spread, cuts, ins, outs, send_sem, recv_sem, own_sem):
        self.axis, self.spread, self.ins, self.outs = axis, spread, ins, outs
        self.send_sem, self.recv_sem, self.own_sem = send_sem, recv_sem, own_sem
        self.cuts = cuts
        self.firsts = [sum(cuts[:i]) for i in range(len(cuts))]
        self.pieces = [(i, k) for i in range(len(cuts)) for k in range(cuts[i])]
        self.place, self.peers = lax.axis_index(axis), around(axis, size)

    @staticmethod
    def scratch(size, cuts):
        sems = pltpu.SemaphoreType.DMA
        return [sems((sum(cuts), size)), sems((sum(cuts), size)), sems((len(cuts),))]

    def source(self, i, block):
        return self.ins[i] if self.spread[i] else self.ins[i].at[block]

    def staying(self, i):
        target = self.outs[i].at[self.place]
        return pltpu.make_async_copy(self.source(i, self.place), target, self.own_sem.at[i])

    def sending(self, i, k, shift, landing):
        peer = self.peers[shift]
        source, target, q = self.source(i, peer), self.outs[i].at[landing], self.firsts[i] + k
        if self.cuts[i] > 1:
            rows = target.shape[0] // self.cuts[i]
            source, target = source.at[pl.ds(k * rows, rows)], target.at[pl.ds(k * rows, rows)]
        sems = self.send_sem.at[q, shift], self.recv_sem.at[q, landing]
        return remote(source, target, *sems, {self.axis: peer})

    def send(self, i, k):
        for shift in range(len(self.peers)):
            self.sending(i, k, shift, self.place).start()

    def stay(self):
        for i in range(len(self.spread)):
            self.staying(i).start()

    def begin(self):
        for i, k in self.pieces:
            self.send(i, k)
        self.stay()

    def land(self):
        for shift, peer in enumerate(self.peers):
            for i, k in self.pieces:
                self.sending(i, k, shift, peer).wait_recv()

    def arrive(self):
        self.land()
        for i in range(len(self.spread)):
            self.staying(i).wait()

    def finish(self):
        for shift in range(len(self.peers)):
            for i, k in self.pieces:
                self.sending(i, k, shift, self.place).wait_send()


def exchange_kernel(axis, size, spread, *refs):
    count = len(spread)
    ins, outs, sems = refs[:count], refs[count : 2 * count], refs[2 * count :]
    moves = Exchange(axis, size, spread, (1,) * count, ins, outs, *sems)
    greet(axis, [(peer, None) for peer in moves.peers])
    pl.semaphore_wait(pltpu.get_barrier_semaphore(), size - 1)
    moves.begin()
    moves.arrive()
    moves.finish()


def exchange_outs(size, arrays, spread):
    return [
        jax.ShapeDtypeStruct((size,) + a.shape if flat else a.shape, a.dtype)
        for a, flat in zip(arrays, spread)
    ]


def exchange(axis, size, arrays, spread, number):
    return call(
        functools.partial(exchange_kernel, axis, size, tuple(spread)),
        "exchange_" + axis,
        number,
        exchange_outs(size, arrays, spread),
        Exchange.scratch(size, (1,) * len(arrays)),
        arrays,
        30_000_000,
    )


def opening_kernel(size, dp_count, count, cuts, *refs):
    levels = size // 2
    ins, (w_ref, small_ref, sheet_ref) = refs[:count], refs[count : count + 3]
    outs, rest = refs[count + 3 : 2 * count + 3], refs[2 * count + 3 :]
    w_out, small_out, sheet_out = rest[:3]
    line = LineGather(levels, cuts, ins, outs, *rest[3:8])
    send_sem, recv_sem, own_sem = rest[8:11]
    level, side, other = line.level, line.side, line.other
    place, mine = line.place, lax.axis_index("dp")
    peers = around("expert", size)
    width = w_out.shape[3] // 3
    mine_refs = [w_out.at[mine], small_out.at[mine]]
    across = Exchange(
        "dp", dp_count, (True,) * 2, (size,) * 2, mine_refs, [w_out, small_out], *rest[11:14]
    )
    up_send, down_send, line_recv, dp_send, dp_recv, side_send, side_recv, sheet_own = rest[14:]
    greet("expert", [(peer, None) for peer in peers])
    greet("dp", [(peer, None) for peer in across.peers])
    pl.semaphore_wait(pltpu.get_barrier_semaphore(), size + dp_count - 2)

    def ends(peer, landing, j):
        if j == 3:
            return small_ref, small_out.at[mine, landing]
        start = pl.multiple_of(j * width * size + peer * width, 128)
        target = w_out.at[mine, landing, :, pl.ds(j * width, width)]
        return w_ref.at[:, pl.ds(start, width)], target

    def sending(shift, landing, j):
        source, target = ends(peers[shift], landing, j)
        sems = send_sem.at[shift, j], recv_sem.at[landing, j]
        return remote(source, target, *sems, {"expert": peers[shift]})

    def sheet_line(far, own, send, target):
        landing = sheet_out.at[mine, 2 * far + side]
        source = sheet_ref if own else landing
        return remote(source, landing, send.at[far], line_recv.at[far], {"expert": target})

    def sheet_up(far, own=False):
        return sheet_line(far, own, up_send, place + 2)

    def sheet_down(far, own=False):
        return sheet_line(far, own, down_send, place - 2)

    def sheet_dp(far, shift, copy, own=False):
        landing = sheet_out.at[copy, 2 * far + side]
        source = sheet_ref if own else landing
        sems = dp_send.at[shift, far], dp_recv.at[copy, far]
        return remote(source, landing, *sems, {"dp": across.peers[shift]})

    def sheet_side(far, copy, whose, own=False):
        landing = sheet_out.at[copy, 2 * far + whose]
        source = sheet_ref if own else landing
        sems = side_send.at[copy, far], side_recv.at[copy, far]
        return remote(source, landing, *sems, {"expert": other})

    def spread_sheet(far, own=False):
        for shift in range(dp_count - 1):
            sheet_dp(far, shift, mine, own).start()
        sheet_side(far, mine, side, own).start()

    own = [pltpu.make_async_copy(*ends(place, place, j), own_sem.at[j]) for j in range(4)]
    sheet_stays = pltpu.make_async_copy(sheet_ref, sheet_out.at[mine, place], sheet_own.at[0])
    for shift in range(size - 1):
        for j in range(4):
            sending(shift, place, j).start()
    for copy in own:
        copy.start()
    sheet_stays.start()
    pl.when(line.has_up)(sheet_up(level, True).start)
    pl.when(line.has_down)(sheet_down(level, True).start)
    spread_sheet(level, True)
    line.begin()
    for copy in own:
        copy.wait()
    across.send(0, place)
    across.send(1, place)
    for shift, peer in enumerate(peers):
        for j in range(4):
            sending(shift, peer, j).wait_recv()
        across.send(0, peer)
        across.send(1, peer)

    def pass_sheets(step):
        @pl.when(level >= step)
        def _():
            sheet_up(level - step).wait_recv()
            pl.when(line.has_up)(sheet_up(level - step).start)
            spread_sheet(level - step)

        @pl.when(level + step < levels)
        def _():
            sheet_down(level + step).wait_recv()
            pl.when(line.has_down)(sheet_down(level + step).start)
            spread_sheet(level + step)

    line.main(before=pass_sheets)
    for shift, peer in enumerate(across.peers):
        for far in range(levels):
            sheet_dp(far, shift, peer).wait_recv()
            sheet_side(far, peer, side).start()
    line.finish()
    for shift in range(size - 1):
        for j in range(4):
            sending(shift, place, j).wait_send()
    across.land()
    across.finish()
    for far in range(levels):
        pl.when(line.has_up & (level >= far))(sheet_up(far).wait_send)
        pl.when(line.has_down & (level <= far))(sheet_down(far).wait_send)
        for shift in range(dp_count - 1):
            sheet_dp(far, shift, mine).wait_send()
        for copy in range(dp_count):
            sheet_side(far, copy, 1 - side).wait_recv()
            sheet_side(far, copy, side).wait_send()
    sheet_stays.wait()


def opening(size, dp_count, arrays, cuts, weights, small, sheet, number):
    sems = pltpu.SemaphoreType.DMA
    levels = size // 2
    outs = [jax.ShapeDtypeStruct((size,) + a.shape, a.dtype) for a in arrays]
    rows, columns = weights.shape
    whole = (dp_count, size, rows)
    outs.append(jax.ShapeDtypeStruct(whole + (columns // size,), weights.dtype))
    outs.append(jax.ShapeDtypeStruct(whole + (small.shape[1],), small.dtype))
    outs.append(jax.ShapeDtypeStruct((dp_count, size) + sheet.shape, sheet.dtype))
    return call(
        functools.partial(opening_kernel, size, dp_count, len(arrays), cuts),
        "opening",
        number,
        outs,
        LineGather.scratch(size, cuts, len(arrays))
        + [sems((size, 4)), sems((size, 4)), sems((4,))]
        + Exchange.scratch(dp_count, (size, size))
        + [sems((levels,))] * 3
        + [sems((dp_count, levels))] * 4
        + [sems((1,))],
        list(arrays) + [weights, small, sheet],
        200_000_000,
    )


VMEM = pl.BlockSpec(memory_space=pltpu.VMEM)
COLUMNS = 512


def gather_place_kernel(levels, cuts, *refs):
    rows_ref, gates_ref, table_ref, dy_ref, x_out, dy_out, gates_out = refs[:7]
    held, dy_held, x_stage, dy_stage = refs[7:11]
    line_sems, (dy_sem, x_sems, dy_sems) = refs[11:16], refs[16:]
    line = LineGather(levels, cuts, [rows_ref, gates_ref], [held, gates_out], *line_sems)
    size, width = 2 * levels, held.shape[2]
    _, local_count, capacity, _ = x_stage.shape

    def leaving(block, stage, out, sems):
        target = out.at[:, pl.ds(pl.multiple_of(block * capacity, 8), capacity)]
        return pltpu.make_async_copy(stage.at[block], target, sems.at[block])

    def place(block, rows, stage, out, sems):
        table = table_ref[block]

        @pl.loop(0, width // COLUMNS)
        def _(n):
            columns = pl.ds(pl.multiple_of(n * COLUMNS, COLUMNS), COLUMNS)
            placed = jnp.dot(table, rows[block, :, columns], preferred_element_type=FULL)
            for j in range(local_count):
                part = placed[j * capacity : (j + 1) * capacity]
                stage[block, j, :, columns] = part.astype(stage.dtype)

        leaving(block, stage, out, sems).start()

    def place_x(block):
        place(block, held, x_stage, x_out, x_sems)

    loading = pltpu.make_async_copy(dy_ref, dy_held, dy_sem.at[0])
    loading.start()
    line_barrier(levels)
    line.begin()
    loading.wait()

    @pl.loop(0, size)
    def _(block):
        place(block, dy_held, dy_stage, dy_out, dy_sems)

    line.staying(0).wait()
    line.main(place_x)
    line.finish(held=1)

    @pl.loop(0, size)
    def _(block):
        leaving(block, x_stage, x_out, x_sems).wait()
        leaving(block, dy_stage, dy_out, dy_sems).wait()


def gather_place(size, rows, gates, table, dy, local_count, number):
    cuts = 4
    tokens, width = rows.shape
    capacity = table.shape[1] // local_count
    placed = jax.ShapeDtypeStruct((local_count, size * capacity, width), rows.dtype)
    sems = pltpu.SemaphoreType.DMA
    return pl.pallas_call(
        functools.partial(gather_place_kernel, size // 2, cuts),
        out_shape=[placed, placed, jax.ShapeDtypeStruct((size,) + gates.shape, gates.dtype)],
        in_specs=[ANY, ANY, VMEM, ANY],
        out_specs=[ANY] * 3,
        scratch_shapes=[pltpu.VMEM((size, tokens, width), rows.dtype)] * 2
        + [pltpu.VMEM((size, local_count, capacity, width), rows.dtype)] * 2
        + LineGather.scratch(size, cuts, 2)
        + [sems((1,)), sems((size,)), sems((size,))],
        compiler_params=pltpu.CompilerParams(
            collective_id=number, has_side_effects=True, vmem_limit_bytes=48 << 20
        ),
        cost_estimate=pl.CostEstimate(
            flops=4 * table.size * width, transcendentals=0, bytes_accessed=150_000_000
        ),
        name="gather_place",
    )(rows, gates, table, dy)


def collect_block(tables, slots, block, target):
    @pl.loop(0, target.shape[1] // COLUMNS)
    def _(n):
        columns = pl.ds(pl.multiple_of(n * COLUMNS, COLUMNS), COLUMNS)
        total = 0.0
        for table, rows in zip(tables, slots):
            total += jnp.dot(table[block], rows[block, :, columns], preferred_element_type=FULL)
        target[:, columns] = total.astype(target.dtype)


def collect_reduce_kernel(levels, cuts, local_count, *refs):
    tables, slots, small_ref = refs[:local_count], refs[local_count : 2 * local_count], refs[2 * local_count]
    total_ref, small_out = refs[2 * local_count + 1 : 2 * local_count + 3]
    away, rest = refs[2 * local_count + 3], refs[2 * local_count + 4 :]
    line = LineReduce(levels, cuts, away, total_ref, *rest[:12])
    small = Exchange("expert", 2 * levels, (False,), (1,), [small_ref], [small_out], *rest[12:])
    greet("expert", [(peer, None) for peer in small.peers])
    pl.semaphore_wait(pltpu.get_barrier_semaphore(), 2 * levels - 1)

    make = functools.partial(collect_block, tables, slots)
    small.begin()

    @pl.loop(0, 4)
    def _(turn):
        line.prepare(turn, make)

    def beside(turn):
        pl.when(turn + 4 < 2 * levels)(lambda: line.prepare(turn + 4, make))

    line.main(beside)
    small.arrive()
    line.finish()
    small.finish()


def collect_reduce(size, tables, slots, small, number):
    levels, cuts = size // 2, 4
    block = (tables[0].shape[1], slots[0].shape[2])
    kind = slots[0].dtype
    return pl.pallas_call(
        functools.partial(collect_reduce_kernel, levels, cuts, len(tables)),
        out_shape=[
            jax.ShapeDtypeStruct(block, kind),
            jax.ShapeDtypeStruct(small.shape, small.dtype),
        ],
        in_specs=[VMEM] * (2 * len(tables)) + [ANY],
        out_specs=[ANY, ANY],
        scratch_shapes=[pltpu.VMEM((levels,) + block, kind)]
        + LineReduce.scratch(size, block, kind, cuts)
        + Exchange.scratch(size, (1,)),
        compiler_params=pltpu.CompilerParams(
            collective_id=number, has_side_effects=True, vmem_limit_bytes=48 << 20
        ),
        cost_estimate=pl.CostEstimate(flops=0, transcendentals=0, bytes_accessed=150_000_000),
        name="collect_reduce",
    )(*tables, *slots, small)


def closing_kernel(size, dp_count, local_count, cuts, sum_cuts, *refs):
    tables, slots = refs[:local_count], refs[local_count : 2 * local_count]
    parts_ref, *sum_refs = refs[2 * local_count : 2 * local_count + 5]
    outs, rest = refs[2 * local_count + 5 : 2 * local_count + 11], refs[2 * local_count + 11 :]
    levels = size // 2
    back = LineReduce(levels, cuts, parts_ref, outs[0], *rest[:12])
    mixed = LineReduce(levels, cuts, rest[12], outs[1], *rest[13:25])
    qkv_got, out_got, gain_got, got, half, last = rest[25:31]
    sems = rest[31:]
    lands = [qkv_got, out_got, gain_got]
    sums = Exchange("dp", dp_count, (False, False, True), sum_cuts, sum_refs[:3], lands, *sems[:3])
    first = Exchange("expert", size, (False,), (1,), sum_refs[3:], [got], *sems[3:6])
    second = Exchange("dp", dp_count, (False,), (1,), [half], [last], *sems[6:9])
    back.load()
    greet("expert", [(peer, None) for peer in first.peers])
    greet("dp", [(peer, None) for peer in sums.peers])
    pl.semaphore_wait(pltpu.get_barrier_semaphore(), size + dp_count - 2)
    first.begin()
    back.begin()
    sums.stay()
    tall = half.shape[1]
    make = functools.partial(collect_block, tables, slots)

    def beside(turn):
        pl.when(turn < sum_cuts[0])(lambda: sums.send(0, turn))
        after = turn - sum_cuts[0]
        pl.when((after >= 0) & (after < sum_cuts[1]))(lambda: sums.send(1, after))

        @pl.when(after == sum_cuts[1])
        def _():
            sums.send(2, 0)
            first.arrive()
            for copy in range(dp_count):
                rows = pl.ds(copy * tall, tall)
                half[copy] = sum(got[i, rows, :] for i in range(size))
            second.begin()

        pl.when(turn < 2 * levels)(lambda: mixed.prepare(turn, make))

    back.main(beside)
    mixed.main()
    second.arrive()
    outs[5][...] = sum(last[i] for i in range(dp_count))
    sums.arrive()
    wide = outs[2].shape[2]
    for j in range(3):
        columns = slice(j * wide, (j + 1) * wide)
        outs[2][j] = sum(qkv_got[copy, :, columns].astype(FULL) for copy in range(dp_count))
    outs[3][...] = sum(out_got[copy].astype(FULL) for copy in range(dp_count))
    outs[4][...] = sum(gain_got[copy] for copy in range(dp_count))
    for moves in (back, mixed, first, second, sums):
        moves.finish()


def closing(size, dp_count, parts, tables, slots, cuts, sums, shared, number):
    block = parts.shape[1:]
    tall = shared.shape[1] // dp_count
    wide = shared.shape[2]
    sum_cuts = (8, 2, 1)
    qkv, out, gain = exchange_outs(dp_count, sums, (False, False, True))
    shapes = [(3, qkv.shape[1], qkv.shape[2] // 3), out.shape[1:], gain.shape[1:], (tall, wide)]
    outs = [jax.ShapeDtypeStruct(block, parts.dtype)] * 2
    outs += [jax.ShapeDtypeStruct(shape, FULL) for shape in shapes]
    line = LineReduce.scratch(size, block, parts.dtype, cuts)
    return pl.pallas_call(
        functools.partial(closing_kernel, size, dp_count, len(tables), cuts, sum_cuts),
        out_shape=outs,
        in_specs=[VMEM] * (2 * len(tables)) + [ANY] * 5,
        out_specs=[ANY] * 2 + [VMEM] * 4,
        scratch_shapes=line
        + [pltpu.VMEM((size // 2,) + block, parts.dtype)]
        + line
        + [pltpu.VMEM(a.shape, a.dtype) for a in (qkv, out, gain)]
        + [pltpu.VMEM((size,) + shared.shape[1:], FULL)]
        + [pltpu.VMEM((dp_count, tall, wide), FULL)] * 2
        + Exchange.scratch(dp_count, sum_cuts)
        + Exchange.scratch(size, (1,))
        + Exchange.scratch(dp_count, (1,)),
        compiler_params=pltpu.CompilerParams(
            collective_id=number, has_side_effects=True, vmem_limit_bytes=56 << 20
        ),
        cost_estimate=pl.CostEstimate(flops=0, transcendentals=0, bytes_accessed=200_000_000),
        name="closing",
    )(*tables, *slots, parts, *sums, shared)


def across_cols(left_side, right_side):
    return lax.dot_general(
        left_side, right_side, (((1,), (1,)), ((), ())), preferred_element_type=FULL
    )


def expert_kernel(first, count, tiles, x_ref, dy_ref, scale_ref, side_ref, down_ref, grads_ref, out_ref, back_ref, dots_ref,
                  side_w, down_w, turned, turned_act, act, grad_side, side_buf, down_buf, w_sems, sems):
    e, step = pl.program_id(0), pl.program_id(1)
    slot = lax.rem(e, 2)
    hidden, model = down_w.shape[1], down_w.shape[2]
    width, wide = hidden // tiles, model // tiles
    copies = grads_ref.shape[0]
    high, low = model // copies, hidden // copies
    part = side_buf.shape[1]

    def loads(e, tile):
        slot = lax.rem(e, 2)
        out = []
        for half in range(2):
            columns = pl.ds(pl.multiple_of(half * hidden + tile * width, 128), width)
            out.append(pltpu.make_async_copy(side_ref.at[first + e, :, columns], side_w.at[slot, :, columns], w_sems.at[slot, tile, half]))
        rows = pl.ds(pl.multiple_of(tile * width, 128), width)
        out.append(pltpu.make_async_copy(down_ref.at[first + e, rows], down_w.at[slot, rows], w_sems.at[slot, tile, 2]))
        return out

    def leaving(at):
        e, chunk = lax.div(at, tiles), lax.rem(at, tiles)
        slot = lax.rem(at, 2)
        base = e * (high + low)
        columns = pl.ds(pl.multiple_of(chunk * wide, 128), wide)
        if wide >= high:
            target = grads_ref.at[pl.ds(chunk * part, part), pl.ds(base, high)]
        else:
            target = grads_ref.at[pl.ds(lax.div(chunk * wide, high), 1), pl.ds(base + lax.rem(chunk * wide, high), wide)]
        return (pltpu.make_async_copy(side_buf.at[slot], target, sems.at[slot, 0]),
                pltpu.make_async_copy(down_buf.at[slot], grads_ref.at[:, pl.ds(base + high, low), columns], sems.at[slot, 1]))

    @pl.when((e == 0) & (step == 0))
    def _():
        for tile in range(tiles):
            for copy in loads(e, tile): copy.start()

    @pl.when((e + 1 < count) & (step == 0))
    def _():
        for tile in range(tiles):
            for copy in loads(e + 1, tile): copy.start()

    @pl.when(step == 0)
    def _():
        turned[...] = x_ref[0].T
        dots_ref[...] = jnp.zeros_like(dots_ref)

    @pl.when(step < tiles)
    def _():
        for copy in loads(e, step): copy.wait()
        rows, grads, scale = x_ref[0], dy_ref[0], scale_ref[0]
        columns = pl.ds(pl.multiple_of(step * width, 128), width)
        others = pl.ds(pl.multiple_of(hidden + step * width, 128), width)
        gate = jnp.dot(rows, side_w[slot, :, columns], preferred_element_type=FULL)
        up = jnp.dot(rows, side_w[slot, :, others], preferred_element_type=FULL)
        grad_act = across_cols(grads, down_w[slot, columns, :])
        sigmoid = jax.nn.sigmoid(gate)
        silu = gate * sigmoid
        raw = silu * up
        dots_ref[0] += jnp.sum(raw * grad_act, axis=-1, keepdims=True)
        weighted = (scale * raw).astype(LOW)
        act[:, columns] = weighted
        turned_act[columns, :] = weighted.T
        grad_act = grad_act * scale
        grad_side[:, columns] = (grad_act * up * sigmoid * (1.0 + gate * (1.0 - sigmoid))).astype(LOW)
        grad_side[:, others] = (grad_act * silu).astype(LOW)

    @pl.when(step >= tiles)
    def _():
        chunk = step - tiles
        at = e * tiles + chunk
        spot = lax.rem(at, 2)
        columns = pl.ds(pl.multiple_of(chunk * wide, 128), wide)

        @pl.when(at >= 2)
        def _():
            for copy in leaving(at - 2): copy.wait()
        total = jnp.dot(turned[columns, :], grad_side[...], preferred_element_type=FULL)
        side_buf[spot] = total.astype(LOW).reshape(side_buf.shape[1:])
        leaving(at)[0].start()
        total = jnp.dot(turned_act[...], dy_ref[0, :, columns], preferred_element_type=FULL)
        down_buf[spot] = total.astype(LOW).reshape(down_buf.shape[1:])
        leaving(at)[1].start()
        back_ref[0, :, columns] = across_cols(grad_side[...], side_w[slot, columns, :]).astype(LOW)
        out_ref[0, :, columns] = jnp.dot(act[...], down_w[slot, :, columns], preferred_element_type=FULL).astype(LOW)

        @pl.when(at == count * tiles - 1)
        def _():
            for copy in leaving(at - 1) + leaving(at): copy.wait()

def expert(first, count, dp_count, x_rows, dy_rows, scales, w_gate_up, w_down, tiles=4):
    _, slots, width = x_rows.shape
    hidden = w_down.shape[1]
    high, low = width // dp_count, hidden // dp_count
    wide = width // tiles
    part = max(1, wide // high)
    rs = pl.BlockSpec((1, slots, width), lambda e, f: (first + e, 0, 0))
    os = pl.BlockSpec((1, slots, width), lambda e, f: (e, 0, 0))
    sems = pltpu.SemaphoreType.DMA
    return pl.pallas_call(
        functools.partial(expert_kernel, first, count, tiles),
        out_shape=[jax.ShapeDtypeStruct((dp_count, count * (high + low), width), LOW),
                   jax.ShapeDtypeStruct((count, slots, width), LOW), jax.ShapeDtypeStruct((count, slots, width), LOW),
                   jax.ShapeDtypeStruct((count, slots, 1), FULL)],
        grid=(count, 2 * tiles),
        in_specs=[rs, rs, pl.BlockSpec((1, slots, 1), lambda e, f: (first + e, 0, 0)), ANY, ANY],
        out_specs=[ANY, os, os, pl.BlockSpec((1, slots, 1), lambda e, f: (e, 0, 0))],
        scratch_shapes=[pltpu.VMEM((min(2, count), width, 2 * hidden), LOW), pltpu.VMEM((min(2, count), hidden, width), LOW),
                        pltpu.VMEM((width, slots), LOW), pltpu.VMEM((hidden, slots), LOW), pltpu.VMEM((slots, hidden), LOW), pltpu.VMEM((slots, 2 * hidden), LOW),
                        pltpu.VMEM((2, part, min(wide, high), 2 * hidden), LOW), pltpu.VMEM((2, dp_count, low, wide), LOW),
                        sems((min(2, count), tiles, 3)), sems((2, 2))],
        compiler_params=pltpu.CompilerParams(vmem_limit_bytes=62 << 20),
        cost_estimate=pl.CostEstimate(
            flops=18 * count * slots * width * hidden,
            transcendentals=count * slots * hidden,
            bytes_accessed=12 * count * width * hidden,
        ),
        name="expert",
    )(x_rows, dy_rows, scales, w_gate_up, w_down)


def rms_scale(values):
    return lax.rsqrt(jnp.mean(values * values, axis=-1, keepdims=True) + NORM_EPS)


def rotary_tables(length, size):
    index = jnp.arange(size // 2, dtype=FULL)
    frequency = jnp.exp(index * (-2.0 * math.log(10000.0) / size))
    angles = jnp.arange(length, dtype=FULL)[:, None] * frequency[None, :]
    cosine, sine = jnp.cos(angles), jnp.sin(angles)
    return jnp.stack(
        [jnp.concatenate([cosine, cosine], axis=1), jnp.concatenate([-sine, sine], axis=1)]
    )


def norm_back(grad_normed, normed, scale_rows):
    return scale_rows * (
        grad_normed - normed * jnp.mean(grad_normed * normed, axis=-1, keepdims=True)
    )


def contract_rows(left_side, right_side):
    return lax.dot_general(
        left_side, right_side, (((0,), (0,)), ((), ())), preferred_element_type=FULL
    )


def contract_cols(left_side, right_side):
    return lax.dot_general(
        left_side, right_side, (((1,), (1,)), ((), ())), preferred_element_type=FULL
    )


def einsum(spec, left_side, right_side):
    return jnp.einsum(spec, left_side, right_side, preferred_element_type=FULL)


def turn(values, cosine, sine):
    return values * cosine + pltpu.roll(values, values.shape[1] // 2, 1) * sine


def allowed_pairs(column, row):
    shape = (column.shape[0], row.shape[1])
    later = lax.broadcasted_iota(jnp.int32, shape, 0) >= lax.broadcasted_iota(jnp.int32, shape, 1)
    return later & (column == row)


def softmax(query, key, allowed):
    scores = across_cols(query, key) * (1.0 / math.sqrt(query.shape[1]))
    scores = jnp.where(allowed, scores, -1e30)
    powers = jnp.exp(scores - jnp.max(scores, axis=-1, keepdims=True))
    return powers / jnp.sum(powers, axis=-1, keepdims=True)


def attend_kernel(
    heads, rows_ref, scale_ref, gain_ref, turn_ref, column_ref, row_ref, kept_ref, out_ref
):
    width = out_ref.shape[2]
    size = width // heads
    allowed = allowed_pairs(column_ref[0], row_ref[0])
    cosine, sine = turn_ref[0], turn_ref[1]
    for h in range(heads):
        parts = []
        for part in range(3):
            columns = pl.ds(part * width + h * size, size)
            values = rows_ref[0, :, columns]
            if part < 2:
                values = values * scale_ref[0, :, part : part + 1]
                values = values * gain_ref[part : part + 1, h * size : (h + 1) * size]
                values = turn(values, cosine, sine)
            parts.append(values.astype(LOW))
            kept_ref[0, :, columns] = parts[-1]
        query, key, value = parts
        probs = softmax(query, key, allowed).astype(LOW)
        out_ref[0, :, pl.ds(h * size, size)] = jnp.dot(
            probs, value, preferred_element_type=FULL
        ).astype(LOW)


def block_of(array):
    rest = array.shape[1:]
    return pl.BlockSpec((1,) + rest, lambda g: (g,) + (0,) * len(rest))


def whole_of(array):
    return pl.BlockSpec(array.shape, lambda g: (0,) * array.ndim, pipeline_mode=pl.Buffered(1))


def attend(heads, rows, scales, gains, turns, column, row):
    groups, length, width = rows.shape
    kept = jax.ShapeDtypeStruct((groups, length, width), LOW)
    out = jax.ShapeDtypeStruct((groups, length, width // 3), LOW)
    return pl.pallas_call(
        functools.partial(attend_kernel, heads),
        out_shape=[kept, out],
        grid=(groups,),
        in_specs=[
            block_of(rows),
            block_of(scales),
            whole_of(gains),
            whole_of(turns),
            block_of(column),
            block_of(row),
        ],
        out_specs=[block_of(kept), block_of(out)],
        cost_estimate=pl.CostEstimate(
            flops=4 * groups * length * length * width, transcendentals=0, bytes_accessed=8 * rows.size
        ),
        name="attend",
    )(rows, scales, gains, turns, column, row)


def attend_back_block(heads, block, grad_ref, refs, back_ref, dots_ref, gains_ref, w_sum):
    w_ref, kept_ref, out_ref, rows_ref, scale_ref, gain_ref, turn_ref, column_ref, row_ref = refs
    width = out_ref.shape[2]
    size = width // heads
    scaling = 1.0 / math.sqrt(size)
    allowed = allowed_pairs(column_ref[block], row_ref[block])
    cosine, sine = turn_ref[0], turn_ref[1]
    grad_rows = grad_ref[block]
    grad_out = across_cols(grad_rows, w_ref[...]).astype(LOW)
    w_sum[...] += contract_rows(out_ref[block], grad_rows)
    dots = [0.0, 0.0]
    for h in range(heads):
        mine = slice(h * size, (h + 1) * size)
        query, key, value = (
            kept_ref[block, :, pl.ds(p * width + h * size, size)] for p in range(3)
        )
        probs = softmax(query, key, allowed)
        grad = grad_out[:, mine]
        grad_value = contract_rows(probs.astype(LOW), grad)
        grad_probs = across_cols(grad, value)
        delta = jnp.sum(grad_probs * probs, axis=-1, keepdims=True)
        grad_scores = (probs * (grad_probs - delta)).astype(LOW)
        grad_query = jnp.dot(grad_scores, key, preferred_element_type=FULL) * scaling
        grad_key = contract_rows(grad_scores, query) * scaling
        for part, grad_turned in enumerate((grad_query, grad_key)):
            columns = pl.ds(part * width + h * size, size)
            grad_normed = turn(grad_turned, cosine, -sine)
            normed = rows_ref[block, :, columns] * scale_ref[block, :, part : part + 1]
            gains_ref[part : part + 1, mine] += jnp.sum(grad_normed * normed, axis=0, keepdims=True)
            weighted = grad_normed * gain_ref[part : part + 1, mine]
            dots[part] += jnp.sum(weighted * normed, axis=-1, keepdims=True)
            back_ref[block, :, columns] = weighted
        back_ref[block, :, pl.ds(2 * width + h * size, size)] = grad_value
    dots_ref[block] = jnp.concatenate(dots, axis=1)


def attend_back_kernel(levels, cuts, heads, grad_ref, *refs):
    reads, (back_ref, dots_ref, gains_ref, w_grad_ref, w_sum, held), sems = refs[:9], refs[9:15], refs[15:]
    line = LineGather(levels, cuts, [grad_ref], [held], *sems)
    line_barrier(levels)
    line.begin()
    w_sum[...] = jnp.zeros_like(w_sum)
    gains_ref[...] = jnp.zeros_like(gains_ref)
    line.staying(0).wait()

    def landed(block):
        attend_back_block(heads, block, held, reads, back_ref, dots_ref, gains_ref, w_sum)

    line.main(landed)
    wide = w_grad_ref.shape[2]
    for copy in range(w_grad_ref.shape[0]):
        w_grad_ref[copy] = w_sum[:, copy * wide : (copy + 1) * wide].astype(LOW)
    line.finish(held=1)


def attend_back(size, dp_count, heads, grad, arrays, number):
    w_here, _, out, rows = arrays[:4]
    width = out.shape[2]
    tokens, model_dim = grad.shape
    return pl.pallas_call(
        functools.partial(attend_back_kernel, size // 2, 4, heads),
        out_shape=[
            jax.ShapeDtypeStruct(rows.shape, FULL),
            jax.ShapeDtypeStruct((size, tokens, 2), FULL),
            jax.ShapeDtypeStruct((2, width), FULL),
            jax.ShapeDtypeStruct((dp_count, width, model_dim // dp_count), LOW),
        ],
        in_specs=[ANY] + [VMEM] * len(arrays),
        out_specs=[VMEM] * 4,
        scratch_shapes=[
            pltpu.VMEM((width, model_dim), FULL),
            pltpu.VMEM((size, tokens, model_dim), LOW),
        ]
        + LineGather.scratch(size, 4, 1),
        compiler_params=pltpu.CompilerParams(
            collective_id=number, has_side_effects=True, vmem_limit_bytes=48 << 20
        ),
        cost_estimate=pl.CostEstimate(flops=0, transcendentals=0, bytes_accessed=150_000_000),
        name="attend_back",
    )(grad, *arrays)


def on_device(
    dp_count,
    line_count,
    layer_input,
    out_cotangent,
    segments,
    routes,
    w_qkv,
    w_out,
    w_router,
    attn_gain,
    mlp_gain,
    query_gain,
    key_gain,
    w_gate_up,
    w_down,
):
    row_count, model_dim = layer_input.shape
    top_count = routes.shape[1]
    expert_count = w_router.shape[1]
    local_count = w_gate_up.shape[0]
    head_size = model_dim // HEADS
    head_cols = model_dim // line_count
    heads_here = head_cols // head_size
    capacity = (row_count * top_count * 9 // 8 + expert_count - 1) // expert_count
    scaling = 1.0 / math.sqrt(head_size)
    place = lax.axis_index("expert")
    all_rows = line_count * row_count
    shard = w_qkv.shape[0]

    small = jnp.concatenate(
        [w_router] + [g[:, None] for g in (attn_gain, mlp_gain, query_gain, key_gain)], axis=1
    )
    small = jnp.pad(small, ((0, 0), (0, 128 - small.shape[1])))
    numbers = jnp.concatenate([routes.T, segments, jnp.zeros((7, row_count), jnp.int32)], axis=0)
    x_all, numbers_all, qkv_here, small, out_full = opening(
        line_count, dp_count, [layer_input, numbers], 4, w_qkv, small, w_out, 1
    )
    out_full = out_full.reshape(model_dim, model_dim)
    late_cotangent, x_all = lax.optimization_barrier((out_cotangent, x_all))
    dy_all = lax.all_gather(late_cotangent, "expert", axis=0)
    qkv_here = qkv_here.reshape(model_dim, 3 * head_cols)
    small = small.reshape(model_dim, small.shape[3])
    router_full = small[:, :expert_count]
    gains = small[:, expert_count : expert_count + 4].astype(FULL)
    gain_attn, gain_mlp = gains[:, 0], gains[:, 1]
    own_gains = lax.dynamic_slice_in_dim(gains, place * head_cols, head_cols, axis=0)
    gain_query, gain_key = own_gains[:, 2], own_gains[:, 3]

    routes_all = numbers_all[:, :top_count]
    segments_all = numbers_all[:, top_count]
    inputs_all = x_all.reshape(all_rows, model_dim).astype(FULL)
    normed_all = inputs_all * rms_scale(inputs_all)
    hidden_one = (normed_all * gain_attn).astype(LOW)
    projected = jnp.dot(hidden_one, qkv_here, preferred_element_type=FULL)
    query_rows = projected[:, :head_cols]
    key_rows = projected[:, head_cols : 2 * head_cols]
    value_rows = projected[:, 2 * head_cols :]
    squares = jnp.stack(
        [jnp.sum(query_rows * query_rows, axis=-1), jnp.sum(key_rows * key_rows, axis=-1)]
    ).reshape(2 * line_count, row_count)
    (squares,) = exchange("expert", line_count, [squares], [True], 4)
    squares = jnp.sum(squares, axis=0).reshape(2, line_count, row_count)
    scales = lax.rsqrt(squares / model_dim + NORM_EPS).transpose(1, 2, 0)
    tables = rotary_tables(row_count, head_size)
    both_gains = jnp.stack([gain_query, gain_key])
    column, row = segments_all[:, :, None], segments_all[:, None, :]
    projected = projected.reshape(line_count, row_count, 3 * head_cols)
    kept, attended = attend(heads_here, projected, scales, both_gains, tables, column, row)
    (own_attended,) = exchange("expert", line_count, [attended], [False], 5)
    own_attended = own_attended.transpose(1, 0, 2).reshape(row_count, model_dim)
    inputs = layer_input.astype(FULL)
    scale_attn = rms_scale(inputs)
    normed_attn = inputs * scale_attn
    residual = inputs + jnp.dot(own_attended, out_full, preferred_element_type=FULL)
    scale_mlp = rms_scale(residual)
    normed_mlp = residual * scale_mlp
    hidden_two = (normed_mlp * gain_mlp).astype(LOW)

    logits = jnp.dot(hidden_two, router_full, preferred_element_type=FULL)
    chosen = jnp.any(routes[:, :, None] == jnp.arange(expert_count)[None, None, :], axis=1)
    masked = jnp.where(chosen, logits, -1e30)
    powers = jnp.where(chosen, jnp.exp(masked - jnp.max(masked, axis=-1, keepdims=True)), 0.0)
    gates = powers / jnp.sum(powers, axis=-1, keepdims=True)

    local = place * local_count + jnp.arange(local_count)
    used = jnp.any(routes_all[:, None] == local[None, :, None, None], axis=2)
    position = jnp.arange(row_count)
    lower = (position[:, None] < position[None, :]).astype(LOW)
    rank = einsum("gju,ut->gjt", used.astype(LOW), lower).astype(jnp.int32)
    rank = jnp.where(used, rank, -1)
    spots = jnp.arange(capacity)
    table = (rank[:, :, None, :] == spots[None, None, :, None]).astype(LOW)
    returns = [(rank[:, j, :, None] == spots[None, None, :]).astype(LOW) for j in range(local_count)]
    slots = line_count * capacity
    flat_table = table.reshape(line_count, local_count * capacity, row_count)
    expert_rows, dy_rows, gates_all = gather_place(
        line_count, hidden_two, gates.T, flat_table, dy_all, local_count, 6
    )
    local_gates = lax.dynamic_slice_in_dim(gates_all, place * local_count, local_count, axis=1)
    slot_gates = jnp.sum(table.astype(FULL) * local_gates[:, :, None, :], axis=-1)
    slot_gates = slot_gates.transpose(1, 0, 2).reshape(local_count, slots, 1)
    out_rows, back_rows, slot_grads, grad_sums = [], [], [], []
    both_rows = model_dim // dp_count + w_down.shape[1] // dp_count
    for first, count in ((0, 1), (1, local_count - 1)):
        grads, out_row, back_row, dots = expert(
            first, count, dp_count, expert_rows, dy_rows, slot_gates, w_gate_up, w_down
        )
        grads = grads.reshape(-1, model_dim)
        grads = lax.psum_scatter(grads, "dp", scatter_dimension=0, tiled=True)
        grad_sums.append(grads.reshape(count, both_rows, model_dim))
        for kept_list, rows in ((out_rows, out_row), (back_rows, back_row), (slot_grads, dots)):
            for j in range(count):
                kept_list.append(rows[j].reshape(line_count, capacity, rows.shape[2]))
    gate_rows = model_dim // dp_count
    sum_gate_up = jnp.concatenate([both[:, :gate_rows] for both in grad_sums]).astype(FULL)
    sum_down = jnp.concatenate([both[:, gate_rows:] for both in grad_sums]).astype(FULL)
    slot_grads = jnp.stack([dots[:, :, 0] for dots in slot_grads], axis=1)
    grad_gates = jnp.sum(table.astype(FULL) * slot_grads[:, :, :, None], axis=2)
    grad_two, grad_gates = collect_reduce(line_count, returns, back_rows, grad_gates, 8)
    grad_gates = grad_gates.reshape(expert_count, row_count).T
    grad_two = grad_two.astype(FULL)

    grad_out_rows = out_cotangent.astype(FULL)
    grad_logits = gates * (grad_gates - jnp.sum(gates * grad_gates, axis=-1, keepdims=True))
    grad_logits = grad_logits.astype(LOW)
    grad_router = contract_rows(grad_logits, hidden_two)
    grad_two = grad_two + contract_cols(grad_logits, router_full)
    grad_gain_mlp = jnp.sum(grad_two * normed_mlp, axis=0)
    grad_resid = grad_out_rows + norm_back(grad_two * gain_mlp, normed_mlp, scale_mlp)
    grad_attn = grad_resid.astype(LOW)

    out_here = lax.dynamic_slice_in_dim(out_full, place * head_cols, head_cols, axis=0)
    arrays = [out_here, kept, attended, projected, scales, both_gains, tables, column, row]
    back, dots, gain_pair, out_parts = attend_back(
        line_count, dp_count, heads_here, grad_attn, arrays, 11
    )
    dots = dots.transpose(2, 0, 1).reshape(2 * line_count, row_count)
    (dots,) = exchange("expert", line_count, [dots], [True], 12)
    dots = jnp.sum(dots, axis=0).reshape(2, all_rows, 1) / model_dim
    flat_scales = scales.reshape(all_rows, 2)
    back = back.reshape(all_rows, 3 * head_cols)
    projected = projected.reshape(all_rows, 3 * head_cols)
    grads = []
    for part in range(2):
        columns = slice(part * head_cols, (part + 1) * head_cols)
        scale = flat_scales[:, part : part + 1]
        normed = projected[:, columns] * scale
        grads.append(scale * (back[:, columns] - normed * dots[part]))
    grad_proj = jnp.concatenate(grads + [back[:, 2 * head_cols :]], axis=-1).astype(LOW)
    grad_one = contract_cols(grad_proj, qkv_here)
    grad_gain_attn = jnp.sum(grad_one * normed_all, axis=0)
    grad_one = grad_one.astype(LOW).reshape(line_count, row_count, model_dim)
    grad_w_qkv = contract_rows(hidden_one, grad_proj)

    out_cols = model_dim // dp_count
    qkv_parts = grad_w_qkv.astype(LOW).reshape(dp_count, out_cols, 3 * head_cols)
    shared = jnp.concatenate([grad_router, grad_gain_attn[None], grad_gain_mlp[None]], axis=0)
    tall = shared.shape[0] + -shared.shape[0] % 8
    shared = jnp.pad(shared, ((0, tall - shared.shape[0]), (0, 0)))
    shared = shared.reshape(tall, dp_count, line_count, shard).transpose(2, 1, 0, 3)
    shared = shared.reshape(line_count, dp_count * tall, shard)
    shared = jnp.pad(shared, ((0, 0), (0, 0), (0, 128 - shard)))
    grad_one, mixture, sum_qkv, sum_out, gain_pair, shared = closing(
        line_count,
        dp_count,
        grad_one,
        returns,
        out_rows,
        4,
        [qkv_parts, out_parts, gain_pair],
        shared,
        14,
    )
    output = (residual + mixture.astype(FULL)).astype(LOW)
    sum_qkv = sum_qkv.transpose(1, 0, 2)
    shared = shared[:, :shard]
    grad_one = grad_one.astype(FULL)
    grad_inputs = grad_resid + norm_back(grad_one * gain_attn, normed_attn, scale_attn)
    return (
        output,
        grad_inputs,
        sum_qkv,
        sum_out,
        shared[:expert_count].T,
        shared[expert_count],
        shared[expert_count + 1],
        gain_pair[0],
        gain_pair[1],
        sum_gate_up.astype(FULL),
        sum_down.astype(FULL),
    )


def solution(mesh):
    both = ("dp", "expert")
    rows, flat = P(both, None), P(both)
    placed = (rows,) * 7 + (flat,) * 4 + (P("expert", None, None),) * 2
    return jax.shard_map(
        functools.partial(on_device, mesh.shape["dp"], mesh.shape["expert"]),
        mesh=mesh,
        in_specs=placed,
        out_specs=(
            rows,
            rows,
            P("dp", None, "expert"),
            P("expert", "dp"),
            rows,
            flat,
            flat,
            P("expert"),
            P("expert"),
            P("expert", "dp", None),
            P("expert", "dp", None),
        ),
        check_vma=False,
    )
```

```python
import functools
import math

import jax
import jax.numpy as jnp
from jax import lax
from jax.experimental import pallas as pl
from jax.experimental.pallas import tpu as pltpu
from jax.sharding import PartitionSpec as P

HEADS = 16
NORM_EPS = 1e-05
MESH = pl.DeviceIdType.MESH
ANY = pl.BlockSpec(memory_space=pl.ANY)
LOW = jnp.bfloat16
FULL = jnp.float32


def line_place():
    place = lax.axis_index("expert")
    level, side = lax.div(place, 2), lax.rem(place, 2)
    return place, level, side, place + 1 - 2 * side


def greet(axis, targets):
    barrier = pltpu.get_barrier_semaphore()
    for target, there in targets:

        def signal(target=target):
            pl.semaphore_signal(barrier, inc=1, device_id={axis: target}, device_id_type=MESH)

        if there is None:
            signal()
        else:
            pl.when(there)(signal)


def line_barrier(levels):
    place, level, _, other = line_place()
    has_up, has_down = level < levels - 1, level > 0
    greet("expert", [(other, None), (place + 2, has_up), (place - 2, has_down)])
    count = 1 + has_up.astype(jnp.int32) + has_down.astype(jnp.int32)
    pl.semaphore_wait(pltpu.get_barrier_semaphore(), count)


def around(axis, size):
    place = lax.axis_index(axis)
    return [lax.rem(place + shift, size) for shift in range(1, size)]


def remote(source, target, send, recv, device):
    return pltpu.make_async_remote_copy(
        src_ref=source,
        dst_ref=target,
        send_sem=send,
        recv_sem=recv,
        device_id=device,
        device_id_type=MESH,
    )


class LineGather:
    def __init__(self, levels, cuts, ins, outs, up_sem, down_sem, side_sem, recv_sem, own_sem):
        self.levels, self.cuts, self.ins, self.outs = levels, cuts, ins, outs
        self.up_sem, self.down_sem, self.side_sem = up_sem, down_sem, side_sem
        self.recv_sem, self.own_sem = recv_sem, own_sem
        self.place, self.level, self.side, self.other = line_place()
        self.has_up, self.has_down = self.level < levels - 1, self.level > 0

    @staticmethod
    def scratch(size, cuts, count):
        levels, total = size // 2, cuts + count - 1
        shapes = ((levels, total), (levels, total), (2 * levels - 1, total), (size, total))
        return [pltpu.SemaphoreType.DMA(shape) for shape in shapes + ((count,),)]

    def pieces(self):
        return [(0, k) for k in range(self.cuts)] + [(i, 0) for i in range(1, len(self.ins))]

    def staying(self, i):
        target = self.outs[i].at[self.place]
        return pltpu.make_async_copy(self.ins[i], target, self.own_sem.at[i])

    def sending(self, piece, block, own, sem, target):
        i, k = piece
        landing, source, q = self.outs[i].at[block], self.ins[i], k
        if i:
            q = self.cuts + i - 1
        else:
            rows = source.shape[0] // self.cuts
            landing, source = landing.at[pl.ds(k * rows, rows)], source.at[pl.ds(k * rows, rows)]
        sems = sem.at[q], self.recv_sem.at[block, q]
        return remote(source if own else landing, landing, *sems, {"expert": target})

    def up(self, piece, step, own=False):
        block = self.place - 2 * step
        return self.sending(piece, block, own, self.up_sem.at[step], self.place + 2)

    def down(self, piece, step, own=False):
        block = self.place + 2 * step
        return self.sending(piece, block, own, self.down_sem.at[step], self.place - 2)

    def across(self, piece, step, own=False):
        sem = self.side_sem.at[step + self.levels - 1]
        return self.sending(piece, self.place - 2 * step, own, sem, self.other)

    def begin(self):
        for piece in self.pieces():
            pl.when(self.has_up)(self.up(piece, 0, True).start)
            pl.when(self.has_down)(self.down(piece, 0, True).start)
        for piece in self.pieces():
            self.across(piece, 0, True).start()
        for i in range(len(self.ins)):
            self.staying(i).start()

    def forward(self, step, piece):
        @pl.when(self.level >= step)
        def _():
            self.across(piece, step).wait_recv()
            pl.when(self.has_up)(self.up(piece, step).start)
            self.across(piece, step).start()

        @pl.when(self.level + step < self.levels)
        def _():
            self.across(piece, -step).wait_recv()
            pl.when(self.has_down)(self.down(piece, step).start)
            self.across(piece, -step).start()

    def land_across(self, block):
        for piece in self.pieces():
            self.sending(piece, block, False, self.side_sem.at[0], self.other).wait_recv()

    def main(self, landed=None, before=None):
        levels, cuts = self.levels, self.cuts

        @pl.loop(0, levels * cuts)
        def _(turn):
            step, k = lax.div(turn, cuts) + 1, lax.rem(turn, cuts)

            @pl.when(step < levels)
            def _():
                if before:
                    pl.when(k == 0)(lambda: before(step))
                self.forward(step, (0, k))

                @pl.when(k == cuts - 1)
                def _():
                    for i in range(1, len(self.ins)):
                        self.forward(step, (i, 0))

            group, sign, crossed = step - 1, 2 * lax.rem(k, 2) - 1, lax.div(k, 2)
            crossed = jnp.where(group == 0, k, crossed)
            far = jnp.where(group == 0, self.level, self.level + sign * group)

            @pl.when((far >= 0) & (far < levels) & (k < 4) & ((group > 0) | (k < 2)))
            def _():
                block = 2 * far + self.side + crossed * (1 - 2 * self.side)

                @pl.when(crossed == 1)
                def _():
                    self.land_across(block)

                if landed:
                    landed(block)

    def finish(self, held=0):
        for piece in self.pieces():
            self.across(piece, 0).wait_send()
            for step in range(self.levels):
                above, below = self.level >= step, self.level + step < self.levels
                pl.when(self.has_up & above)(self.up(piece, step).wait_send)
                pl.when(self.has_down & below)(self.down(piece, step).wait_send)
                if step:
                    pl.when(above)(self.across(piece, step).wait_send)
                    pl.when(below)(self.across(piece, -step).wait_send)
        for i in range(held, len(self.ins)):
            self.staying(i).wait()


def call(kernel, name, number, outs, scratch, arrays, moved):
    return pl.pallas_call(
        kernel,
        out_shape=outs,
        in_specs=[ANY] * len(arrays),
        out_specs=[ANY] * len(outs),
        scratch_shapes=scratch,
        compiler_params=pltpu.CompilerParams(
            collective_id=number, has_side_effects=True, vmem_limit_bytes=48 << 20
        ),
        cost_estimate=pl.CostEstimate(flops=0, transcendentals=0, bytes_accessed=moved),
        name=name,
    )(*arrays)


class LineReduce:
    def __init__(self, levels, cuts, parts, total, own, beside, rising, falling, *sems):
        self.levels, self.cuts, self.parts, self.total = levels, cuts, parts, total
        self.made = parts.shape[0] == levels
        self.own, self.beside, self.rising, self.falling = own, beside, rising, falling
        self.load_sem, self.side_send, self.side_recv = sems[:3]
        self.up_send, self.up_recv, self.down_send, self.down_recv, self.out_sem = sems[3:]
        self.place, self.level, self.side, self.other = line_place()
        self.has_up, self.has_down = self.level < levels - 1, self.level > 0
        self.rows = parts.shape[1] // cuts

    @staticmethod
    def scratch(size, block, dtype, cuts):
        levels = size // 2
        return (
            [pltpu.VMEM((levels,) + block, dtype)] * 4
            + [pltpu.SemaphoreType.DMA((levels, cuts))] * 7
            + [pltpu.SemaphoreType.DMA((cuts,))]
        )

    def cut(self, ref, block, k):
        return ref.at[block, pl.ds(k * self.rows, self.rows)]

    def loading(self, far, k):
        source = self.cut(self.parts, 2 * far + self.side, k)
        return pltpu.make_async_copy(source, self.cut(self.own, far, k), self.load_sem.at[far, k])

    def across(self, far, k):
        source = self.cut(self.parts, far if self.made else 2 * far + 1 - self.side, k)
        sems = self.side_send.at[far, k], self.side_recv.at[far, k]
        return remote(source, self.cut(self.beside, far, k), *sems, {"expert": self.other})

    def up(self, far, k):
        sems = self.up_send.at[far, k], self.up_recv.at[far, k]
        target = {"expert": self.place + 2}
        return remote(self.cut(self.own, far, k), self.cut(self.rising, far, k), *sems, target)

    def down(self, far, k):
        sems = self.down_send.at[far, k], self.down_recv.at[far, k]
        target = {"expert": self.place - 2}
        return remote(self.cut(self.own, far, k), self.cut(self.falling, far, k), *sems, target)

    def value(self, ref, block, k):
        return self.cut(ref, block, k)[...].astype(FULL)

    def load(self):
        for i in range(self.levels):
            for k in range(self.cuts):
                self.loading(self.far(i), k).start()

    def begin(self):
        for i in range(self.levels):
            for k in range(self.cuts):
                self.across(self.far(i), k).start()

    def far(self, i):
        return jnp.where(lax.rem(i, 2) == 0, self.levels - 1 - lax.div(i, 2), lax.div(i, 2))

    def prepare(self, turn, make):
        far = self.far(lax.div(turn, 2))

        @pl.when(lax.rem(turn, 2) == 0)
        def _():
            make(2 * far + 1 - self.side, self.parts.at[far])
            for k in range(self.cuts):
                self.across(far, k).start()

        @pl.when(lax.rem(turn, 2) == 1)
        def _():
            make(2 * far + self.side, self.own.at[far])

    def pair(self, far, k):
        if not self.made:
            self.loading(far, k).wait()
        self.across(far, k).wait_recv()
        return self.value(self.own, far, k) + self.value(self.beside, far, k)

    def store(self, far, k, total):
        self.cut(self.own, far, k)[...] = total.astype(self.own.dtype)

    def toward(self, far, k, ahead, behind, move, arrived):
        @pl.when(ahead & behind)
        def _():
            both = self.pair(far, k)
            move(far, k).wait_recv()
            self.store(far, k, both + self.value(arrived, far, k))

        @pl.when(ahead & jnp.logical_not(behind))
        def _():
            self.store(far, k, self.pair(far, k))

        pl.when(ahead)(move(far, k).start)

    def main(self, beside=None):
        @pl.loop(0, (self.levels - 1) * self.cuts)
        def _(turn):
            step, k = lax.div(turn, self.cuts), lax.rem(turn, self.cuts)
            high, low = self.levels - 1 - step, step
            if beside:
                beside(turn)
            self.toward(high, k, self.level < high, self.has_down, self.up, self.rising)
            self.toward(low, k, self.level > low, self.has_up, self.down, self.falling)

        @pl.loop(0, self.cuts)
        def _(k):
            self.store(self.level, k, self.pair(self.level, k))
            for there, move, arrived in (
                (self.has_down, self.up, self.rising),
                (self.has_up, self.down, self.falling),
            ):

                @pl.when(there)
                def _():
                    move(self.level, k).wait_recv()
                    total = self.value(self.own, self.level, k) + self.value(arrived, self.level, k)
                    self.store(self.level, k, total)

            self.leaving(k).start()

    def leaving(self, k):
        target = self.total.at[pl.ds(k * self.rows, self.rows)]
        return pltpu.make_async_copy(self.cut(self.own, self.level, k), target, self.out_sem.at[k])

    def finish(self):
        for k in range(self.cuts):
            self.leaving(k).wait()
            for far in range(self.levels):
                self.across(far, k).wait_send()
                pl.when(self.level < far)(self.up(far, k).wait_send)
                pl.when(self.level > far)(self.down(far, k).wait_send)


class Exchange:
    def __init__(self, axis, size, spread, cuts, ins, outs, send_sem, recv_sem, own_sem):
        self.axis, self.spread, self.ins, self.outs = axis, spread, ins, outs
        self.send_sem, self.recv_sem, self.own_sem = send_sem, recv_sem, own_sem
        self.cuts = cuts
        self.firsts = [sum(cuts[:i]) for i in range(len(cuts))]
        self.pieces = [(i, k) for i in range(len(cuts)) for k in range(cuts[i])]
        self.place, self.peers = lax.axis_index(axis), around(axis, size)

    @staticmethod
    def scratch(size, cuts):
        sems = pltpu.SemaphoreType.DMA
        return [sems((sum(cuts), size)), sems((sum(cuts), size)), sems((len(cuts),))]

    def source(self, i, block):
        return self.ins[i] if self.spread[i] else self.ins[i].at[block]

    def staying(self, i):
        target = self.outs[i].at[self.place]
        return pltpu.make_async_copy(self.source(i, self.place), target, self.own_sem.at[i])

    def sending(self, i, k, shift, landing):
        peer = self.peers[shift]
        source, target, q = self.source(i, peer), self.outs[i].at[landing], self.firsts[i] + k
        if self.cuts[i] > 1:
            rows = target.shape[0] // self.cuts[i]
            source, target = source.at[pl.ds(k * rows, rows)], target.at[pl.ds(k * rows, rows)]
        sems = self.send_sem.at[q, shift], self.recv_sem.at[q, landing]
        return remote(source, target, *sems, {self.axis: peer})

    def send(self, i, k):
        for shift in range(len(self.peers)):
            self.sending(i, k, shift, self.place).start()

    def stay(self):
        for i in range(len(self.spread)):
            self.staying(i).start()

    def begin(self):
        for i, k in self.pieces:
            self.send(i, k)
        self.stay()

    def land(self):
        for shift, peer in enumerate(self.peers):
            for i, k in self.pieces:
                self.sending(i, k, shift, peer).wait_recv()

    def arrive(self):
        self.land()
        for i in range(len(self.spread)):
            self.staying(i).wait()

    def finish(self):
        for shift in range(len(self.peers)):
            for i, k in self.pieces:
                self.sending(i, k, shift, self.place).wait_send()


def exchange_kernel(axis, size, spread, *refs):
    count = len(spread)
    ins, outs, sems = refs[:count], refs[count : 2 * count], refs[2 * count :]
    moves = Exchange(axis, size, spread, (1,) * count, ins, outs, *sems)
    greet(axis, [(peer, None) for peer in moves.peers])
    pl.semaphore_wait(pltpu.get_barrier_semaphore(), size - 1)
    moves.begin()
    moves.arrive()
    moves.finish()


def exchange_outs(size, arrays, spread):
    return [
        jax.ShapeDtypeStruct((size,) + a.shape if flat else a.shape, a.dtype)
        for a, flat in zip(arrays, spread)
    ]


def exchange(axis, size, arrays, spread, number):
    return call(
        functools.partial(exchange_kernel, axis, size, tuple(spread)),
        "exchange_" + axis,
        number,
        exchange_outs(size, arrays, spread),
        Exchange.scratch(size, (1,) * len(arrays)),
        arrays,
        30_000_000,
    )


def opening_kernel(size, dp_count, count, cuts, *refs):
    ins, (w_ref, small_ref) = refs[:count], refs[count : count + 2]
    outs, (w_out, small_out), rest = refs[count + 2 : 2 * count + 2], refs[2 * count + 2 :][:2], refs[2 * count + 4 :]
    line = LineGather(size // 2, cuts, ins, outs, *rest[:5])
    send_sem, recv_sem, own_sem = rest[5:8]
    place, mine = line.place, lax.axis_index("dp")
    peers = around("expert", size)
    width = w_out.shape[3] // 3
    mine_refs = [w_out.at[mine], small_out.at[mine]]
    across = Exchange(
        "dp", dp_count, (True,) * 2, (size,) * 2, mine_refs, [w_out, small_out], *rest[8:]
    )
    greet("expert", [(peer, None) for peer in peers])
    greet("dp", [(peer, None) for peer in across.peers])
    pl.semaphore_wait(pltpu.get_barrier_semaphore(), size + dp_count - 2)

    def ends(peer, landing, j):
        if j == 3:
            return small_ref, small_out.at[mine, landing]
        start = pl.multiple_of(j * width * size + peer * width, 128)
        target = w_out.at[mine, landing, :, pl.ds(j * width, width)]
        return w_ref.at[:, pl.ds(start, width)], target

    def sending(shift, landing, j):
        source, target = ends(peers[shift], landing, j)
        sems = send_sem.at[shift, j], recv_sem.at[landing, j]
        return remote(source, target, *sems, {"expert": peers[shift]})

    own = [pltpu.make_async_copy(*ends(place, place, j), own_sem.at[j]) for j in range(4)]
    for shift in range(size - 1):
        for j in range(4):
            sending(shift, place, j).start()
    for copy in own:
        copy.start()
    line.begin()
    for copy in own:
        copy.wait()
    across.send(0, place)
    across.send(1, place)
    for shift, peer in enumerate(peers):
        for j in range(4):
            sending(shift, peer, j).wait_recv()
        across.send(0, peer)
        across.send(1, peer)
    line.main()
    line.finish()
    for shift in range(size - 1):
        for j in range(4):
            sending(shift, place, j).wait_send()
    across.land()
    across.finish()


def opening(size, dp_count, arrays, cuts, weights, small, number):
    sems = pltpu.SemaphoreType.DMA
    outs = [jax.ShapeDtypeStruct((size,) + a.shape, a.dtype) for a in arrays]
    rows, columns = weights.shape
    whole = (dp_count, size, rows)
    outs.append(jax.ShapeDtypeStruct(whole + (columns // size,), weights.dtype))
    outs.append(jax.ShapeDtypeStruct(whole + (small.shape[1],), small.dtype))
    return call(
        functools.partial(opening_kernel, size, dp_count, len(arrays), cuts),
        "opening",
        number,
        outs,
        LineGather.scratch(size, cuts, len(arrays))
        + [sems((size, 4)), sems((size, 4)), sems((4,))]
        + Exchange.scratch(dp_count, (size, size)),
        list(arrays) + [weights, small],
        200_000_000,
    )


class Sheets:
    def __init__(self, size, dp_count, source, target, *sems):
        self.levels, self.dp_count, self.ins, self.out = size // 2, dp_count, source, target
        self.up_send, self.down_send, self.line_recv, self.dp_send, self.dp_recv = sems[:5]
        self.side_send, self.side_recv, self.own_sem = sems[5:]
        self.place, self.level, self.side, self.other = line_place()
        self.has_up, self.has_down = self.level < self.levels - 1, self.level > 0
        self.mine, self.peers = lax.axis_index("dp"), around("dp", dp_count)

    @staticmethod
    def scratch(size, dp_count):
        sems, levels = pltpu.SemaphoreType.DMA, size // 2
        return [sems((levels,))] * 3 + [sems((dp_count, levels))] * 4 + [sems((1,))]

    def along(self, far, own, send, target):
        landing = self.out.at[self.mine, 2 * far + self.side]
        source = self.ins if own else landing
        return remote(source, landing, send.at[far], self.line_recv.at[far], {"expert": target})

    def up(self, far, own=False):
        return self.along(far, own, self.up_send, self.place + 2)

    def down(self, far, own=False):
        return self.along(far, own, self.down_send, self.place - 2)

    def over(self, far, shift, copy, own=False):
        landing = self.out.at[copy, 2 * far + self.side]
        source = self.ins if own else landing
        sems = self.dp_send.at[shift, far], self.dp_recv.at[copy, far]
        return remote(source, landing, *sems, {"dp": self.peers[shift]})

    def across(self, far, copy, whose, own=False):
        landing = self.out.at[copy, 2 * far + whose]
        source = self.ins if own else landing
        sems = self.side_send.at[copy, far], self.side_recv.at[copy, far]
        return remote(source, landing, *sems, {"expert": self.other})

    def spread(self, far, own=False):
        for shift in range(self.dp_count - 1):
            self.over(far, shift, self.mine, own).start()
        self.across(far, self.mine, self.side, own).start()

    def staying(self):
        target = self.out.at[self.mine, self.place]
        return pltpu.make_async_copy(self.ins, target, self.own_sem.at[0])

    def begin(self):
        pl.when(self.has_up)(self.up(self.level, True).start)
        pl.when(self.has_down)(self.down(self.level, True).start)
        self.spread(self.level, True)
        self.staying().start()

    def forward(self, step):
        @pl.when(self.level >= step)
        def _():
            self.up(self.level - step).wait_recv()
            pl.when(self.has_up)(self.up(self.level - step).start)
            self.spread(self.level - step)

        @pl.when(self.level + step < self.levels)
        def _():
            self.down(self.level + step).wait_recv()
            pl.when(self.has_down)(self.down(self.level + step).start)
            self.spread(self.level + step)

    def cross(self, far):
        for shift, peer in enumerate(self.peers):
            self.over(far, shift, peer).wait_recv()
            self.across(far, peer, self.side).start()

    def finish(self):
        @pl.loop(0, self.levels)
        def _(far):
            pl.when(self.has_up & (self.level >= far))(self.up(far).wait_send)
            pl.when(self.has_down & (self.level <= far))(self.down(far).wait_send)
            for shift in range(self.dp_count - 1):
                self.over(far, shift, self.mine).wait_send()
            for copy in range(self.dp_count):
                self.across(far, copy, 1 - self.side).wait_recv()
                self.across(far, copy, self.side).wait_send()

        self.staying().wait()


VMEM = pl.BlockSpec(memory_space=pltpu.VMEM)
COLUMNS = 512


def gather_place_kernel(levels, cuts, *refs):
    rows_ref, gates_ref, table_ref, dy_ref, x_out, dy_out, gates_out = refs[:7]
    held, dy_held, x_stage, dy_stage = refs[7:11]
    line_sems, (dy_sem, x_sems, dy_sems) = refs[11:16], refs[16:]
    line = LineGather(levels, cuts, [rows_ref, gates_ref], [held, gates_out], *line_sems)
    size, width = 2 * levels, held.shape[2]
    _, local_count, capacity, _ = x_stage.shape

    def leaving(block, stage, out, sems):
        target = out.at[:, pl.ds(pl.multiple_of(block * capacity, 8), capacity)]
        return pltpu.make_async_copy(stage.at[block], target, sems.at[block])

    def place(block, rows, stage, out, sems):
        table = table_ref[block]

        @pl.loop(0, width // COLUMNS)
        def _(n):
            columns = pl.ds(pl.multiple_of(n * COLUMNS, COLUMNS), COLUMNS)
            placed = jnp.dot(table, rows[block, :, columns], preferred_element_type=FULL)
            for j in range(local_count):
                part = placed[j * capacity : (j + 1) * capacity]
                stage[block, j, :, columns] = part.astype(stage.dtype)

        leaving(block, stage, out, sems).start()

    def place_x(block):
        place(block, held, x_stage, x_out, x_sems)

    loading = pltpu.make_async_copy(dy_ref, dy_held, dy_sem.at[0])
    loading.start()
    line_barrier(levels)
    line.begin()
    loading.wait()

    @pl.loop(0, size)
    def _(block):
        place(block, dy_held, dy_stage, dy_out, dy_sems)

    line.staying(0).wait()
    line.main(place_x)
    line.finish(held=1)

    @pl.loop(0, size)
    def _(block):
        leaving(block, x_stage, x_out, x_sems).wait()
        leaving(block, dy_stage, dy_out, dy_sems).wait()


def gather_place(size, rows, gates, table, dy, local_count, number):
    cuts = 4
    tokens, width = rows.shape
    capacity = table.shape[1] // local_count
    placed = jax.ShapeDtypeStruct((local_count, size * capacity, width), rows.dtype)
    sems = pltpu.SemaphoreType.DMA
    return pl.pallas_call(
        functools.partial(gather_place_kernel, size // 2, cuts),
        out_shape=[placed, placed, jax.ShapeDtypeStruct((size,) + gates.shape, gates.dtype)],
        in_specs=[ANY, ANY, VMEM, ANY],
        out_specs=[ANY] * 3,
        scratch_shapes=[pltpu.VMEM((size, tokens, width), rows.dtype)] * 2
        + [pltpu.VMEM((size, local_count, capacity, width), rows.dtype)] * 2
        + LineGather.scratch(size, cuts, 2)
        + [sems((1,)), sems((size,)), sems((size,))],
        compiler_params=pltpu.CompilerParams(
            collective_id=number, has_side_effects=True, vmem_limit_bytes=48 << 20
        ),
        cost_estimate=pl.CostEstimate(
            flops=4 * table.size * width, transcendentals=0, bytes_accessed=150_000_000
        ),
        name="gather_place",
    )(rows, gates, table, dy)


def collect_block(tables, slots, block, target):
    @pl.loop(0, target.shape[1] // COLUMNS)
    def _(n):
        columns = pl.ds(pl.multiple_of(n * COLUMNS, COLUMNS), COLUMNS)
        total = 0.0
        for table, rows in zip(tables, slots):
            total += jnp.dot(table[block], rows[block, :, columns], preferred_element_type=FULL)
        target[:, columns] = total.astype(target.dtype)


def collect_reduce_kernel(levels, cuts, local_count, *refs):
    tables, slots, small_ref = refs[:local_count], refs[local_count : 2 * local_count], refs[2 * local_count]
    total_ref, small_out = refs[2 * local_count + 1 : 2 * local_count + 3]
    away, rest = refs[2 * local_count + 3], refs[2 * local_count + 4 :]
    line = LineReduce(levels, cuts, away, total_ref, *rest[:12])
    small = Exchange("expert", 2 * levels, (False,), (1,), [small_ref], [small_out], *rest[12:])
    greet("expert", [(peer, None) for peer in small.peers])
    pl.semaphore_wait(pltpu.get_barrier_semaphore(), 2 * levels - 1)

    make = functools.partial(collect_block, tables, slots)
    small.begin()

    @pl.loop(0, 4)
    def _(turn):
        line.prepare(turn, make)

    def beside(turn):
        pl.when(turn + 4 < 2 * levels)(lambda: line.prepare(turn + 4, make))

    line.main(beside)
    small.arrive()
    line.finish()
    small.finish()


def collect_reduce(size, tables, slots, small, number):
    levels, cuts = size // 2, 4
    block = (tables[0].shape[1], slots[0].shape[2])
    kind = slots[0].dtype
    return pl.pallas_call(
        functools.partial(collect_reduce_kernel, levels, cuts, len(tables)),
        out_shape=[
            jax.ShapeDtypeStruct(block, kind),
            jax.ShapeDtypeStruct(small.shape, small.dtype),
        ],
        in_specs=[VMEM] * (2 * len(tables)) + [ANY],
        out_specs=[ANY, ANY],
        scratch_shapes=[pltpu.VMEM((levels,) + block, kind)]
        + LineReduce.scratch(size, block, kind, cuts)
        + Exchange.scratch(size, (1,)),
        compiler_params=pltpu.CompilerParams(
            collective_id=number, has_side_effects=True, vmem_limit_bytes=48 << 20
        ),
        cost_estimate=pl.CostEstimate(flops=0, transcendentals=0, bytes_accessed=150_000_000),
        name="collect_reduce",
    )(*tables, *slots, small)


def closing_kernel(size, dp_count, local_count, cuts, sum_cuts, *refs):
    tables, slots = refs[:local_count], refs[local_count : 2 * local_count]
    parts_ref, *sum_refs = refs[2 * local_count : 2 * local_count + 5]
    outs, rest = refs[2 * local_count + 5 : 2 * local_count + 11], refs[2 * local_count + 11 :]
    levels = size // 2
    back = LineReduce(levels, cuts, parts_ref, outs[0], *rest[:12])
    mixed = LineReduce(levels, cuts, rest[12], outs[1], *rest[13:25])
    qkv_got, out_got, gain_got, got, half, last = rest[25:31]
    sems = rest[31:]
    lands = [qkv_got, out_got, gain_got]
    sums = Exchange("dp", dp_count, (False, False, True), sum_cuts, sum_refs[:3], lands, *sems[:3])
    first = Exchange("expert", size, (False,), (1,), sum_refs[3:], [got], *sems[3:6])
    second = Exchange("dp", dp_count, (False,), (1,), [half], [last], *sems[6:9])
    back.load()
    greet("expert", [(peer, None) for peer in first.peers])
    greet("dp", [(peer, None) for peer in sums.peers])
    pl.semaphore_wait(pltpu.get_barrier_semaphore(), size + dp_count - 2)
    first.begin()
    back.begin()
    sums.stay()
    tall = half.shape[1]
    make = functools.partial(collect_block, tables, slots)

    def beside(turn):
        pl.when(turn < sum_cuts[0])(lambda: sums.send(0, turn))
        after = turn - sum_cuts[0]
        pl.when((after >= 0) & (after < sum_cuts[1]))(lambda: sums.send(1, after))

        @pl.when(after == sum_cuts[1])
        def _():
            sums.send(2, 0)
            first.arrive()
            for copy in range(dp_count):
                rows = pl.ds(copy * tall, tall)
                half[copy] = sum(got[i, rows, :] for i in range(size))
            second.begin()

        pl.when(turn < 2 * levels)(lambda: mixed.prepare(turn, make))

    back.main(beside)
    mixed.main()
    second.arrive()
    outs[5][...] = sum(last[i] for i in range(dp_count))
    sums.arrive()
    wide = outs[2].shape[2]
    for j in range(3):
        columns = slice(j * wide, (j + 1) * wide)
        outs[2][j] = sum(qkv_got[copy, :, columns].astype(FULL) for copy in range(dp_count))
    outs[3][...] = sum(out_got[copy].astype(FULL) for copy in range(dp_count))
    outs[4][...] = sum(gain_got[copy] for copy in range(dp_count))
    for moves in (back, mixed, first, second, sums):
        moves.finish()


def closing(size, dp_count, parts, tables, slots, cuts, sums, shared, number):
    block = parts.shape[1:]
    tall = shared.shape[1] // dp_count
    wide = shared.shape[2]
    sum_cuts = (8, 2, 1)
    qkv, out, gain = exchange_outs(dp_count, sums, (False, False, True))
    shapes = [(3, qkv.shape[1], qkv.shape[2] // 3), out.shape[1:], gain.shape[1:], (tall, wide)]
    outs = [jax.ShapeDtypeStruct(block, parts.dtype)] * 2
    outs += [jax.ShapeDtypeStruct(shape, FULL) for shape in shapes]
    line = LineReduce.scratch(size, block, parts.dtype, cuts)
    return pl.pallas_call(
        functools.partial(closing_kernel, size, dp_count, len(tables), cuts, sum_cuts),
        out_shape=outs,
        in_specs=[VMEM] * (2 * len(tables)) + [ANY] * 5,
        out_specs=[ANY] * 2 + [VMEM] * 4,
        scratch_shapes=line
        + [pltpu.VMEM((size // 2,) + block, parts.dtype)]
        + line
        + [pltpu.VMEM(a.shape, a.dtype) for a in (qkv, out, gain)]
        + [pltpu.VMEM((size,) + shared.shape[1:], FULL)]
        + [pltpu.VMEM((dp_count, tall, wide), FULL)] * 2
        + Exchange.scratch(dp_count, sum_cuts)
        + Exchange.scratch(size, (1,))
        + Exchange.scratch(dp_count, (1,)),
        compiler_params=pltpu.CompilerParams(
            collective_id=number, has_side_effects=True, vmem_limit_bytes=56 << 20
        ),
        cost_estimate=pl.CostEstimate(flops=0, transcendentals=0, bytes_accessed=200_000_000),
        name="closing",
    )(*tables, *slots, parts, *sums, shared)


def across_cols(left_side, right_side):
    return lax.dot_general(
        left_side, right_side, (((1,), (1,)), ((), ())), preferred_element_type=FULL
    )


def expert_kernel(first, count, tiles, x_ref, dy_ref, scale_ref, side_ref, down_ref, grads_ref, out_ref, back_ref, dots_ref,
                  side_w, down_w, turned, turned_act, act, grad_side, side_buf, down_buf, w_sems, sems):
    e, step = pl.program_id(0), pl.program_id(1)
    slot = lax.rem(e, 2)
    hidden, model = down_w.shape[1], down_w.shape[2]
    width, wide = hidden // tiles, model // tiles
    copies = grads_ref.shape[0]
    high, low = model // copies, hidden // copies
    part = side_buf.shape[1]

    def loads(e, tile):
        slot = lax.rem(e, 2)
        out = []
        for half in range(2):
            columns = pl.ds(pl.multiple_of(half * hidden + tile * width, 128), width)
            out.append(pltpu.make_async_copy(side_ref.at[first + e, :, columns], side_w.at[slot, :, columns], w_sems.at[slot, tile, half]))
        rows = pl.ds(pl.multiple_of(tile * width, 128), width)
        out.append(pltpu.make_async_copy(down_ref.at[first + e, rows], down_w.at[slot, rows], w_sems.at[slot, tile, 2]))
        return out

    def leaving(at):
        e, chunk = lax.div(at, tiles), lax.rem(at, tiles)
        slot = lax.rem(at, 2)
        base = e * (high + low)
        columns = pl.ds(pl.multiple_of(chunk * wide, 128), wide)
        if wide >= high:
            target = grads_ref.at[pl.ds(chunk * part, part), pl.ds(base, high)]
        else:
            target = grads_ref.at[pl.ds(lax.div(chunk * wide, high), 1), pl.ds(base + lax.rem(chunk * wide, high), wide)]
        return (pltpu.make_async_copy(side_buf.at[slot], target, sems.at[slot, 0]),
                pltpu.make_async_copy(down_buf.at[slot], grads_ref.at[:, pl.ds(base + high, low), columns], sems.at[slot, 1]))

    @pl.when((e == 0) & (step == 0))
    def _():
        for tile in range(tiles):
            for copy in loads(e, tile): copy.start()

    @pl.when((e + 1 < count) & (step == 0))
    def _():
        for tile in range(tiles):
            for copy in loads(e + 1, tile): copy.start()

    @pl.when(step == 0)
    def _():
        turned[...] = x_ref[0].T
        dots_ref[...] = jnp.zeros_like(dots_ref)

    @pl.when(step < tiles)
    def _():
        for copy in loads(e, step): copy.wait()
        rows, grads, scale = x_ref[0], dy_ref[0], scale_ref[0]
        columns = pl.ds(pl.multiple_of(step * width, 128), width)
        others = pl.ds(pl.multiple_of(hidden + step * width, 128), width)
        gate = jnp.dot(rows, side_w[slot, :, columns], preferred_element_type=FULL)
        up = jnp.dot(rows, side_w[slot, :, others], preferred_element_type=FULL)
        grad_act = across_cols(grads, down_w[slot, columns, :])
        sigmoid = jax.nn.sigmoid(gate)
        silu = gate * sigmoid
        raw = silu * up
        dots_ref[0] += jnp.sum(raw * grad_act, axis=-1, keepdims=True)
        weighted = (scale * raw).astype(LOW)
        act[:, columns] = weighted
        turned_act[columns, :] = weighted.T
        grad_act = grad_act * scale
        grad_side[:, columns] = (grad_act * up * sigmoid * (1.0 + gate * (1.0 - sigmoid))).astype(LOW)
        grad_side[:, others] = (grad_act * silu).astype(LOW)

    @pl.when(step >= tiles)
    def _():
        chunk = step - tiles
        at = e * tiles + chunk
        spot = lax.rem(at, 2)
        columns = pl.ds(pl.multiple_of(chunk * wide, 128), wide)

        @pl.when(at >= 2)
        def _():
            for copy in leaving(at - 2): copy.wait()
        total = jnp.dot(turned[columns, :], grad_side[...], preferred_element_type=FULL)
        side_buf[spot] = total.astype(LOW).reshape(side_buf.shape[1:])
        leaving(at)[0].start()
        total = jnp.dot(turned_act[...], dy_ref[0, :, columns], preferred_element_type=FULL)
        down_buf[spot] = total.astype(LOW).reshape(down_buf.shape[1:])
        leaving(at)[1].start()
        back_ref[0, :, columns] = across_cols(grad_side[...], side_w[slot, columns, :]).astype(LOW)
        out_ref[0, :, columns] = jnp.dot(act[...], down_w[slot, :, columns], preferred_element_type=FULL).astype(LOW)

        @pl.when(at == count * tiles - 1)
        def _():
            for copy in leaving(at - 1) + leaving(at): copy.wait()

def expert(first, count, dp_count, x_rows, dy_rows, scales, w_gate_up, w_down, tiles=4):
    _, slots, width = x_rows.shape
    hidden = w_down.shape[1]
    high, low = width // dp_count, hidden // dp_count
    wide = width // tiles
    part = max(1, wide // high)
    rs = pl.BlockSpec((1, slots, width), lambda e, f: (first + e, 0, 0))
    os = pl.BlockSpec((1, slots, width), lambda e, f: (e, 0, 0))
    sems = pltpu.SemaphoreType.DMA
    return pl.pallas_call(
        functools.partial(expert_kernel, first, count, tiles),
        out_shape=[jax.ShapeDtypeStruct((dp_count, count * (high + low), width), LOW),
                   jax.ShapeDtypeStruct((count, slots, width), LOW), jax.ShapeDtypeStruct((count, slots, width), LOW),
                   jax.ShapeDtypeStruct((count, slots, 1), FULL)],
        grid=(count, 2 * tiles),
        in_specs=[rs, rs, pl.BlockSpec((1, slots, 1), lambda e, f: (first + e, 0, 0)), ANY, ANY],
        out_specs=[ANY, os, os, pl.BlockSpec((1, slots, 1), lambda e, f: (e, 0, 0))],
        scratch_shapes=[pltpu.VMEM((min(2, count), width, 2 * hidden), LOW), pltpu.VMEM((min(2, count), hidden, width), LOW),
                        pltpu.VMEM((width, slots), LOW), pltpu.VMEM((hidden, slots), LOW), pltpu.VMEM((slots, hidden), LOW), pltpu.VMEM((slots, 2 * hidden), LOW),
                        pltpu.VMEM((2, part, min(wide, high), 2 * hidden), LOW), pltpu.VMEM((2, dp_count, low, wide), LOW),
                        sems((min(2, count), tiles, 3)), sems((2, 2))],
        compiler_params=pltpu.CompilerParams(vmem_limit_bytes=62 << 20),
        cost_estimate=pl.CostEstimate(
            flops=18 * count * slots * width * hidden,
            transcendentals=count * slots * hidden,
            bytes_accessed=12 * count * width * hidden,
        ),
        name="expert",
    )(x_rows, dy_rows, scales, w_gate_up, w_down)


def rms_scale(values):
    return lax.rsqrt(jnp.mean(values * values, axis=-1, keepdims=True) + NORM_EPS)


def rotary_tables(length, size):
    index = jnp.arange(size // 2, dtype=FULL)
    frequency = jnp.exp(index * (-2.0 * math.log(10000.0) / size))
    angles = jnp.arange(length, dtype=FULL)[:, None] * frequency[None, :]
    cosine, sine = jnp.cos(angles), jnp.sin(angles)
    return jnp.stack(
        [jnp.concatenate([cosine, cosine], axis=1), jnp.concatenate([-sine, sine], axis=1)]
    )


def norm_back(grad_normed, normed, scale_rows):
    return scale_rows * (
        grad_normed - normed * jnp.mean(grad_normed * normed, axis=-1, keepdims=True)
    )


def contract_rows(left_side, right_side):
    return lax.dot_general(
        left_side, right_side, (((0,), (0,)), ((), ())), preferred_element_type=FULL
    )


def contract_cols(left_side, right_side):
    return lax.dot_general(
        left_side, right_side, (((1,), (1,)), ((), ())), preferred_element_type=FULL
    )


def einsum(spec, left_side, right_side):
    return jnp.einsum(spec, left_side, right_side, preferred_element_type=FULL)


def turn(values, cosine, sine):
    return values * cosine + pltpu.roll(values, values.shape[1] // 2, 1) * sine


def allowed_pairs(column, row):
    shape = (column.shape[0], row.shape[1])
    later = lax.broadcasted_iota(jnp.int32, shape, 0) >= lax.broadcasted_iota(jnp.int32, shape, 1)
    return later & (column == row)


def softmax(query, key, allowed):
    scores = across_cols(query, key) * (1.0 / math.sqrt(query.shape[1]))
    scores = jnp.where(allowed, scores, -1e30)
    powers = jnp.exp(scores - jnp.max(scores, axis=-1, keepdims=True))
    return powers / jnp.sum(powers, axis=-1, keepdims=True)


def attend_block(heads, block, rows_ref, scales, gain_ref, turn_ref, column, row, kept_ref, out_ref):
    width = out_ref.shape[2]
    size = width // heads
    allowed = allowed_pairs(column, row)
    cosine, sine = turn_ref[0], turn_ref[1]
    for h in range(heads):
        parts = []
        for part in range(3):
            columns = pl.ds(part * width + h * size, size)
            values = rows_ref[block, :, columns]
            if part < 2:
                values = values * scales[part]
                values = values * gain_ref[part : part + 1, h * size : (h + 1) * size]
                values = turn(values, cosine, sine)
            parts.append(values.astype(LOW))
            kept_ref[block, :, columns] = parts[-1]
        query, key, value = parts
        probs = softmax(query, key, allowed).astype(LOW)
        out_ref[block, :, pl.ds(h * size, size)] = jnp.dot(
            probs, value, preferred_element_type=FULL
        ).astype(LOW)


def attention_kernel(size, dp_count, heads, *refs):
    x_ref, w_ref, gain_ref, gains_ref, turn_ref, column_ref, row_ref, sheet_ref = refs[:8]
    h_out, rows_out, scale_ref, kept_ref, out_ref, own_out, sheet_out = refs[8:15]
    x_held, h_held, rows, sums, squares, got = refs[15:21]
    x_sem, h_sem, rows_sem, send_sem, recv_sem, stay_sem = refs[21:27]
    square_sems, sheet_sems = refs[27:30], refs[30:]
    sheets = Sheets(size, dp_count, sheet_ref, sheet_out, *sheet_sems)
    small = Exchange("expert", size, (True,), (1,), [squares], [got], *square_sems)
    place, model_dim = sheets.place, x_ref.shape[2]
    width = out_ref.shape[2]

    def loading(g):
        return pltpu.make_async_copy(x_ref.at[g], x_held.at[g], x_sem.at[g])

    def leaving(g):
        return (
            pltpu.make_async_copy(h_held.at[g], h_out.at[g], h_sem.at[g]),
            pltpu.make_async_copy(rows.at[g], rows_out.at[g], rows_sem.at[g]),
        )

    for g in range(size):
        loading(g).start()
    greet("expert", [(peer, None) for peer in small.peers])
    greet("dp", [(peer, None) for peer in sheets.peers])
    pl.semaphore_wait(pltpu.get_barrier_semaphore(), size + dp_count - 2)
    sheets.begin()
    sums[...] = jnp.zeros_like(sums)
    lanes = lax.broadcasted_iota(jnp.int32, sums.shape, 1)

    @pl.loop(0, size)
    def _(g):
        loading(g).wait()
        values = x_held[g].astype(FULL)
        hidden = (values * rms_scale(values) * gain_ref[...]).astype(LOW)
        h_held[g] = hidden
        projected = jnp.dot(hidden, w_ref[...], preferred_element_type=FULL)
        rows[g] = projected
        for copy in leaving(g):
            copy.start()
        for part in range(2):
            half = projected[:, part * width : (part + 1) * width]
            total = jnp.sum(half * half, axis=-1, keepdims=True)
            sums[...] += jnp.where(lanes == part * size + g, total, 0.0)
        pl.when((lax.rem(g, 2) == 0) & (g > 0))(lambda: sheets.forward(lax.div(g, 2)))

    squares[...] = sums[...].T[: 2 * size]
    small.begin()
    small.arrive()
    total = sum(got[i] for i in range(size))
    sums[:, : 2 * size] = lax.rsqrt(total / model_dim + NORM_EPS).T

    def sending(g, source):
        columns = pl.ds(pl.multiple_of(source * width, 128), width)
        target = own_out.at[:, columns]
        return remote(out_ref.at[g], target, send_sem.at[g], recv_sem.at[source], {"expert": g})

    own_columns = pl.ds(pl.multiple_of(place * width, 128), width)
    staying = pltpu.make_async_copy(out_ref.at[place], own_out.at[:, own_columns], stay_sem.at[0])

    @pl.loop(0, size)
    def _(i):
        g = lax.rem(place + 1 + i, size)
        scales = [
            jnp.sum(jnp.where(lanes == part * size + g, sums[...], 0.0), axis=-1, keepdims=True)
            for part in range(2)
        ]
        scale_ref[g] = jnp.concatenate(scales, axis=1)
        attend_block(
            heads, g, rows, scales, gains_ref, turn_ref, column_ref[g], row_ref[g], kept_ref, out_ref
        )
        pl.when(g != place)(lambda: sending(g, place).start())
        pl.when((lax.rem(i, 2) == 1) & (i < 2 * (size // 2)))(lambda: sheets.cross(lax.div(i, 2)))

    staying.start()

    @pl.loop(1, size)
    def _(i):
        peer = lax.rem(place + i, size)
        sending(peer, peer).wait_recv()
        sending(peer, place).wait_send()

    @pl.loop(0, size)
    def _(g):
        for copy in leaving(g):
            copy.wait()

    staying.wait()
    small.finish()
    sheets.finish()


def attention(size, dp_count, heads, x_all, w_here, gain, gains, turns, column, row, sheet, number):
    _, tokens, model_dim = x_all.shape
    columns = w_here.shape[1]
    width = columns // 3
    sems = pltpu.SemaphoreType.DMA
    seqs = (size, tokens)
    small = (2 * size, tokens)
    return pl.pallas_call(
        functools.partial(attention_kernel, size, dp_count, heads),
        out_shape=[
            jax.ShapeDtypeStruct(x_all.shape, LOW),
            jax.ShapeDtypeStruct(seqs + (columns,), FULL),
            jax.ShapeDtypeStruct(seqs + (2,), FULL),
            jax.ShapeDtypeStruct(seqs + (columns,), LOW),
            jax.ShapeDtypeStruct(seqs + (width,), LOW),
            jax.ShapeDtypeStruct((tokens, model_dim), LOW),
            jax.ShapeDtypeStruct((dp_count, size) + sheet.shape, LOW),
        ],
        in_specs=[ANY] + [VMEM] * 6 + [ANY],
        out_specs=[ANY] * 2 + [VMEM] * 3 + [ANY] * 2,
        scratch_shapes=[
            pltpu.VMEM(x_all.shape, LOW),
            pltpu.VMEM(x_all.shape, LOW),
            pltpu.VMEM(seqs + (columns,), FULL),
            pltpu.VMEM((tokens, 128), FULL),
            pltpu.VMEM(small, FULL),
            pltpu.VMEM((size,) + small, FULL),
            sems((size,)),
            sems((size,)),
            sems((size,)),
            sems((size,)),
            sems((size,)),
            sems((1,)),
        ]
        + Exchange.scratch(size, (1,))
        + Sheets.scratch(size, dp_count),
        compiler_params=pltpu.CompilerParams(
            collective_id=number, has_side_effects=True, vmem_limit_bytes=48 << 20
        ),
        cost_estimate=pl.CostEstimate(
            flops=2 * x_all.size * columns, transcendentals=0, bytes_accessed=100_000_000
        ),
        name="attention",
    )(x_all, w_here, gain, gains, turns, column, row, sheet)


def attend_back_block(heads, block, grad_ref, refs, back_ref, dots_ref, gains_ref, w_sum):
    w_ref, kept_ref, out_ref, rows_ref, scale_ref, gain_ref, turn_ref, column_ref, row_ref = refs
    width = out_ref.shape[2]
    size = width // heads
    scaling = 1.0 / math.sqrt(size)
    allowed = allowed_pairs(column_ref[block], row_ref[block])
    cosine, sine = turn_ref[0], turn_ref[1]
    grad_rows = grad_ref[block]
    grad_out = across_cols(grad_rows, w_ref[...]).astype(LOW)
    w_sum[...] += contract_rows(out_ref[block], grad_rows)
    dots = [0.0, 0.0]
    for h in range(heads):
        mine = slice(h * size, (h + 1) * size)
        query, key, value = (
            kept_ref[block, :, pl.ds(p * width + h * size, size)] for p in range(3)
        )
        probs = softmax(query, key, allowed)
        grad = grad_out[:, mine]
        grad_value = contract_rows(probs.astype(LOW), grad)
        grad_probs = across_cols(grad, value)
        delta = jnp.sum(grad_probs * probs, axis=-1, keepdims=True)
        grad_scores = (probs * (grad_probs - delta)).astype(LOW)
        grad_query = jnp.dot(grad_scores, key, preferred_element_type=FULL) * scaling
        grad_key = contract_rows(grad_scores, query) * scaling
        for part, grad_turned in enumerate((grad_query, grad_key)):
            columns = pl.ds(part * width + h * size, size)
            grad_normed = turn(grad_turned, cosine, -sine)
            normed = rows_ref[block, :, columns] * scale_ref[block, :, part : part + 1]
            gains_ref[part : part + 1, mine] += jnp.sum(grad_normed * normed, axis=0, keepdims=True)
            weighted = grad_normed * gain_ref[part : part + 1, mine]
            dots[part] += jnp.sum(weighted * normed, axis=-1, keepdims=True)
            back_ref[block, :, columns] = weighted
        back_ref[block, :, pl.ds(2 * width + h * size, size)] = grad_value
    dots_ref[block] = jnp.concatenate(dots, axis=1)


def attend_back_kernel(levels, cuts, heads, grad_ref, *refs):
    reads, (back_ref, dots_ref, gains_ref, w_grad_ref, w_sum, held), sems = refs[:9], refs[9:15], refs[15:]
    line = LineGather(levels, cuts, [grad_ref], [held], *sems)
    line_barrier(levels)
    line.begin()
    w_sum[...] = jnp.zeros_like(w_sum)
    gains_ref[...] = jnp.zeros_like(gains_ref)
    line.staying(0).wait()

    def landed(block):
        attend_back_block(heads, block, held, reads, back_ref, dots_ref, gains_ref, w_sum)

    line.main(landed)
    wide = w_grad_ref.shape[2]
    for copy in range(w_grad_ref.shape[0]):
        w_grad_ref[copy] = w_sum[:, copy * wide : (copy + 1) * wide].astype(LOW)
    line.finish(held=1)


def attend_back(size, dp_count, heads, grad, arrays, number):
    w_here, _, out, rows = arrays[:4]
    width = out.shape[2]
    tokens, model_dim = grad.shape
    return pl.pallas_call(
        functools.partial(attend_back_kernel, size // 2, 4, heads),
        out_shape=[
            jax.ShapeDtypeStruct(rows.shape, FULL),
            jax.ShapeDtypeStruct((size, tokens, 2), FULL),
            jax.ShapeDtypeStruct((2, width), FULL),
            jax.ShapeDtypeStruct((dp_count, width, model_dim // dp_count), LOW),
        ],
        in_specs=[ANY] + [VMEM] * len(arrays),
        out_specs=[VMEM] * 4,
        scratch_shapes=[
            pltpu.VMEM((width, model_dim), FULL),
            pltpu.VMEM((size, tokens, model_dim), LOW),
        ]
        + LineGather.scratch(size, 4, 1),
        compiler_params=pltpu.CompilerParams(
            collective_id=number, has_side_effects=True, vmem_limit_bytes=48 << 20
        ),
        cost_estimate=pl.CostEstimate(flops=0, transcendentals=0, bytes_accessed=150_000_000),
        name="attend_back",
    )(grad, *arrays)


def on_device(
    dp_count,
    line_count,
    layer_input,
    out_cotangent,
    segments,
    routes,
    w_qkv,
    w_out,
    w_router,
    attn_gain,
    mlp_gain,
    query_gain,
    key_gain,
    w_gate_up,
    w_down,
):
    row_count, model_dim = layer_input.shape
    top_count = routes.shape[1]
    expert_count = w_router.shape[1]
    local_count = w_gate_up.shape[0]
    head_size = model_dim // HEADS
    head_cols = model_dim // line_count
    heads_here = head_cols // head_size
    capacity = (row_count * top_count * 9 // 8 + expert_count - 1) // expert_count
    scaling = 1.0 / math.sqrt(head_size)
    place = lax.axis_index("expert")
    all_rows = line_count * row_count
    shard = w_qkv.shape[0]

    small = jnp.concatenate(
        [w_router] + [g[:, None] for g in (attn_gain, mlp_gain, query_gain, key_gain)], axis=1
    )
    small = jnp.pad(small, ((0, 0), (0, 128 - small.shape[1])))
    numbers = jnp.concatenate([routes.T, segments, jnp.zeros((7, row_count), jnp.int32)], axis=0)
    x_all, numbers_all, qkv_here, small = opening(
        line_count, dp_count, [layer_input, numbers], 4, w_qkv, small, 1
    )
    late_cotangent, x_all = lax.optimization_barrier((out_cotangent, x_all))
    dy_all = lax.all_gather(late_cotangent, "expert", axis=0)
    qkv_here = qkv_here.reshape(model_dim, 3 * head_cols)
    small = small.reshape(model_dim, small.shape[3])
    router_full = small[:, :expert_count]
    gains = small[:, expert_count : expert_count + 4].astype(FULL)
    gain_attn, gain_mlp = gains[:, 0], gains[:, 1]
    own_gains = lax.dynamic_slice_in_dim(gains, place * head_cols, head_cols, axis=0)
    gain_query, gain_key = own_gains[:, 2], own_gains[:, 3]

    routes_all = numbers_all[:, :top_count]
    segments_all = numbers_all[:, top_count]
    turns = rotary_tables(row_count, head_size)
    both_gains = jnp.stack([gain_query, gain_key])
    column, row = segments_all[:, :, None], segments_all[:, None, :]
    hidden_one, projected, scales, kept, attended, own_attended, out_full = attention(
        line_count,
        dp_count,
        heads_here,
        x_all,
        qkv_here,
        gain_attn[None],
        both_gains,
        turns,
        column,
        row,
        w_out,
        4,
    )
    out_full = out_full.reshape(model_dim, model_dim)
    hidden_one = hidden_one.reshape(all_rows, model_dim)
    inputs_all = x_all.reshape(all_rows, model_dim).astype(FULL)
    normed_all = inputs_all * rms_scale(inputs_all)
    inputs = layer_input.astype(FULL)
    scale_attn = rms_scale(inputs)
    normed_attn = inputs * scale_attn
    residual = inputs + jnp.dot(own_attended, out_full, preferred_element_type=FULL)
    scale_mlp = rms_scale(residual)
    normed_mlp = residual * scale_mlp
    hidden_two = (normed_mlp * gain_mlp).astype(LOW)

    logits = jnp.dot(hidden_two, router_full, preferred_element_type=FULL)
    chosen = jnp.any(routes[:, :, None] == jnp.arange(expert_count)[None, None, :], axis=1)
    masked = jnp.where(chosen, logits, -1e30)
    powers = jnp.where(chosen, jnp.exp(masked - jnp.max(masked, axis=-1, keepdims=True)), 0.0)
    gates = powers / jnp.sum(powers, axis=-1, keepdims=True)

    local = place * local_count + jnp.arange(local_count)
    used = jnp.any(routes_all[:, None] == local[None, :, None, None], axis=2)
    position = jnp.arange(row_count)
    lower = (position[:, None] < position[None, :]).astype(LOW)
    rank = einsum("gju,ut->gjt", used.astype(LOW), lower).astype(jnp.int32)
    rank = jnp.where(used, rank, -1)
    spots = jnp.arange(capacity)
    table = (rank[:, :, None, :] == spots[None, None, :, None]).astype(LOW)
    returns = [(rank[:, j, :, None] == spots[None, None, :]).astype(LOW) for j in range(local_count)]
    slots = line_count * capacity
    flat_table = table.reshape(line_count, local_count * capacity, row_count)
    expert_rows, dy_rows, gates_all = gather_place(
        line_count, hidden_two, gates.T, flat_table, dy_all, local_count, 6
    )
    local_gates = lax.dynamic_slice_in_dim(gates_all, place * local_count, local_count, axis=1)
    slot_gates = jnp.sum(table.astype(FULL) * local_gates[:, :, None, :], axis=-1)
    slot_gates = slot_gates.transpose(1, 0, 2).reshape(local_count, slots, 1)
    out_rows, back_rows, slot_grads, grad_sums = [], [], [], []
    both_rows = model_dim // dp_count + w_down.shape[1] // dp_count
    for first, count in ((0, 1), (1, local_count - 1)):
        grads, out_row, back_row, dots = expert(
            first, count, dp_count, expert_rows, dy_rows, slot_gates, w_gate_up, w_down
        )
        grads = grads.reshape(-1, model_dim)
        grads = lax.psum_scatter(grads, "dp", scatter_dimension=0, tiled=True)
        grad_sums.append(grads.reshape(count, both_rows, model_dim))
        for kept_list, rows in ((out_rows, out_row), (back_rows, back_row), (slot_grads, dots)):
            for j in range(count):
                kept_list.append(rows[j].reshape(line_count, capacity, rows.shape[2]))
    gate_rows = model_dim // dp_count
    sum_gate_up = jnp.concatenate([both[:, :gate_rows] for both in grad_sums]).astype(FULL)
    sum_down = jnp.concatenate([both[:, gate_rows:] for both in grad_sums]).astype(FULL)
    slot_grads = jnp.stack([dots[:, :, 0] for dots in slot_grads], axis=1)
    grad_gates = jnp.sum(table.astype(FULL) * slot_grads[:, :, :, None], axis=2)
    grad_two, grad_gates = collect_reduce(line_count, returns, back_rows, grad_gates, 8)
    grad_gates = grad_gates.reshape(expert_count, row_count).T
    grad_two = grad_two.astype(FULL)

    grad_out_rows = out_cotangent.astype(FULL)
    grad_logits = gates * (grad_gates - jnp.sum(gates * grad_gates, axis=-1, keepdims=True))
    grad_logits = grad_logits.astype(LOW)
    grad_router = contract_rows(grad_logits, hidden_two)
    grad_two = grad_two + contract_cols(grad_logits, router_full)
    grad_gain_mlp = jnp.sum(grad_two * normed_mlp, axis=0)
    grad_resid = grad_out_rows + norm_back(grad_two * gain_mlp, normed_mlp, scale_mlp)
    grad_attn = grad_resid.astype(LOW)

    out_here = lax.dynamic_slice_in_dim(out_full, place * head_cols, head_cols, axis=0)
    arrays = [out_here, kept, attended, projected, scales, both_gains, turns, column, row]
    back, dots, gain_pair, out_parts = attend_back(
        line_count, dp_count, heads_here, grad_attn, arrays, 11
    )
    dots = dots.transpose(2, 0, 1).reshape(2 * line_count, row_count)
    (dots,) = exchange("expert", line_count, [dots], [True], 12)
    dots = jnp.sum(dots, axis=0).reshape(2, all_rows, 1) / model_dim
    flat_scales = scales.reshape(all_rows, 2)
    back = back.reshape(all_rows, 3 * head_cols)
    projected = projected.reshape(all_rows, 3 * head_cols)
    grads = []
    for part in range(2):
        columns = slice(part * head_cols, (part + 1) * head_cols)
        scale = flat_scales[:, part : part + 1]
        normed = projected[:, columns] * scale
        grads.append(scale * (back[:, columns] - normed * dots[part]))
    grad_proj = jnp.concatenate(grads + [back[:, 2 * head_cols :]], axis=-1).astype(LOW)
    grad_one = contract_cols(grad_proj, qkv_here)
    grad_gain_attn = jnp.sum(grad_one * normed_all, axis=0)
    grad_one = grad_one.astype(LOW).reshape(line_count, row_count, model_dim)
    grad_w_qkv = contract_rows(hidden_one, grad_proj)

    out_cols = model_dim // dp_count
    qkv_parts = grad_w_qkv.astype(LOW).reshape(dp_count, out_cols, 3 * head_cols)
    shared = jnp.concatenate([grad_router, grad_gain_attn[None], grad_gain_mlp[None]], axis=0)
    tall = shared.shape[0] + -shared.shape[0] % 8
    shared = jnp.pad(shared, ((0, tall - shared.shape[0]), (0, 0)))
    shared = shared.reshape(tall, dp_count, line_count, shard).transpose(2, 1, 0, 3)
    shared = shared.reshape(line_count, dp_count * tall, shard)
    shared = jnp.pad(shared, ((0, 0), (0, 0), (0, 128 - shard)))
    grad_one, mixture, sum_qkv, sum_out, gain_pair, shared = closing(
        line_count,
        dp_count,
        grad_one,
        returns,
        out_rows,
        4,
        [qkv_parts, out_parts, gain_pair],
        shared,
        14,
    )
    output = (residual + mixture.astype(FULL)).astype(LOW)
    sum_qkv = sum_qkv.transpose(1, 0, 2)
    shared = shared[:, :shard]
    grad_one = grad_one.astype(FULL)
    grad_inputs = grad_resid + norm_back(grad_one * gain_attn, normed_attn, scale_attn)
    return (
        output,
        grad_inputs,
        sum_qkv,
        sum_out,
        shared[:expert_count].T,
        shared[expert_count],
        shared[expert_count + 1],
        gain_pair[0],
        gain_pair[1],
        sum_gate_up.astype(FULL),
        sum_down.astype(FULL),
    )


def solution(mesh):
    both = ("dp", "expert")
    rows, flat = P(both, None), P(both)
    placed = (rows,) * 7 + (flat,) * 4 + (P("expert", None, None),) * 2
    return jax.shard_map(
        functools.partial(on_device, mesh.shape["dp"], mesh.shape["expert"]),
        mesh=mesh,
        in_specs=placed,
        out_specs=(
            rows,
            rows,
            P("dp", None, "expert"),
            P("expert", "dp"),
            rows,
            flat,
            flat,
            P("expert"),
            P("expert"),
            P("expert", "dp", None),
            P("expert", "dp", None),
        ),
        check_vma=False,
    )
```

```python
import functools
import math

import jax
import jax.numpy as jnp
from jax import lax
from jax.experimental import pallas as pl
from jax.experimental.pallas import tpu as pltpu
from jax.sharding import PartitionSpec as P

HEADS = 16
NORM_EPS = 1e-05
MESH = pl.DeviceIdType.MESH
ANY = pl.BlockSpec(memory_space=pl.ANY)
LOW = jnp.bfloat16
FULL = jnp.float32


def line_place():
    place = lax.axis_index("expert")
    level, side = lax.div(place, 2), lax.rem(place, 2)
    return place, level, side, place + 1 - 2 * side


def greet(axis, targets):
    barrier = pltpu.get_barrier_semaphore()
    for target, there in targets:

        def signal(target=target):
            pl.semaphore_signal(barrier, inc=1, device_id={axis: target}, device_id_type=MESH)

        if there is None:
            signal()
        else:
            pl.when(there)(signal)


def line_barrier(levels):
    place, level, _, other = line_place()
    has_up, has_down = level < levels - 1, level > 0
    greet("expert", [(other, None), (place + 2, has_up), (place - 2, has_down)])
    count = 1 + has_up.astype(jnp.int32) + has_down.astype(jnp.int32)
    pl.semaphore_wait(pltpu.get_barrier_semaphore(), count)


def around(axis, size):
    place = lax.axis_index(axis)
    return [lax.rem(place + shift, size) for shift in range(1, size)]


def remote(source, target, send, recv, device):
    return pltpu.make_async_remote_copy(
        src_ref=source,
        dst_ref=target,
        send_sem=send,
        recv_sem=recv,
        device_id=device,
        device_id_type=MESH,
    )


class LineGather:
    def __init__(self, levels, cuts, ins, outs, up_sem, down_sem, side_sem, recv_sem, own_sem):
        self.levels, self.cuts, self.ins, self.outs = levels, cuts, ins, outs
        self.up_sem, self.down_sem, self.side_sem = up_sem, down_sem, side_sem
        self.recv_sem, self.own_sem = recv_sem, own_sem
        self.place, self.level, self.side, self.other = line_place()
        self.has_up, self.has_down = self.level < levels - 1, self.level > 0

    @staticmethod
    def scratch(size, cuts, count):
        levels, total = size // 2, cuts + count - 1
        shapes = ((levels, total), (levels, total), (2 * levels - 1, total), (size, total))
        return [pltpu.SemaphoreType.DMA(shape) for shape in shapes + ((count,),)]

    def pieces(self):
        return [(0, k) for k in range(self.cuts)] + [(i, 0) for i in range(1, len(self.ins))]

    def staying(self, i):
        target = self.outs[i].at[self.place]
        return pltpu.make_async_copy(self.ins[i], target, self.own_sem.at[i])

    def sending(self, piece, block, own, sem, target):
        i, k = piece
        landing, source, q = self.outs[i].at[block], self.ins[i], k
        if i:
            q = self.cuts + i - 1
        else:
            rows = source.shape[0] // self.cuts
            landing, source = landing.at[pl.ds(k * rows, rows)], source.at[pl.ds(k * rows, rows)]
        sems = sem.at[q], self.recv_sem.at[block, q]
        return remote(source if own else landing, landing, *sems, {"expert": target})

    def up(self, piece, step, own=False):
        block = self.place - 2 * step
        return self.sending(piece, block, own, self.up_sem.at[step], self.place + 2)

    def down(self, piece, step, own=False):
        block = self.place + 2 * step
        return self.sending(piece, block, own, self.down_sem.at[step], self.place - 2)

    def across(self, piece, step, own=False):
        sem = self.side_sem.at[step + self.levels - 1]
        return self.sending(piece, self.place - 2 * step, own, sem, self.other)

    def begin(self):
        for piece in self.pieces():
            pl.when(self.has_up)(self.up(piece, 0, True).start)
            pl.when(self.has_down)(self.down(piece, 0, True).start)
        for piece in self.pieces():
            self.across(piece, 0, True).start()
        for i in range(len(self.ins)):
            self.staying(i).start()

    def forward(self, step, piece):
        @pl.when(self.level >= step)
        def _():
            self.across(piece, step).wait_recv()
            pl.when(self.has_up)(self.up(piece, step).start)
            self.across(piece, step).start()

        @pl.when(self.level + step < self.levels)
        def _():
            self.across(piece, -step).wait_recv()
            pl.when(self.has_down)(self.down(piece, step).start)
            self.across(piece, -step).start()

    def land_across(self, block):
        for piece in self.pieces():
            self.sending(piece, block, False, self.side_sem.at[0], self.other).wait_recv()

    def turn(self, turn, landed=None):
        levels, cuts = self.levels, self.cuts
        step, k = lax.div(turn, cuts) + 1, lax.rem(turn, cuts)

        @pl.when(step < levels)
        def _():
            self.forward(step, (0, k))

            @pl.when(k == cuts - 1)
            def _():
                for i in range(1, len(self.ins)):
                    self.forward(step, (i, 0))

        group, sign, crossed = step - 1, 2 * lax.rem(k, 2) - 1, lax.div(k, 2)
        crossed = jnp.where(group == 0, k, crossed)
        far = jnp.where(group == 0, self.level, self.level + sign * group)

        @pl.when((far >= 0) & (far < levels) & (k < 4) & ((group > 0) | (k < 2)))
        def _():
            block = 2 * far + self.side + crossed * (1 - 2 * self.side)

            @pl.when(crossed == 1)
            def _():
                self.land_across(block)

            if landed:
                landed(block)

    def main(self, landed=None):
        @pl.loop(0, self.levels * self.cuts)
        def _(turn):
            self.turn(turn, landed)

    def finish(self, held=0):
        for piece in self.pieces():
            self.across(piece, 0).wait_send()
            for step in range(self.levels):
                above, below = self.level >= step, self.level + step < self.levels
                pl.when(self.has_up & above)(self.up(piece, step).wait_send)
                pl.when(self.has_down & below)(self.down(piece, step).wait_send)
                if step:
                    pl.when(above)(self.across(piece, step).wait_send)
                    pl.when(below)(self.across(piece, -step).wait_send)
        for i in range(held, len(self.ins)):
            self.staying(i).wait()


def call(kernel, name, number, outs, scratch, arrays, moved):
    return pl.pallas_call(
        kernel,
        out_shape=outs,
        in_specs=[ANY] * len(arrays),
        out_specs=[ANY] * len(outs),
        scratch_shapes=scratch,
        compiler_params=pltpu.CompilerParams(
            collective_id=number, has_side_effects=True, vmem_limit_bytes=48 << 20
        ),
        cost_estimate=pl.CostEstimate(flops=0, transcendentals=0, bytes_accessed=moved),
        name=name,
    )(*arrays)


class LineReduce:
    def __init__(self, levels, cuts, parts, total, own, beside, rising, falling, *sems):
        self.levels, self.cuts, self.parts, self.total = levels, cuts, parts, total
        self.made = parts.shape[0] == levels
        self.own, self.beside, self.rising, self.falling = own, beside, rising, falling
        self.load_sem, self.side_send, self.side_recv = sems[:3]
        self.up_send, self.up_recv, self.down_send, self.down_recv, self.out_sem = sems[3:]
        self.place, self.level, self.side, self.other = line_place()
        self.has_up, self.has_down = self.level < levels - 1, self.level > 0
        self.rows = parts.shape[1] // cuts

    @staticmethod
    def scratch(size, block, dtype, cuts):
        levels = size // 2
        return (
            [pltpu.VMEM((levels,) + block, dtype)] * 4
            + [pltpu.SemaphoreType.DMA((levels, cuts))] * 7
            + [pltpu.SemaphoreType.DMA((cuts,))]
        )

    def cut(self, ref, block, k):
        return ref.at[block, pl.ds(k * self.rows, self.rows)]

    def loading(self, far, k):
        source = self.cut(self.parts, 2 * far + self.side, k)
        return pltpu.make_async_copy(source, self.cut(self.own, far, k), self.load_sem.at[far, k])

    def across(self, far, k):
        source = self.cut(self.parts, far if self.made else 2 * far + 1 - self.side, k)
        sems = self.side_send.at[far, k], self.side_recv.at[far, k]
        return remote(source, self.cut(self.beside, far, k), *sems, {"expert": self.other})

    def up(self, far, k):
        sems = self.up_send.at[far, k], self.up_recv.at[far, k]
        target = {"expert": self.place + 2}
        return remote(self.cut(self.own, far, k), self.cut(self.rising, far, k), *sems, target)

    def down(self, far, k):
        sems = self.down_send.at[far, k], self.down_recv.at[far, k]
        target = {"expert": self.place - 2}
        return remote(self.cut(self.own, far, k), self.cut(self.falling, far, k), *sems, target)

    def value(self, ref, block, k):
        return self.cut(ref, block, k)[...].astype(FULL)

    def load(self):
        for i in range(self.levels):
            for k in range(self.cuts):
                self.loading(self.far(i), k).start()

    def begin(self):
        for i in range(self.levels):
            for k in range(self.cuts):
                self.across(self.far(i), k).start()

    def far(self, i):
        return jnp.where(lax.rem(i, 2) == 0, self.levels - 1 - lax.div(i, 2), lax.div(i, 2))

    def prepare(self, turn, make):
        far = self.far(lax.div(turn, 2))

        @pl.when(lax.rem(turn, 2) == 0)
        def _():
            make(2 * far + 1 - self.side, self.parts.at[far])
            for k in range(self.cuts):
                self.across(far, k).start()

        @pl.when(lax.rem(turn, 2) == 1)
        def _():
            make(2 * far + self.side, self.own.at[far])

    def pair(self, far, k):
        if not self.made:
            self.loading(far, k).wait()
        self.across(far, k).wait_recv()
        return self.value(self.own, far, k) + self.value(self.beside, far, k)

    def store(self, far, k, total):
        self.cut(self.own, far, k)[...] = total.astype(self.own.dtype)

    def toward(self, far, k, ahead, behind, move, arrived):
        @pl.when(ahead & behind)
        def _():
            both = self.pair(far, k)
            move(far, k).wait_recv()
            self.store(far, k, both + self.value(arrived, far, k))

        @pl.when(ahead & jnp.logical_not(behind))
        def _():
            self.store(far, k, self.pair(far, k))

        pl.when(ahead)(move(far, k).start)

    def main(self, beside=None):
        @pl.loop(0, (self.levels - 1) * self.cuts)
        def _(turn):
            step, k = lax.div(turn, self.cuts), lax.rem(turn, self.cuts)
            high, low = self.levels - 1 - step, step
            if beside:
                beside(turn)
            self.toward(high, k, self.level < high, self.has_down, self.up, self.rising)
            self.toward(low, k, self.level > low, self.has_up, self.down, self.falling)

        @pl.loop(0, self.cuts)
        def _(k):
            self.store(self.level, k, self.pair(self.level, k))
            for there, move, arrived in (
                (self.has_down, self.up, self.rising),
                (self.has_up, self.down, self.falling),
            ):

                @pl.when(there)
                def _():
                    move(self.level, k).wait_recv()
                    total = self.value(self.own, self.level, k) + self.value(arrived, self.level, k)
                    self.store(self.level, k, total)

            self.leaving(k).start()

    def leaving(self, k):
        target = self.total.at[pl.ds(k * self.rows, self.rows)]
        return pltpu.make_async_copy(self.cut(self.own, self.level, k), target, self.out_sem.at[k])

    def finish(self):
        for k in range(self.cuts):
            self.leaving(k).wait()
            for far in range(self.levels):
                self.across(far, k).wait_send()
                pl.when(self.level < far)(self.up(far, k).wait_send)
                pl.when(self.level > far)(self.down(far, k).wait_send)


class Exchange:
    def __init__(self, axis, size, spread, cuts, ins, outs, send_sem, recv_sem, own_sem):
        self.axis, self.spread, self.ins, self.outs = axis, spread, ins, outs
        self.send_sem, self.recv_sem, self.own_sem = send_sem, recv_sem, own_sem
        self.cuts = cuts
        self.firsts = [sum(cuts[:i]) for i in range(len(cuts))]
        self.pieces = [(i, k) for i in range(len(cuts)) for k in range(cuts[i])]
        self.place, self.peers = lax.axis_index(axis), around(axis, size)

    @staticmethod
    def scratch(size, cuts):
        sems = pltpu.SemaphoreType.DMA
        return [sems((sum(cuts), size)), sems((sum(cuts), size)), sems((len(cuts),))]

    def source(self, i, block):
        return self.ins[i] if self.spread[i] else self.ins[i].at[block]

    def staying(self, i):
        target = self.outs[i].at[self.place]
        return pltpu.make_async_copy(self.source(i, self.place), target, self.own_sem.at[i])

    def sending(self, i, k, shift, landing):
        peer = self.peers[shift]
        source, target, q = self.source(i, peer), self.outs[i].at[landing], self.firsts[i] + k
        if self.cuts[i] > 1:
            rows = target.shape[0] // self.cuts[i]
            source, target = source.at[pl.ds(k * rows, rows)], target.at[pl.ds(k * rows, rows)]
        sems = self.send_sem.at[q, shift], self.recv_sem.at[q, landing]
        return remote(source, target, *sems, {self.axis: peer})

    def send(self, i, k):
        for shift in range(len(self.peers)):
            self.sending(i, k, shift, self.place).start()

    def stay(self):
        for i in range(len(self.spread)):
            self.staying(i).start()

    def begin(self):
        for i, k in self.pieces:
            self.send(i, k)
        self.stay()

    def land(self):
        for shift, peer in enumerate(self.peers):
            for i, k in self.pieces:
                self.sending(i, k, shift, peer).wait_recv()

    def arrive(self):
        self.land()
        for i in range(len(self.spread)):
            self.staying(i).wait()

    def finish(self):
        for shift in range(len(self.peers)):
            for i, k in self.pieces:
                self.sending(i, k, shift, self.place).wait_send()


def exchange_kernel(axis, size, spread, *refs):
    count = len(spread)
    ins, outs, sems = refs[:count], refs[count : 2 * count], refs[2 * count :]
    moves = Exchange(axis, size, spread, (1,) * count, ins, outs, *sems)
    greet(axis, [(peer, None) for peer in moves.peers])
    pl.semaphore_wait(pltpu.get_barrier_semaphore(), size - 1)
    moves.begin()
    moves.arrive()
    moves.finish()


def exchange_outs(size, arrays, spread):
    return [
        jax.ShapeDtypeStruct((size,) + a.shape if flat else a.shape, a.dtype)
        for a, flat in zip(arrays, spread)
    ]


def exchange(axis, size, arrays, spread, number):
    return call(
        functools.partial(exchange_kernel, axis, size, tuple(spread)),
        "exchange_" + axis,
        number,
        exchange_outs(size, arrays, spread),
        Exchange.scratch(size, (1,) * len(arrays)),
        arrays,
        30_000_000,
    )


def opening_kernel(size, dp_count, count, cuts, *refs):
    ins, (w_ref, small_ref) = refs[:count], refs[count : count + 2]
    outs, (w_out, small_out), rest = refs[count + 2 : 2 * count + 2], refs[2 * count + 2 :][:2], refs[2 * count + 4 :]
    line = LineGather(size // 2, cuts, ins, outs, *rest[:5])
    send_sem, recv_sem, own_sem = rest[5:8]
    place, mine = line.place, lax.axis_index("dp")
    peers = around("expert", size)
    width = w_out.shape[3] // 3
    mine_refs = [w_out.at[mine], small_out.at[mine]]
    across = Exchange(
        "dp", dp_count, (True,) * 2, (size,) * 2, mine_refs, [w_out, small_out], *rest[8:]
    )
    greet("expert", [(peer, None) for peer in peers])
    greet("dp", [(peer, None) for peer in across.peers])
    pl.semaphore_wait(pltpu.get_barrier_semaphore(), size + dp_count - 2)

    def ends(peer, landing, j):
        if j == 3:
            return small_ref, small_out.at[mine, landing]
        start = pl.multiple_of(j * width * size + peer * width, 128)
        target = w_out.at[mine, landing, :, pl.ds(j * width, width)]
        return w_ref.at[:, pl.ds(start, width)], target

    def sending(shift, landing, j):
        source, target = ends(peers[shift], landing, j)
        sems = send_sem.at[shift, j], recv_sem.at[landing, j]
        return remote(source, target, *sems, {"expert": peers[shift]})

    own = [pltpu.make_async_copy(*ends(place, place, j), own_sem.at[j]) for j in range(4)]
    for shift in range(size - 1):
        for j in range(4):
            sending(shift, place, j).start()
    for copy in own:
        copy.start()
    line.begin()
    for copy in own:
        copy.wait()
    across.send(0, place)
    across.send(1, place)
    for shift, peer in enumerate(peers):
        for j in range(4):
            sending(shift, peer, j).wait_recv()
        across.send(0, peer)
        across.send(1, peer)
    line.main()
    line.finish()
    for shift in range(size - 1):
        for j in range(4):
            sending(shift, place, j).wait_send()
    across.land()
    across.finish()


def opening(size, dp_count, arrays, cuts, weights, small, number):
    sems = pltpu.SemaphoreType.DMA
    outs = [jax.ShapeDtypeStruct((size,) + a.shape, a.dtype) for a in arrays]
    rows, columns = weights.shape
    whole = (dp_count, size, rows)
    outs.append(jax.ShapeDtypeStruct(whole + (columns // size,), weights.dtype))
    outs.append(jax.ShapeDtypeStruct(whole + (small.shape[1],), small.dtype))
    return call(
        functools.partial(opening_kernel, size, dp_count, len(arrays), cuts),
        "opening",
        number,
        outs,
        LineGather.scratch(size, cuts, len(arrays))
        + [sems((size, 4)), sems((size, 4)), sems((4,))]
        + Exchange.scratch(dp_count, (size, size)),
        list(arrays) + [weights, small],
        200_000_000,
    )


class Sheets:
    def __init__(self, size, dp_count, source, target, *sems):
        self.levels, self.dp_count, self.ins, self.out = size // 2, dp_count, source, target
        self.up_send, self.down_send, self.line_recv, self.dp_send, self.dp_recv = sems[:5]
        self.side_send, self.side_recv, self.own_sem = sems[5:]
        self.place, self.level, self.side, self.other = line_place()
        self.has_up, self.has_down = self.level < self.levels - 1, self.level > 0
        self.mine, self.peers = lax.axis_index("dp"), around("dp", dp_count)

    @staticmethod
    def scratch(size, dp_count):
        sems, levels = pltpu.SemaphoreType.DMA, size // 2
        return [sems((levels,))] * 3 + [sems((dp_count, levels))] * 4 + [sems((1,))]

    def along(self, far, own, send, target):
        landing = self.out.at[self.mine, 2 * far + self.side]
        source = self.ins if own else landing
        return remote(source, landing, send.at[far], self.line_recv.at[far], {"expert": target})

    def up(self, far, own=False):
        return self.along(far, own, self.up_send, self.place + 2)

    def down(self, far, own=False):
        return self.along(far, own, self.down_send, self.place - 2)

    def over(self, far, shift, copy, own=False):
        landing = self.out.at[copy, 2 * far + self.side]
        source = self.ins if own else landing
        sems = self.dp_send.at[shift, far], self.dp_recv.at[copy, far]
        return remote(source, landing, *sems, {"dp": self.peers[shift]})

    def across(self, far, copy, whose, own=False):
        landing = self.out.at[copy, 2 * far + whose]
        source = self.ins if own else landing
        sems = self.side_send.at[copy, far], self.side_recv.at[copy, far]
        return remote(source, landing, *sems, {"expert": self.other})

    def spread(self, far, own=False):
        for shift in range(self.dp_count - 1):
            self.over(far, shift, self.mine, own).start()
        self.across(far, self.mine, self.side, own).start()

    def staying(self):
        target = self.out.at[self.mine, self.place]
        return pltpu.make_async_copy(self.ins, target, self.own_sem.at[0])

    def begin(self):
        pl.when(self.has_up)(self.up(self.level, True).start)
        pl.when(self.has_down)(self.down(self.level, True).start)
        self.spread(self.level, True)
        self.staying().start()

    def forward(self, step):
        @pl.when(self.level >= step)
        def _():
            self.up(self.level - step).wait_recv()
            pl.when(self.has_up)(self.up(self.level - step).start)
            self.spread(self.level - step)

        @pl.when(self.level + step < self.levels)
        def _():
            self.down(self.level + step).wait_recv()
            pl.when(self.has_down)(self.down(self.level + step).start)
            self.spread(self.level + step)

    def cross(self, far):
        for shift, peer in enumerate(self.peers):
            self.over(far, shift, peer).wait_recv()
            self.across(far, peer, self.side).start()

    def finish(self):
        @pl.loop(0, self.levels)
        def _(far):
            pl.when(self.has_up & (self.level >= far))(self.up(far).wait_send)
            pl.when(self.has_down & (self.level <= far))(self.down(far).wait_send)
            for shift in range(self.dp_count - 1):
                self.over(far, shift, self.mine).wait_send()
            for copy in range(self.dp_count):
                self.across(far, copy, 1 - self.side).wait_recv()
                self.across(far, copy, self.side).wait_send()

        self.staying().wait()


VMEM = pl.BlockSpec(memory_space=pltpu.VMEM)
COLUMNS = 512


def gather_place_kernel(levels, cuts, *refs):
    rows_ref, gates_ref, table_ref, dy_ref, x_out, dy_out, gates_out = refs[:7]
    held, dy_held, x_stage, dy_stage = refs[7:11]
    line_sems, (dy_sem, x_sems, dy_sems) = refs[11:16], refs[16:]
    line = LineGather(levels, cuts, [rows_ref, gates_ref], [held, gates_out], *line_sems)
    size, width = 2 * levels, held.shape[2]
    _, local_count, capacity, _ = x_stage.shape

    def leaving(block, stage, out, sems):
        target = out.at[:, pl.ds(pl.multiple_of(block * capacity, 8), capacity)]
        return pltpu.make_async_copy(stage.at[block], target, sems.at[block])

    def place(block, rows, stage, out, sems):
        table = table_ref[block]

        @pl.loop(0, width // COLUMNS)
        def _(n):
            columns = pl.ds(pl.multiple_of(n * COLUMNS, COLUMNS), COLUMNS)
            placed = jnp.dot(table, rows[block, :, columns], preferred_element_type=FULL)
            for j in range(local_count):
                part = placed[j * capacity : (j + 1) * capacity]
                stage[block, j, :, columns] = part.astype(stage.dtype)

        leaving(block, stage, out, sems).start()

    def place_x(block):
        place(block, held, x_stage, x_out, x_sems)

    loading = pltpu.make_async_copy(dy_ref, dy_held, dy_sem.at[0])
    loading.start()
    line_barrier(levels)
    line.begin()
    loading.wait()

    @pl.loop(0, size)
    def _(block):
        place(block, dy_held, dy_stage, dy_out, dy_sems)

    line.staying(0).wait()
    line.main(place_x)
    line.finish(held=1)

    @pl.loop(0, size)
    def _(block):
        leaving(block, x_stage, x_out, x_sems).wait()
        leaving(block, dy_stage, dy_out, dy_sems).wait()


def gather_place(size, rows, gates, table, dy, local_count, number):
    cuts = 4
    tokens, width = rows.shape
    capacity = table.shape[1] // local_count
    placed = jax.ShapeDtypeStruct((local_count, size * capacity, width), rows.dtype)
    sems = pltpu.SemaphoreType.DMA
    return pl.pallas_call(
        functools.partial(gather_place_kernel, size // 2, cuts),
        out_shape=[placed, placed, jax.ShapeDtypeStruct((size,) + gates.shape, gates.dtype)],
        in_specs=[ANY, ANY, VMEM, ANY],
        out_specs=[ANY] * 3,
        scratch_shapes=[pltpu.VMEM((size, tokens, width), rows.dtype)] * 2
        + [pltpu.VMEM((size, local_count, capacity, width), rows.dtype)] * 2
        + LineGather.scratch(size, cuts, 2)
        + [sems((1,)), sems((size,)), sems((size,))],
        compiler_params=pltpu.CompilerParams(
            collective_id=number, has_side_effects=True, vmem_limit_bytes=48 << 20
        ),
        cost_estimate=pl.CostEstimate(
            flops=4 * table.size * width, transcendentals=0, bytes_accessed=150_000_000
        ),
        name="gather_place",
    )(rows, gates, table, dy)


def collect_block(tables, slots, block, target):
    @pl.loop(0, target.shape[1] // COLUMNS)
    def _(n):
        columns = pl.ds(pl.multiple_of(n * COLUMNS, COLUMNS), COLUMNS)
        total = 0.0
        for table, rows in zip(tables, slots):
            total += jnp.dot(table[block], rows[block, :, columns], preferred_element_type=FULL)
        target[:, columns] = total.astype(target.dtype)


def collect_reduce_kernel(levels, cuts, local_count, *refs):
    tables, slots = refs[:local_count], refs[local_count : 2 * local_count]
    dots, table_ref = refs[2 * local_count : 3 * local_count], refs[3 * local_count]
    total_ref, gates_out, away = refs[3 * local_count + 1 : 3 * local_count + 4]
    rest, (gates, *sems) = refs[3 * local_count + 4 :][:12], refs[3 * local_count + 16 :]
    line = LineReduce(levels, cuts, away, total_ref, *rest)
    small = Exchange("expert", 2 * levels, (False,), (1,), [gates], [gates_out], *sems)
    greet("expert", [(peer, None) for peer in small.peers])
    pl.semaphore_wait(pltpu.get_barrier_semaphore(), 2 * levels - 1)
    make = functools.partial(collect_block, tables, slots)

    @pl.loop(0, 4)
    def _(turn):
        line.prepare(turn, make)

    @pl.loop(0, 2 * levels)
    def _(block):
        table = table_ref[block].astype(FULL)
        capacity = table.shape[0] // local_count
        for j in range(local_count):
            part = table[j * capacity : (j + 1) * capacity] * dots[j][block]
            gates[block, j : j + 1] = jnp.sum(part, axis=0, keepdims=True)

    small.begin()

    def beside(turn):
        pl.when(turn + 4 < 2 * levels)(lambda: line.prepare(turn + 4, make))

    line.main(beside)
    small.arrive()
    line.finish()
    small.finish()


def collect_reduce(size, tables, slots, dots, table, number):
    levels, cuts = size // 2, 4
    block = (tables[0].shape[1], slots[0].shape[2])
    kind = slots[0].dtype
    gates = (size, len(tables), block[0])
    return pl.pallas_call(
        functools.partial(collect_reduce_kernel, levels, cuts, len(tables)),
        out_shape=[jax.ShapeDtypeStruct(block, kind), jax.ShapeDtypeStruct(gates, FULL)],
        in_specs=[VMEM] * (3 * len(tables) + 1),
        out_specs=[ANY, ANY],
        scratch_shapes=[pltpu.VMEM((levels,) + block, kind)]
        + LineReduce.scratch(size, block, kind, cuts)
        + [pltpu.VMEM(gates, FULL)]
        + Exchange.scratch(size, (1,)),
        compiler_params=pltpu.CompilerParams(
            collective_id=number, has_side_effects=True, vmem_limit_bytes=48 << 20
        ),
        cost_estimate=pl.CostEstimate(flops=0, transcendentals=0, bytes_accessed=150_000_000),
        name="collect_reduce",
    )(*tables, *slots, *dots, table)


def closing_kernel(size, dp_count, local_count, cuts, sum_cuts, *refs):
    tables, slots = refs[:local_count], refs[local_count : 2 * local_count]
    parts_ref, *sum_refs = refs[2 * local_count : 2 * local_count + 5]
    outs, rest = refs[2 * local_count + 5 : 2 * local_count + 11], refs[2 * local_count + 11 :]
    levels = size // 2
    back = LineReduce(levels, cuts, parts_ref, outs[0], *rest[:12])
    mixed = LineReduce(levels, cuts, rest[12], outs[1], *rest[13:25])
    qkv_got, out_got, gain_got, got, half, last = rest[25:31]
    sems = rest[31:]
    lands = [qkv_got, out_got, gain_got]
    sums = Exchange("dp", dp_count, (False, False, True), sum_cuts, sum_refs[:3], lands, *sems[:3])
    first = Exchange("expert", size, (False,), (1,), sum_refs[3:], [got], *sems[3:6])
    second = Exchange("dp", dp_count, (False,), (1,), [half], [last], *sems[6:9])
    back.load()
    greet("expert", [(peer, None) for peer in first.peers])
    greet("dp", [(peer, None) for peer in sums.peers])
    pl.semaphore_wait(pltpu.get_barrier_semaphore(), size + dp_count - 2)
    first.begin()
    back.begin()
    sums.stay()
    tall = half.shape[1]
    make = functools.partial(collect_block, tables, slots)

    def beside(turn):
        pl.when(turn < sum_cuts[0])(lambda: sums.send(0, turn))
        after = turn - sum_cuts[0]
        pl.when((after >= 0) & (after < sum_cuts[1]))(lambda: sums.send(1, after))

        @pl.when(after == sum_cuts[1])
        def _():
            sums.send(2, 0)
            first.arrive()
            for copy in range(dp_count):
                rows = pl.ds(copy * tall, tall)
                half[copy] = sum(got[i, rows, :] for i in range(size))
            second.begin()

        pl.when(turn < 2 * levels)(lambda: mixed.prepare(turn, make))

    back.main(beside)
    mixed.main()
    second.arrive()
    outs[5][...] = sum(last[i] for i in range(dp_count))
    sums.arrive()
    wide = outs[2].shape[2]
    for j in range(3):
        columns = slice(j * wide, (j + 1) * wide)
        outs[2][j] = sum(qkv_got[copy, :, columns].astype(FULL) for copy in range(dp_count))
    outs[3][...] = sum(out_got[copy].astype(FULL) for copy in range(dp_count))
    outs[4][...] = sum(gain_got[copy] for copy in range(dp_count))
    for moves in (back, mixed, first, second, sums):
        moves.finish()


def closing(size, dp_count, parts, tables, slots, cuts, sums, shared, number):
    block = parts.shape[1:]
    tall = shared.shape[1] // dp_count
    wide = shared.shape[2]
    sum_cuts = (8, 2, 1)
    qkv, out, gain = exchange_outs(dp_count, sums, (False, False, True))
    shapes = [(3, qkv.shape[1], qkv.shape[2] // 3), out.shape[1:], gain.shape[1:], (tall, wide)]
    outs = [jax.ShapeDtypeStruct(block, parts.dtype)] * 2
    outs += [jax.ShapeDtypeStruct(shape, FULL) for shape in shapes]
    line = LineReduce.scratch(size, block, parts.dtype, cuts)
    return pl.pallas_call(
        functools.partial(closing_kernel, size, dp_count, len(tables), cuts, sum_cuts),
        out_shape=outs,
        in_specs=[VMEM] * (2 * len(tables)) + [ANY] * 5,
        out_specs=[ANY] * 2 + [VMEM] * 4,
        scratch_shapes=line
        + [pltpu.VMEM((size // 2,) + block, parts.dtype)]
        + line
        + [pltpu.VMEM(a.shape, a.dtype) for a in (qkv, out, gain)]
        + [pltpu.VMEM((size,) + shared.shape[1:], FULL)]
        + [pltpu.VMEM((dp_count, tall, wide), FULL)] * 2
        + Exchange.scratch(dp_count, sum_cuts)
        + Exchange.scratch(size, (1,))
        + Exchange.scratch(dp_count, (1,)),
        compiler_params=pltpu.CompilerParams(
            collective_id=number, has_side_effects=True, vmem_limit_bytes=56 << 20
        ),
        cost_estimate=pl.CostEstimate(flops=0, transcendentals=0, bytes_accessed=200_000_000),
        name="closing",
    )(*tables, *slots, parts, *sums, shared)


def across_cols(left_side, right_side):
    return lax.dot_general(
        left_side, right_side, (((1,), (1,)), ((), ())), preferred_element_type=FULL
    )


def expert_kernel(first, count, tiles, x_ref, dy_ref, scale_ref, side_ref, down_ref, grads_ref, out_ref, back_ref, dots_ref,
                  side_w, down_w, turned, turned_act, act, grad_side, side_buf, down_buf, w_sems, sems):
    e, step = pl.program_id(0), pl.program_id(1)
    slot = lax.rem(e, 2)
    hidden, model = down_w.shape[1], down_w.shape[2]
    width, wide = hidden // tiles, model // tiles
    copies = grads_ref.shape[0]
    high, low = model // copies, hidden // copies
    part = side_buf.shape[1]

    def loads(e, tile):
        slot = lax.rem(e, 2)
        out = []
        for half in range(2):
            columns = pl.ds(pl.multiple_of(half * hidden + tile * width, 128), width)
            out.append(pltpu.make_async_copy(side_ref.at[first + e, :, columns], side_w.at[slot, :, columns], w_sems.at[slot, tile, half]))
        rows = pl.ds(pl.multiple_of(tile * width, 128), width)
        out.append(pltpu.make_async_copy(down_ref.at[first + e, rows], down_w.at[slot, rows], w_sems.at[slot, tile, 2]))
        return out

    def leaving(at):
        e, chunk = lax.div(at, tiles), lax.rem(at, tiles)
        slot = lax.rem(at, 2)
        base = e * (high + low)
        columns = pl.ds(pl.multiple_of(chunk * wide, 128), wide)
        if wide >= high:
            target = grads_ref.at[pl.ds(chunk * part, part), pl.ds(base, high)]
        else:
            target = grads_ref.at[pl.ds(lax.div(chunk * wide, high), 1), pl.ds(base + lax.rem(chunk * wide, high), wide)]
        return (pltpu.make_async_copy(side_buf.at[slot], target, sems.at[slot, 0]),
                pltpu.make_async_copy(down_buf.at[slot], grads_ref.at[:, pl.ds(base + high, low), columns], sems.at[slot, 1]))

    @pl.when((e == 0) & (step == 0))
    def _():
        for tile in range(tiles):
            for copy in loads(e, tile): copy.start()

    @pl.when((e + 1 < count) & (step == 0))
    def _():
        for tile in range(tiles):
            for copy in loads(e + 1, tile): copy.start()

    @pl.when(step == 0)
    def _():
        turned[...] = x_ref[0].T
        dots_ref[...] = jnp.zeros_like(dots_ref)

    @pl.when(step < tiles)
    def _():
        for copy in loads(e, step): copy.wait()
        rows, grads, scale = x_ref[0], dy_ref[0], scale_ref[0]
        columns = pl.ds(pl.multiple_of(step * width, 128), width)
        others = pl.ds(pl.multiple_of(hidden + step * width, 128), width)
        gate = jnp.dot(rows, side_w[slot, :, columns], preferred_element_type=FULL)
        up = jnp.dot(rows, side_w[slot, :, others], preferred_element_type=FULL)
        grad_act = across_cols(grads, down_w[slot, columns, :])
        sigmoid = jax.nn.sigmoid(gate)
        silu = gate * sigmoid
        raw = silu * up
        dots_ref[0] += jnp.sum(raw * grad_act, axis=-1, keepdims=True)
        weighted = (scale * raw).astype(LOW)
        act[:, columns] = weighted
        turned_act[columns, :] = weighted.T
        grad_act = grad_act * scale
        grad_side[:, columns] = (grad_act * up * sigmoid * (1.0 + gate * (1.0 - sigmoid))).astype(LOW)
        grad_side[:, others] = (grad_act * silu).astype(LOW)

    @pl.when(step >= tiles)
    def _():
        chunk = step - tiles
        at = e * tiles + chunk
        spot = lax.rem(at, 2)
        columns = pl.ds(pl.multiple_of(chunk * wide, 128), wide)

        @pl.when(at >= 2)
        def _():
            for copy in leaving(at - 2): copy.wait()
        total = jnp.dot(turned[columns, :], grad_side[...], preferred_element_type=FULL)
        side_buf[spot] = total.astype(LOW).reshape(side_buf.shape[1:])
        leaving(at)[0].start()
        total = jnp.dot(turned_act[...], dy_ref[0, :, columns], preferred_element_type=FULL)
        down_buf[spot] = total.astype(LOW).reshape(down_buf.shape[1:])
        leaving(at)[1].start()
        back_ref[0, :, columns] = across_cols(grad_side[...], side_w[slot, columns, :]).astype(LOW)
        out_ref[0, :, columns] = jnp.dot(act[...], down_w[slot, :, columns], preferred_element_type=FULL).astype(LOW)

        @pl.when(at == count * tiles - 1)
        def _():
            for copy in leaving(at - 1) + leaving(at): copy.wait()

def expert(first, count, dp_count, x_rows, dy_rows, scales, w_gate_up, w_down, tiles=4):
    _, slots, width = x_rows.shape
    hidden = w_down.shape[1]
    high, low = width // dp_count, hidden // dp_count
    wide = width // tiles
    part = max(1, wide // high)
    rs = pl.BlockSpec((1, slots, width), lambda e, f: (first + e, 0, 0))
    os = pl.BlockSpec((1, slots, width), lambda e, f: (e, 0, 0))
    sems = pltpu.SemaphoreType.DMA
    return pl.pallas_call(
        functools.partial(expert_kernel, first, count, tiles),
        out_shape=[jax.ShapeDtypeStruct((dp_count, count * (high + low), width), LOW),
                   jax.ShapeDtypeStruct((count, slots, width), LOW), jax.ShapeDtypeStruct((count, slots, width), LOW),
                   jax.ShapeDtypeStruct((count, slots, 1), FULL)],
        grid=(count, 2 * tiles),
        in_specs=[rs, rs, pl.BlockSpec((1, slots, 1), lambda e, f: (first + e, 0, 0)), ANY, ANY],
        out_specs=[ANY, os, os, pl.BlockSpec((1, slots, 1), lambda e, f: (e, 0, 0))],
        scratch_shapes=[pltpu.VMEM((min(2, count), width, 2 * hidden), LOW), pltpu.VMEM((min(2, count), hidden, width), LOW),
                        pltpu.VMEM((width, slots), LOW), pltpu.VMEM((hidden, slots), LOW), pltpu.VMEM((slots, hidden), LOW), pltpu.VMEM((slots, 2 * hidden), LOW),
                        pltpu.VMEM((2, part, min(wide, high), 2 * hidden), LOW), pltpu.VMEM((2, dp_count, low, wide), LOW),
                        sems((min(2, count), tiles, 3)), sems((2, 2))],
        compiler_params=pltpu.CompilerParams(vmem_limit_bytes=62 << 20),
        cost_estimate=pl.CostEstimate(
            flops=18 * count * slots * width * hidden,
            transcendentals=count * slots * hidden,
            bytes_accessed=12 * count * width * hidden,
        ),
        name="expert",
    )(x_rows, dy_rows, scales, w_gate_up, w_down)


def rms_scale(values):
    return lax.rsqrt(jnp.mean(values * values, axis=-1, keepdims=True) + NORM_EPS)


def rotary_tables(length, size):
    index = jnp.arange(size // 2, dtype=FULL)
    frequency = jnp.exp(index * (-2.0 * math.log(10000.0) / size))
    angles = jnp.arange(length, dtype=FULL)[:, None] * frequency[None, :]
    cosine, sine = jnp.cos(angles), jnp.sin(angles)
    return jnp.stack(
        [jnp.concatenate([cosine, cosine], axis=1), jnp.concatenate([-sine, sine], axis=1)]
    )


def norm_back(grad_normed, normed, scale_rows):
    return scale_rows * (
        grad_normed - normed * jnp.mean(grad_normed * normed, axis=-1, keepdims=True)
    )


def contract_rows(left_side, right_side):
    return lax.dot_general(
        left_side, right_side, (((0,), (0,)), ((), ())), preferred_element_type=FULL
    )


def contract_cols(left_side, right_side):
    return lax.dot_general(
        left_side, right_side, (((1,), (1,)), ((), ())), preferred_element_type=FULL
    )


def einsum(spec, left_side, right_side):
    return jnp.einsum(spec, left_side, right_side, preferred_element_type=FULL)


def widen_kernel(steps, *refs):
    low_ref, high_ref, down_ref = refs[0], refs[-2], refs[-1]
    step = pl.program_id(1)

    @pl.when(step < steps)
    def _():
        high_ref[...] = low_ref[...].astype(FULL)

    @pl.when(step >= steps)
    def _():
        down_ref[...] = low_ref[...].astype(FULL)


def widen(first, total, high, grads, held=()):
    count, both, width = grads.shape
    low = both - high
    rows = low // 2
    steps = high // rows
    block = (1, rows, width)
    return pl.pallas_call(
        functools.partial(widen_kernel, steps),
        out_shape=[
            jax.ShapeDtypeStruct((total, high, width), FULL),
            jax.ShapeDtypeStruct((total, low, width), FULL),
        ],
        grid=(count, steps + 2),
        in_specs=[pl.BlockSpec(block, lambda e, r: (e, r, 0))] + [ANY] * len(held),
        out_specs=[
            pl.BlockSpec(block, lambda e, r: (first + e, jnp.minimum(r, steps - 1), 0)),
            pl.BlockSpec(block, lambda e, r: (first + e, jnp.maximum(r - steps, 0), 0)),
        ],
        input_output_aliases={1: 0, 2: 1} if held else {},
        cost_estimate=pl.CostEstimate(
            flops=grads.size, transcendentals=0, bytes_accessed=6 * grads.size
        ),
        name="widen",
    )(grads, *held)


def turn(values, cosine, sine):
    return values * cosine + pltpu.roll(values, values.shape[1] // 2, 1) * sine


def allowed_pairs(column, row):
    shape = (column.shape[0], row.shape[1])
    later = lax.broadcasted_iota(jnp.int32, shape, 0) >= lax.broadcasted_iota(jnp.int32, shape, 1)
    return later & (column == row)


def softmax(query, key, allowed):
    scores = across_cols(query, key) * (1.0 / math.sqrt(query.shape[1]))
    scores = jnp.where(allowed, scores, -1e30)
    powers = jnp.exp(scores - jnp.max(scores, axis=-1, keepdims=True))
    return powers / jnp.sum(powers, axis=-1, keepdims=True)


def attend_block(heads, block, rows_ref, scales, gain_ref, turn_ref, column, row, kept_ref, out_ref):
    width = out_ref.shape[2]
    size = width // heads
    allowed = allowed_pairs(column, row)
    cosine, sine = turn_ref[0], turn_ref[1]
    for h in range(heads):
        parts = []
        for part in range(3):
            columns = pl.ds(part * width + h * size, size)
            values = rows_ref[block, :, columns]
            if part < 2:
                values = values * scales[part]
                values = values * gain_ref[part : part + 1, h * size : (h + 1) * size]
                values = turn(values, cosine, sine)
            parts.append(values.astype(LOW))
            kept_ref[block, :, columns] = parts[-1]
        query, key, value = parts
        probs = softmax(query, key, allowed).astype(LOW)
        out_ref[block, :, pl.ds(h * size, size)] = jnp.dot(
            probs, value, preferred_element_type=FULL
        ).astype(LOW)


def attention_kernel(size, dp_count, heads, *refs):
    x_ref, w_ref, gain_ref, gains_ref, turn_ref, column_ref, row_ref, sheet_ref, dy_ref = refs[:9]
    h_out, rows_out, scale_ref, root_ref, kept_ref, out_ref, own_out, sheet_out, dy_out = refs[9:18]
    x_held, h_held, rows, sums, squares, got = refs[18:24]
    x_sem, h_sem, rows_sem, send_sem, recv_sem, stay_sem = refs[24:30]
    square_sems, line_sems, sheet_sems = refs[30:33], refs[33:38], refs[38:]
    line = LineGather(size // 2, 4, [dy_ref], [dy_out], *line_sems)
    sheets = Sheets(size, dp_count, sheet_ref, sheet_out, *sheet_sems)
    small = Exchange("expert", size, (True,), (1,), [squares], [got], *square_sems)
    place, model_dim = sheets.place, x_ref.shape[2]
    width = out_ref.shape[2]

    def loading(g):
        return pltpu.make_async_copy(x_ref.at[g], x_held.at[g], x_sem.at[g])

    def leaving(g):
        return (
            pltpu.make_async_copy(h_held.at[g], h_out.at[g], h_sem.at[g]),
            pltpu.make_async_copy(rows.at[g], rows_out.at[g], rows_sem.at[g]),
        )

    for g in range(size):
        loading(g).start()
    greet("expert", [(peer, None) for peer in small.peers])
    greet("dp", [(peer, None) for peer in sheets.peers])
    pl.semaphore_wait(pltpu.get_barrier_semaphore(), size + dp_count - 2)
    sheets.begin()
    line.begin()
    sums[...] = jnp.zeros_like(sums)
    lanes = lax.broadcasted_iota(jnp.int32, sums.shape, 1)

    @pl.loop(0, size)
    def _(g):
        loading(g).wait()
        values = x_held[g].astype(FULL)
        root = rms_scale(values)
        root_ref[g] = root
        hidden = (values * root * gain_ref[...]).astype(LOW)
        h_held[g] = hidden
        projected = jnp.dot(hidden, w_ref[...], preferred_element_type=FULL)
        rows[g] = projected
        for copy in leaving(g):
            copy.start()
        for part in range(2):
            half = projected[:, part * width : (part + 1) * width]
            total = jnp.sum(half * half, axis=-1, keepdims=True)
            sums[...] += jnp.where(lanes == part * size + g, total, 0.0)
        line.turn(g)
        pl.when((lax.rem(g, 2) == 0) & (g > 0))(lambda: sheets.forward(lax.div(g, 2)))

    squares[...] = sums[...].T[: 2 * size]
    small.begin()
    small.arrive()
    total = sum(got[i] for i in range(size))
    sums[:, : 2 * size] = lax.rsqrt(total / model_dim + NORM_EPS).T

    def sending(g, source):
        columns = pl.ds(pl.multiple_of(source * width, 128), width)
        target = own_out.at[:, columns]
        return remote(out_ref.at[g], target, send_sem.at[g], recv_sem.at[source], {"expert": g})

    own_columns = pl.ds(pl.multiple_of(place * width, 128), width)
    staying = pltpu.make_async_copy(out_ref.at[place], own_out.at[:, own_columns], stay_sem.at[0])

    @pl.loop(0, size)
    def _(i):
        g = lax.rem(place + 1 + i, size)
        scales = [
            jnp.sum(jnp.where(lanes == part * size + g, sums[...], 0.0), axis=-1, keepdims=True)
            for part in range(2)
        ]
        scale_ref[g] = jnp.concatenate(scales, axis=1)
        attend_block(
            heads, g, rows, scales, gains_ref, turn_ref, column_ref[g], row_ref[g], kept_ref, out_ref
        )
        pl.when(g != place)(lambda: sending(g, place).start())
        line.turn(size + i)
        pl.when((lax.rem(i, 2) == 1) & (i < 2 * (size // 2)))(lambda: sheets.cross(lax.div(i, 2)))

    staying.start()

    @pl.loop(1, size)
    def _(i):
        peer = lax.rem(place + i, size)
        sending(peer, peer).wait_recv()
        sending(peer, place).wait_send()

    @pl.loop(0, size)
    def _(g):
        for copy in leaving(g):
            copy.wait()

    staying.wait()
    small.finish()
    line.finish()
    sheets.finish()


def attention(size, dp_count, heads, arrays, number):
    x_all, w_here, sheet, dy = arrays[0], arrays[1], arrays[7], arrays[8]
    _, tokens, model_dim = x_all.shape
    columns = w_here.shape[1]
    width = columns // 3
    sems = pltpu.SemaphoreType.DMA
    seqs = (size, tokens)
    small = (2 * size, tokens)
    return pl.pallas_call(
        functools.partial(attention_kernel, size, dp_count, heads),
        out_shape=[
            jax.ShapeDtypeStruct(x_all.shape, LOW),
            jax.ShapeDtypeStruct(seqs + (columns,), FULL),
            jax.ShapeDtypeStruct(seqs + (2,), FULL),
            jax.ShapeDtypeStruct(seqs + (1,), FULL),
            jax.ShapeDtypeStruct(seqs + (columns,), LOW),
            jax.ShapeDtypeStruct(seqs + (width,), LOW),
            jax.ShapeDtypeStruct((tokens, model_dim), LOW),
            jax.ShapeDtypeStruct((dp_count, size) + sheet.shape, LOW),
            jax.ShapeDtypeStruct((size,) + dy.shape, LOW),
        ],
        in_specs=[ANY] + [VMEM] * 6 + [ANY] * 2,
        out_specs=[ANY] * 2 + [VMEM] * 4 + [ANY] * 3,
        scratch_shapes=[
            pltpu.VMEM(x_all.shape, LOW),
            pltpu.VMEM(x_all.shape, LOW),
            pltpu.VMEM(seqs + (columns,), FULL),
            pltpu.VMEM((tokens, 128), FULL),
            pltpu.VMEM(small, FULL),
            pltpu.VMEM((size,) + small, FULL),
            sems((size,)),
            sems((size,)),
            sems((size,)),
            sems((size,)),
            sems((size,)),
            sems((1,)),
        ]
        + Exchange.scratch(size, (1,))
        + LineGather.scratch(size, 4, 1)
        + Sheets.scratch(size, dp_count),
        compiler_params=pltpu.CompilerParams(
            collective_id=number, has_side_effects=True, vmem_limit_bytes=48 << 20
        ),
        cost_estimate=pl.CostEstimate(
            flops=2 * x_all.size * columns, transcendentals=0, bytes_accessed=100_000_000
        ),
        name="attention",
    )(*arrays)


def attend_back_block(heads, block, grad_ref, refs, back_ref, dots_ref, gains_ref, w_sum):
    w_ref, kept_ref, out_ref, rows_ref, scale_ref, gain_ref, turn_ref, column_ref, row_ref = refs
    width = out_ref.shape[2]
    size = width // heads
    scaling = 1.0 / math.sqrt(size)
    allowed = allowed_pairs(column_ref[block], row_ref[block])
    cosine, sine = turn_ref[0], turn_ref[1]
    grad_rows = grad_ref[block]
    grad_out = across_cols(grad_rows, w_ref[...]).astype(LOW)
    w_sum[...] += contract_rows(out_ref[block], grad_rows)
    dots = [0.0, 0.0]
    for h in range(heads):
        mine = slice(h * size, (h + 1) * size)
        query, key, value = (
            kept_ref[block, :, pl.ds(p * width + h * size, size)] for p in range(3)
        )
        probs = softmax(query, key, allowed)
        grad = grad_out[:, mine]
        grad_value = contract_rows(probs.astype(LOW), grad)
        grad_probs = across_cols(grad, value)
        delta = jnp.sum(grad_probs * probs, axis=-1, keepdims=True)
        grad_scores = (probs * (grad_probs - delta)).astype(LOW)
        grad_query = jnp.dot(grad_scores, key, preferred_element_type=FULL) * scaling
        grad_key = contract_rows(grad_scores, query) * scaling
        for part, grad_turned in enumerate((grad_query, grad_key)):
            columns = pl.ds(part * width + h * size, size)
            grad_normed = turn(grad_turned, cosine, -sine)
            normed = rows_ref[block, :, columns] * scale_ref[block, :, part : part + 1]
            gains_ref[part : part + 1, mine] += jnp.sum(grad_normed * normed, axis=0, keepdims=True)
            weighted = grad_normed * gain_ref[part : part + 1, mine]
            dots[part] += jnp.sum(weighted * normed, axis=-1, keepdims=True)
            back_ref[block, :, columns] = weighted
        back_ref[block, :, pl.ds(2 * width + h * size, size)] = grad_value
    dots_ref[block] = jnp.concatenate(dots, axis=1)


def attend_back_kernel(levels, cuts, heads, grad_ref, *refs):
    w_ref, others = refs[0], refs[1:9]
    back_ref, dots_ref, gains_ref, w_grad_ref, w_sum, held, w_held, w_sem, *sems = refs[9:]
    reads = (w_held,) + tuple(others)
    line = LineGather(levels, cuts, [grad_ref], [held], *sems)
    mine = pl.ds(pl.multiple_of(line.place * w_held.shape[0], 128), w_held.shape[0])
    loading = pltpu.make_async_copy(w_ref.at[mine], w_held, w_sem.at[0])
    loading.start()
    line_barrier(levels)
    line.begin()
    w_sum[...] = jnp.zeros_like(w_sum)
    gains_ref[...] = jnp.zeros_like(gains_ref)
    loading.wait()
    line.staying(0).wait()

    def landed(block):
        attend_back_block(heads, block, held, reads, back_ref, dots_ref, gains_ref, w_sum)

    line.main(landed)
    wide = w_grad_ref.shape[2]
    for copy in range(w_grad_ref.shape[0]):
        w_grad_ref[copy] = w_sum[:, copy * wide : (copy + 1) * wide].astype(LOW)
    line.finish(held=1)


def attend_back(size, dp_count, heads, grad, arrays, number):
    _, _, out, rows = arrays[:4]
    width = out.shape[2]
    tokens, model_dim = grad.shape
    return pl.pallas_call(
        functools.partial(attend_back_kernel, size // 2, 4, heads),
        out_shape=[
            jax.ShapeDtypeStruct(rows.shape, FULL),
            jax.ShapeDtypeStruct((size, tokens, 2), FULL),
            jax.ShapeDtypeStruct((2, width), FULL),
            jax.ShapeDtypeStruct((dp_count, width, model_dim // dp_count), LOW),
        ],
        in_specs=[ANY] * 2 + [VMEM] * (len(arrays) - 1),
        out_specs=[VMEM] * 4,
        scratch_shapes=[
            pltpu.VMEM((width, model_dim), FULL),
            pltpu.VMEM((size, tokens, model_dim), LOW),
            pltpu.VMEM((width, model_dim), LOW),
            pltpu.SemaphoreType.DMA((1,)),
        ]
        + LineGather.scratch(size, 4, 1),
        compiler_params=pltpu.CompilerParams(
            collective_id=number, has_side_effects=True, vmem_limit_bytes=48 << 20
        ),
        cost_estimate=pl.CostEstimate(flops=0, transcendentals=0, bytes_accessed=150_000_000),
        name="attend_back",
    )(grad, *arrays)


def on_device(
    dp_count,
    line_count,
    layer_input,
    out_cotangent,
    segments,
    routes,
    w_qkv,
    w_out,
    w_router,
    attn_gain,
    mlp_gain,
    query_gain,
    key_gain,
    w_gate_up,
    w_down,
):
    row_count, model_dim = layer_input.shape
    top_count = routes.shape[1]
    expert_count = w_router.shape[1]
    local_count = w_gate_up.shape[0]
    head_size = model_dim // HEADS
    head_cols = model_dim // line_count
    heads_here = head_cols // head_size
    capacity = (row_count * top_count * 9 // 8 + expert_count - 1) // expert_count
    scaling = 1.0 / math.sqrt(head_size)
    place = lax.axis_index("expert")
    all_rows = line_count * row_count
    shard = w_qkv.shape[0]

    small = jnp.concatenate(
        [w_router] + [g[:, None] for g in (attn_gain, mlp_gain, query_gain, key_gain)], axis=1
    )
    small = jnp.pad(small, ((0, 0), (0, 128 - small.shape[1])))
    numbers = jnp.concatenate([routes.T, segments, jnp.zeros((7, row_count), jnp.int32)], axis=0)
    x_all, numbers_all, qkv_here, small = opening(
        line_count, dp_count, [layer_input, numbers], 4, w_qkv, small, 1
    )
    qkv_here = qkv_here.reshape(model_dim, 3 * head_cols)
    small = small.reshape(model_dim, small.shape[3])
    router_full = small[:, :expert_count]
    gains = small[:, expert_count : expert_count + 4].astype(FULL)
    gain_attn, gain_mlp = gains[:, 0], gains[:, 1]
    own_gains = lax.dynamic_slice_in_dim(gains, place * head_cols, head_cols, axis=0)
    gain_query, gain_key = own_gains[:, 2], own_gains[:, 3]

    routes_all = numbers_all[:, :top_count]
    segments_all = numbers_all[:, top_count]
    turns = rotary_tables(row_count, head_size)
    both_gains = jnp.stack([gain_query, gain_key])
    column, row = segments_all[:, :, None], segments_all[:, None, :]
    arrays = [x_all, qkv_here, gain_attn[None], both_gains, turns, column, row, w_out, out_cotangent]
    hidden_one, projected, scales, roots, kept, attended, own_attended, out_full, dy_all = attention(
        line_count, dp_count, heads_here, arrays, 4
    )
    out_full = out_full.reshape(model_dim, model_dim)
    hidden_one = hidden_one.reshape(all_rows, model_dim)
    inputs_all = x_all.reshape(all_rows, model_dim).astype(FULL)
    normed_all = inputs_all * roots.reshape(all_rows, 1)
    inputs = layer_input.astype(FULL)
    scale_attn = rms_scale(inputs)
    normed_attn = inputs * scale_attn
    residual = inputs + jnp.dot(own_attended, out_full, preferred_element_type=FULL)
    scale_mlp = rms_scale(residual)
    normed_mlp = residual * scale_mlp
    hidden_two = (normed_mlp * gain_mlp).astype(LOW)

    logits = jnp.dot(hidden_two, router_full, preferred_element_type=FULL)
    chosen = jnp.any(routes[:, :, None] == jnp.arange(expert_count)[None, None, :], axis=1)
    masked = jnp.where(chosen, logits, -1e30)
    powers = jnp.where(chosen, jnp.exp(masked - jnp.max(masked, axis=-1, keepdims=True)), 0.0)
    gates = powers / jnp.sum(powers, axis=-1, keepdims=True)

    local = place * local_count + jnp.arange(local_count)
    used = jnp.any(routes_all[:, None] == local[None, :, None, None], axis=2)
    position = jnp.arange(row_count)
    lower = (position[:, None] < position[None, :]).astype(LOW)
    rank = einsum("gju,ut->gjt", used.astype(LOW), lower).astype(jnp.int32)
    rank = jnp.where(used, rank, -1)
    spots = jnp.arange(capacity)
    table = (rank[:, :, None, :] == spots[None, None, :, None]).astype(LOW)
    returns = [(rank[:, j, :, None] == spots[None, None, :]).astype(LOW) for j in range(local_count)]
    slots = line_count * capacity
    flat_table = table.reshape(line_count, local_count * capacity, row_count)
    expert_rows, dy_rows, gates_all = gather_place(
        line_count, hidden_two, gates.T, flat_table, dy_all, local_count, 6
    )
    local_gates = lax.dynamic_slice_in_dim(gates_all, place * local_count, local_count, axis=1)
    slot_gates = jnp.sum(table.astype(FULL) * local_gates[:, :, None, :], axis=-1)
    slot_gates = slot_gates.transpose(1, 0, 2).reshape(local_count, slots, 1)
    out_rows, back_rows, slot_grads, grad_sums = [], [], [], []
    both_rows = model_dim // dp_count + w_down.shape[1] // dp_count
    for first, count in ((0, 1), (1, local_count - 1)):
        grads, out_row, back_row, dots = expert(
            first, count, dp_count, expert_rows, dy_rows, slot_gates, w_gate_up, w_down
        )
        grads = grads.reshape(-1, model_dim)
        grads = lax.psum_scatter(grads, "dp", scatter_dimension=0, tiled=True)
        grad_sums.append(grads.reshape(count, both_rows, model_dim))
        for kept_list, rows in ((out_rows, out_row), (back_rows, back_row), (slot_grads, dots)):
            for j in range(count):
                kept_list.append(rows[j].reshape(line_count, capacity, rows.shape[2]))
    gate_rows = model_dim // dp_count
    grad_two, grad_gates = collect_reduce(
        line_count, returns, back_rows, slot_grads, flat_table, 8
    )
    grad_gates = grad_gates.reshape(expert_count, row_count).T
    grad_two = grad_two.astype(FULL)

    grad_out_rows = out_cotangent.astype(FULL)
    grad_logits = gates * (grad_gates - jnp.sum(gates * grad_gates, axis=-1, keepdims=True))
    grad_logits = grad_logits.astype(LOW)
    grad_router = contract_rows(grad_logits, hidden_two)
    grad_two = grad_two + contract_cols(grad_logits, router_full)
    grad_gain_mlp = jnp.sum(grad_two * normed_mlp, axis=0)
    grad_resid = grad_out_rows + norm_back(grad_two * gain_mlp, normed_mlp, scale_mlp)
    grad_attn = grad_resid.astype(LOW)

    arrays = [out_full, kept, attended, projected, scales, both_gains, turns, column, row]
    back, dots, gain_pair, out_parts = attend_back(
        line_count, dp_count, heads_here, grad_attn, arrays, 11
    )
    dots = dots.transpose(2, 0, 1).reshape(2 * line_count, row_count)
    (dots,) = exchange("expert", line_count, [dots], [True], 12)
    dots = jnp.sum(dots, axis=0).reshape(2, all_rows, 1) / model_dim
    flat_scales = scales.reshape(all_rows, 2)
    back = back.reshape(all_rows, 3 * head_cols)
    projected = projected.reshape(all_rows, 3 * head_cols)
    grads = []
    for part in range(2):
        columns = slice(part * head_cols, (part + 1) * head_cols)
        scale = flat_scales[:, part : part + 1]
        normed = projected[:, columns] * scale
        grads.append(scale * (back[:, columns] - normed * dots[part]))
    grad_proj = jnp.concatenate(grads + [back[:, 2 * head_cols :]], axis=-1).astype(LOW)
    grad_one = contract_cols(grad_proj, qkv_here)
    grad_gain_attn = jnp.sum(grad_one * normed_all, axis=0)
    grad_one = grad_one.astype(LOW).reshape(line_count, row_count, model_dim)
    grad_w_qkv = contract_rows(hidden_one, grad_proj)

    out_cols = model_dim // dp_count
    qkv_parts = grad_w_qkv.astype(LOW).reshape(dp_count, out_cols, 3 * head_cols)
    shared = jnp.concatenate([grad_router, grad_gain_attn[None], grad_gain_mlp[None]], axis=0)
    tall = shared.shape[0] + -shared.shape[0] % 8
    shared = jnp.pad(shared, ((0, tall - shared.shape[0]), (0, 0)))
    shared = shared.reshape(tall, dp_count, line_count, shard).transpose(2, 1, 0, 3)
    shared = shared.reshape(line_count, dp_count * tall, shard)
    shared = jnp.pad(shared, ((0, 0), (0, 0), (0, 128 - shard)))
    grad_one, mixture, sum_qkv, sum_out, gain_pair, shared = closing(
        line_count,
        dp_count,
        grad_one,
        returns,
        out_rows,
        4,
        [qkv_parts, out_parts, gain_pair],
        shared,
        14,
    )
    output = (residual + mixture.astype(FULL)).astype(LOW)
    sum_qkv = sum_qkv.transpose(1, 0, 2)
    first_sums, output = lax.optimization_barrier((grad_sums[0], output))
    wide = widen(0, local_count, gate_rows, first_sums)
    sum_gate_up, sum_down = widen(1, local_count, gate_rows, grad_sums[1], wide)
    shared = shared[:, :shard]
    grad_one = grad_one.astype(FULL)
    grad_inputs = grad_resid + norm_back(grad_one * gain_attn, normed_attn, scale_attn)
    return (
        output,
        grad_inputs,
        sum_qkv,
        sum_out,
        shared[:expert_count].T,
        shared[expert_count],
        shared[expert_count + 1],
        gain_pair[0],
        gain_pair[1],
        sum_gate_up,
        sum_down,
    )


def solution(mesh):
    both = ("dp", "expert")
    rows, flat = P(both, None), P(both)
    placed = (rows,) * 7 + (flat,) * 4 + (P("expert", None, None),) * 2
    return jax.shard_map(
        functools.partial(on_device, mesh.shape["dp"], mesh.shape["expert"]),
        mesh=mesh,
        in_specs=placed,
        out_specs=(
            rows,
            rows,
            P("dp", None, "expert"),
            P("expert", "dp"),
            rows,
            flat,
            flat,
            P("expert"),
            P("expert"),
            P("expert", "dp", None),
            P("expert", "dp", None),
        ),
        check_vma=False,
    )
```

```python
import functools
import math

import jax
import jax.numpy as jnp
import numpy as np
from jax import lax
from jax.experimental import pallas as pl
from jax.experimental.pallas import tpu as pltpu
from jax.sharding import PartitionSpec as P

HEADS = 16
NORM_EPS = 1e-05
MESH = pl.DeviceIdType.MESH
ANY = pl.BlockSpec(memory_space=pl.ANY)
LOW = jnp.bfloat16
FULL = jnp.float32


def line_place():
    place = lax.axis_index("expert")
    level, side = lax.div(place, 2), lax.rem(place, 2)
    return place, level, side, place + 1 - 2 * side


def greet(axis, targets):
    barrier = pltpu.get_barrier_semaphore()
    for target, there in targets:

        def signal(target=target):
            pl.semaphore_signal(barrier, inc=1, device_id={axis: target}, device_id_type=MESH)

        if there is None:
            signal()
        else:
            pl.when(there)(signal)


def line_barrier(levels):
    place, level, _, other = line_place()
    has_up, has_down = level < levels - 1, level > 0
    greet("expert", [(other, None), (place + 2, has_up), (place - 2, has_down)])
    count = 1 + has_up.astype(jnp.int32) + has_down.astype(jnp.int32)
    pl.semaphore_wait(pltpu.get_barrier_semaphore(), count)


def around(axis, size):
    place = lax.axis_index(axis)
    return [lax.rem(place + shift, size) for shift in range(1, size)]


def remote(source, target, send, recv, device):
    return pltpu.make_async_remote_copy(
        src_ref=source,
        dst_ref=target,
        send_sem=send,
        recv_sem=recv,
        device_id=device,
        device_id_type=MESH,
    )


class LineGather:
    def __init__(self, levels, cuts, ins, outs, up_sem, down_sem, side_sem, recv_sem, own_sem):
        self.levels, self.cuts, self.ins, self.outs = levels, cuts, ins, outs
        self.up_sem, self.down_sem, self.side_sem = up_sem, down_sem, side_sem
        self.recv_sem, self.own_sem = recv_sem, own_sem
        self.place, self.level, self.side, self.other = line_place()
        self.has_up, self.has_down = self.level < levels - 1, self.level > 0

    @staticmethod
    def scratch(size, cuts, count):
        levels, total = size // 2, cuts + count - 1
        shapes = ((levels, total), (levels, total), (2 * levels - 1, total), (size, total))
        return [pltpu.SemaphoreType.DMA(shape) for shape in shapes + ((count,),)]

    def pieces(self):
        return [(0, k) for k in range(self.cuts)] + [(i, 0) for i in range(1, len(self.ins))]

    def staying(self, i):
        target = self.outs[i].at[self.place]
        return pltpu.make_async_copy(self.ins[i], target, self.own_sem.at[i])

    def sending(self, piece, block, own, sem, target):
        i, k = piece
        landing, source, q = self.outs[i].at[block], self.ins[i], k
        if i:
            q = self.cuts + i - 1
        else:
            rows = source.shape[0] // self.cuts
            landing, source = landing.at[pl.ds(k * rows, rows)], source.at[pl.ds(k * rows, rows)]
        sems = sem.at[q], self.recv_sem.at[block, q]
        return remote(source if own else landing, landing, *sems, {"expert": target})

    def up(self, piece, step, own=False):
        block = self.place - 2 * step
        return self.sending(piece, block, own, self.up_sem.at[step], self.place + 2)

    def down(self, piece, step, own=False):
        block = self.place + 2 * step
        return self.sending(piece, block, own, self.down_sem.at[step], self.place - 2)

    def across(self, piece, step, own=False):
        sem = self.side_sem.at[step + self.levels - 1]
        return self.sending(piece, self.place - 2 * step, own, sem, self.other)

    def begin(self):
        for piece in self.pieces():
            pl.when(self.has_up)(self.up(piece, 0, True).start)
            pl.when(self.has_down)(self.down(piece, 0, True).start)
        for piece in self.pieces():
            self.across(piece, 0, True).start()
        for i in range(len(self.ins)):
            self.staying(i).start()

    def forward(self, step, piece):
        @pl.when(self.level >= step)
        def _():
            self.across(piece, step).wait_recv()
            pl.when(self.has_up)(self.up(piece, step).start)
            self.across(piece, step).start()

        @pl.when(self.level + step < self.levels)
        def _():
            self.across(piece, -step).wait_recv()
            pl.when(self.has_down)(self.down(piece, step).start)
            self.across(piece, -step).start()

    def land_across(self, block):
        for piece in self.pieces():
            self.sending(piece, block, False, self.side_sem.at[0], self.other).wait_recv()

    def turn(self, turn, landed=None):
        levels, cuts = self.levels, self.cuts
        step, k = lax.div(turn, cuts) + 1, lax.rem(turn, cuts)

        @pl.when(step < levels)
        def _():
            self.forward(step, (0, k))

            @pl.when(k == cuts - 1)
            def _():
                for i in range(1, len(self.ins)):
                    self.forward(step, (i, 0))

        group, sign, crossed = step - 1, 2 * lax.rem(k, 2) - 1, lax.div(k, 2)
        crossed = jnp.where(group == 0, k, crossed)
        far = jnp.where(group == 0, self.level, self.level + sign * group)

        @pl.when((far >= 0) & (far < levels) & (k < 4) & ((group > 0) | (k < 2)))
        def _():
            block = 2 * far + self.side + crossed * (1 - 2 * self.side)

            @pl.when(crossed == 1)
            def _():
                self.land_across(block)

            if landed:
                landed(block)

    def main(self, landed=None):
        @pl.loop(0, self.levels * self.cuts)
        def _(turn):
            self.turn(turn, landed)

    def finish(self, held=0):
        for piece in self.pieces():
            self.across(piece, 0).wait_send()
            for step in range(self.levels):
                above, below = self.level >= step, self.level + step < self.levels
                pl.when(self.has_up & above)(self.up(piece, step).wait_send)
                pl.when(self.has_down & below)(self.down(piece, step).wait_send)
                if step:
                    pl.when(above)(self.across(piece, step).wait_send)
                    pl.when(below)(self.across(piece, -step).wait_send)
        for i in range(held, len(self.ins)):
            self.staying(i).wait()


def call(kernel, name, number, outs, scratch, arrays, moved):
    return pl.pallas_call(
        kernel,
        out_shape=outs,
        in_specs=[ANY] * len(arrays),
        out_specs=[ANY] * len(outs),
        scratch_shapes=scratch,
        compiler_params=pltpu.CompilerParams(
            collective_id=number, has_side_effects=True, vmem_limit_bytes=48 << 20
        ),
        cost_estimate=pl.CostEstimate(flops=0, transcendentals=0, bytes_accessed=moved),
        name=name,
    )(*arrays)


class LineReduce:
    def __init__(self, levels, cuts, parts, total, own, beside, rising, falling, *sems):
        self.levels, self.cuts, self.parts, self.total = levels, cuts, parts, total
        self.made = parts.shape[0] == levels
        self.own, self.beside, self.rising, self.falling = own, beside, rising, falling
        self.load_sem, self.side_send, self.side_recv = sems[:3]
        self.up_send, self.up_recv, self.down_send, self.down_recv, self.out_sem = sems[3:]
        self.place, self.level, self.side, self.other = line_place()
        self.has_up, self.has_down = self.level < levels - 1, self.level > 0
        self.rows = parts.shape[1] // cuts

    @staticmethod
    def scratch(size, block, dtype, cuts):
        levels = size // 2
        return (
            [pltpu.VMEM((levels,) + block, dtype)] * 2
            + [pltpu.VMEM((levels - 1,) + block, dtype)] * 2
            + [pltpu.SemaphoreType.DMA((levels, cuts))] * 7
            + [pltpu.SemaphoreType.DMA((cuts,))]
        )

    def cut(self, ref, block, k):
        return ref.at[block, pl.ds(k * self.rows, self.rows)]

    def loading(self, far, k):
        source = self.cut(self.parts, 2 * far + self.side, k)
        return pltpu.make_async_copy(source, self.cut(self.own, far, k), self.load_sem.at[far, k])

    def across(self, far, k):
        source = self.cut(self.parts, far if self.made else 2 * far + 1 - self.side, k)
        sems = self.side_send.at[far, k], self.side_recv.at[far, k]
        return remote(source, self.cut(self.beside, far, k), *sems, {"expert": self.other})

    def up(self, far, k):
        sems = self.up_send.at[far, k], self.up_recv.at[far, k]
        target = {"expert": self.place + 2}
        return remote(self.cut(self.own, far, k), self.cut(self.rising, far - 1, k), *sems, target)

    def down(self, far, k):
        sems = self.down_send.at[far, k], self.down_recv.at[far, k]
        target = {"expert": self.place - 2}
        return remote(self.cut(self.own, far, k), self.cut(self.falling, far, k), *sems, target)

    def value(self, ref, block, k):
        return self.cut(ref, block, k)[...].astype(FULL)

    def load(self):
        for i in range(self.levels):
            for k in range(self.cuts):
                self.loading(self.far(i), k).start()

    def begin(self):
        for i in range(self.levels):
            for k in range(self.cuts):
                self.across(self.far(i), k).start()

    def far(self, i):
        return jnp.where(lax.rem(i, 2) == 0, self.levels - 1 - lax.div(i, 2), lax.div(i, 2))

    def prepare(self, turn, make):
        far = self.far(lax.div(turn, 2))

        @pl.when(lax.rem(turn, 2) == 0)
        def _():
            make(2 * far + 1 - self.side, self.parts.at[far])
            for k in range(self.cuts):
                self.across(far, k).start()

        @pl.when(lax.rem(turn, 2) == 1)
        def _():
            make(2 * far + self.side, self.own.at[far])

    def pair(self, far, k):
        if not self.made:
            self.loading(far, k).wait()
        self.across(far, k).wait_recv()
        return self.value(self.own, far, k) + self.value(self.beside, far, k)

    def store(self, far, k, total):
        self.cut(self.own, far, k)[...] = total.astype(self.own.dtype)

    def toward(self, far, k, ahead, behind, move, arrived, shift):
        @pl.when(ahead & behind)
        def _():
            both = self.pair(far, k)
            move(far, k).wait_recv()
            self.store(far, k, both + self.value(arrived, far - shift, k))

        @pl.when(ahead & jnp.logical_not(behind))
        def _():
            self.store(far, k, self.pair(far, k))

        pl.when(ahead)(move(far, k).start)

    def main(self, beside=None):
        @pl.loop(0, (self.levels - 1) * self.cuts)
        def _(turn):
            step, k = lax.div(turn, self.cuts), lax.rem(turn, self.cuts)
            high, low = self.levels - 1 - step, step
            if beside:
                beside(turn)
            self.toward(high, k, self.level < high, self.has_down, self.up, self.rising, 1)
            self.toward(low, k, self.level > low, self.has_up, self.down, self.falling, 0)

        @pl.loop(0, self.cuts)
        def _(k):
            self.store(self.level, k, self.pair(self.level, k))
            for there, move, arrived, shift in (
                (self.has_down, self.up, self.rising, 1),
                (self.has_up, self.down, self.falling, 0),
            ):

                @pl.when(there)
                def _():
                    move(self.level, k).wait_recv()
                    total = self.value(self.own, self.level, k)
                    total += self.value(arrived, self.level - shift, k)
                    self.store(self.level, k, total)

            self.leaving(k).start()

    def leaving(self, k):
        target = self.total.at[pl.ds(k * self.rows, self.rows)]
        return pltpu.make_async_copy(self.cut(self.own, self.level, k), target, self.out_sem.at[k])

    def finish(self):
        for k in range(self.cuts):
            self.leaving(k).wait()
            for far in range(self.levels):
                self.across(far, k).wait_send()
                pl.when(self.level < far)(self.up(far, k).wait_send)
                pl.when(self.level > far)(self.down(far, k).wait_send)


class Exchange:
    def __init__(self, axis, size, spread, cuts, ins, outs, send_sem, recv_sem, own_sem):
        self.axis, self.spread, self.ins, self.outs = axis, spread, ins, outs
        self.send_sem, self.recv_sem, self.own_sem = send_sem, recv_sem, own_sem
        self.cuts = cuts
        self.firsts = [sum(cuts[:i]) for i in range(len(cuts))]
        self.pieces = [(i, k) for i in range(len(cuts)) for k in range(cuts[i])]
        self.place, self.peers = lax.axis_index(axis), around(axis, size)

    @staticmethod
    def scratch(size, cuts):
        sems = pltpu.SemaphoreType.DMA
        return [sems((sum(cuts), size)), sems((sum(cuts), size)), sems((len(cuts),))]

    def source(self, i, block):
        return self.ins[i] if self.spread[i] else self.ins[i].at[block]

    def staying(self, i):
        target = self.outs[i].at[self.place]
        return pltpu.make_async_copy(self.source(i, self.place), target, self.own_sem.at[i])

    def sending(self, i, k, shift, landing):
        peer = self.peers[shift]
        source, target, q = self.source(i, peer), self.outs[i].at[landing], self.firsts[i] + k
        if self.cuts[i] > 1:
            rows = target.shape[0] // self.cuts[i]
            source, target = source.at[pl.ds(k * rows, rows)], target.at[pl.ds(k * rows, rows)]
        sems = self.send_sem.at[q, shift], self.recv_sem.at[q, landing]
        return remote(source, target, *sems, {self.axis: peer})

    def send(self, i, k):
        for shift in range(len(self.peers)):
            self.sending(i, k, shift, self.place).start()

    def stay(self):
        for i in range(len(self.spread)):
            self.staying(i).start()

    def begin(self):
        for i, k in self.pieces:
            self.send(i, k)
        self.stay()

    def land(self):
        for shift, peer in enumerate(self.peers):
            for i, k in self.pieces:
                self.sending(i, k, shift, peer).wait_recv()

    def arrive(self):
        self.land()
        for i in range(len(self.spread)):
            self.staying(i).wait()

    def finish(self):
        for shift in range(len(self.peers)):
            for i, k in self.pieces:
                self.sending(i, k, shift, self.place).wait_send()


def exchange_kernel(axis, size, spread, *refs):
    count = len(spread)
    ins, outs, sems = refs[:count], refs[count : 2 * count], refs[2 * count :]
    moves = Exchange(axis, size, spread, (1,) * count, ins, outs, *sems)
    greet(axis, [(peer, None) for peer in moves.peers])
    pl.semaphore_wait(pltpu.get_barrier_semaphore(), size - 1)
    moves.begin()
    moves.arrive()
    moves.finish()


def exchange_outs(size, arrays, spread):
    return [
        jax.ShapeDtypeStruct((size,) + a.shape if flat else a.shape, a.dtype)
        for a, flat in zip(arrays, spread)
    ]


def exchange(axis, size, arrays, spread, number):
    return call(
        functools.partial(exchange_kernel, axis, size, tuple(spread)),
        "exchange_" + axis,
        number,
        exchange_outs(size, arrays, spread),
        Exchange.scratch(size, (1,) * len(arrays)),
        arrays,
        30_000_000,
    )


def opening_kernel(size, dp_count, count, cuts, *refs):
    ins, (w_ref, *small_refs) = refs[:count], refs[count : count + 3]
    outs, rest = refs[count + 3 : 2 * count + 3], refs[2 * count + 6 :]
    w_out, *small_outs = refs[2 * count + 3 : 2 * count + 6]
    line = LineGather(size // 2, cuts, ins, outs, *rest[:5])
    send_sem, recv_sem, own_sem = rest[5:8]
    place, mine = line.place, lax.axis_index("dp")
    peers = around("expert", size)
    width = w_out.shape[3] // 3
    lands = [w_out] + small_outs
    across = Exchange(
        "dp", dp_count, (True,) * 3, (size,) * 3, [a.at[mine] for a in lands], lands, *rest[8:]
    )
    greet("expert", [(peer, None) for peer in peers])
    greet("dp", [(peer, None) for peer in across.peers])
    pl.semaphore_wait(pltpu.get_barrier_semaphore(), size + dp_count - 2)

    def ends(peer, landing, j):
        if j >= 3:
            return small_refs[j - 3], small_outs[j - 3].at[mine, landing]
        start = pl.multiple_of(j * width * size + peer * width, 128)
        target = w_out.at[mine, landing, :, pl.ds(j * width, width)]
        return w_ref.at[:, pl.ds(start, width)], target

    def sending(shift, landing, j):
        source, target = ends(peers[shift], landing, j)
        sems = send_sem.at[shift, j], recv_sem.at[landing, j]
        return remote(source, target, *sems, {"expert": peers[shift]})

    own = [pltpu.make_async_copy(*ends(place, place, j), own_sem.at[j]) for j in range(5)]
    for shift in range(size - 1):
        for j in range(5):
            sending(shift, place, j).start()
    for copy in own:
        copy.start()
    line.begin()
    for copy in own:
        copy.wait()
    for i in range(3):
        across.send(i, place)
    for shift, peer in enumerate(peers):
        for j in range(5):
            sending(shift, peer, j).wait_recv()
        for i in range(3):
            across.send(i, peer)
    line.main()
    line.finish()
    for shift in range(size - 1):
        for j in range(5):
            sending(shift, place, j).wait_send()
    across.land()
    across.finish()


def opening(size, dp_count, arrays, cuts, weights, small, number):
    sems = pltpu.SemaphoreType.DMA
    outs = [jax.ShapeDtypeStruct((size,) + a.shape, a.dtype) for a in arrays]
    rows, columns = weights.shape
    whole = (dp_count, size, rows)
    outs.append(jax.ShapeDtypeStruct(whole + (columns // size,), weights.dtype))
    outs += [jax.ShapeDtypeStruct((dp_count, size) + a.shape, a.dtype) for a in small]
    return call(
        functools.partial(opening_kernel, size, dp_count, len(arrays), cuts),
        "opening",
        number,
        outs,
        LineGather.scratch(size, cuts, len(arrays))
        + [sems((size, 5)), sems((size, 5)), sems((5,))]
        + Exchange.scratch(dp_count, (size,) * 3),
        list(arrays) + [weights] + small,
        200_000_000,
    )


class Sheets:
    def __init__(self, size, dp_count, source, target, *sems):
        self.levels, self.dp_count, self.ins, self.out = size // 2, dp_count, source, target
        self.up_send, self.down_send, self.line_recv, self.dp_send, self.dp_recv = sems[:5]
        self.side_send, self.side_recv, self.own_sem = sems[5:]
        self.place, self.level, self.side, self.other = line_place()
        self.has_up, self.has_down = self.level < self.levels - 1, self.level > 0
        self.mine, self.peers = lax.axis_index("dp"), around("dp", dp_count)

    @staticmethod
    def scratch(size, dp_count):
        sems, levels = pltpu.SemaphoreType.DMA, size // 2
        return [sems((levels,))] * 3 + [sems((dp_count, levels))] * 4 + [sems((1,))]

    def along(self, far, own, send, target):
        landing = self.out.at[self.mine, 2 * far + self.side]
        source = self.ins if own else landing
        return remote(source, landing, send.at[far], self.line_recv.at[far], {"expert": target})

    def up(self, far, own=False):
        return self.along(far, own, self.up_send, self.place + 2)

    def down(self, far, own=False):
        return self.along(far, own, self.down_send, self.place - 2)

    def over(self, far, shift, copy, own=False):
        landing = self.out.at[copy, 2 * far + self.side]
        source = self.ins if own else landing
        sems = self.dp_send.at[shift, far], self.dp_recv.at[copy, far]
        return remote(source, landing, *sems, {"dp": self.peers[shift]})

    def across(self, far, copy, whose, own=False):
        landing = self.out.at[copy, 2 * far + whose]
        source = self.ins if own else landing
        sems = self.side_send.at[copy, far], self.side_recv.at[copy, far]
        return remote(source, landing, *sems, {"expert": self.other})

    def spread(self, far, own=False):
        for shift in range(self.dp_count - 1):
            self.over(far, shift, self.mine, own).start()
        self.across(far, self.mine, self.side, own).start()

    def staying(self):
        target = self.out.at[self.mine, self.place]
        return pltpu.make_async_copy(self.ins, target, self.own_sem.at[0])

    def begin(self):
        pl.when(self.has_up)(self.up(self.level, True).start)
        pl.when(self.has_down)(self.down(self.level, True).start)
        self.spread(self.level, True)
        self.staying().start()

    def forward(self, step):
        @pl.when(self.level >= step)
        def _():
            self.up(self.level - step).wait_recv()
            pl.when(self.has_up)(self.up(self.level - step).start)
            self.spread(self.level - step)

        @pl.when(self.level + step < self.levels)
        def _():
            self.down(self.level + step).wait_recv()
            pl.when(self.has_down)(self.down(self.level + step).start)
            self.spread(self.level + step)

    def cross(self, far):
        for shift, peer in enumerate(self.peers):
            self.over(far, shift, peer).wait_recv()
            self.across(far, peer, self.side).start()

    def finish(self):
        @pl.loop(0, self.levels)
        def _(far):
            pl.when(self.has_up & (self.level >= far))(self.up(far).wait_send)
            pl.when(self.has_down & (self.level <= far))(self.down(far).wait_send)
            for shift in range(self.dp_count - 1):
                self.over(far, shift, self.mine).wait_send()
            for copy in range(self.dp_count):
                self.across(far, copy, 1 - self.side).wait_recv()
                self.across(far, copy, self.side).wait_send()

        self.staying().wait()


VMEM = pl.BlockSpec(memory_space=pltpu.VMEM)
COLUMNS = 512


def gather_place_kernel(levels, cuts, *refs):
    rows_ref, gates_ref, table_ref, dy_ref, x_out, dy_out, gates_out = refs[:7]
    held, dy_held, x_stage, dy_stage = refs[7:11]
    line_sems, (dy_sem, x_sems, dy_sems) = refs[11:16], refs[16:]
    line = LineGather(levels, cuts, [rows_ref, gates_ref], [held, gates_out], *line_sems)
    size, width = 2 * levels, held.shape[2]
    _, local_count, capacity, _ = x_stage.shape

    def leaving(block, stage, out, sems):
        target = out.at[:, pl.ds(pl.multiple_of(block * capacity, 8), capacity)]
        return pltpu.make_async_copy(stage.at[block], target, sems.at[block])

    def place(block, rows, stage, out, sems):
        table = table_ref[block]

        @pl.loop(0, width // COLUMNS)
        def _(n):
            columns = pl.ds(pl.multiple_of(n * COLUMNS, COLUMNS), COLUMNS)
            placed = jnp.dot(table, rows[block, :, columns], preferred_element_type=FULL)
            for j in range(local_count):
                part = placed[j * capacity : (j + 1) * capacity]
                stage[block, j, :, columns] = part.astype(stage.dtype)

        leaving(block, stage, out, sems).start()

    def place_x(block):
        place(block, held, x_stage, x_out, x_sems)

    loading = pltpu.make_async_copy(dy_ref, dy_held, dy_sem.at[0])
    loading.start()
    line_barrier(levels)
    line.begin()
    loading.wait()

    @pl.loop(0, size)
    def _(block):
        place(block, dy_held, dy_stage, dy_out, dy_sems)

    line.staying(0).wait()
    line.main(place_x)
    line.finish(held=1)

    @pl.loop(0, size)
    def _(block):
        leaving(block, x_stage, x_out, x_sems).wait()
        leaving(block, dy_stage, dy_out, dy_sems).wait()


def gather_place(size, rows, gates, table, dy, local_count, number):
    cuts = 4
    tokens, width = rows.shape
    capacity = table.shape[1] // local_count
    placed = jax.ShapeDtypeStruct((local_count, size * capacity, width), rows.dtype)
    sems = pltpu.SemaphoreType.DMA
    return pl.pallas_call(
        functools.partial(gather_place_kernel, size // 2, cuts),
        out_shape=[placed, placed, jax.ShapeDtypeStruct((size,) + gates.shape, gates.dtype)],
        in_specs=[ANY, ANY, VMEM, ANY],
        out_specs=[ANY] * 3,
        scratch_shapes=[pltpu.VMEM((size, tokens, width), rows.dtype)] * 2
        + [pltpu.VMEM((size, local_count, capacity, width), rows.dtype)] * 2
        + LineGather.scratch(size, cuts, 2)
        + [sems((1,)), sems((size,)), sems((size,))],
        compiler_params=pltpu.CompilerParams(
            collective_id=number, has_side_effects=True, vmem_limit_bytes=48 << 20
        ),
        cost_estimate=pl.CostEstimate(
            flops=4 * table.size * width, transcendentals=0, bytes_accessed=150_000_000
        ),
        name="gather_place",
    )(rows, gates, table, dy)


def split_at(arrays, j, block):
    for array in arrays:
        if j < array.shape[0]:
            return array.at[j, block]
        j -= array.shape[0]


def collect_block(tables, slots, block, target):
    @pl.loop(0, target.shape[1] // COLUMNS)
    def _(n):
        columns = pl.ds(pl.multiple_of(n * COLUMNS, COLUMNS), COLUMNS)
        total = 0.0
        for j, table in enumerate(tables):
            rows = split_at(slots, j, block)[:, columns]
            total += jnp.dot(table[block], rows, preferred_element_type=FULL)
        target[:, columns] = total.astype(target.dtype)


def collect_reduce_kernel(levels, cuts, local_count, *refs):
    tables, refs = refs[:local_count], refs[local_count:]
    slots, dots, (table_ref, total_ref, gates_out, away) = refs[:2], refs[2:4], refs[4:8]
    rest, (gates, *sems) = refs[8:20], refs[20:]
    line = LineReduce(levels, cuts, away, total_ref, *rest)
    small = Exchange("expert", 2 * levels, (False,), (1,), [gates], [gates_out], *sems)
    greet("expert", [(peer, None) for peer in small.peers])
    pl.semaphore_wait(pltpu.get_barrier_semaphore(), 2 * levels - 1)
    make = functools.partial(collect_block, tables, slots)

    @pl.loop(0, 4)
    def _(turn):
        line.prepare(turn, make)

    @pl.loop(0, 2 * levels)
    def _(block):
        table = table_ref[block].astype(FULL)
        capacity = table.shape[0] // local_count
        for j in range(local_count):
            part = table[j * capacity : (j + 1) * capacity] * split_at(dots, j, block)[...]
            gates[block, j : j + 1] = jnp.sum(part, axis=0, keepdims=True)

    small.begin()

    def beside(turn):
        pl.when(turn + 4 < 2 * levels)(lambda: line.prepare(turn + 4, make))

    line.main(beside)
    small.arrive()
    line.finish()
    small.finish()


def collect_reduce(size, tables, slots, dots, table, number):
    levels, cuts = size // 2, 4
    block = (tables[0].shape[1], slots[0].shape[3])
    kind = slots[0].dtype
    gates = (size, len(tables), block[0])
    return pl.pallas_call(
        functools.partial(collect_reduce_kernel, levels, cuts, len(tables)),
        out_shape=[jax.ShapeDtypeStruct(block, kind), jax.ShapeDtypeStruct(gates, FULL)],
        in_specs=[VMEM] * (len(tables) + 5),
        out_specs=[ANY, ANY],
        scratch_shapes=[pltpu.VMEM((levels,) + block, kind)]
        + LineReduce.scratch(size, block, kind, cuts)
        + [pltpu.VMEM(gates, FULL)]
        + Exchange.scratch(size, (1,)),
        compiler_params=pltpu.CompilerParams(
            collective_id=number, has_side_effects=True, vmem_limit_bytes=48 << 20
        ),
        cost_estimate=pl.CostEstimate(flops=0, transcendentals=0, bytes_accessed=150_000_000),
        name="collect_reduce",
    )(*tables, *slots, *dots, table)


def closing_kernel(size, dp_count, local_count, cuts, sum_cuts, *refs):
    refs, levels = list(refs), size // 2

    def take(count):
        taken = refs[:count]
        del refs[:count]
        return taken

    tables, slots = take(local_count), take(2)
    proj_ref, w_ref, h_ref, gain_ref, out_parts, gain_pair, shared_ref = take(7)
    back_out, mixed_out, qkv_out, w_out, gains_out, gain_out, shared_out = take(7)
    back = LineReduce(levels, cuts, *take(1), back_out, *take(12))
    mixed = LineReduce(levels, cuts, *take(1), mixed_out, *take(12))
    qkv_parts, qkv_got, out_got, gains_got = take(4)
    got, half, last, gain_sum, gain_got, gain_half, gain_last = take(7)
    parts, lands = [qkv_parts, out_parts, gain_pair], [qkv_got, out_got, gains_got]
    sums = Exchange("dp", dp_count, (False, False, True), sum_cuts, parts, lands, *take(3))
    first = Exchange("expert", size, (False,), (1,), [shared_ref], [got], *take(3))
    second = Exchange("dp", dp_count, (False,), (1,), [half], [last], *take(3))
    gain_first = Exchange("expert", size, (True,), (1,), [gain_sum], [gain_got], *take(3))
    gain_second = Exchange("dp", dp_count, (True,), (1,), [gain_half], [gain_last], *take(3))
    greet("expert", [(peer, None) for peer in first.peers])
    greet("dp", [(peer, None) for peer in sums.peers])
    pl.semaphore_wait(pltpu.get_barrier_semaphore(), size + dp_count - 2)
    first.begin()
    sums.staying(1).start()
    sums.staying(2).start()
    gain_sum[...] = jnp.zeros_like(gain_sum)
    groups, tokens, model_dim = h_ref.shape
    tall, high = half.shape[1], model_dim // dp_count

    def make_back(block, target):
        @pl.loop(0, model_dim // COLUMNS)
        def _(n):
            columns = pl.ds(pl.multiple_of(n * COLUMNS, COLUMNS), COLUMNS)
            grad = across_cols(proj_ref[block], w_ref[columns, :])
            target[:, columns] = grad.astype(target.dtype)
            weighted = grad * h_ref[block, :, columns].astype(FULL)
            gain_sum[:, columns] += jnp.sum(weighted, axis=0, keepdims=True)

    def piece(k):
        @pl.loop(0, dp_count)
        def _(copy):
            columns = pl.ds(pl.multiple_of(copy * high + k * 128, 128), 128)
            rows = h_ref[:, :, columns].reshape(groups * tokens, 128)
            grads = proj_ref[...].reshape(groups * tokens, proj_ref.shape[2])
            qkv_parts[copy, pl.ds(k * 128, 128)] = contract_rows(rows, grads).astype(LOW)

        sums.send(0, k)
        pl.when(k == sum_cuts[0] - 1)(sums.staying(0).start)

    make_mixed = functools.partial(collect_block, tables, slots)
    ahead = levels

    @pl.loop(0, ahead)
    def _(turn):
        back.prepare(turn, make_back)

    def beside(turn):
        later = turn - ahead
        pl.when(turn + ahead < 2 * levels)(lambda: back.prepare(turn + ahead, make_back))
        pl.when(turn < sum_cuts[1])(lambda: sums.send(1, turn))
        pl.when(turn == sum_cuts[1])(lambda: sums.send(2, 0))
        pl.when(later == 0)(gain_first.begin)
        pl.when((later >= 0) & (later < 2 * levels))(lambda: mixed.prepare(later, make_mixed))
        pl.when((later >= 0) & (later < sum_cuts[0]))(lambda: piece(later))

        @pl.when(later == ahead)
        def _():
            first.arrive()
            for copy in range(dp_count):
                rows = pl.ds(copy * tall, tall)
                half[copy] = sum(got[i, rows, :] for i in range(size))
            second.begin()
            gain_first.arrive()
            gain_half[...] = sum(gain_got[i] for i in range(size))
            gain_second.begin()

    back.main(beside)
    mixed.main()
    second.arrive()
    shared_out[...] = sum(last[i] for i in range(dp_count))
    gain_second.arrive()
    gain_out[...] = sum(gain_last[i] for i in range(dp_count)) / gain_ref[...]
    sums.arrive()
    wide = qkv_out.shape[2]
    for j in range(3):
        columns = slice(j * wide, (j + 1) * wide)
        qkv_out[j] = sum(qkv_got[copy, :, columns].astype(FULL) for copy in range(dp_count))
    w_out[...] = sum(out_got[copy].astype(FULL) for copy in range(dp_count))
    gains_out[...] = sum(gains_got[copy] for copy in range(dp_count))
    for moves in (back, mixed, first, second, sums, gain_first, gain_second):
        moves.finish()


def closing(size, dp_count, tables, slots, arrays, sums, shared, number):
    proj, _, hidden, gain = arrays
    levels, cuts = size // 2, 4
    _, tokens, model_dim = hidden.shape
    columns, high = proj.shape[2], model_dim // dp_count
    block = (tokens, model_dim)
    tall = shared.shape[1] // dp_count
    wide = shared.shape[2]
    sum_cuts = (high // 128, 2, 1)
    out, pair = exchange_outs(dp_count, sums, (False, True))
    shapes = [(3, high, columns // 3), out.shape[1:], pair.shape[1:], gain.shape, (tall, wide)]
    outs = [jax.ShapeDtypeStruct(block, LOW)] * 2
    outs += [jax.ShapeDtypeStruct(shape, FULL) for shape in shapes]
    line = [pltpu.VMEM((levels,) + block, LOW)] + LineReduce.scratch(size, block, LOW, cuts)
    return pl.pallas_call(
        functools.partial(closing_kernel, size, dp_count, len(tables), cuts, sum_cuts),
        out_shape=outs,
        in_specs=[VMEM] * (len(tables) + 6) + [ANY] * 3,
        out_specs=[ANY] * 2 + [VMEM] * 5,
        scratch_shapes=line
        + line
        + [pltpu.VMEM((dp_count, high, columns), LOW)] * 2
        + [pltpu.VMEM(a.shape, a.dtype) for a in (out, pair)]
        + [pltpu.VMEM((size,) + shared.shape[1:], FULL)]
        + [pltpu.VMEM((dp_count, tall, wide), FULL)] * 2
        + [
            pltpu.VMEM(gain.shape, FULL),
            pltpu.VMEM((size,) + gain.shape, FULL),
            pltpu.VMEM(gain.shape, FULL),
            pltpu.VMEM((dp_count,) + gain.shape, FULL),
        ]
        + Exchange.scratch(dp_count, sum_cuts)
        + Exchange.scratch(size, (1,))
        + Exchange.scratch(dp_count, (1,))
        + Exchange.scratch(size, (1,))
        + Exchange.scratch(dp_count, (1,)),
        compiler_params=pltpu.CompilerParams(
            collective_id=number, has_side_effects=True, vmem_limit_bytes=62 << 20
        ),
        cost_estimate=pl.CostEstimate(flops=0, transcendentals=0, bytes_accessed=200_000_000),
        name="closing",
    )(*tables, *slots, *arrays, *sums, shared)


def across_cols(left_side, right_side):
    return lax.dot_general(
        left_side, right_side, (((1,), (1,)), ((), ())), preferred_element_type=FULL
    )


def expert_kernel(first, count, tiles, x_ref, dy_ref, scale_ref, side_ref, down_ref, grads_ref, out_ref, back_ref, dots_ref,
                  side_w, down_w, turned, turned_act, act, grad_side, side_buf, down_buf, w_sems, sems):
    e, step = pl.program_id(0), pl.program_id(1)
    slot = lax.rem(e, 2)
    hidden, model = down_w.shape[1], down_w.shape[2]
    width, wide = hidden // tiles, model // tiles
    copies = grads_ref.shape[0]
    high, low = model // copies, hidden // copies
    part = side_buf.shape[1]

    def loads(e, tile):
        slot = lax.rem(e, 2)
        out = []
        for half in range(2):
            columns = pl.ds(pl.multiple_of(half * hidden + tile * width, 128), width)
            out.append(pltpu.make_async_copy(side_ref.at[first + e, :, columns], side_w.at[slot, :, columns], w_sems.at[slot, tile, half]))
        rows = pl.ds(pl.multiple_of(tile * width, 128), width)
        out.append(pltpu.make_async_copy(down_ref.at[first + e, rows], down_w.at[slot, rows], w_sems.at[slot, tile, 2]))
        return out

    def leaving(at):
        e, chunk = lax.div(at, tiles), lax.rem(at, tiles)
        slot = lax.rem(at, 2)
        base = e * (high + low)
        columns = pl.ds(pl.multiple_of(chunk * wide, 128), wide)
        if wide >= high:
            target = grads_ref.at[pl.ds(chunk * part, part), pl.ds(base, high)]
        else:
            target = grads_ref.at[pl.ds(lax.div(chunk * wide, high), 1), pl.ds(base + lax.rem(chunk * wide, high), wide)]
        return (pltpu.make_async_copy(side_buf.at[slot], target, sems.at[slot, 0]),
                pltpu.make_async_copy(down_buf.at[slot], grads_ref.at[:, pl.ds(base + high, low), columns], sems.at[slot, 1]))

    @pl.when((e == 0) & (step == 0))
    def _():
        for tile in range(tiles):
            for copy in loads(e, tile): copy.start()

    @pl.when((e + 1 < count) & (step == 0))
    def _():
        for tile in range(tiles):
            for copy in loads(e + 1, tile): copy.start()

    @pl.when(step == 0)
    def _():
        turned[...] = x_ref[0].T
        dots_ref[...] = jnp.zeros_like(dots_ref)

    @pl.when(step < tiles)
    def _():
        for copy in loads(e, step): copy.wait()
        rows, grads, scale = x_ref[0], dy_ref[0], scale_ref[0]
        columns = pl.ds(pl.multiple_of(step * width, 128), width)
        others = pl.ds(pl.multiple_of(hidden + step * width, 128), width)
        gate = jnp.dot(rows, side_w[slot, :, columns], preferred_element_type=FULL)
        up = jnp.dot(rows, side_w[slot, :, others], preferred_element_type=FULL)
        grad_act = across_cols(grads, down_w[slot, columns, :])
        sigmoid = jax.nn.sigmoid(gate)
        silu = gate * sigmoid
        raw = silu * up
        dots_ref[0] += jnp.sum(raw * grad_act, axis=-1, keepdims=True)
        weighted = (scale * raw).astype(LOW)
        act[:, columns] = weighted
        turned_act[columns, :] = weighted.T
        grad_act = grad_act * scale
        grad_side[:, columns] = (grad_act * up * sigmoid * (1.0 + gate * (1.0 - sigmoid))).astype(LOW)
        grad_side[:, others] = (grad_act * silu).astype(LOW)

    @pl.when(step >= tiles)
    def _():
        chunk = step - tiles
        at = e * tiles + chunk
        spot = lax.rem(at, 2)
        columns = pl.ds(pl.multiple_of(chunk * wide, 128), wide)

        @pl.when(at >= 2)
        def _():
            for copy in leaving(at - 2): copy.wait()
        total = jnp.dot(turned[columns, :], grad_side[...], preferred_element_type=FULL)
        side_buf[spot] = total.astype(LOW).reshape(side_buf.shape[1:])
        leaving(at)[0].start()
        total = jnp.dot(turned_act[...], dy_ref[0, :, columns], preferred_element_type=FULL)
        down_buf[spot] = total.astype(LOW).reshape(down_buf.shape[1:])
        leaving(at)[1].start()
        back_ref[0, :, columns] = across_cols(grad_side[...], side_w[slot, columns, :]).astype(LOW)
        out_ref[0, :, columns] = jnp.dot(act[...], down_w[slot, :, columns], preferred_element_type=FULL).astype(LOW)

        @pl.when(at == count * tiles - 1)
        def _():
            for copy in leaving(at - 1) + leaving(at): copy.wait()

def expert(first, count, dp_count, x_rows, dy_rows, scales, w_gate_up, w_down, tiles=4):
    _, slots, width = x_rows.shape
    hidden = w_down.shape[1]
    high, low = width // dp_count, hidden // dp_count
    wide = width // tiles
    part = max(1, wide // high)
    rs = pl.BlockSpec((1, slots, width), lambda e, f: (first + e, 0, 0))
    os = pl.BlockSpec((1, slots, width), lambda e, f: (e, 0, 0))
    sems = pltpu.SemaphoreType.DMA
    return pl.pallas_call(
        functools.partial(expert_kernel, first, count, tiles),
        out_shape=[jax.ShapeDtypeStruct((dp_count, count * (high + low), width), LOW),
                   jax.ShapeDtypeStruct((count, slots, width), LOW), jax.ShapeDtypeStruct((count, slots, width), LOW),
                   jax.ShapeDtypeStruct((count, slots, 1), FULL)],
        grid=(count, 2 * tiles),
        in_specs=[rs, rs, pl.BlockSpec((1, slots, 1), lambda e, f: (first + e, 0, 0)), ANY, ANY],
        out_specs=[ANY, os, os, pl.BlockSpec((1, slots, 1), lambda e, f: (e, 0, 0))],
        scratch_shapes=[pltpu.VMEM((min(2, count), width, 2 * hidden), LOW), pltpu.VMEM((min(2, count), hidden, width), LOW),
                        pltpu.VMEM((width, slots), LOW), pltpu.VMEM((hidden, slots), LOW), pltpu.VMEM((slots, hidden), LOW), pltpu.VMEM((slots, 2 * hidden), LOW),
                        pltpu.VMEM((2, part, min(wide, high), 2 * hidden), LOW), pltpu.VMEM((2, dp_count, low, wide), LOW),
                        sems((min(2, count), tiles, 3)), sems((2, 2))],
        compiler_params=pltpu.CompilerParams(vmem_limit_bytes=62 << 20),
        cost_estimate=pl.CostEstimate(
            flops=18 * count * slots * width * hidden,
            transcendentals=count * slots * hidden,
            bytes_accessed=12 * count * width * hidden,
        ),
        name="expert",
    )(x_rows, dy_rows, scales, w_gate_up, w_down)


def rms_scale(values):
    return lax.rsqrt(jnp.mean(values * values, axis=-1, keepdims=True) + NORM_EPS)


def rotary_tables(length, size):
    index = np.arange(size // 2, dtype=np.float32)
    frequency = np.exp(index * np.float32(-2.0 * math.log(10000.0) / size))
    angles = np.arange(length, dtype=np.float32)[:, None] * frequency[None, :]
    cosine, sine = np.cos(angles), np.sin(angles)
    halves = [np.concatenate([cosine, cosine], axis=1), np.concatenate([-sine, sine], axis=1)]
    return jnp.asarray(np.stack(halves).astype(np.float32))


def norm_back(grad_normed, normed, scale_rows):
    return scale_rows * (
        grad_normed - normed * jnp.mean(grad_normed * normed, axis=-1, keepdims=True)
    )


def contract_rows(left_side, right_side):
    return lax.dot_general(
        left_side, right_side, (((0,), (0,)), ((), ())), preferred_element_type=FULL
    )


def contract_cols(left_side, right_side):
    return lax.dot_general(
        left_side, right_side, (((1,), (1,)), ((), ())), preferred_element_type=FULL
    )


def einsum(spec, left_side, right_side):
    return jnp.einsum(spec, left_side, right_side, preferred_element_type=FULL)


def widen_kernel(steps, *refs):
    low_ref, high_ref, down_ref = refs[0], refs[-2], refs[-1]
    step = pl.program_id(1)

    @pl.when(step < steps)
    def _():
        high_ref[...] = low_ref[...].astype(FULL)

    @pl.when(step >= steps)
    def _():
        down_ref[...] = low_ref[...].astype(FULL)


def widen(first, total, high, grads, held=()):
    count, both, width = grads.shape
    low = both - high
    rows = low // 2
    steps = high // rows
    block = (1, rows, width)
    return pl.pallas_call(
        functools.partial(widen_kernel, steps),
        out_shape=[
            jax.ShapeDtypeStruct((total, high, width), FULL),
            jax.ShapeDtypeStruct((total, low, width), FULL),
        ],
        grid=(count, steps + 2),
        in_specs=[pl.BlockSpec(block, lambda e, r: (e, r, 0))] + [ANY] * len(held),
        out_specs=[
            pl.BlockSpec(block, lambda e, r: (first + e, jnp.minimum(r, steps - 1), 0)),
            pl.BlockSpec(block, lambda e, r: (first + e, jnp.maximum(r - steps, 0), 0)),
        ],
        input_output_aliases={1: 0, 2: 1} if held else {},
        cost_estimate=pl.CostEstimate(
            flops=grads.size, transcendentals=0, bytes_accessed=6 * grads.size
        ),
        name="widen",
    )(grads, *held)


def turn(values, cosine, sine):
    return values * cosine + pltpu.roll(values, values.shape[1] // 2, 1) * sine


def allowed_pairs(column, row):
    shape = (column.shape[0], row.shape[1])
    later = lax.broadcasted_iota(jnp.int32, shape, 0) >= lax.broadcasted_iota(jnp.int32, shape, 1)
    return later & (column == row)


def softmax(query, key, allowed):
    scores = across_cols(query, key) * (1.0 / math.sqrt(query.shape[1]))
    scores = jnp.where(allowed, scores, -1e30)
    powers = jnp.exp(scores - jnp.max(scores, axis=-1, keepdims=True))
    return powers / jnp.sum(powers, axis=-1, keepdims=True)


def attend_block(heads, block, rows_ref, scales, gain_ref, turn_ref, column, row, kept_ref, out_ref):
    width = out_ref.shape[2]
    size = width // heads
    allowed = allowed_pairs(column, row)
    cosine, sine = turn_ref[0], turn_ref[1]
    for h in range(heads):
        parts = []
        for part in range(3):
            columns = pl.ds(part * width + h * size, size)
            values = rows_ref[block, :, columns]
            if part < 2:
                values = values * scales[part]
                values = values * gain_ref[part : part + 1, h * size : (h + 1) * size]
                values = turn(values, cosine, sine)
            parts.append(values.astype(LOW))
            kept_ref[block, :, columns] = parts[-1]
        query, key, value = parts
        probs = softmax(query, key, allowed).astype(LOW)
        out_ref[block, :, pl.ds(h * size, size)] = jnp.dot(
            probs, value, preferred_element_type=FULL
        ).astype(LOW)


def attention_kernel(size, dp_count, heads, *refs):
    x_ref, w_ref, gain_ref, gains_ref, turn_ref, column_ref, row_ref, sheet_ref, dy_ref = refs[:9]
    h_out, rows_out, scale_ref, root_ref, kept_ref, out_ref, own_out, sheet_out, dy_out = refs[9:18]
    x_held, h_held, rows, sums, squares, got = refs[18:24]
    x_sem, h_sem, rows_sem, send_sem, recv_sem, stay_sem = refs[24:30]
    square_sems, line_sems, sheet_sems = refs[30:33], refs[33:38], refs[38:]
    line = LineGather(size // 2, 4, [dy_ref], [dy_out], *line_sems)
    sheets = Sheets(size, dp_count, sheet_ref, sheet_out, *sheet_sems)
    small = Exchange("expert", size, (True,), (1,), [squares], [got], *square_sems)
    place, model_dim = sheets.place, x_ref.shape[2]
    width = out_ref.shape[2]

    def loading(g):
        return pltpu.make_async_copy(x_ref.at[g], x_held.at[g], x_sem.at[g])

    def leaving(g):
        return (
            pltpu.make_async_copy(h_held.at[g], h_out.at[g], h_sem.at[g]),
            pltpu.make_async_copy(rows.at[g], rows_out.at[g], rows_sem.at[g]),
        )

    for g in range(size):
        loading(g).start()
    greet("expert", [(peer, None) for peer in small.peers])
    greet("dp", [(peer, None) for peer in sheets.peers])
    pl.semaphore_wait(pltpu.get_barrier_semaphore(), size + dp_count - 2)
    sheets.begin()
    line.begin()
    sums[...] = jnp.zeros_like(sums)
    lanes = lax.broadcasted_iota(jnp.int32, sums.shape, 1)

    @pl.loop(0, size)
    def _(g):
        loading(g).wait()
        values = x_held[g].astype(FULL)
        root = rms_scale(values)
        root_ref[g] = root
        hidden = (values * root * gain_ref[...]).astype(LOW)
        h_held[g] = hidden
        projected = jnp.dot(hidden, w_ref[...], preferred_element_type=FULL)
        rows[g] = projected
        for copy in leaving(g):
            copy.start()
        for part in range(2):
            half = projected[:, part * width : (part + 1) * width]
            total = jnp.sum(half * half, axis=-1, keepdims=True)
            sums[...] += jnp.where(lanes == part * size + g, total, 0.0)
        pl.when(g >= size // 2)(lambda: line.turn(g - size // 2))
        pl.when(g == size // 2)(lambda: sheets.forward(1))

    squares[...] = sums[...].T[: 2 * size]
    small.begin()
    small.arrive()
    total = sum(got[i] for i in range(size))
    sums[:, : 2 * size] = lax.rsqrt(total / model_dim + NORM_EPS).T

    def sending(g, source):
        columns = pl.ds(pl.multiple_of(source * width, 128), width)
        target = own_out.at[:, columns]
        return remote(out_ref.at[g], target, send_sem.at[g], recv_sem.at[source], {"expert": g})

    own_columns = pl.ds(pl.multiple_of(place * width, 128), width)
    staying = pltpu.make_async_copy(out_ref.at[place], own_out.at[:, own_columns], stay_sem.at[0])

    @pl.loop(0, size)
    def _(i):
        g = lax.rem(place + 1 + i, size)
        scales = [
            jnp.sum(jnp.where(lanes == part * size + g, sums[...], 0.0), axis=-1, keepdims=True)
            for part in range(2)
        ]
        scale_ref[g] = jnp.concatenate(scales, axis=1)
        attend_block(
            heads, g, rows, scales, gains_ref, turn_ref, column_ref[g], row_ref[g], kept_ref, out_ref
        )
        pl.when(g != place)(lambda: sending(g, place).start())
        pl.when(i >= size // 2)(lambda: line.turn(i))
        pl.when(i == size // 2)(lambda: sheets.forward(2))

    staying.start()

    @pl.loop(size, 2 * size)
    def _(i):
        line.turn(i)
        for step in range(3, size // 2):
            pl.when(i == size)(lambda: sheets.forward(step))
        after = i - size - size // 2
        pl.when((after >= 0) & (after < size // 2))(lambda: sheets.cross(after))


    @pl.loop(1, size)
    def _(i):
        peer = lax.rem(place + i, size)
        sending(peer, peer).wait_recv()
        sending(peer, place).wait_send()

    @pl.loop(0, size)
    def _(g):
        for copy in leaving(g):
            copy.wait()

    staying.wait()
    small.finish()
    line.finish()
    sheets.finish()


def attention(size, dp_count, heads, arrays, number):
    x_all, w_here, sheet, dy = arrays[0], arrays[1], arrays[7], arrays[8]
    _, tokens, model_dim = x_all.shape
    columns = w_here.shape[1]
    width = columns // 3
    sems = pltpu.SemaphoreType.DMA
    seqs = (size, tokens)
    small = (2 * size, tokens)
    return pl.pallas_call(
        functools.partial(attention_kernel, size, dp_count, heads),
        out_shape=[
            jax.ShapeDtypeStruct(x_all.shape, LOW),
            jax.ShapeDtypeStruct(seqs + (columns,), FULL),
            jax.ShapeDtypeStruct(seqs + (2,), FULL),
            jax.ShapeDtypeStruct(seqs + (1,), FULL),
            jax.ShapeDtypeStruct(seqs + (columns,), LOW),
            jax.ShapeDtypeStruct(seqs + (width,), LOW),
            jax.ShapeDtypeStruct((tokens, model_dim), LOW),
            jax.ShapeDtypeStruct((dp_count, size) + sheet.shape, LOW),
            jax.ShapeDtypeStruct((size,) + dy.shape, LOW),
        ],
        in_specs=[ANY] + [VMEM] * 6 + [ANY] * 2,
        out_specs=[ANY] * 2 + [VMEM] * 4 + [ANY] * 3,
        scratch_shapes=[
            pltpu.VMEM(x_all.shape, LOW),
            pltpu.VMEM(x_all.shape, LOW),
            pltpu.VMEM(seqs + (columns,), FULL),
            pltpu.VMEM((tokens, 128), FULL),
            pltpu.VMEM(small, FULL),
            pltpu.VMEM((size,) + small, FULL),
            sems((size,)),
            sems((size,)),
            sems((size,)),
            sems((size,)),
            sems((size,)),
            sems((1,)),
        ]
        + Exchange.scratch(size, (1,))
        + LineGather.scratch(size, 4, 1)
        + Sheets.scratch(size, dp_count),
        compiler_params=pltpu.CompilerParams(
            collective_id=number, has_side_effects=True, vmem_limit_bytes=48 << 20
        ),
        cost_estimate=pl.CostEstimate(
            flops=2 * x_all.size * columns, transcendentals=0, bytes_accessed=100_000_000
        ),
        name="attention",
    )(*arrays)


def attend_back_block(heads, block, grad_ref, refs, back_ref, dots_ref, lanes, gains_ref, w_sum):
    w_ref, kept_ref, out_ref, rows_ref, scale_ref, gain_ref, turn_ref, column_ref, row_ref = refs
    width = out_ref.shape[2]
    size = width // heads
    scaling = 1.0 / math.sqrt(size)
    allowed = allowed_pairs(column_ref[block], row_ref[block])
    cosine, sine = turn_ref[0], turn_ref[1]
    grad_rows = grad_ref[block]
    grad_out = across_cols(grad_rows, w_ref[...]).astype(LOW)
    w_sum[...] += contract_rows(out_ref[block], grad_rows)
    dots = [0.0, 0.0]
    for h in range(heads):
        mine = slice(h * size, (h + 1) * size)
        query, key, value = (
            kept_ref[block, :, pl.ds(p * width + h * size, size)] for p in range(3)
        )
        probs = softmax(query, key, allowed)
        grad = grad_out[:, mine]
        grad_value = contract_rows(probs.astype(LOW), grad)
        grad_probs = across_cols(grad, value)
        delta = jnp.sum(grad_probs * probs, axis=-1, keepdims=True)
        grad_scores = (probs * (grad_probs - delta)).astype(LOW)
        grad_query = jnp.dot(grad_scores, key, preferred_element_type=FULL) * scaling
        grad_key = contract_rows(grad_scores, query) * scaling
        for part, grad_turned in enumerate((grad_query, grad_key)):
            columns = pl.ds(part * width + h * size, size)
            grad_normed = turn(grad_turned, cosine, -sine)
            normed = rows_ref[block, :, columns] * scale_ref[block, :, part : part + 1]
            gains_ref[part : part + 1, mine] += jnp.sum(grad_normed * normed, axis=0, keepdims=True)
            weighted = grad_normed * gain_ref[part : part + 1, mine]
            dots[part] += jnp.sum(weighted * normed, axis=-1, keepdims=True)
            back_ref[block, :, columns] = weighted
        back_ref[block, :, pl.ds(2 * width + h * size, size)] = grad_value
    groups = grad_ref.shape[0]
    for part in range(2):
        dots_ref[...] += jnp.where(lanes == part * groups + block, dots[part], 0.0)


def attend_back_kernel(levels, cuts, heads, grad_ref, *refs):
    w_ref, others, refs = refs[0], refs[1:9], refs[9:]
    proj_ref, gains_ref, w_grad_ref, w_sum, held, w_held, back, dots, squares, got, w_sem = refs[:11]
    reads = (w_held,) + tuple(others)
    rows_ref, scale_ref = others[2:4]
    size, model_dim = 2 * levels, grad_ref.shape[1]
    line = LineGather(levels, cuts, [grad_ref], [held], *refs[11:16])
    small = Exchange("expert", size, (True,), (1,), [squares], [got], *refs[16:])
    mine = pl.ds(pl.multiple_of(line.place * w_held.shape[0], 128), w_held.shape[0])
    loading = pltpu.make_async_copy(w_ref.at[mine], w_held, w_sem.at[0])
    loading.start()
    greet("expert", [(peer, None) for peer in small.peers])
    pl.semaphore_wait(pltpu.get_barrier_semaphore(), size - 1)
    line.begin()
    w_sum[...] = jnp.zeros_like(w_sum)
    gains_ref[...] = jnp.zeros_like(gains_ref)
    dots[...] = jnp.zeros_like(dots)
    lanes = lax.broadcasted_iota(jnp.int32, dots.shape, 1)
    loading.wait()
    line.staying(0).wait()

    def landed(block):
        attend_back_block(heads, block, held, reads, back, dots, lanes, gains_ref, w_sum)

    line.main(landed)
    squares[...] = dots[...].T[: 2 * size]
    small.begin()
    wide = w_grad_ref.shape[2]
    for copy in range(w_grad_ref.shape[0]):
        w_grad_ref[copy] = w_sum[:, copy * wide : (copy + 1) * wide].astype(LOW)
    small.arrive()
    dots[:, : 2 * size] = sum(got[i] for i in range(size)).T / model_dim
    width = w_held.shape[0]

    @pl.loop(0, size)
    def _(block):
        for part in range(2):
            columns = pl.ds(part * width, width)
            scale = scale_ref[block, :, part : part + 1]
            mean = jnp.where(lanes == part * size + block, dots[...], 0.0)
            mean = jnp.sum(mean, axis=-1, keepdims=True)
            normed = rows_ref[block, :, columns] * scale
            proj_ref[block, :, columns] = (scale * (back[block, :, columns] - normed * mean)).astype(LOW)
        columns = pl.ds(2 * width, width)
        proj_ref[block, :, columns] = back[block, :, columns].astype(LOW)

    line.finish(held=1)
    small.finish()


def attend_back(size, dp_count, heads, grad, arrays, number):
    _, _, out, rows = arrays[:4]
    width = out.shape[2]
    tokens, model_dim = grad.shape
    small = (2 * size, tokens)
    return pl.pallas_call(
        functools.partial(attend_back_kernel, size // 2, 4, heads),
        out_shape=[
            jax.ShapeDtypeStruct(rows.shape, LOW),
            jax.ShapeDtypeStruct((2, width), FULL),
            jax.ShapeDtypeStruct((dp_count, width, model_dim // dp_count), LOW),
        ],
        in_specs=[ANY] * 2 + [VMEM] * (len(arrays) - 1),
        out_specs=[VMEM] * 3,
        scratch_shapes=[
            pltpu.VMEM((width, model_dim), FULL),
            pltpu.VMEM((size, tokens, model_dim), LOW),
            pltpu.VMEM((width, model_dim), LOW),
            pltpu.VMEM(rows.shape, FULL),
            pltpu.VMEM((tokens, 128), FULL),
            pltpu.VMEM(small, FULL),
            pltpu.VMEM((size,) + small, FULL),
            pltpu.SemaphoreType.DMA((1,)),
        ]
        + LineGather.scratch(size, 4, 1)
        + Exchange.scratch(size, (1,)),
        compiler_params=pltpu.CompilerParams(
            collective_id=number, has_side_effects=True, vmem_limit_bytes=48 << 20
        ),
        cost_estimate=pl.CostEstimate(flops=0, transcendentals=0, bytes_accessed=150_000_000),
        name="attend_back",
    )(grad, *arrays)


def on_device(
    dp_count,
    line_count,
    layer_input,
    out_cotangent,
    segments,
    routes,
    w_qkv,
    w_out,
    w_router,
    attn_gain,
    mlp_gain,
    query_gain,
    key_gain,
    w_gate_up,
    w_down,
):
    row_count, model_dim = layer_input.shape
    top_count = routes.shape[1]
    expert_count = w_router.shape[1]
    local_count = w_gate_up.shape[0]
    head_size = model_dim // HEADS
    head_cols = model_dim // line_count
    heads_here = head_cols // head_size
    capacity = (row_count * top_count * 9 // 8 + expert_count - 1) // expert_count
    scaling = 1.0 / math.sqrt(head_size)
    place = lax.axis_index("expert")
    shard = w_qkv.shape[0]

    numbers = jnp.concatenate([routes.T, segments, jnp.zeros((7, row_count), jnp.int32)], axis=0)
    x_all, numbers_all, qkv_here, router_full, gains = opening(
        line_count,
        dp_count,
        [layer_input, numbers],
        4,
        w_qkv,
        [w_router, jnp.stack([attn_gain, mlp_gain, query_gain, key_gain])],
        1,
    )
    qkv_here = qkv_here.reshape(model_dim, 3 * head_cols)
    router_full = router_full.reshape(model_dim, expert_count)
    gains = gains.transpose(2, 0, 1, 3).reshape(4, model_dim).astype(FULL)
    gain_attn, gain_mlp = gains[0], gains[1]
    both_gains = lax.dynamic_slice_in_dim(gains[2:], place * head_cols, head_cols, axis=1)

    routes_all = numbers_all[:, :top_count]
    segments_all = numbers_all[:, top_count]
    turns = rotary_tables(row_count, head_size)
    column, row = segments_all[:, :, None], segments_all[:, None, :]
    arrays = [x_all, qkv_here, gain_attn[None], both_gains, turns, column, row, w_out, out_cotangent]
    hidden_one, projected, scales, roots, kept, attended, own_attended, out_full, dy_all = attention(
        line_count, dp_count, heads_here, arrays, 4
    )
    out_full = out_full.reshape(model_dim, model_dim)
    inputs = layer_input.astype(FULL)
    scale_attn = rms_scale(inputs)
    normed_attn = inputs * scale_attn
    residual = inputs + jnp.dot(own_attended, out_full, preferred_element_type=FULL)
    scale_mlp = rms_scale(residual)
    normed_mlp = residual * scale_mlp
    hidden_two = (normed_mlp * gain_mlp).astype(LOW)

    logits = jnp.dot(hidden_two, router_full, preferred_element_type=FULL)
    chosen = jnp.any(routes[:, :, None] == jnp.arange(expert_count)[None, None, :], axis=1)
    masked = jnp.where(chosen, logits, -1e30)
    powers = jnp.where(chosen, jnp.exp(masked - jnp.max(masked, axis=-1, keepdims=True)), 0.0)
    gates = powers / jnp.sum(powers, axis=-1, keepdims=True)

    local = place * local_count + jnp.arange(local_count)
    used = jnp.any(routes_all[:, None] == local[None, :, None, None], axis=2)
    position = jnp.arange(row_count)
    lower = (position[:, None] < position[None, :]).astype(LOW)
    rank = einsum("gju,ut->gjt", used.astype(LOW), lower).astype(jnp.int32)
    rank = jnp.where(used, rank, -1)
    spots = jnp.arange(capacity)
    table = (rank[:, :, None, :] == spots[None, None, :, None]).astype(LOW)
    returns = [(rank[:, j, :, None] == spots[None, None, :]).astype(LOW) for j in range(local_count)]
    slots = line_count * capacity
    flat_table = table.reshape(line_count, local_count * capacity, row_count)
    expert_rows, dy_rows, gates_all = gather_place(
        line_count, hidden_two, gates.T, flat_table, dy_all, local_count, 6
    )
    local_gates = lax.dynamic_slice_in_dim(gates_all, place * local_count, local_count, axis=1)
    slot_gates = jnp.sum(table.astype(FULL) * local_gates[:, :, None, :], axis=-1)
    slot_gates = slot_gates.transpose(1, 0, 2).reshape(local_count, slots, 1)
    out_rows, back_rows, slot_grads, grad_sums = [], [], [], []
    both_rows = model_dim // dp_count + w_down.shape[1] // dp_count
    for first, count in ((0, 1), (1, local_count - 1)):
        grads, out_row, back_row, dots = expert(
            first, count, dp_count, expert_rows, dy_rows, slot_gates, w_gate_up, w_down
        )
        grads = grads.reshape(-1, model_dim)
        grads = lax.psum_scatter(grads, "dp", scatter_dimension=0, tiled=True)
        grad_sums.append(grads.reshape(count, both_rows, model_dim))
        for kept_list, rows in ((out_rows, out_row), (back_rows, back_row), (slot_grads, dots)):
            kept_list.append(rows.reshape(count, line_count, capacity, rows.shape[2]))
    gate_rows = model_dim // dp_count
    grad_two, grad_gates = collect_reduce(
        line_count, returns, back_rows, slot_grads, flat_table, 8
    )
    grad_gates = grad_gates.reshape(expert_count, row_count).T
    grad_two = grad_two.astype(FULL)

    grad_out_rows = out_cotangent.astype(FULL)
    grad_logits = gates * (grad_gates - jnp.sum(gates * grad_gates, axis=-1, keepdims=True))
    grad_logits = grad_logits.astype(LOW)
    grad_router = contract_rows(grad_logits, hidden_two)
    grad_two = grad_two + contract_cols(grad_logits, router_full)
    grad_gain_mlp = jnp.sum(grad_two * normed_mlp, axis=0)
    grad_resid = grad_out_rows + norm_back(grad_two * gain_mlp, normed_mlp, scale_mlp)
    grad_attn = grad_resid.astype(LOW)

    arrays = [out_full, kept, attended, projected, scales, both_gains, turns, column, row]
    grad_proj, gain_pair, out_parts = attend_back(
        line_count, dp_count, heads_here, grad_attn, arrays, 11
    )

    shared = jnp.concatenate([grad_router, grad_gain_mlp[None]], axis=0)
    tall = shared.shape[0] + -shared.shape[0] % 8
    shared = jnp.pad(shared, ((0, tall - shared.shape[0]), (0, 0)))
    shared = shared.reshape(tall, dp_count, line_count, shard).transpose(2, 1, 0, 3)
    shared = shared.reshape(line_count, dp_count * tall, shard)
    shared = jnp.pad(shared, ((0, 0), (0, 0), (0, 128 - shard)))
    arrays = [grad_proj, qkv_here, hidden_one, gain_attn[None]]
    grad_one, mixture, sum_qkv, sum_out, gain_pair, gain_sum, shared = closing(
        line_count, dp_count, returns, out_rows, arrays, [out_parts, gain_pair], shared, 14
    )
    here = (lax.axis_index("dp") * line_count + place) * shard
    grad_gain_attn = lax.dynamic_slice_in_dim(gain_sum[0], here, shard)
    output = (residual + mixture.astype(FULL)).astype(LOW)
    sum_qkv = sum_qkv.transpose(1, 0, 2)
    first_sums, output = lax.optimization_barrier((grad_sums[0], output))
    wide = widen(0, local_count, gate_rows, first_sums)
    sum_gate_up, sum_down = widen(1, local_count, gate_rows, grad_sums[1], wide)
    shared = shared[:, :shard]
    grad_one = grad_one.astype(FULL)
    grad_inputs = grad_resid + norm_back(grad_one * gain_attn, normed_attn, scale_attn)
    return (
        output,
        grad_inputs,
        sum_qkv,
        sum_out,
        shared[:expert_count].T,
        grad_gain_attn,
        shared[expert_count],
        gain_pair[0],
        gain_pair[1],
        sum_gate_up,
        sum_down,
    )


def solution(mesh):
    both = ("dp", "expert")
    rows, flat = P(both, None), P(both)
    placed = (rows,) * 7 + (flat,) * 4 + (P("expert", None, None),) * 2
    return jax.shard_map(
        functools.partial(on_device, mesh.shape["dp"], mesh.shape["expert"]),
        mesh=mesh,
        in_specs=placed,
        out_specs=(
            rows,
            rows,
            P("dp", None, "expert"),
            P("expert", "dp"),
            rows,
            flat,
            flat,
            P("expert"),
            P("expert"),
            P("expert", "dp", None),
            P("expert", "dp", None),
        ),
        check_vma=False,
    )
```

```python
import functools
import math

import jax
import jax.numpy as jnp
import numpy as np
from jax import lax
from jax.experimental import pallas as pl
from jax.experimental.pallas import tpu as pltpu
from jax.sharding import PartitionSpec as P

HEADS = 16
NORM_EPS = 1e-05
MESH = pl.DeviceIdType.MESH
ANY = pl.BlockSpec(memory_space=pl.ANY)
LOW = jnp.bfloat16
FULL = jnp.float32


def line_place():
    place = lax.axis_index("expert")
    level, side = lax.div(place, 2), lax.rem(place, 2)
    return place, level, side, place + 1 - 2 * side


def greet(axis, targets):
    barrier = pltpu.get_barrier_semaphore()
    for target, there in targets:

        def signal(target=target):
            pl.semaphore_signal(barrier, inc=1, device_id={axis: target}, device_id_type=MESH)

        if there is None:
            signal()
        else:
            pl.when(there)(signal)


def line_barrier(levels):
    place, level, _, other = line_place()
    has_up, has_down = level < levels - 1, level > 0
    greet("expert", [(other, None), (place + 2, has_up), (place - 2, has_down)])
    count = 1 + has_up.astype(jnp.int32) + has_down.astype(jnp.int32)
    pl.semaphore_wait(pltpu.get_barrier_semaphore(), count)


def around(axis, size):
    place = lax.axis_index(axis)
    return [lax.rem(place + shift, size) for shift in range(1, size)]


def remote(source, target, send, recv, device):
    return pltpu.make_async_remote_copy(
        src_ref=source,
        dst_ref=target,
        send_sem=send,
        recv_sem=recv,
        device_id=device,
        device_id_type=MESH,
    )


class LineGather:
    def __init__(self, levels, cuts, ins, outs, up_sem, down_sem, side_sem, recv_sem, own_sem):
        self.levels, self.cuts, self.ins, self.outs = levels, cuts, ins, outs
        self.up_sem, self.down_sem, self.side_sem = up_sem, down_sem, side_sem
        self.recv_sem, self.own_sem = recv_sem, own_sem
        self.place, self.level, self.side, self.other = line_place()
        self.has_up, self.has_down = self.level < levels - 1, self.level > 0

    @staticmethod
    def scratch(size, cuts, count):
        levels, total = size // 2, cuts + count - 1
        shapes = ((levels, total), (levels, total), (2 * levels - 1, total), (size, total))
        return [pltpu.SemaphoreType.DMA(shape) for shape in shapes + ((count,),)]

    def pieces(self):
        return [(0, k) for k in range(self.cuts)] + [(i, 0) for i in range(1, len(self.ins))]

    def staying(self, i):
        target = self.outs[i].at[self.place]
        return pltpu.make_async_copy(self.ins[i], target, self.own_sem.at[i])

    def sending(self, piece, block, own, sem, target):
        i, k = piece
        landing, source, q = self.outs[i].at[block], self.ins[i], k
        if i:
            q = self.cuts + i - 1
        else:
            rows = source.shape[0] // self.cuts
            landing, source = landing.at[pl.ds(k * rows, rows)], source.at[pl.ds(k * rows, rows)]
        sems = sem.at[q], self.recv_sem.at[block, q]
        return remote(source if own else landing, landing, *sems, {"expert": target})

    def up(self, piece, step, own=False):
        block = self.place - 2 * step
        return self.sending(piece, block, own, self.up_sem.at[step], self.place + 2)

    def down(self, piece, step, own=False):
        block = self.place + 2 * step
        return self.sending(piece, block, own, self.down_sem.at[step], self.place - 2)

    def across(self, piece, step, own=False):
        sem = self.side_sem.at[step + self.levels - 1]
        return self.sending(piece, self.place - 2 * step, own, sem, self.other)

    def begin(self):
        for piece in self.pieces():
            pl.when(self.has_up)(self.up(piece, 0, True).start)
            pl.when(self.has_down)(self.down(piece, 0, True).start)
        for piece in self.pieces():
            self.across(piece, 0, True).start()
        for i in range(len(self.ins)):
            self.staying(i).start()

    def forward(self, step, piece):
        @pl.when(self.level >= step)
        def _():
            self.across(piece, step).wait_recv()
            pl.when(self.has_up)(self.up(piece, step).start)
            self.across(piece, step).start()

        @pl.when(self.level + step < self.levels)
        def _():
            self.across(piece, -step).wait_recv()
            pl.when(self.has_down)(self.down(piece, step).start)
            self.across(piece, -step).start()

    def land_across(self, block):
        for piece in self.pieces():
            self.sending(piece, block, False, self.side_sem.at[0], self.other).wait_recv()

    def turn(self, turn, landed=None):
        levels, cuts = self.levels, self.cuts
        step, k = lax.div(turn, cuts) + 1, lax.rem(turn, cuts)

        @pl.when(step < levels)
        def _():
            self.forward(step, (0, k))

            @pl.when(k == cuts - 1)
            def _():
                for i in range(1, len(self.ins)):
                    self.forward(step, (i, 0))

        group, sign, crossed = step - 1, 2 * lax.rem(k, 2) - 1, lax.div(k, 2)
        crossed = jnp.where(group == 0, k, crossed)
        far = jnp.where(group == 0, self.level, self.level + sign * group)

        @pl.when((far >= 0) & (far < levels) & (k < 4) & ((group > 0) | (k < 2)))
        def _():
            block = 2 * far + self.side + crossed * (1 - 2 * self.side)

            @pl.when(crossed == 1)
            def _():
                self.land_across(block)

            if landed:
                landed(block)

    def main(self, landed=None):
        @pl.loop(0, self.levels * self.cuts)
        def _(turn):
            self.turn(turn, landed)

    def finish(self, held=0):
        for piece in self.pieces():
            self.across(piece, 0).wait_send()
            for step in range(self.levels):
                above, below = self.level >= step, self.level + step < self.levels
                pl.when(self.has_up & above)(self.up(piece, step).wait_send)
                pl.when(self.has_down & below)(self.down(piece, step).wait_send)
                if step:
                    pl.when(above)(self.across(piece, step).wait_send)
                    pl.when(below)(self.across(piece, -step).wait_send)
        for i in range(held, len(self.ins)):
            self.staying(i).wait()


def call(kernel, name, number, outs, scratch, arrays, moved):
    return pl.pallas_call(
        kernel,
        out_shape=outs,
        in_specs=[ANY] * len(arrays),
        out_specs=[ANY] * len(outs),
        scratch_shapes=scratch,
        compiler_params=pltpu.CompilerParams(
            collective_id=number, has_side_effects=True, vmem_limit_bytes=48 << 20
        ),
        cost_estimate=pl.CostEstimate(flops=0, transcendentals=0, bytes_accessed=moved),
        name=name,
    )(*arrays)


class LineReduce:
    def __init__(self, levels, cuts, parts, total, own, beside, rising, falling, *sems):
        self.levels, self.cuts, self.parts, self.total = levels, cuts, parts, total
        self.made = parts.shape[0] == levels
        self.own, self.beside, self.rising, self.falling = own, beside, rising, falling
        self.load_sem, self.side_send, self.side_recv = sems[:3]
        self.up_send, self.up_recv, self.down_send, self.down_recv, self.out_sem = sems[3:]
        self.place, self.level, self.side, self.other = line_place()
        self.has_up, self.has_down = self.level < levels - 1, self.level > 0
        self.rows = parts.shape[1] // cuts

    @staticmethod
    def scratch(size, block, dtype, cuts):
        levels = size // 2
        return (
            [pltpu.VMEM((levels,) + block, dtype)] * 2
            + [pltpu.VMEM((levels - 1,) + block, dtype)] * 2
            + [pltpu.SemaphoreType.DMA((levels, cuts))] * 7
            + [pltpu.SemaphoreType.DMA((cuts,))]
        )

    def cut(self, ref, block, k):
        return ref.at[block, pl.ds(k * self.rows, self.rows)]

    def loading(self, far, k):
        source = self.cut(self.parts, 2 * far + self.side, k)
        return pltpu.make_async_copy(source, self.cut(self.own, far, k), self.load_sem.at[far, k])

    def across(self, far, k):
        source = self.cut(self.parts, far if self.made else 2 * far + 1 - self.side, k)
        sems = self.side_send.at[far, k], self.side_recv.at[far, k]
        return remote(source, self.cut(self.beside, far, k), *sems, {"expert": self.other})

    def up(self, far, k):
        sems = self.up_send.at[far, k], self.up_recv.at[far, k]
        target = {"expert": self.place + 2}
        return remote(self.cut(self.own, far, k), self.cut(self.rising, far - 1, k), *sems, target)

    def down(self, far, k):
        sems = self.down_send.at[far, k], self.down_recv.at[far, k]
        target = {"expert": self.place - 2}
        return remote(self.cut(self.own, far, k), self.cut(self.falling, far, k), *sems, target)

    def value(self, ref, block, k):
        return self.cut(ref, block, k)[...].astype(FULL)

    def load(self):
        for i in range(self.levels):
            for k in range(self.cuts):
                self.loading(self.far(i), k).start()

    def begin(self):
        for i in range(self.levels):
            for k in range(self.cuts):
                self.across(self.far(i), k).start()

    def far(self, i):
        return jnp.where(lax.rem(i, 2) == 0, self.levels - 1 - lax.div(i, 2), lax.div(i, 2))

    def prepare(self, turn, make):
        far = self.far(lax.div(turn, 2))

        @pl.when(lax.rem(turn, 2) == 0)
        def _():
            make(2 * far + 1 - self.side, self.parts.at[far])
            for k in range(self.cuts):
                self.across(far, k).start()

        @pl.when(lax.rem(turn, 2) == 1)
        def _():
            make(2 * far + self.side, self.own.at[far])

    def pair(self, far, k):
        if not self.made:
            self.loading(far, k).wait()
        self.across(far, k).wait_recv()
        return self.value(self.own, far, k) + self.value(self.beside, far, k)

    def store(self, far, k, total):
        self.cut(self.own, far, k)[...] = total.astype(self.own.dtype)

    def toward(self, far, k, ahead, behind, move, arrived, shift):
        @pl.when(ahead & behind)
        def _():
            both = self.pair(far, k)
            move(far, k).wait_recv()
            self.store(far, k, both + self.value(arrived, far - shift, k))

        @pl.when(ahead & jnp.logical_not(behind))
        def _():
            self.store(far, k, self.pair(far, k))

        pl.when(ahead)(move(far, k).start)

    def main(self, beside=None):
        @pl.loop(0, (self.levels - 1) * self.cuts)
        def _(turn):
            step, k = lax.div(turn, self.cuts), lax.rem(turn, self.cuts)
            high, low = self.levels - 1 - step, step
            if beside:
                beside(turn)
            self.toward(high, k, self.level < high, self.has_down, self.up, self.rising, 1)
            self.toward(low, k, self.level > low, self.has_up, self.down, self.falling, 0)

        @pl.loop(0, self.cuts)
        def _(k):
            self.store(self.level, k, self.pair(self.level, k))
            for there, move, arrived, shift in (
                (self.has_down, self.up, self.rising, 1),
                (self.has_up, self.down, self.falling, 0),
            ):

                @pl.when(there)
                def _():
                    move(self.level, k).wait_recv()
                    total = self.value(self.own, self.level, k)
                    total += self.value(arrived, self.level - shift, k)
                    self.store(self.level, k, total)

            self.leaving(k).start()

    def leaving(self, k):
        target = self.total.at[pl.ds(k * self.rows, self.rows)]
        return pltpu.make_async_copy(self.cut(self.own, self.level, k), target, self.out_sem.at[k])

    def finish(self):
        for k in range(self.cuts):
            self.leaving(k).wait()
            for far in range(self.levels):
                self.across(far, k).wait_send()
                pl.when(self.level < far)(self.up(far, k).wait_send)
                pl.when(self.level > far)(self.down(far, k).wait_send)


class Exchange:
    def __init__(self, axis, size, spread, cuts, ins, outs, send_sem, recv_sem, own_sem):
        self.axis, self.spread, self.ins, self.outs = axis, spread, ins, outs
        self.send_sem, self.recv_sem, self.own_sem = send_sem, recv_sem, own_sem
        self.cuts = cuts
        self.firsts = [sum(cuts[:i]) for i in range(len(cuts))]
        self.pieces = [(i, k) for i in range(len(cuts)) for k in range(cuts[i])]
        self.place, self.peers = lax.axis_index(axis), around(axis, size)

    @staticmethod
    def scratch(size, cuts):
        sems = pltpu.SemaphoreType.DMA
        return [sems((sum(cuts), size)), sems((sum(cuts), size)), sems((len(cuts),))]

    def source(self, i, block):
        return self.ins[i] if self.spread[i] else self.ins[i].at[block]

    def staying(self, i):
        target = self.outs[i].at[self.place]
        return pltpu.make_async_copy(self.source(i, self.place), target, self.own_sem.at[i])

    def sending(self, i, k, shift, landing):
        peer = self.peers[shift]
        source, target, q = self.source(i, peer), self.outs[i].at[landing], self.firsts[i] + k
        if self.cuts[i] > 1:
            rows = target.shape[0] // self.cuts[i]
            source, target = source.at[pl.ds(k * rows, rows)], target.at[pl.ds(k * rows, rows)]
        sems = self.send_sem.at[q, shift], self.recv_sem.at[q, landing]
        return remote(source, target, *sems, {self.axis: peer})

    def send(self, i, k):
        for shift in range(len(self.peers)):
            self.sending(i, k, shift, self.place).start()

    def stay(self):
        for i in range(len(self.spread)):
            self.staying(i).start()

    def begin(self):
        for i, k in self.pieces:
            self.send(i, k)
        self.stay()

    def land(self):
        for shift, peer in enumerate(self.peers):
            for i, k in self.pieces:
                self.sending(i, k, shift, peer).wait_recv()

    def arrive(self):
        self.land()
        for i in range(len(self.spread)):
            self.staying(i).wait()

    def finish(self):
        for shift in range(len(self.peers)):
            for i, k in self.pieces:
                self.sending(i, k, shift, self.place).wait_send()


def exchange_kernel(axis, size, spread, *refs):
    count = len(spread)
    ins, outs, sems = refs[:count], refs[count : 2 * count], refs[2 * count :]
    moves = Exchange(axis, size, spread, (1,) * count, ins, outs, *sems)
    greet(axis, [(peer, None) for peer in moves.peers])
    pl.semaphore_wait(pltpu.get_barrier_semaphore(), size - 1)
    moves.begin()
    moves.arrive()
    moves.finish()


def exchange_outs(size, arrays, spread):
    return [
        jax.ShapeDtypeStruct((size,) + a.shape if flat else a.shape, a.dtype)
        for a, flat in zip(arrays, spread)
    ]


def exchange(axis, size, arrays, spread, number):
    return call(
        functools.partial(exchange_kernel, axis, size, tuple(spread)),
        "exchange_" + axis,
        number,
        exchange_outs(size, arrays, spread),
        Exchange.scratch(size, (1,) * len(arrays)),
        arrays,
        30_000_000,
    )


def opening_kernel(size, dp_count, count, cuts, *refs):
    ins, (w_ref, *small_refs) = refs[:count], refs[count : count + 3]
    outs, rest = refs[count + 3 : 2 * count + 3], refs[2 * count + 6 :]
    w_out, *small_outs = refs[2 * count + 3 : 2 * count + 6]
    line = LineGather(size // 2, cuts, ins, outs, *rest[:5])
    send_sem, recv_sem, own_sem = rest[5:8]
    place, mine = line.place, lax.axis_index("dp")
    peers = around("expert", size)
    width = w_out.shape[3] // 3
    lands = [w_out] + small_outs
    across = Exchange(
        "dp", dp_count, (True,) * 3, (size,) * 3, [a.at[mine] for a in lands], lands, *rest[8:]
    )
    greet("expert", [(peer, None) for peer in peers])
    greet("dp", [(peer, None) for peer in across.peers])
    pl.semaphore_wait(pltpu.get_barrier_semaphore(), size + dp_count - 2)

    def ends(peer, landing, j):
        if j >= 3:
            return small_refs[j - 3], small_outs[j - 3].at[mine, landing]
        start = pl.multiple_of(j * width * size + peer * width, 128)
        target = w_out.at[mine, landing, :, pl.ds(j * width, width)]
        return w_ref.at[:, pl.ds(start, width)], target

    def sending(shift, landing, j):
        source, target = ends(peers[shift], landing, j)
        sems = send_sem.at[shift, j], recv_sem.at[landing, j]
        return remote(source, target, *sems, {"expert": peers[shift]})

    own = [pltpu.make_async_copy(*ends(place, place, j), own_sem.at[j]) for j in range(5)]
    for shift in range(size - 1):
        for j in range(5):
            sending(shift, place, j).start()
    for copy in own:
        copy.start()
    line.begin()
    for copy in own:
        copy.wait()
    for i in range(3):
        across.send(i, place)
    for shift, peer in enumerate(peers):
        for j in range(5):
            sending(shift, peer, j).wait_recv()
        for i in range(3):
            across.send(i, peer)
    line.main()
    line.finish()
    for shift in range(size - 1):
        for j in range(5):
            sending(shift, place, j).wait_send()
    across.land()
    across.finish()


def opening(size, dp_count, arrays, cuts, weights, small, number):
    sems = pltpu.SemaphoreType.DMA
    outs = [jax.ShapeDtypeStruct((size,) + a.shape, a.dtype) for a in arrays]
    rows, columns = weights.shape
    whole = (dp_count, size, rows)
    outs.append(jax.ShapeDtypeStruct(whole + (columns // size,), weights.dtype))
    outs += [jax.ShapeDtypeStruct((dp_count, size) + a.shape, a.dtype) for a in small]
    return call(
        functools.partial(opening_kernel, size, dp_count, len(arrays), cuts),
        "opening",
        number,
        outs,
        LineGather.scratch(size, cuts, len(arrays))
        + [sems((size, 5)), sems((size, 5)), sems((5,))]
        + Exchange.scratch(dp_count, (size,) * 3),
        list(arrays) + [weights] + small,
        200_000_000,
    )


class Sheets:
    def __init__(self, size, dp_count, source, target, *sems):
        self.levels, self.dp_count, self.ins, self.out = size // 2, dp_count, source, target
        self.up_send, self.down_send, self.line_recv, self.dp_send, self.dp_recv = sems[:5]
        self.side_send, self.side_recv, self.own_sem = sems[5:]
        self.place, self.level, self.side, self.other = line_place()
        self.has_up, self.has_down = self.level < self.levels - 1, self.level > 0
        self.mine, self.peers = lax.axis_index("dp"), around("dp", dp_count)

    @staticmethod
    def scratch(size, dp_count):
        sems, levels = pltpu.SemaphoreType.DMA, size // 2
        return [sems((levels,))] * 3 + [sems((dp_count, levels))] * 4 + [sems((1,))]

    def along(self, far, own, send, target):
        landing = self.out.at[self.mine, 2 * far + self.side]
        source = self.ins if own else landing
        return remote(source, landing, send.at[far], self.line_recv.at[far], {"expert": target})

    def up(self, far, own=False):
        return self.along(far, own, self.up_send, self.place + 2)

    def down(self, far, own=False):
        return self.along(far, own, self.down_send, self.place - 2)

    def over(self, far, shift, copy, own=False):
        landing = self.out.at[copy, 2 * far + self.side]
        source = self.ins if own else landing
        sems = self.dp_send.at[shift, far], self.dp_recv.at[copy, far]
        return remote(source, landing, *sems, {"dp": self.peers[shift]})

    def across(self, far, copy, whose, own=False):
        landing = self.out.at[copy, 2 * far + whose]
        source = self.ins if own else landing
        sems = self.side_send.at[copy, far], self.side_recv.at[copy, far]
        return remote(source, landing, *sems, {"expert": self.other})

    def spread(self, far, own=False):
        for shift in range(self.dp_count - 1):
            self.over(far, shift, self.mine, own).start()
        self.across(far, self.mine, self.side, own).start()

    def staying(self):
        target = self.out.at[self.mine, self.place]
        return pltpu.make_async_copy(self.ins, target, self.own_sem.at[0])

    def begin(self):
        pl.when(self.has_up)(self.up(self.level, True).start)
        pl.when(self.has_down)(self.down(self.level, True).start)
        self.spread(self.level, True)
        self.staying().start()

    def forward(self, step):
        @pl.when(self.level >= step)
        def _():
            self.up(self.level - step).wait_recv()
            pl.when(self.has_up)(self.up(self.level - step).start)
            self.spread(self.level - step)

        @pl.when(self.level + step < self.levels)
        def _():
            self.down(self.level + step).wait_recv()
            pl.when(self.has_down)(self.down(self.level + step).start)
            self.spread(self.level + step)

    def cross(self, far):
        for shift, peer in enumerate(self.peers):
            self.over(far, shift, peer).wait_recv()
            self.across(far, peer, self.side).start()

    def finish(self):
        @pl.loop(0, self.levels)
        def _(far):
            pl.when(self.has_up & (self.level >= far))(self.up(far).wait_send)
            pl.when(self.has_down & (self.level <= far))(self.down(far).wait_send)
            for shift in range(self.dp_count - 1):
                self.over(far, shift, self.mine).wait_send()
            for copy in range(self.dp_count):
                self.across(far, copy, 1 - self.side).wait_recv()
                self.across(far, copy, self.side).wait_send()

        self.staying().wait()


VMEM = pl.BlockSpec(memory_space=pltpu.VMEM)
COLUMNS = 512


def gather_place_kernel(levels, cuts, *refs):
    rows_ref, gates_ref, table_ref, dy_ref, x_out, dy_out, gates_out = refs[:7]
    held, dy_held, x_stage, dy_stage = refs[7:11]
    line_sems, (dy_sem, x_sems, dy_sems) = refs[11:16], refs[16:]
    line = LineGather(levels, cuts, [rows_ref, gates_ref], [held, gates_out], *line_sems)
    size, width = 2 * levels, held.shape[2]
    _, local_count, capacity, _ = x_stage.shape

    def leaving(block, stage, out, sems):
        target = out.at[:, pl.ds(pl.multiple_of(block * capacity, 8), capacity)]
        return pltpu.make_async_copy(stage.at[block], target, sems.at[block])

    def place(block, rows, stage, out, sems):
        table = table_ref[block]

        @pl.loop(0, width // COLUMNS)
        def _(n):
            columns = pl.ds(pl.multiple_of(n * COLUMNS, COLUMNS), COLUMNS)
            placed = jnp.dot(table, rows[block, :, columns], preferred_element_type=FULL)
            for j in range(local_count):
                part = placed[j * capacity : (j + 1) * capacity]
                stage[block, j, :, columns] = part.astype(stage.dtype)

        leaving(block, stage, out, sems).start()

    def place_x(block):
        place(block, held, x_stage, x_out, x_sems)

    loading = pltpu.make_async_copy(dy_ref, dy_held, dy_sem.at[0])
    loading.start()
    line_barrier(levels)
    line.begin()
    loading.wait()

    @pl.loop(0, size)
    def _(block):
        place(block, dy_held, dy_stage, dy_out, dy_sems)

    line.staying(0).wait()
    line.main(place_x)
    line.finish(held=1)

    @pl.loop(0, size)
    def _(block):
        leaving(block, x_stage, x_out, x_sems).wait()
        leaving(block, dy_stage, dy_out, dy_sems).wait()


def gather_place(size, rows, gates, table, dy, local_count, number):
    cuts = 4
    tokens, width = rows.shape
    capacity = table.shape[1] // local_count
    placed = jax.ShapeDtypeStruct((local_count, size * capacity, width), rows.dtype)
    sems = pltpu.SemaphoreType.DMA
    return pl.pallas_call(
        functools.partial(gather_place_kernel, size // 2, cuts),
        out_shape=[placed, placed, jax.ShapeDtypeStruct((size,) + gates.shape, gates.dtype)],
        in_specs=[ANY, ANY, VMEM, ANY],
        out_specs=[ANY] * 3,
        scratch_shapes=[pltpu.VMEM((size, tokens, width), rows.dtype)] * 2
        + [pltpu.VMEM((size, local_count, capacity, width), rows.dtype)] * 2
        + LineGather.scratch(size, cuts, 2)
        + [sems((1,)), sems((size,)), sems((size,))],
        compiler_params=pltpu.CompilerParams(
            collective_id=number, has_side_effects=True, vmem_limit_bytes=48 << 20
        ),
        cost_estimate=pl.CostEstimate(
            flops=4 * table.size * width, transcendentals=0, bytes_accessed=150_000_000
        ),
        name="gather_place",
    )(rows, gates, table, dy)


def split_at(arrays, j, block):
    for array in arrays:
        if j < array.shape[0]:
            return array.at[j, block]
        j -= array.shape[0]


def collect_block(tables, slots, block, target):
    @pl.loop(0, target.shape[1] // COLUMNS)
    def _(n):
        columns = pl.ds(pl.multiple_of(n * COLUMNS, COLUMNS), COLUMNS)
        total = 0.0
        for j, table in enumerate(tables):
            rows = split_at(slots, j, block)[:, columns]
            total += jnp.dot(table[block], rows, preferred_element_type=FULL)
        target[:, columns] = total.astype(target.dtype)


def collect_reduce_kernel(levels, cuts, local_count, *refs):
    tables, refs = refs[:local_count], refs[local_count:]
    slots, dots, (table_ref, total_ref, gates_out, away) = refs[:2], refs[2:4], refs[4:8]
    rest, (gates, *sems) = refs[8:20], refs[20:]
    line = LineReduce(levels, cuts, away, total_ref, *rest)
    small = Exchange("expert", 2 * levels, (False,), (1,), [gates], [gates_out], *sems)
    greet("expert", [(peer, None) for peer in small.peers])
    pl.semaphore_wait(pltpu.get_barrier_semaphore(), 2 * levels - 1)
    make = functools.partial(collect_block, tables, slots)

    @pl.loop(0, 4)
    def _(turn):
        line.prepare(turn, make)

    def gate_block(block):
        table = table_ref[block].astype(FULL)
        capacity = table.shape[0] // local_count
        for j in range(local_count):
            part = table[j * capacity : (j + 1) * capacity] * split_at(dots, j, block)[...]
            gates[block, j : j + 1] = jnp.sum(part, axis=0, keepdims=True)

    def beside(turn):
        pl.when(turn + 4 < 2 * levels)(lambda: line.prepare(turn + 4, make))
        pl.when(turn >= levels)(lambda: gate_block(turn - levels))
        pl.when(turn == 3 * levels - 1)(small.begin)

    line.main(beside)
    small.arrive()
    line.finish()
    small.finish()


def collect_reduce(size, tables, slots, dots, table, number):
    levels, cuts = size // 2, 4
    block = (tables[0].shape[1], slots[0].shape[3])
    kind = slots[0].dtype
    gates = (size, len(tables), block[0])
    return pl.pallas_call(
        functools.partial(collect_reduce_kernel, levels, cuts, len(tables)),
        out_shape=[jax.ShapeDtypeStruct(block, kind), jax.ShapeDtypeStruct(gates, FULL)],
        in_specs=[VMEM] * (len(tables) + 5),
        out_specs=[ANY, ANY],
        scratch_shapes=[pltpu.VMEM((levels,) + block, kind)]
        + LineReduce.scratch(size, block, kind, cuts)
        + [pltpu.VMEM(gates, FULL)]
        + Exchange.scratch(size, (1,)),
        compiler_params=pltpu.CompilerParams(
            collective_id=number, has_side_effects=True, vmem_limit_bytes=48 << 20
        ),
        cost_estimate=pl.CostEstimate(flops=0, transcendentals=0, bytes_accessed=150_000_000),
        name="collect_reduce",
    )(*tables, *slots, *dots, table)


def closing_kernel(size, dp_count, local_count, cuts, sum_cuts, *refs):
    refs, levels = list(refs), size // 2

    def take(count):
        taken = refs[:count]
        del refs[:count]
        return taken

    tables, slots = take(local_count), take(2)
    proj_ref, w_ref, h_ref, gain_ref, out_parts, gain_pair, shared_ref = take(7)
    back_out, mixed_out, qkv_out, w_out, gains_out, gain_out, shared_out = take(7)
    back = LineReduce(levels, cuts, *take(1), back_out, *take(12))
    mixed = LineReduce(levels, cuts, *take(1), mixed_out, *take(12))
    qkv_parts, qkv_got, out_got, gains_got = take(4)
    got, half, last, gain_sum, gain_got, gain_half, gain_last = take(7)
    parts, lands = [qkv_parts, out_parts, gain_pair], [qkv_got, out_got, gains_got]
    sums = Exchange("dp", dp_count, (False, False, True), sum_cuts, parts, lands, *take(3))
    first = Exchange("expert", size, (False,), (1,), [shared_ref], [got], *take(3))
    second = Exchange("dp", dp_count, (False,), (1,), [half], [last], *take(3))
    gain_first = Exchange("expert", size, (True,), (1,), [gain_sum], [gain_got], *take(3))
    gain_second = Exchange("dp", dp_count, (True,), (1,), [gain_half], [gain_last], *take(3))
    greet("expert", [(peer, None) for peer in first.peers])
    greet("dp", [(peer, None) for peer in sums.peers])
    pl.semaphore_wait(pltpu.get_barrier_semaphore(), size + dp_count - 2)
    first.begin()
    sums.staying(1).start()
    sums.staying(2).start()
    gain_sum[...] = jnp.zeros_like(gain_sum)
    groups, tokens, model_dim = h_ref.shape
    tall, high = half.shape[1], model_dim // dp_count

    def make_back(block, target):
        @pl.loop(0, model_dim // COLUMNS)
        def _(n):
            columns = pl.ds(pl.multiple_of(n * COLUMNS, COLUMNS), COLUMNS)
            grad = across_cols(proj_ref[block], w_ref[columns, :])
            target[:, columns] = grad.astype(target.dtype)
            weighted = grad * h_ref[block, :, columns].astype(FULL)
            gain_sum[:, columns] += jnp.sum(weighted, axis=0, keepdims=True)

    def piece(turn):
        k, copy = lax.div(turn, dp_count), lax.rem(turn, dp_count)
        columns = pl.ds(pl.multiple_of(copy * high + k * 128, 128), 128)
        rows = h_ref[:, :, columns].reshape(groups * tokens, 128)
        grads = proj_ref[...].reshape(groups * tokens, proj_ref.shape[2])
        products = contract_rows(rows, grads).astype(LOW)
        qkv_parts[copy, pl.ds(pl.multiple_of(k * 128, 128), 128)] = products
        pl.when(copy == dp_count - 1)(lambda: sums.send(0, k))
        pl.when(turn == sum_cuts[0] * dp_count - 1)(lambda: sums.staying(0).start())

    make_mixed = functools.partial(collect_block, tables, slots)
    ahead = levels

    @pl.loop(0, ahead)
    def _(turn):
        back.prepare(turn, make_back)

    def beside(turn):
        later = turn - ahead
        pl.when(turn + ahead < 2 * levels)(lambda: back.prepare(turn + ahead, make_back))
        pl.when(turn < sum_cuts[1])(lambda: sums.send(1, turn))
        pl.when(turn == sum_cuts[1])(lambda: sums.send(2, 0))
        pl.when(later == 0)(gain_first.begin)
        pl.when((later >= 0) & (later < 2 * levels))(lambda: mixed.prepare(later, make_mixed))
        pl.when(later >= 0)(lambda: piece(later))

        @pl.when(later == ahead)
        def _():
            first.arrive()
            for copy in range(dp_count):
                rows = pl.ds(copy * tall, tall)
                half[copy] = sum(got[i, rows, :] for i in range(size))
            second.begin()
            gain_first.arrive()
            gain_half[...] = sum(gain_got[i] for i in range(size))
            gain_second.begin()

    back.main(beside)
    mixed.main(lambda turn: pl.when(turn < 2 * levels)(lambda: piece(2 * levels + turn)))
    second.arrive()
    shared_out[...] = sum(last[i] for i in range(dp_count))
    gain_second.arrive()
    gain_out[...] = sum(gain_last[i] for i in range(dp_count)) / gain_ref[...]
    sums.arrive()
    wide = qkv_out.shape[2]
    for j in range(3):
        columns = slice(j * wide, (j + 1) * wide)
        qkv_out[j] = sum(qkv_got[copy, :, columns].astype(FULL) for copy in range(dp_count))
    w_out[...] = sum(out_got[copy].astype(FULL) for copy in range(dp_count))
    gains_out[...] = sum(gains_got[copy] for copy in range(dp_count))
    for moves in (back, mixed, first, second, sums, gain_first, gain_second):
        moves.finish()


def closing(size, dp_count, tables, slots, arrays, sums, shared, number):
    proj, _, hidden, gain = arrays
    levels, cuts = size // 2, 4
    _, tokens, model_dim = hidden.shape
    columns, high = proj.shape[2], model_dim // dp_count
    block = (tokens, model_dim)
    tall = shared.shape[1] // dp_count
    wide = shared.shape[2]
    sum_cuts = (high // 128, 2, 1)
    out, pair = exchange_outs(dp_count, sums, (False, True))
    shapes = [(3, high, columns // 3), out.shape[1:], pair.shape[1:], gain.shape, (tall, wide)]
    outs = [jax.ShapeDtypeStruct(block, LOW)] * 2
    outs += [jax.ShapeDtypeStruct(shape, FULL) for shape in shapes]
    line = [pltpu.VMEM((levels,) + block, LOW)] + LineReduce.scratch(size, block, LOW, cuts)
    return pl.pallas_call(
        functools.partial(closing_kernel, size, dp_count, len(tables), cuts, sum_cuts),
        out_shape=outs,
        in_specs=[VMEM] * (len(tables) + 6) + [ANY] * 3,
        out_specs=[ANY] * 2 + [VMEM] * 5,
        scratch_shapes=line
        + line
        + [pltpu.VMEM((dp_count, high, columns), LOW)] * 2
        + [pltpu.VMEM(a.shape, a.dtype) for a in (out, pair)]
        + [pltpu.VMEM((size,) + shared.shape[1:], FULL)]
        + [pltpu.VMEM((dp_count, tall, wide), FULL)] * 2
        + [
            pltpu.VMEM(gain.shape, FULL),
            pltpu.VMEM((size,) + gain.shape, FULL),
            pltpu.VMEM(gain.shape, FULL),
            pltpu.VMEM((dp_count,) + gain.shape, FULL),
        ]
        + Exchange.scratch(dp_count, sum_cuts)
        + Exchange.scratch(size, (1,))
        + Exchange.scratch(dp_count, (1,))
        + Exchange.scratch(size, (1,))
        + Exchange.scratch(dp_count, (1,)),
        compiler_params=pltpu.CompilerParams(
            collective_id=number, has_side_effects=True, vmem_limit_bytes=62 << 20
        ),
        cost_estimate=pl.CostEstimate(flops=0, transcendentals=0, bytes_accessed=200_000_000),
        name="closing",
    )(*tables, *slots, *arrays, *sums, shared)


def across_cols(left_side, right_side):
    return lax.dot_general(
        left_side, right_side, (((1,), (1,)), ((), ())), preferred_element_type=FULL
    )


def expert_kernel(first, count, tiles, x_ref, dy_ref, scale_ref, side_ref, down_ref, grads_ref, out_ref, back_ref, dots_ref,
                  side_w, down_w, turned, turned_act, act, grad_side, side_buf, down_buf, w_sems, sems):
    e, step = pl.program_id(0), pl.program_id(1)
    slot = lax.rem(e, 2)
    hidden, model = down_w.shape[1], down_w.shape[2]
    width, wide = hidden // tiles, model // tiles
    copies = grads_ref.shape[0]
    high, low = model // copies, hidden // copies
    part = side_buf.shape[1]

    def loads(e, tile):
        slot = lax.rem(e, 2)
        out = []
        for half in range(2):
            columns = pl.ds(pl.multiple_of(half * hidden + tile * width, 128), width)
            out.append(pltpu.make_async_copy(side_ref.at[first + e, :, columns], side_w.at[slot, :, columns], w_sems.at[slot, tile, half]))
        rows = pl.ds(pl.multiple_of(tile * width, 128), width)
        out.append(pltpu.make_async_copy(down_ref.at[first + e, rows], down_w.at[slot, rows], w_sems.at[slot, tile, 2]))
        return out

    def leaving(at):
        e, chunk = lax.div(at, tiles), lax.rem(at, tiles)
        slot = lax.rem(at, 2)
        base = e * (high + low)
        columns = pl.ds(pl.multiple_of(chunk * wide, 128), wide)
        if wide >= high:
            target = grads_ref.at[pl.ds(chunk * part, part), pl.ds(base, high)]
        else:
            target = grads_ref.at[pl.ds(lax.div(chunk * wide, high), 1), pl.ds(base + lax.rem(chunk * wide, high), wide)]
        return (pltpu.make_async_copy(side_buf.at[slot], target, sems.at[slot, 0]),
                pltpu.make_async_copy(down_buf.at[slot], grads_ref.at[:, pl.ds(base + high, low), columns], sems.at[slot, 1]))

    @pl.when((e == 0) & (step == 0))
    def _():
        for tile in range(tiles):
            for copy in loads(e, tile): copy.start()

    @pl.when((e + 1 < count) & (step == 0))
    def _():
        for tile in range(tiles):
            for copy in loads(e + 1, tile): copy.start()

    @pl.when(step == 0)
    def _():
        turned[...] = x_ref[0].T
        dots_ref[...] = jnp.zeros_like(dots_ref)

    @pl.when(step < tiles)
    def _():
        for copy in loads(e, step): copy.wait()
        rows, grads, scale = x_ref[0], dy_ref[0], scale_ref[0]
        columns = pl.ds(pl.multiple_of(step * width, 128), width)
        others = pl.ds(pl.multiple_of(hidden + step * width, 128), width)
        gate = jnp.dot(rows, side_w[slot, :, columns], preferred_element_type=FULL)
        up = jnp.dot(rows, side_w[slot, :, others], preferred_element_type=FULL)
        grad_act = across_cols(grads, down_w[slot, columns, :])
        sigmoid = jax.nn.sigmoid(gate)
        silu = gate * sigmoid
        raw = silu * up
        dots_ref[0] += jnp.sum(raw * grad_act, axis=-1, keepdims=True)
        weighted = (scale * raw).astype(LOW)
        act[:, columns] = weighted
        turned_act[columns, :] = weighted.T
        grad_act = grad_act * scale
        grad_side[:, columns] = (grad_act * up * sigmoid * (1.0 + gate * (1.0 - sigmoid))).astype(LOW)
        grad_side[:, others] = (grad_act * silu).astype(LOW)

    @pl.when(step >= tiles)
    def _():
        chunk = step - tiles
        at = e * tiles + chunk
        spot = lax.rem(at, 2)
        columns = pl.ds(pl.multiple_of(chunk * wide, 128), wide)

        @pl.when(at >= 2)
        def _():
            for copy in leaving(at - 2): copy.wait()
        total = jnp.dot(turned[columns, :], grad_side[...], preferred_element_type=FULL)
        side_buf[spot] = total.astype(LOW).reshape(side_buf.shape[1:])
        leaving(at)[0].start()
        total = jnp.dot(turned_act[...], dy_ref[0, :, columns], preferred_element_type=FULL)
        down_buf[spot] = total.astype(LOW).reshape(down_buf.shape[1:])
        leaving(at)[1].start()
        back_ref[0, :, columns] = across_cols(grad_side[...], side_w[slot, columns, :]).astype(LOW)
        out_ref[0, :, columns] = jnp.dot(act[...], down_w[slot, :, columns], preferred_element_type=FULL).astype(LOW)

        @pl.when(at == count * tiles - 1)
        def _():
            for copy in leaving(at - 1) + leaving(at): copy.wait()

def expert(first, count, dp_count, x_rows, dy_rows, scales, w_gate_up, w_down, tiles=4):
    _, slots, width = x_rows.shape
    hidden = w_down.shape[1]
    high, low = width // dp_count, hidden // dp_count
    wide = width // tiles
    part = max(1, wide // high)
    rs = pl.BlockSpec((1, slots, width), lambda e, f: (first + e, 0, 0))
    os = pl.BlockSpec((1, slots, width), lambda e, f: (e, 0, 0))
    sems = pltpu.SemaphoreType.DMA
    return pl.pallas_call(
        functools.partial(expert_kernel, first, count, tiles),
        out_shape=[jax.ShapeDtypeStruct((dp_count, count * (high + low), width), LOW),
                   jax.ShapeDtypeStruct((count, slots, width), LOW), jax.ShapeDtypeStruct((count, slots, width), LOW),
                   jax.ShapeDtypeStruct((count, slots, 1), FULL)],
        grid=(count, 2 * tiles),
        in_specs=[rs, rs, pl.BlockSpec((1, slots, 1), lambda e, f: (first + e, 0, 0)), ANY, ANY],
        out_specs=[ANY, os, os, pl.BlockSpec((1, slots, 1), lambda e, f: (e, 0, 0))],
        scratch_shapes=[pltpu.VMEM((min(2, count), width, 2 * hidden), LOW), pltpu.VMEM((min(2, count), hidden, width), LOW),
                        pltpu.VMEM((width, slots), LOW), pltpu.VMEM((hidden, slots), LOW), pltpu.VMEM((slots, hidden), LOW), pltpu.VMEM((slots, 2 * hidden), LOW),
                        pltpu.VMEM((2, part, min(wide, high), 2 * hidden), LOW), pltpu.VMEM((2, dp_count, low, wide), LOW),
                        sems((min(2, count), tiles, 3)), sems((2, 2))],
        compiler_params=pltpu.CompilerParams(vmem_limit_bytes=62 << 20),
        cost_estimate=pl.CostEstimate(
            flops=18 * count * slots * width * hidden,
            transcendentals=count * slots * hidden,
            bytes_accessed=12 * count * width * hidden,
        ),
        name="expert",
    )(x_rows, dy_rows, scales, w_gate_up, w_down)


def rms_scale(values):
    return lax.rsqrt(jnp.mean(values * values, axis=-1, keepdims=True) + NORM_EPS)


def rotary_tables(length, size):
    index = np.arange(size // 2, dtype=np.float32)
    frequency = np.exp(index * np.float32(-2.0 * math.log(10000.0) / size))
    angles = np.arange(length, dtype=np.float32)[:, None] * frequency[None, :]
    cosine, sine = np.cos(angles), np.sin(angles)
    halves = [np.concatenate([cosine, cosine], axis=1), np.concatenate([-sine, sine], axis=1)]
    return jnp.asarray(np.stack(halves).astype(np.float32))


def norm_back(grad_normed, normed, scale_rows):
    return scale_rows * (
        grad_normed - normed * jnp.mean(grad_normed * normed, axis=-1, keepdims=True)
    )


def contract_rows(left_side, right_side):
    return lax.dot_general(
        left_side, right_side, (((0,), (0,)), ((), ())), preferred_element_type=FULL
    )


def contract_cols(left_side, right_side):
    return lax.dot_general(
        left_side, right_side, (((1,), (1,)), ((), ())), preferred_element_type=FULL
    )


def einsum(spec, left_side, right_side):
    return jnp.einsum(spec, left_side, right_side, preferred_element_type=FULL)


def widen_kernel(steps, *refs):
    low_ref, high_ref, down_ref = refs[0], refs[-2], refs[-1]
    step = pl.program_id(1)

    @pl.when(step < steps)
    def _():
        high_ref[...] = low_ref[...].astype(FULL)

    @pl.when(step >= steps)
    def _():
        down_ref[...] = low_ref[...].astype(FULL)


def widen(first, total, high, grads, held=()):
    count, both, width = grads.shape
    low = both - high
    rows = low
    steps = high // rows
    block = (1, rows, width)
    return pl.pallas_call(
        functools.partial(widen_kernel, steps),
        out_shape=[
            jax.ShapeDtypeStruct((total, high, width), FULL),
            jax.ShapeDtypeStruct((total, low, width), FULL),
        ],
        grid=(count, steps + 1),
        in_specs=[pl.BlockSpec(block, lambda e, r: (e, r, 0))] + [ANY] * len(held),
        out_specs=[
            pl.BlockSpec(block, lambda e, r: (first + e, jnp.minimum(r, steps - 1), 0)),
            pl.BlockSpec(block, lambda e, r: (first + e, jnp.maximum(r - steps, 0), 0)),
        ],
        input_output_aliases={1: 0, 2: 1} if held else {},
        cost_estimate=pl.CostEstimate(
            flops=grads.size, transcendentals=0, bytes_accessed=6 * grads.size
        ),
        name="widen",
    )(grads, *held)


def turn(values, cosine, sine):
    return values * cosine + pltpu.roll(values, values.shape[1] // 2, 1) * sine


def allowed_pairs(column, row):
    shape = (column.shape[0], row.shape[1])
    later = lax.broadcasted_iota(jnp.int32, shape, 0) >= lax.broadcasted_iota(jnp.int32, shape, 1)
    return later & (column == row)


def softmax(query, key, allowed):
    scores = across_cols(query, key) * (1.0 / math.sqrt(query.shape[1]))
    scores = jnp.where(allowed, scores, -1e30)
    powers = jnp.exp(scores - jnp.max(scores, axis=-1, keepdims=True))
    return powers / jnp.sum(powers, axis=-1, keepdims=True)


def attend_block(heads, block, rows_ref, scales, gain_ref, turn_ref, column, row, kept_ref, out_ref):
    width = out_ref.shape[2]
    size = width // heads
    allowed = allowed_pairs(column, row)
    cosine, sine = turn_ref[0], turn_ref[1]
    for h in range(heads):
        parts = []
        for part in range(3):
            columns = pl.ds(part * width + h * size, size)
            values = rows_ref[block, :, columns]
            if part < 2:
                values = values * scales[part]
                values = values * gain_ref[part : part + 1, h * size : (h + 1) * size]
                values = turn(values, cosine, sine)
            parts.append(values.astype(LOW))
            kept_ref[block, :, columns] = parts[-1]
        query, key, value = parts
        probs = softmax(query, key, allowed).astype(LOW)
        out_ref[block, :, pl.ds(h * size, size)] = jnp.dot(
            probs, value, preferred_element_type=FULL
        ).astype(LOW)


def attention_kernel(size, dp_count, heads, *refs):
    x_ref, w_ref, gain_ref, gains_ref, turn_ref, column_ref, row_ref, sheet_ref, dy_ref = refs[:9]
    h_out, rows_out, scale_ref, kept_ref, out_ref, own_out, sheet_out, dy_out = refs[9:17]
    x_held, h_held, rows, sums, squares, got = refs[17:23]
    x_sem, h_sem, rows_sem, send_sem, recv_sem, stay_sem = refs[23:29]
    square_sems, line_sems, sheet_sems = refs[29:32], refs[32:37], refs[37:]
    line = LineGather(size // 2, 4, [dy_ref], [dy_out], *line_sems)
    sheets = Sheets(size, dp_count, sheet_ref, sheet_out, *sheet_sems)
    small = Exchange("expert", size, (True,), (1,), [squares], [got], *square_sems)
    place, model_dim = sheets.place, x_ref.shape[2]
    width = out_ref.shape[2]

    def loading(g):
        return pltpu.make_async_copy(x_ref.at[g], x_held.at[g], x_sem.at[g])

    def leaving(g):
        return (
            pltpu.make_async_copy(h_held.at[g], h_out.at[g], h_sem.at[g]),
            pltpu.make_async_copy(rows.at[g], rows_out.at[g], rows_sem.at[g]),
        )

    for g in range(size):
        loading(g).start()
    greet("expert", [(peer, None) for peer in small.peers])
    greet("dp", [(peer, None) for peer in sheets.peers])
    pl.semaphore_wait(pltpu.get_barrier_semaphore(), size + dp_count - 2)
    sheets.begin()
    line.begin()
    sums[...] = jnp.zeros_like(sums)
    lanes = lax.broadcasted_iota(jnp.int32, sums.shape, 1)

    @pl.loop(0, size)
    def _(g):
        loading(g).wait()
        values = x_held[g].astype(FULL)
        hidden = (values * rms_scale(values) * gain_ref[...]).astype(LOW)
        h_held[g] = hidden
        projected = jnp.dot(hidden, w_ref[...], preferred_element_type=FULL)
        rows[g] = projected
        for copy in leaving(g):
            copy.start()
        for part in range(2):
            half = projected[:, part * width : (part + 1) * width]
            total = jnp.sum(half * half, axis=-1, keepdims=True)
            sums[...] += jnp.where(lanes == part * size + g, total, 0.0)

    squares[...] = sums[...].T[: 2 * size]
    small.begin()
    sheets.forward(1)
    small.arrive()
    total = sum(got[i] for i in range(size))
    sums[:, : 2 * size] = lax.rsqrt(total / model_dim + NORM_EPS).T

    def sending(g, source):
        columns = pl.ds(pl.multiple_of(source * width, 128), width)
        target = own_out.at[:, columns]
        return remote(out_ref.at[g], target, send_sem.at[g], recv_sem.at[source], {"expert": g})

    own_columns = pl.ds(pl.multiple_of(place * width, 128), width)
    staying = pltpu.make_async_copy(out_ref.at[place], own_out.at[:, own_columns], stay_sem.at[0])

    @pl.loop(0, size)
    def _(i):
        g = lax.rem(place + 1 + i, size)
        scales = [
            jnp.sum(jnp.where(lanes == part * size + g, sums[...], 0.0), axis=-1, keepdims=True)
            for part in range(2)
        ]
        scale_ref[g] = jnp.concatenate(scales, axis=1)
        attend_block(
            heads, g, rows, scales, gains_ref, turn_ref, column_ref[g], row_ref[g], kept_ref, out_ref
        )
        pl.when(g != place)(lambda: sending(g, place).start())
        pl.when(lax.rem(i, 2) == 1)(lambda: line.turn(lax.div(i, 2)))

    staying.start()

    @pl.loop(size // 2, 2 * size)
    def _(i):
        for step in range(2, size // 2):
            pl.when(i == (step - 1) * (size // 2))(lambda: sheets.forward(step))
        line.turn(i)
        after = i - size - size // 2
        pl.when((after >= 0) & (after < size // 2))(lambda: sheets.cross(after))


    @pl.loop(1, size)
    def _(i):
        peer = lax.rem(place + i, size)
        sending(peer, peer).wait_recv()
        sending(peer, place).wait_send()

    @pl.loop(0, size)
    def _(g):
        for copy in leaving(g):
            copy.wait()

    staying.wait()
    small.finish()
    line.finish()
    sheets.finish()


def attention(size, dp_count, heads, arrays, number):
    x_all, w_here, sheet, dy = arrays[0], arrays[1], arrays[7], arrays[8]
    _, tokens, model_dim = x_all.shape
    columns = w_here.shape[1]
    width = columns // 3
    sems = pltpu.SemaphoreType.DMA
    seqs = (size, tokens)
    small = (2 * size, tokens)
    return pl.pallas_call(
        functools.partial(attention_kernel, size, dp_count, heads),
        out_shape=[
            jax.ShapeDtypeStruct(x_all.shape, LOW),
            jax.ShapeDtypeStruct(seqs + (columns,), FULL),
            jax.ShapeDtypeStruct(seqs + (2,), FULL),
            jax.ShapeDtypeStruct(seqs + (columns,), LOW),
            jax.ShapeDtypeStruct(seqs + (width,), LOW),
            jax.ShapeDtypeStruct((tokens, model_dim), LOW),
            jax.ShapeDtypeStruct((dp_count, size) + sheet.shape, LOW),
            jax.ShapeDtypeStruct((size,) + dy.shape, LOW),
        ],
        in_specs=[ANY] + [VMEM] * 6 + [ANY] * 2,
        out_specs=[ANY] * 2 + [VMEM] * 3 + [ANY] * 3,
        scratch_shapes=[
            pltpu.VMEM(x_all.shape, LOW),
            pltpu.VMEM(x_all.shape, LOW),
            pltpu.VMEM(seqs + (columns,), FULL),
            pltpu.VMEM((tokens, 128), FULL),
            pltpu.VMEM(small, FULL),
            pltpu.VMEM((size,) + small, FULL),
            sems((size,)),
            sems((size,)),
            sems((size,)),
            sems((size,)),
            sems((size,)),
            sems((1,)),
        ]
        + Exchange.scratch(size, (1,))
        + LineGather.scratch(size, 4, 1)
        + Sheets.scratch(size, dp_count),
        compiler_params=pltpu.CompilerParams(
            collective_id=number, has_side_effects=True, vmem_limit_bytes=48 << 20
        ),
        cost_estimate=pl.CostEstimate(
            flops=2 * x_all.size * columns, transcendentals=0, bytes_accessed=100_000_000
        ),
        name="attention",
    )(*arrays)


def attend_back_block(heads, block, grad_ref, refs, back_ref, dots_ref, lanes, gains_ref, w_sum):
    w_ref, kept_ref, out_ref, rows_ref, scale_ref, gain_ref, turn_ref, column_ref, row_ref = refs
    width = out_ref.shape[2]
    size = width // heads
    scaling = 1.0 / math.sqrt(size)
    allowed = allowed_pairs(column_ref[block], row_ref[block])
    cosine, sine = turn_ref[0], turn_ref[1]
    grad_rows = grad_ref[block]
    grad_out = across_cols(grad_rows, w_ref[...]).astype(LOW)
    w_sum[...] += contract_rows(out_ref[block], grad_rows)
    dots = [0.0, 0.0]
    for h in range(heads):
        mine = slice(h * size, (h + 1) * size)
        query, key, value = (
            kept_ref[block, :, pl.ds(p * width + h * size, size)] for p in range(3)
        )
        probs = softmax(query, key, allowed)
        grad = grad_out[:, mine]
        grad_value = contract_rows(probs.astype(LOW), grad)
        grad_probs = across_cols(grad, value)
        delta = jnp.sum(grad_probs * probs, axis=-1, keepdims=True)
        grad_scores = (probs * (grad_probs - delta)).astype(LOW)
        grad_query = jnp.dot(grad_scores, key, preferred_element_type=FULL) * scaling
        grad_key = contract_rows(grad_scores, query) * scaling
        for part, grad_turned in enumerate((grad_query, grad_key)):
            columns = pl.ds(part * width + h * size, size)
            grad_normed = turn(grad_turned, cosine, -sine)
            normed = rows_ref[block, :, columns] * scale_ref[block, :, part : part + 1]
            gains_ref[part : part + 1, mine] += jnp.sum(grad_normed * normed, axis=0, keepdims=True)
            weighted = grad_normed * gain_ref[part : part + 1, mine]
            dots[part] += jnp.sum(weighted * normed, axis=-1, keepdims=True)
            back_ref[block, :, columns] = weighted
        back_ref[block, :, pl.ds(2 * width + h * size, size)] = grad_value
    groups = grad_ref.shape[0]
    for part in range(2):
        dots_ref[...] += jnp.where(lanes == part * groups + block, dots[part], 0.0)


def attend_back_kernel(levels, cuts, heads, grad_ref, *refs):
    w_ref, others, refs = refs[0], refs[1:9], refs[9:]
    proj_ref, gains_ref, w_grad_ref, w_sum, held, w_held, back, dots, squares, got, w_sem = refs[:11]
    reads = (w_held,) + tuple(others)
    rows_ref, scale_ref = others[2:4]
    size, model_dim = 2 * levels, grad_ref.shape[1]
    line = LineGather(levels, cuts, [grad_ref], [held], *refs[11:16])
    small = Exchange("expert", size, (True,), (1,), [squares], [got], *refs[16:])
    mine = pl.ds(pl.multiple_of(line.place * w_held.shape[0], 128), w_held.shape[0])
    loading = pltpu.make_async_copy(w_ref.at[mine], w_held, w_sem.at[0])
    loading.start()
    greet("expert", [(peer, None) for peer in small.peers])
    pl.semaphore_wait(pltpu.get_barrier_semaphore(), size - 1)
    line.begin()
    w_sum[...] = jnp.zeros_like(w_sum)
    gains_ref[...] = jnp.zeros_like(gains_ref)
    dots[...] = jnp.zeros_like(dots)
    lanes = lax.broadcasted_iota(jnp.int32, dots.shape, 1)
    loading.wait()
    line.staying(0).wait()

    def landed(block):
        attend_back_block(heads, block, held, reads, back, dots, lanes, gains_ref, w_sum)

    line.main(landed)
    squares[...] = dots[...].T[: 2 * size]
    small.begin()
    wide = w_grad_ref.shape[2]
    for copy in range(w_grad_ref.shape[0]):
        w_grad_ref[copy] = w_sum[:, copy * wide : (copy + 1) * wide].astype(LOW)
    small.arrive()
    dots[:, : 2 * size] = sum(got[i] for i in range(size)).T / model_dim
    width = w_held.shape[0]

    @pl.loop(0, size)
    def _(block):
        for part in range(2):
            columns = pl.ds(part * width, width)
            scale = scale_ref[block, :, part : part + 1]
            mean = jnp.where(lanes == part * size + block, dots[...], 0.0)
            mean = jnp.sum(mean, axis=-1, keepdims=True)
            normed = rows_ref[block, :, columns] * scale
            proj_ref[block, :, columns] = (scale * (back[block, :, columns] - normed * mean)).astype(LOW)
        columns = pl.ds(2 * width, width)
        proj_ref[block, :, columns] = back[block, :, columns].astype(LOW)

    line.finish(held=1)
    small.finish()


def attend_back(size, dp_count, heads, grad, arrays, number):
    _, _, out, rows = arrays[:4]
    width = out.shape[2]
    tokens, model_dim = grad.shape
    small = (2 * size, tokens)
    return pl.pallas_call(
        functools.partial(attend_back_kernel, size // 2, 4, heads),
        out_shape=[
            jax.ShapeDtypeStruct(rows.shape, LOW),
            jax.ShapeDtypeStruct((2, width), FULL),
            jax.ShapeDtypeStruct((dp_count, width, model_dim // dp_count), LOW),
        ],
        in_specs=[ANY] * 2 + [VMEM] * (len(arrays) - 1),
        out_specs=[VMEM] * 3,
        scratch_shapes=[
            pltpu.VMEM((width, model_dim), FULL),
            pltpu.VMEM((size, tokens, model_dim), LOW),
            pltpu.VMEM((width, model_dim), LOW),
            pltpu.VMEM(rows.shape, FULL),
            pltpu.VMEM((tokens, 128), FULL),
            pltpu.VMEM(small, FULL),
            pltpu.VMEM((size,) + small, FULL),
            pltpu.SemaphoreType.DMA((1,)),
        ]
        + LineGather.scratch(size, 4, 1)
        + Exchange.scratch(size, (1,)),
        compiler_params=pltpu.CompilerParams(
            collective_id=number, has_side_effects=True, vmem_limit_bytes=48 << 20
        ),
        cost_estimate=pl.CostEstimate(flops=0, transcendentals=0, bytes_accessed=150_000_000),
        name="attend_back",
    )(grad, *arrays)


def on_device(
    dp_count,
    line_count,
    layer_input,
    out_cotangent,
    segments,
    routes,
    w_qkv,
    w_out,
    w_router,
    attn_gain,
    mlp_gain,
    query_gain,
    key_gain,
    w_gate_up,
    w_down,
):
    row_count, model_dim = layer_input.shape
    top_count = routes.shape[1]
    expert_count = w_router.shape[1]
    local_count = w_gate_up.shape[0]
    head_size = model_dim // HEADS
    head_cols = model_dim // line_count
    heads_here = head_cols // head_size
    capacity = (row_count * top_count * 9 // 8 + expert_count - 1) // expert_count
    scaling = 1.0 / math.sqrt(head_size)
    place = lax.axis_index("expert")
    shard = w_qkv.shape[0]

    numbers = jnp.concatenate([routes.T, segments, jnp.zeros((7, row_count), jnp.int32)], axis=0)
    x_all, numbers_all, qkv_here, router_full, gains = opening(
        line_count,
        dp_count,
        [layer_input, numbers],
        4,
        w_qkv,
        [w_router, jnp.stack([attn_gain, mlp_gain, query_gain, key_gain])],
        1,
    )
    qkv_here = qkv_here.reshape(model_dim, 3 * head_cols)
    router_full = router_full.reshape(model_dim, expert_count)
    gains = gains.transpose(2, 0, 1, 3).reshape(4, model_dim).astype(FULL)
    gain_attn, gain_mlp = gains[0], gains[1]
    both_gains = lax.dynamic_slice_in_dim(gains[2:], place * head_cols, head_cols, axis=1)

    routes_all = numbers_all[:, :top_count]
    segments_all = numbers_all[:, top_count]
    turns = rotary_tables(row_count, head_size)
    column, row = segments_all[:, :, None], segments_all[:, None, :]
    arrays = [x_all, qkv_here, gain_attn[None], both_gains, turns, column, row, w_out, out_cotangent]
    hidden_one, projected, scales, kept, attended, own_attended, out_full, dy_all = attention(
        line_count, dp_count, heads_here, arrays, 4
    )
    out_full = out_full.reshape(model_dim, model_dim)
    inputs = layer_input.astype(FULL)
    scale_attn = rms_scale(inputs)
    normed_attn = inputs * scale_attn
    residual = inputs + jnp.dot(own_attended, out_full, preferred_element_type=FULL)
    scale_mlp = rms_scale(residual)
    normed_mlp = residual * scale_mlp
    hidden_two = (normed_mlp * gain_mlp).astype(LOW)

    logits = jnp.dot(hidden_two, router_full, preferred_element_type=FULL)
    chosen = jnp.any(routes[:, :, None] == jnp.arange(expert_count)[None, None, :], axis=1)
    masked = jnp.where(chosen, logits, -1e30)
    powers = jnp.where(chosen, jnp.exp(masked - jnp.max(masked, axis=-1, keepdims=True)), 0.0)
    gates = powers / jnp.sum(powers, axis=-1, keepdims=True)

    local = place * local_count + jnp.arange(local_count)
    used = jnp.any(routes_all[:, None] == local[None, :, None, None], axis=2)
    position = jnp.arange(row_count)
    lower = (position[:, None] < position[None, :]).astype(LOW)
    rank = einsum("gju,ut->gjt", used.astype(LOW), lower).astype(jnp.int32)
    rank = jnp.where(used, rank, -1)
    spots = jnp.arange(capacity)
    table = (rank[:, :, None, :] == spots[None, None, :, None]).astype(LOW)
    returns = [(rank[:, j, :, None] == spots[None, None, :]).astype(LOW) for j in range(local_count)]
    slots = line_count * capacity
    flat_table = table.reshape(line_count, local_count * capacity, row_count)
    expert_rows, dy_rows, gates_all = gather_place(
        line_count, hidden_two, gates.T, flat_table, dy_all, local_count, 6
    )
    local_gates = lax.dynamic_slice_in_dim(gates_all, place * local_count, local_count, axis=1)
    slot_gates = jnp.sum(table.astype(FULL) * local_gates[:, :, None, :], axis=-1)
    slot_gates = slot_gates.transpose(1, 0, 2).reshape(local_count, slots, 1)
    out_rows, back_rows, slot_grads, grad_sums = [], [], [], []
    both_rows = model_dim // dp_count + w_down.shape[1] // dp_count
    for first, count in ((0, 1), (1, local_count - 1)):
        grads, out_row, back_row, dots = expert(
            first, count, dp_count, expert_rows, dy_rows, slot_gates, w_gate_up, w_down
        )
        grads = grads.reshape(-1, model_dim)
        grads = lax.psum_scatter(grads, "dp", scatter_dimension=0, tiled=True)
        grad_sums.append(grads.reshape(count, both_rows, model_dim))
        for kept_list, rows in ((out_rows, out_row), (back_rows, back_row), (slot_grads, dots)):
            kept_list.append(rows.reshape(count, line_count, capacity, rows.shape[2]))
    gate_rows = model_dim // dp_count
    grad_two, grad_gates = collect_reduce(
        line_count, returns, back_rows, slot_grads, flat_table, 8
    )
    grad_gates = grad_gates.reshape(expert_count, row_count).T
    grad_two = grad_two.astype(FULL)

    grad_out_rows = out_cotangent.astype(FULL)
    grad_logits = gates * (grad_gates - jnp.sum(gates * grad_gates, axis=-1, keepdims=True))
    grad_logits = grad_logits.astype(LOW)
    grad_router = contract_rows(grad_logits, hidden_two)
    grad_two = grad_two + contract_cols(grad_logits, router_full)
    grad_gain_mlp = jnp.sum(grad_two * normed_mlp, axis=0)
    grad_resid = grad_out_rows + norm_back(grad_two * gain_mlp, normed_mlp, scale_mlp)
    grad_attn = grad_resid.astype(LOW)

    arrays = [out_full, kept, attended, projected, scales, both_gains, turns, column, row]
    grad_proj, gain_pair, out_parts = attend_back(
        line_count, dp_count, heads_here, grad_attn, arrays, 11
    )

    shared = jnp.concatenate([grad_router, grad_gain_mlp[None]], axis=0)
    tall = shared.shape[0] + -shared.shape[0] % 8
    shared = jnp.pad(shared, ((0, tall - shared.shape[0]), (0, 0)))
    shared = shared.reshape(tall, dp_count, line_count, shard).transpose(2, 1, 0, 3)
    shared = shared.reshape(line_count, dp_count * tall, shard)
    shared = jnp.pad(shared, ((0, 0), (0, 0), (0, 128 - shard)))
    arrays = [grad_proj, qkv_here, hidden_one, gain_attn[None]]
    grad_one, mixture, sum_qkv, sum_out, gain_pair, gain_sum, shared = closing(
        line_count, dp_count, returns, out_rows, arrays, [out_parts, gain_pair], shared, 14
    )
    here = (lax.axis_index("dp") * line_count + place) * shard
    grad_gain_attn = lax.dynamic_slice_in_dim(gain_sum[0], here, shard)
    output = (residual + mixture.astype(FULL)).astype(LOW)
    sum_qkv = sum_qkv.transpose(1, 0, 2)
    first_sums, mixture = lax.optimization_barrier((grad_sums[0], mixture))
    wide = widen(0, local_count, gate_rows, first_sums)
    sum_gate_up, sum_down = widen(1, local_count, gate_rows, grad_sums[1], wide)
    shared = shared[:, :shard]
    grad_one = grad_one.astype(FULL)
    grad_inputs = grad_resid + norm_back(grad_one * gain_attn, normed_attn, scale_attn)
    return (
        output,
        grad_inputs,
        sum_qkv,
        sum_out,
        shared[:expert_count].T,
        grad_gain_attn,
        shared[expert_count],
        gain_pair[0],
        gain_pair[1],
        sum_gate_up,
        sum_down,
    )


def solution(mesh):
    both = ("dp", "expert")
    rows, flat = P(both, None), P(both)
    placed = (rows,) * 7 + (flat,) * 4 + (P("expert", None, None),) * 2
    return jax.shard_map(
        functools.partial(on_device, mesh.shape["dp"], mesh.shape["expert"]),
        mesh=mesh,
        in_specs=placed,
        out_specs=(
            rows,
            rows,
            P("dp", None, "expert"),
            P("expert", "dp"),
            rows,
            flat,
            flat,
            P("expert"),
            P("expert"),
            P("expert", "dp", None),
            P("expert", "dp", None),
        ),
        check_vma=False,
    )
```

```python
import functools
import math

import jax
import jax.numpy as jnp
import numpy as np
from jax import lax
from jax.experimental import pallas as pl
from jax.experimental.pallas import tpu as pltpu
from jax.sharding import PartitionSpec as P

HEADS = 16
NORM_EPS = 1e-05
MESH = pl.DeviceIdType.MESH
ANY = pl.BlockSpec(memory_space=pl.ANY)
LOW = jnp.bfloat16
GATHER_CUTS, REDUCE_CUTS = 4, 3
FULL = jnp.float32


def line_place():
    place = lax.axis_index("expert")
    level, side = lax.div(place, 2), lax.rem(place, 2)
    return place, level, side, place + 1 - 2 * side


def greet(axis, targets):
    barrier = pltpu.get_barrier_semaphore()
    for target, there in targets:

        def signal(target=target):
            pl.semaphore_signal(barrier, inc=1, device_id={axis: target}, device_id_type=MESH)

        if there is None:
            signal()
        else:
            pl.when(there)(signal)


def line_barrier(levels):
    place, level, _, other = line_place()
    has_up, has_down = level < levels - 1, level > 0
    greet("expert", [(other, None), (place + 2, has_up), (place - 2, has_down)])
    count = 1 + has_up.astype(jnp.int32) + has_down.astype(jnp.int32)
    pl.semaphore_wait(pltpu.get_barrier_semaphore(), count)


def around(axis, size):
    place = lax.axis_index(axis)
    return [lax.rem(place + shift, size) for shift in range(1, size)]


def remote(source, target, send, recv, device):
    return pltpu.make_async_remote_copy(
        src_ref=source,
        dst_ref=target,
        send_sem=send,
        recv_sem=recv,
        device_id=device,
        device_id_type=MESH,
    )


class LineGather:
    def __init__(self, levels, cuts, ins, outs, up_sem, down_sem, side_sem, recv_sem, own_sem):
        self.levels, self.cuts, self.ins, self.outs = levels, cuts, ins, outs
        self.up_sem, self.down_sem, self.side_sem = up_sem, down_sem, side_sem
        self.recv_sem, self.own_sem = recv_sem, own_sem
        self.place, self.level, self.side, self.other = line_place()
        self.has_up, self.has_down = self.level < levels - 1, self.level > 0

    @staticmethod
    def scratch(size, cuts, count):
        levels, total = size // 2, cuts + count - 1
        shapes = ((levels, total), (levels, total), (2 * levels - 1, total), (size, total))
        return [pltpu.SemaphoreType.DMA(shape) for shape in shapes + ((count,),)]

    def pieces(self):
        return [(0, k) for k in range(self.cuts)] + [(i, 0) for i in range(1, len(self.ins))]

    def staying(self, i):
        target = self.outs[i].at[self.place]
        return pltpu.make_async_copy(self.ins[i], target, self.own_sem.at[i])

    def sending(self, piece, block, own, sem, target):
        i, k = piece
        landing, source, q = self.outs[i].at[block], self.ins[i], k
        if i:
            q = self.cuts + i - 1
        else:
            rows = source.shape[0] // self.cuts
            landing, source = landing.at[pl.ds(k * rows, rows)], source.at[pl.ds(k * rows, rows)]
        sems = sem.at[q], self.recv_sem.at[block, q]
        return remote(source if own else landing, landing, *sems, {"expert": target})

    def up(self, piece, step, own=False):
        block = self.place - 2 * step
        return self.sending(piece, block, own, self.up_sem.at[step], self.place + 2)

    def down(self, piece, step, own=False):
        block = self.place + 2 * step
        return self.sending(piece, block, own, self.down_sem.at[step], self.place - 2)

    def across(self, piece, step, own=False):
        sem = self.side_sem.at[step + self.levels - 1]
        return self.sending(piece, self.place - 2 * step, own, sem, self.other)

    def begin(self):
        for piece in self.pieces():
            pl.when(self.has_up)(self.up(piece, 0, True).start)
            pl.when(self.has_down)(self.down(piece, 0, True).start)
        for piece in self.pieces():
            self.across(piece, 0, True).start()
        for i in range(len(self.ins)):
            self.staying(i).start()

    def forward(self, step, piece):
        @pl.when(self.level >= step)
        def _():
            self.across(piece, step).wait_recv()
            pl.when(self.has_up)(self.up(piece, step).start)
            self.across(piece, step).start()

        @pl.when(self.level + step < self.levels)
        def _():
            self.across(piece, -step).wait_recv()
            pl.when(self.has_down)(self.down(piece, step).start)
            self.across(piece, -step).start()

    def land_across(self, block):
        for piece in self.pieces():
            self.sending(piece, block, False, self.side_sem.at[0], self.other).wait_recv()

    def turn(self, turn, landed=None):
        levels, cuts = self.levels, self.cuts
        step, k = lax.div(turn, 4) + 1, lax.rem(turn, 4)

        @pl.when((step < levels) & (k < cuts))
        def _():
            self.forward(step, (0, k))

            @pl.when(k == cuts - 1)
            def _():
                for i in range(1, len(self.ins)):
                    self.forward(step, (i, 0))

        group, sign, crossed = step - 1, 2 * lax.rem(k, 2) - 1, lax.div(k, 2)
        crossed = jnp.where(group == 0, k, crossed)
        far = jnp.where(group == 0, self.level, self.level + sign * group)

        @pl.when((far >= 0) & (far < levels) & ((group > 0) | (k < 2)))
        def _():
            block = 2 * far + self.side + crossed * (1 - 2 * self.side)

            @pl.when(crossed == 1)
            def _():
                self.land_across(block)

            if landed:
                landed(block)

    def main(self, landed=None):
        @pl.loop(0, 4 * self.levels)
        def _(turn):
            self.turn(turn, landed)

    def finish(self, held=0):
        for piece in self.pieces():
            self.across(piece, 0).wait_send()
            for step in range(self.levels):
                above, below = self.level >= step, self.level + step < self.levels
                pl.when(self.has_up & above)(self.up(piece, step).wait_send)
                pl.when(self.has_down & below)(self.down(piece, step).wait_send)
                if step:
                    pl.when(above)(self.across(piece, step).wait_send)
                    pl.when(below)(self.across(piece, -step).wait_send)
        for i in range(held, len(self.ins)):
            self.staying(i).wait()


def call(kernel, name, number, outs, scratch, arrays, moved):
    return pl.pallas_call(
        kernel,
        out_shape=outs,
        in_specs=[ANY] * len(arrays),
        out_specs=[ANY] * len(outs),
        scratch_shapes=scratch,
        compiler_params=pltpu.CompilerParams(
            collective_id=number, has_side_effects=True, vmem_limit_bytes=48 << 20
        ),
        cost_estimate=pl.CostEstimate(flops=0, transcendentals=0, bytes_accessed=moved),
        name=name,
    )(*arrays)


class LineReduce:
    def __init__(self, levels, cuts, parts, total, own, beside, rising, falling, *sems):
        self.levels, self.cuts, self.parts, self.total = levels, cuts, parts, total
        self.made = parts.shape[0] == levels
        self.own, self.beside, self.rising, self.falling = own, beside, rising, falling
        self.load_sem, self.side_send, self.side_recv = sems[:3]
        self.up_send, self.up_recv, self.down_send, self.down_recv, self.out_sem = sems[3:]
        self.place, self.level, self.side, self.other = line_place()
        self.has_up, self.has_down = self.level < levels - 1, self.level > 0
        self.rows = parts.shape[1] // cuts

    @staticmethod
    def scratch(size, block, dtype, cuts):
        levels = size // 2
        return (
            [pltpu.VMEM((levels,) + block, dtype)] * 2
            + [pltpu.VMEM((levels - 1,) + block, dtype)] * 2
            + [pltpu.SemaphoreType.DMA((levels, cuts))] * 7
            + [pltpu.SemaphoreType.DMA((cuts,))]
        )

    def cut(self, ref, block, k):
        return ref.at[block, pl.ds(k * self.rows, self.rows)]

    def loading(self, far, k):
        source = self.cut(self.parts, 2 * far + self.side, k)
        return pltpu.make_async_copy(source, self.cut(self.own, far, k), self.load_sem.at[far, k])

    def across(self, far, k):
        source = self.cut(self.parts, far if self.made else 2 * far + 1 - self.side, k)
        sems = self.side_send.at[far, k], self.side_recv.at[far, k]
        return remote(source, self.cut(self.beside, far, k), *sems, {"expert": self.other})

    def up(self, far, k):
        sems = self.up_send.at[far, k], self.up_recv.at[far, k]
        target = {"expert": self.place + 2}
        return remote(self.cut(self.own, far, k), self.cut(self.rising, far - 1, k), *sems, target)

    def down(self, far, k):
        sems = self.down_send.at[far, k], self.down_recv.at[far, k]
        target = {"expert": self.place - 2}
        return remote(self.cut(self.own, far, k), self.cut(self.falling, far, k), *sems, target)

    def value(self, ref, block, k):
        return self.cut(ref, block, k)[...].astype(FULL)

    def load(self):
        for i in range(self.levels):
            for k in range(self.cuts):
                self.loading(self.far(i), k).start()

    def begin(self):
        for i in range(self.levels):
            for k in range(self.cuts):
                self.across(self.far(i), k).start()

    def far(self, i):
        return jnp.where(lax.rem(i, 2) == 0, self.levels - 1 - lax.div(i, 2), lax.div(i, 2))

    def prepare(self, turn, make):
        far = self.far(lax.div(turn, 2))

        @pl.when(lax.rem(turn, 2) == 0)
        def _():
            make(2 * far + 1 - self.side, self.parts.at[far])
            for k in range(self.cuts):
                self.across(far, k).start()

        @pl.when(lax.rem(turn, 2) == 1)
        def _():
            make(2 * far + self.side, self.own.at[far])

    def pair(self, far, k):
        if not self.made:
            self.loading(far, k).wait()
        self.across(far, k).wait_recv()
        return self.value(self.own, far, k) + self.value(self.beside, far, k)

    def store(self, far, k, total):
        self.cut(self.own, far, k)[...] = total.astype(self.own.dtype)

    def toward(self, far, k, ahead, behind, move, arrived, shift):
        @pl.when(ahead & behind)
        def _():
            both = self.pair(far, k)
            move(far, k).wait_recv()
            self.store(far, k, both + self.value(arrived, far - shift, k))

        @pl.when(ahead & jnp.logical_not(behind))
        def _():
            self.store(far, k, self.pair(far, k))

        pl.when(ahead)(move(far, k).start)

    def main(self, beside=None):
        levels, cuts = self.levels, self.cuts
        lower = self.level < levels // 2

        def rise(far, k):
            self.toward(far, k, self.level < far, self.has_down, self.up, self.rising, 1)

        def fall(far, k):
            self.toward(far, k, self.level > far, self.has_up, self.down, self.falling, 0)

        @pl.loop(0, 2 * cuts)
        def _(turn):
            near, k = turn < cuts, lax.rem(turn, cuts)
            if beside:
                beside(turn)
            upward = (near & lower) | jnp.logical_not(near | lower)
            pl.when(upward)(lambda: rise(levels - 1, k))
            pl.when(jnp.logical_not(upward))(lambda: fall(0, k))

        @pl.loop(2 * cuts, levels * cuts)
        def _(turn):
            step, k = lax.div(turn, cuts) - 1, lax.rem(turn, cuts)
            if beside:
                beside(turn)
            rise(levels - 1 - step, k)
            fall(step, k)

    def settle(self):
        @pl.loop(0, self.cuts)
        def _(k):
            self.store(self.level, k, self.pair(self.level, k))
            for there, move, arrived, shift in (
                (self.has_down, self.up, self.rising, 1),
                (self.has_up, self.down, self.falling, 0),
            ):

                @pl.when(there)
                def _():
                    move(self.level, k).wait_recv()
                    total = self.value(self.own, self.level, k)
                    total += self.value(arrived, self.level - shift, k)
                    self.store(self.level, k, total)

            self.leaving(k).start()

    def leaving(self, k):
        target = self.total.at[pl.ds(k * self.rows, self.rows)]
        return pltpu.make_async_copy(self.cut(self.own, self.level, k), target, self.out_sem.at[k])

    def finish(self):
        for k in range(self.cuts):
            self.leaving(k).wait()
            for far in range(self.levels):
                self.across(far, k).wait_send()
                pl.when(self.level < far)(self.up(far, k).wait_send)
                pl.when(self.level > far)(self.down(far, k).wait_send)


class Exchange:
    def __init__(self, axis, size, spread, cuts, ins, outs, send_sem, recv_sem, own_sem):
        self.axis, self.spread, self.ins, self.outs = axis, spread, ins, outs
        self.send_sem, self.recv_sem, self.own_sem = send_sem, recv_sem, own_sem
        self.cuts = cuts
        self.firsts = [sum(cuts[:i]) for i in range(len(cuts))]
        self.pieces = [(i, k) for i in range(len(cuts)) for k in range(cuts[i])]
        self.place, self.peers = lax.axis_index(axis), around(axis, size)

    @staticmethod
    def scratch(size, cuts):
        sems = pltpu.SemaphoreType.DMA
        return [sems((sum(cuts), size)), sems((sum(cuts), size)), sems((len(cuts),))]

    def source(self, i, block):
        return self.ins[i] if self.spread[i] else self.ins[i].at[block]

    def staying(self, i):
        target = self.outs[i].at[self.place]
        return pltpu.make_async_copy(self.source(i, self.place), target, self.own_sem.at[i])

    def sending(self, i, k, shift, landing):
        peer = self.peers[shift]
        source, target, q = self.source(i, peer), self.outs[i].at[landing], self.firsts[i] + k
        if self.cuts[i] > 1:
            rows = target.shape[0] // self.cuts[i]
            source, target = source.at[pl.ds(k * rows, rows)], target.at[pl.ds(k * rows, rows)]
        sems = self.send_sem.at[q, shift], self.recv_sem.at[q, landing]
        return remote(source, target, *sems, {self.axis: peer})

    def send(self, i, k):
        for shift in range(len(self.peers)):
            self.sending(i, k, shift, self.place).start()

    def stay(self):
        for i in range(len(self.spread)):
            self.staying(i).start()

    def begin(self):
        for i, k in self.pieces:
            self.send(i, k)
        self.stay()

    def land(self):
        for shift, peer in enumerate(self.peers):
            for i, k in self.pieces:
                self.sending(i, k, shift, peer).wait_recv()

    def arrive(self):
        self.land()
        for i in range(len(self.spread)):
            self.staying(i).wait()

    def finish(self):
        for shift in range(len(self.peers)):
            for i, k in self.pieces:
                self.sending(i, k, shift, self.place).wait_send()


def exchange_kernel(axis, size, spread, *refs):
    count = len(spread)
    ins, outs, sems = refs[:count], refs[count : 2 * count], refs[2 * count :]
    moves = Exchange(axis, size, spread, (1,) * count, ins, outs, *sems)
    greet(axis, [(peer, None) for peer in moves.peers])
    pl.semaphore_wait(pltpu.get_barrier_semaphore(), size - 1)
    moves.begin()
    moves.arrive()
    moves.finish()


def exchange_outs(size, arrays, spread):
    return [
        jax.ShapeDtypeStruct((size,) + a.shape if flat else a.shape, a.dtype)
        for a, flat in zip(arrays, spread)
    ]


def exchange(axis, size, arrays, spread, number):
    return call(
        functools.partial(exchange_kernel, axis, size, tuple(spread)),
        "exchange_" + axis,
        number,
        exchange_outs(size, arrays, spread),
        Exchange.scratch(size, (1,) * len(arrays)),
        arrays,
        30_000_000,
    )


def opening_kernel(size, dp_count, count, cuts, *refs):
    ins, (w_ref, *small_refs) = refs[:count], refs[count : count + 3]
    outs, rest = refs[count + 3 : 2 * count + 3], refs[2 * count + 6 :]
    w_out, *small_outs = refs[2 * count + 3 : 2 * count + 6]
    line = LineGather(size // 2, cuts, ins, outs, *rest[:5])
    send_sem, recv_sem, own_sem = rest[5:8]
    place, mine = line.place, lax.axis_index("dp")
    peers = around("expert", size)
    width = w_out.shape[3] // 3
    lands = [w_out] + small_outs
    across = Exchange(
        "dp", dp_count, (True,) * 3, (size,) * 3, [a.at[mine] for a in lands], lands, *rest[8:]
    )
    greet("expert", [(peer, None) for peer in peers])
    greet("dp", [(peer, None) for peer in across.peers])
    pl.semaphore_wait(pltpu.get_barrier_semaphore(), size + dp_count - 2)

    def ends(peer, landing, j):
        if j >= 3:
            return small_refs[j - 3], small_outs[j - 3].at[mine, landing]
        start = pl.multiple_of(j * width * size + peer * width, 128)
        target = w_out.at[mine, landing, :, pl.ds(j * width, width)]
        return w_ref.at[:, pl.ds(start, width)], target

    def sending(shift, landing, j):
        source, target = ends(peers[shift], landing, j)
        sems = send_sem.at[shift, j], recv_sem.at[landing, j]
        return remote(source, target, *sems, {"expert": peers[shift]})

    own = [pltpu.make_async_copy(*ends(place, place, j), own_sem.at[j]) for j in range(5)]
    for shift in range(size - 1):
        for j in range(5):
            sending(shift, place, j).start()
    for copy in own:
        copy.start()
    line.begin()
    for copy in own:
        copy.wait()
    for i in range(3):
        across.send(i, place)
    for shift, peer in enumerate(peers):
        for j in range(5):
            sending(shift, peer, j).wait_recv()
        for i in range(3):
            across.send(i, peer)
    line.main()
    line.finish()
    for shift in range(size - 1):
        for j in range(5):
            sending(shift, place, j).wait_send()
    across.land()
    across.finish()


def opening(size, dp_count, arrays, cuts, weights, small, number):
    sems = pltpu.SemaphoreType.DMA
    outs = [jax.ShapeDtypeStruct((size,) + a.shape, a.dtype) for a in arrays]
    rows, columns = weights.shape
    whole = (dp_count, size, rows)
    outs.append(jax.ShapeDtypeStruct(whole + (columns // size,), weights.dtype))
    outs += [jax.ShapeDtypeStruct((dp_count, size) + a.shape, a.dtype) for a in small]
    return call(
        functools.partial(opening_kernel, size, dp_count, len(arrays), cuts),
        "opening",
        number,
        outs,
        LineGather.scratch(size, cuts, len(arrays))
        + [sems((size, 5)), sems((size, 5)), sems((5,))]
        + Exchange.scratch(dp_count, (size,) * 3),
        list(arrays) + [weights] + small,
        200_000_000,
    )


class Sheets:
    def __init__(self, size, dp_count, source, target, *sems):
        self.levels, self.dp_count, self.ins, self.out = size // 2, dp_count, source, target
        self.up_send, self.down_send, self.line_recv, self.dp_send, self.dp_recv = sems[:5]
        self.side_send, self.side_recv, self.own_sem = sems[5:]
        self.place, self.level, self.side, self.other = line_place()
        self.has_up, self.has_down = self.level < self.levels - 1, self.level > 0
        self.mine, self.peers = lax.axis_index("dp"), around("dp", dp_count)

    @staticmethod
    def scratch(size, dp_count):
        sems, levels = pltpu.SemaphoreType.DMA, size // 2
        return [sems((levels,))] * 3 + [sems((dp_count, levels))] * 4 + [sems((1,))]

    def along(self, far, own, send, target):
        landing = self.out.at[self.mine, 2 * far + self.side]
        source = self.ins if own else landing
        return remote(source, landing, send.at[far], self.line_recv.at[far], {"expert": target})

    def up(self, far, own=False):
        return self.along(far, own, self.up_send, self.place + 2)

    def down(self, far, own=False):
        return self.along(far, own, self.down_send, self.place - 2)

    def over(self, far, shift, copy, own=False):
        landing = self.out.at[copy, 2 * far + self.side]
        source = self.ins if own else landing
        sems = self.dp_send.at[shift, far], self.dp_recv.at[copy, far]
        return remote(source, landing, *sems, {"dp": self.peers[shift]})

    def across(self, far, copy, whose, own=False):
        landing = self.out.at[copy, 2 * far + whose]
        source = self.ins if own else landing
        sems = self.side_send.at[copy, far], self.side_recv.at[copy, far]
        return remote(source, landing, *sems, {"expert": self.other})

    def spread(self, far, own=False):
        for shift in range(self.dp_count - 1):
            self.over(far, shift, self.mine, own).start()
        self.across(far, self.mine, self.side, own).start()

    def staying(self):
        target = self.out.at[self.mine, self.place]
        return pltpu.make_async_copy(self.ins, target, self.own_sem.at[0])

    def begin(self):
        pl.when(self.has_up)(self.up(self.level, True).start)
        pl.when(self.has_down)(self.down(self.level, True).start)
        self.spread(self.level, True)
        self.staying().start()

    def forward(self, step):
        @pl.when(self.level >= step)
        def _():
            self.up(self.level - step).wait_recv()
            pl.when(self.has_up)(self.up(self.level - step).start)
            self.spread(self.level - step)

        @pl.when(self.level + step < self.levels)
        def _():
            self.down(self.level + step).wait_recv()
            pl.when(self.has_down)(self.down(self.level + step).start)
            self.spread(self.level + step)

    def cross(self, far):
        for shift, peer in enumerate(self.peers):
            self.over(far, shift, peer).wait_recv()
            self.across(far, peer, self.side).start()

    def finish(self):
        @pl.loop(0, self.levels)
        def _(far):
            pl.when(self.has_up & (self.level >= far))(self.up(far).wait_send)
            pl.when(self.has_down & (self.level <= far))(self.down(far).wait_send)
            for shift in range(self.dp_count - 1):
                self.over(far, shift, self.mine).wait_send()
            for copy in range(self.dp_count):
                self.across(far, copy, 1 - self.side).wait_recv()
                self.across(far, copy, self.side).wait_send()

        self.staying().wait()


VMEM = pl.BlockSpec(memory_space=pltpu.VMEM)
COLUMNS = 512


def gather_place_kernel(levels, cuts, *refs):
    rows_ref, gates_ref, table_ref, dy_ref, x_out, dy_out, gates_out = refs[:7]
    held, dy_held, x_stage, dy_stage = refs[7:11]
    line_sems, (dy_sem, x_sems, dy_sems) = refs[11:16], refs[16:]
    line = LineGather(levels, cuts, [rows_ref, gates_ref], [held, gates_out], *line_sems)
    size, width = 2 * levels, held.shape[2]
    _, local_count, capacity, _ = x_stage.shape

    def leaving(block, stage, out, sems):
        target = out.at[:, pl.ds(pl.multiple_of(block * capacity, 8), capacity)]
        return pltpu.make_async_copy(stage.at[block], target, sems.at[block])

    def place(block, rows, stage, out, sems):
        table = table_ref[block]

        @pl.loop(0, width // COLUMNS)
        def _(n):
            columns = pl.ds(pl.multiple_of(n * COLUMNS, COLUMNS), COLUMNS)
            placed = jnp.dot(table, rows[block, :, columns], preferred_element_type=FULL)
            for j in range(local_count):
                part = placed[j * capacity : (j + 1) * capacity]
                stage[block, j, :, columns] = part.astype(stage.dtype)

        leaving(block, stage, out, sems).start()

    def place_x(block):
        place(block, held, x_stage, x_out, x_sems)

    loading = pltpu.make_async_copy(dy_ref, dy_held, dy_sem.at[0])
    loading.start()
    line_barrier(levels)
    line.begin()
    loading.wait()

    @pl.loop(0, size)
    def _(block):
        place(block, dy_held, dy_stage, dy_out, dy_sems)

    line.staying(0).wait()
    line.main(place_x)
    line.finish(held=1)

    @pl.loop(0, size)
    def _(block):
        leaving(block, x_stage, x_out, x_sems).wait()
        leaving(block, dy_stage, dy_out, dy_sems).wait()


def gather_place(size, rows, gates, table, dy, local_count, number):
    cuts = GATHER_CUTS
    tokens, width = rows.shape
    capacity = table.shape[1] // local_count
    placed = jax.ShapeDtypeStruct((local_count, size * capacity, width), rows.dtype)
    sems = pltpu.SemaphoreType.DMA
    return pl.pallas_call(
        functools.partial(gather_place_kernel, size // 2, cuts),
        out_shape=[placed, placed, jax.ShapeDtypeStruct((size,) + gates.shape, gates.dtype)],
        in_specs=[ANY, ANY, VMEM, ANY],
        out_specs=[ANY] * 3,
        scratch_shapes=[pltpu.VMEM((size, tokens, width), rows.dtype)] * 2
        + [pltpu.VMEM((size, local_count, capacity, width), rows.dtype)] * 2
        + LineGather.scratch(size, cuts, 2)
        + [sems((1,)), sems((size,)), sems((size,))],
        compiler_params=pltpu.CompilerParams(
            collective_id=number, has_side_effects=True, vmem_limit_bytes=48 << 20
        ),
        cost_estimate=pl.CostEstimate(
            flops=4 * table.size * width, transcendentals=0, bytes_accessed=150_000_000
        ),
        name="gather_place",
    )(rows, gates, table, dy)


def several(index, turns, count, work):
    share = -(-count // turns)
    for i in range(share):
        item = share * index + i
        pl.when((index >= 0) & (item < count))(lambda item=item: work(item))


def split_at(arrays, j, block):
    for array in arrays:
        if j < array.shape[0]:
            return array.at[j, block]
        j -= array.shape[0]


def collect_block(tables, slots, block, target):
    @pl.loop(0, target.shape[1] // COLUMNS)
    def _(n):
        columns = pl.ds(pl.multiple_of(n * COLUMNS, COLUMNS), COLUMNS)
        total = 0.0
        for j, table in enumerate(tables):
            rows = split_at(slots, j, block)[:, columns]
            total += jnp.dot(table[block], rows, preferred_element_type=FULL)
        target[:, columns] = total.astype(target.dtype)


def collect_reduce_kernel(levels, cuts, local_count, *refs):
    tables, refs = refs[:local_count], refs[local_count:]
    slots, dots, (table_ref, total_ref, gates_out, away) = refs[:2], refs[2:4], refs[4:8]
    rest, (gates, *sems) = refs[8:20], refs[20:]
    line = LineReduce(levels, cuts, away, total_ref, *rest)
    small = Exchange("expert", 2 * levels, (False,), (1,), [gates], [gates_out], *sems)
    greet("expert", [(peer, None) for peer in small.peers])
    pl.semaphore_wait(pltpu.get_barrier_semaphore(), 2 * levels - 1)
    make = functools.partial(collect_block, tables, slots)

    @pl.loop(0, 4)
    def _(turn):
        line.prepare(turn, make)

    def gate_block(block):
        table = table_ref[block].astype(FULL)
        capacity = table.shape[0] // local_count
        for j in range(local_count):
            part = table[j * capacity : (j + 1) * capacity] * split_at(dots, j, block)[...]
            gates[block, j : j + 1] = jnp.sum(part, axis=0, keepdims=True)

    def beside(turn):
        pl.when(turn + 4 < 2 * levels)(lambda: line.prepare(turn + 4, make))
        turns = levels * cuts - levels
        several(turn - levels, turns, 2 * levels, gate_block)
        pl.when(turn == levels * cuts - 1)(small.begin)

    line.main(beside)
    line.settle()
    small.arrive()
    line.finish()
    small.finish()


def collect_reduce(size, tables, slots, dots, table, number):
    levels, cuts = size // 2, REDUCE_CUTS
    block = (tables[0].shape[1], slots[0].shape[3])
    kind = slots[0].dtype
    gates = (size, len(tables), block[0])
    return pl.pallas_call(
        functools.partial(collect_reduce_kernel, levels, cuts, len(tables)),
        out_shape=[jax.ShapeDtypeStruct(block, kind), jax.ShapeDtypeStruct(gates, FULL)],
        in_specs=[VMEM] * (len(tables) + 5),
        out_specs=[ANY, ANY],
        scratch_shapes=[pltpu.VMEM((levels,) + block, kind)]
        + LineReduce.scratch(size, block, kind, cuts)
        + [pltpu.VMEM(gates, FULL)]
        + Exchange.scratch(size, (1,)),
        compiler_params=pltpu.CompilerParams(
            collective_id=number, has_side_effects=True, vmem_limit_bytes=48 << 20
        ),
        cost_estimate=pl.CostEstimate(flops=0, transcendentals=0, bytes_accessed=150_000_000),
        name="collect_reduce",
    )(*tables, *slots, *dots, table)


def closing_kernel(size, dp_count, local_count, cuts, sum_cuts, *refs):
    refs, levels = list(refs), size // 2

    def take(count):
        taken = refs[:count]
        del refs[:count]
        return taken

    tables, slots = take(local_count), take(2)
    proj_ref, w_ref, h_ref, gain_ref, out_parts, gain_pair, shared_ref = take(7)
    back_out, mixed_out, qkv_out, w_out, gains_out, gain_out, shared_out = take(7)
    back = LineReduce(levels, cuts, *take(1), back_out, *take(12))
    mixed = LineReduce(levels, cuts, *take(1), mixed_out, *take(12))
    qkv_parts, qkv_got, out_got, gains_got = take(4)
    got, half, last, gain_sum, gain_got, gain_half, gain_last = take(7)
    parts, lands = [qkv_parts, out_parts, gain_pair], [qkv_got, out_got, gains_got]
    sums = Exchange("dp", dp_count, (False, False, True), sum_cuts, parts, lands, *take(3))
    first = Exchange("expert", size, (False,), (1,), [shared_ref], [got], *take(3))
    second = Exchange("dp", dp_count, (False,), (1,), [half], [last], *take(3))
    gain_first = Exchange("expert", size, (True,), (1,), [gain_sum], [gain_got], *take(3))
    gain_second = Exchange("dp", dp_count, (True,), (1,), [gain_half], [gain_last], *take(3))
    greet("expert", [(peer, None) for peer in first.peers])
    greet("dp", [(peer, None) for peer in sums.peers])
    pl.semaphore_wait(pltpu.get_barrier_semaphore(), size + dp_count - 2)
    first.begin()
    sums.staying(1).start()
    sums.staying(2).start()
    gain_sum[...] = jnp.zeros_like(gain_sum)
    groups, tokens, model_dim = h_ref.shape
    tall, high = half.shape[1], model_dim // dp_count

    def make_back(block, target):
        @pl.loop(0, model_dim // COLUMNS)
        def _(n):
            columns = pl.ds(pl.multiple_of(n * COLUMNS, COLUMNS), COLUMNS)
            grad = across_cols(proj_ref[block], w_ref[columns, :])
            target[:, columns] = grad.astype(target.dtype)
            weighted = grad * h_ref[block, :, columns].astype(FULL)
            gain_sum[:, columns] += jnp.sum(weighted, axis=0, keepdims=True)

    def piece(turn):
        k, copy = lax.div(turn, dp_count), lax.rem(turn, dp_count)
        columns = pl.ds(pl.multiple_of(copy * high + k * 128, 128), 128)
        rows = h_ref[:, :, columns].reshape(groups * tokens, 128)
        grads = proj_ref[...].reshape(groups * tokens, proj_ref.shape[2])
        products = contract_rows(rows, grads).astype(LOW)
        qkv_parts[copy, pl.ds(pl.multiple_of(k * 128, 128), 128)] = products
        pl.when(copy == dp_count - 1)(lambda: sums.send(0, k))
        pl.when(turn == sum_cuts[0] * dp_count - 1)(lambda: sums.staying(0).start())

    make_mixed = functools.partial(collect_block, tables, slots)
    ahead = levels

    @pl.loop(0, ahead)
    def _(turn):
        back.prepare(turn, make_back)

    rest, count = levels * cuts - ahead, sum_cuts[0] * dp_count

    def beside(turn):
        later = turn - ahead
        pl.when(turn + ahead < 2 * levels)(lambda: back.prepare(turn + ahead, make_back))
        pl.when(turn < sum_cuts[1])(lambda: sums.send(1, turn))
        pl.when(turn == sum_cuts[1])(lambda: sums.send(2, 0))
        pl.when(later == 0)(gain_first.begin)
        several(later, rest, 2 * levels, lambda i: mixed.prepare(i, make_mixed))
        several(later, 2 * rest, count, piece)

        @pl.when(later == rest - 1)
        def _():
            first.arrive()
            for copy in range(dp_count):
                rows = pl.ds(copy * tall, tall)
                half[copy] = sum(got[i, rows, :] for i in range(size))
            second.begin()
            gain_first.arrive()
            gain_half[...] = sum(gain_got[i] for i in range(size))
            gain_second.begin()

    back.main(beside)
    mixed.main(lambda turn: several(rest + turn, 2 * rest, count, piece))
    back.settle()
    mixed.settle()
    second.arrive()
    shared_out[...] = sum(last[i] for i in range(dp_count))
    gain_second.arrive()
    gain_out[...] = sum(gain_last[i] for i in range(dp_count)) / gain_ref[...]
    sums.arrive()
    wide = qkv_out.shape[2]
    for j in range(3):
        columns = slice(j * wide, (j + 1) * wide)
        qkv_out[j] = sum(qkv_got[copy, :, columns].astype(FULL) for copy in range(dp_count))
    w_out[...] = sum(out_got[copy].astype(FULL) for copy in range(dp_count))
    gains_out[...] = sum(gains_got[copy] for copy in range(dp_count))
    for moves in (back, mixed, first, second, sums, gain_first, gain_second):
        moves.finish()


def closing(size, dp_count, tables, slots, arrays, sums, shared, number):
    proj, _, hidden, gain = arrays
    levels, cuts = size // 2, REDUCE_CUTS
    _, tokens, model_dim = hidden.shape
    columns, high = proj.shape[2], model_dim // dp_count
    block = (tokens, model_dim)
    tall = shared.shape[1] // dp_count
    wide = shared.shape[2]
    sum_cuts = (high // 128, 2, 1)
    out, pair = exchange_outs(dp_count, sums, (False, True))
    shapes = [(3, high, columns // 3), out.shape[1:], pair.shape[1:], gain.shape, (tall, wide)]
    outs = [jax.ShapeDtypeStruct(block, LOW)] * 2
    outs += [jax.ShapeDtypeStruct(shape, FULL) for shape in shapes]
    line = [pltpu.VMEM((levels,) + block, LOW)] + LineReduce.scratch(size, block, LOW, cuts)
    return pl.pallas_call(
        functools.partial(closing_kernel, size, dp_count, len(tables), cuts, sum_cuts),
        out_shape=outs,
        in_specs=[VMEM] * (len(tables) + 6) + [ANY] * 3,
        out_specs=[ANY] * 2 + [VMEM] * 5,
        scratch_shapes=line
        + line
        + [pltpu.VMEM((dp_count, high, columns), LOW)] * 2
        + [pltpu.VMEM(a.shape, a.dtype) for a in (out, pair)]
        + [pltpu.VMEM((size,) + shared.shape[1:], FULL)]
        + [pltpu.VMEM((dp_count, tall, wide), FULL)] * 2
        + [
            pltpu.VMEM(gain.shape, FULL),
            pltpu.VMEM((size,) + gain.shape, FULL),
            pltpu.VMEM(gain.shape, FULL),
            pltpu.VMEM((dp_count,) + gain.shape, FULL),
        ]
        + Exchange.scratch(dp_count, sum_cuts)
        + Exchange.scratch(size, (1,))
        + Exchange.scratch(dp_count, (1,))
        + Exchange.scratch(size, (1,))
        + Exchange.scratch(dp_count, (1,)),
        compiler_params=pltpu.CompilerParams(
            collective_id=number, has_side_effects=True, vmem_limit_bytes=62 << 20
        ),
        cost_estimate=pl.CostEstimate(flops=0, transcendentals=0, bytes_accessed=200_000_000),
        name="closing",
    )(*tables, *slots, *arrays, *sums, shared)


def across_cols(left_side, right_side):
    return lax.dot_general(
        left_side, right_side, (((1,), (1,)), ((), ())), preferred_element_type=FULL
    )


def expert_kernel(first, count, tiles, x_ref, dy_ref, scale_ref, side_ref, down_ref, grads_ref, out_ref, back_ref, dots_ref,
                  side_w, down_w, turned, turned_act, act, grad_side, side_buf, down_buf, w_sems, sems):
    e, step = pl.program_id(0), pl.program_id(1)
    slot = lax.rem(e, 2)
    hidden, model = down_w.shape[1], down_w.shape[2]
    width, wide = hidden // tiles, model // tiles
    copies = grads_ref.shape[0]
    high, low = model // copies, hidden // copies
    part = side_buf.shape[1]

    def loads(e, tile):
        slot = lax.rem(e, 2)
        out = []
        for half in range(2):
            columns = pl.ds(pl.multiple_of(half * hidden + tile * width, 128), width)
            out.append(pltpu.make_async_copy(side_ref.at[first + e, :, columns], side_w.at[slot, :, columns], w_sems.at[slot, tile, half]))
        rows = pl.ds(pl.multiple_of(tile * width, 128), width)
        out.append(pltpu.make_async_copy(down_ref.at[first + e, rows], down_w.at[slot, rows], w_sems.at[slot, tile, 2]))
        return out

    def leaving(at):
        e, chunk = lax.div(at, tiles), lax.rem(at, tiles)
        slot = lax.rem(at, 2)
        base = e * (high + low)
        columns = pl.ds(pl.multiple_of(chunk * wide, 128), wide)
        if wide >= high:
            target = grads_ref.at[pl.ds(chunk * part, part), pl.ds(base, high)]
        else:
            target = grads_ref.at[pl.ds(lax.div(chunk * wide, high), 1), pl.ds(base + lax.rem(chunk * wide, high), wide)]
        return (pltpu.make_async_copy(side_buf.at[slot], target, sems.at[slot, 0]),
                pltpu.make_async_copy(down_buf.at[slot], grads_ref.at[:, pl.ds(base + high, low), columns], sems.at[slot, 1]))

    @pl.when((e == 0) & (step == 0))
    def _():
        for tile in range(tiles):
            for copy in loads(e, tile): copy.start()

    @pl.when((e + 1 < count) & (step == 0))
    def _():
        for tile in range(tiles):
            for copy in loads(e + 1, tile): copy.start()

    @pl.when(step == 0)
    def _():
        turned[...] = x_ref[0].T
        dots_ref[...] = jnp.zeros_like(dots_ref)

    @pl.when(step < tiles)
    def _():
        for copy in loads(e, step): copy.wait()
        rows, grads, scale = x_ref[0], dy_ref[0], scale_ref[0]
        columns = pl.ds(pl.multiple_of(step * width, 128), width)
        others = pl.ds(pl.multiple_of(hidden + step * width, 128), width)
        gate = jnp.dot(rows, side_w[slot, :, columns], preferred_element_type=FULL)
        up = jnp.dot(rows, side_w[slot, :, others], preferred_element_type=FULL)
        grad_act = across_cols(grads, down_w[slot, columns, :])
        sigmoid = jax.nn.sigmoid(gate)
        silu = gate * sigmoid
        raw = silu * up
        dots_ref[0] += jnp.sum(raw * grad_act, axis=-1, keepdims=True)
        weighted = (scale * raw).astype(LOW)
        act[:, columns] = weighted
        turned_act[columns, :] = weighted.T
        grad_act = grad_act * scale
        grad_side[:, columns] = (grad_act * up * sigmoid * (1.0 + gate * (1.0 - sigmoid))).astype(LOW)
        grad_side[:, others] = (grad_act * silu).astype(LOW)

    @pl.when(step >= tiles)
    def _():
        chunk = step - tiles
        at = e * tiles + chunk
        spot = lax.rem(at, 2)
        columns = pl.ds(pl.multiple_of(chunk * wide, 128), wide)

        @pl.when(at >= 2)
        def _():
            for copy in leaving(at - 2): copy.wait()
        total = jnp.dot(turned[columns, :], grad_side[...], preferred_element_type=FULL)
        side_buf[spot] = total.astype(LOW).reshape(side_buf.shape[1:])
        leaving(at)[0].start()
        total = jnp.dot(turned_act[...], dy_ref[0, :, columns], preferred_element_type=FULL)
        down_buf[spot] = total.astype(LOW).reshape(down_buf.shape[1:])
        leaving(at)[1].start()
        back_ref[0, :, columns] = across_cols(grad_side[...], side_w[slot, columns, :]).astype(LOW)
        out_ref[0, :, columns] = jnp.dot(act[...], down_w[slot, :, columns], preferred_element_type=FULL).astype(LOW)

        @pl.when(at == count * tiles - 1)
        def _():
            for copy in leaving(at - 1) + leaving(at): copy.wait()

def expert(first, count, dp_count, x_rows, dy_rows, scales, w_gate_up, w_down, tiles=4):
    _, slots, width = x_rows.shape
    hidden = w_down.shape[1]
    high, low = width // dp_count, hidden // dp_count
    wide = width // tiles
    part = max(1, wide // high)
    rs = pl.BlockSpec((1, slots, width), lambda e, f: (first + e, 0, 0))
    os = pl.BlockSpec((1, slots, width), lambda e, f: (e, 0, 0))
    sems = pltpu.SemaphoreType.DMA
    return pl.pallas_call(
        functools.partial(expert_kernel, first, count, tiles),
        out_shape=[jax.ShapeDtypeStruct((dp_count, count * (high + low), width), LOW),
                   jax.ShapeDtypeStruct((count, slots, width), LOW), jax.ShapeDtypeStruct((count, slots, width), LOW),
                   jax.ShapeDtypeStruct((count, slots, 1), FULL)],
        grid=(count, 2 * tiles),
        in_specs=[rs, rs, pl.BlockSpec((1, slots, 1), lambda e, f: (first + e, 0, 0)), ANY, ANY],
        out_specs=[ANY, os, os, pl.BlockSpec((1, slots, 1), lambda e, f: (e, 0, 0))],
        scratch_shapes=[pltpu.VMEM((min(2, count), width, 2 * hidden), LOW), pltpu.VMEM((min(2, count), hidden, width), LOW),
                        pltpu.VMEM((width, slots), LOW), pltpu.VMEM((hidden, slots), LOW), pltpu.VMEM((slots, hidden), LOW), pltpu.VMEM((slots, 2 * hidden), LOW),
                        pltpu.VMEM((2, part, min(wide, high), 2 * hidden), LOW), pltpu.VMEM((2, dp_count, low, wide), LOW),
                        sems((min(2, count), tiles, 3)), sems((2, 2))],
        compiler_params=pltpu.CompilerParams(vmem_limit_bytes=62 << 20),
        cost_estimate=pl.CostEstimate(
            flops=18 * count * slots * width * hidden,
            transcendentals=count * slots * hidden,
            bytes_accessed=12 * count * width * hidden,
        ),
        name="expert",
    )(x_rows, dy_rows, scales, w_gate_up, w_down)


def rms_scale(values):
    return lax.rsqrt(jnp.mean(values * values, axis=-1, keepdims=True) + NORM_EPS)


def rotary_tables(length, size):
    index = np.arange(size // 2, dtype=np.float32)
    frequency = np.exp(index * np.float32(-2.0 * math.log(10000.0) / size))
    angles = np.arange(length, dtype=np.float32)[:, None] * frequency[None, :]
    cosine, sine = np.cos(angles), np.sin(angles)
    halves = [np.concatenate([cosine, cosine], axis=1), np.concatenate([-sine, sine], axis=1)]
    return jnp.asarray(np.stack(halves).astype(np.float32))


def norm_back(grad_normed, normed, scale_rows):
    return scale_rows * (
        grad_normed - normed * jnp.mean(grad_normed * normed, axis=-1, keepdims=True)
    )


def contract_rows(left_side, right_side):
    return lax.dot_general(
        left_side, right_side, (((0,), (0,)), ((), ())), preferred_element_type=FULL
    )


def contract_cols(left_side, right_side):
    return lax.dot_general(
        left_side, right_side, (((1,), (1,)), ((), ())), preferred_element_type=FULL
    )


def einsum(spec, left_side, right_side):
    return jnp.einsum(spec, left_side, right_side, preferred_element_type=FULL)


def widen_kernel(steps, *refs):
    low_ref, high_ref, down_ref = refs[0], refs[-2], refs[-1]
    step = pl.program_id(1)

    @pl.when(step < steps)
    def _():
        high_ref[...] = low_ref[...].astype(FULL)

    @pl.when(step >= steps)
    def _():
        down_ref[...] = low_ref[...].astype(FULL)


def widen(first, total, high, grads, held=()):
    count, both, width = grads.shape
    low = both - high
    rows = low
    steps = high // rows
    block = (1, rows, width)
    return pl.pallas_call(
        functools.partial(widen_kernel, steps),
        out_shape=[
            jax.ShapeDtypeStruct((total, high, width), FULL),
            jax.ShapeDtypeStruct((total, low, width), FULL),
        ],
        grid=(count, steps + 1),
        in_specs=[pl.BlockSpec(block, lambda e, r: (e, r, 0))] + [ANY] * len(held),
        out_specs=[
            pl.BlockSpec(block, lambda e, r: (first + e, jnp.minimum(r, steps - 1), 0)),
            pl.BlockSpec(block, lambda e, r: (first + e, jnp.maximum(r - steps, 0), 0)),
        ],
        input_output_aliases={1: 0, 2: 1} if held else {},
        cost_estimate=pl.CostEstimate(
            flops=grads.size, transcendentals=0, bytes_accessed=6 * grads.size
        ),
        name="widen",
    )(grads, *held)


def turn(values, cosine, sine):
    return values * cosine + pltpu.roll(values, values.shape[1] // 2, 1) * sine


def allowed_pairs(column, row):
    shape = (column.shape[0], row.shape[1])
    later = lax.broadcasted_iota(jnp.int32, shape, 0) >= lax.broadcasted_iota(jnp.int32, shape, 1)
    return later & (column == row)


def softmax(query, key, allowed):
    scores = across_cols(query, key) * (1.0 / math.sqrt(query.shape[1]))
    scores = jnp.where(allowed, scores, -1e30)
    powers = jnp.exp(scores - jnp.max(scores, axis=-1, keepdims=True))
    return powers / jnp.sum(powers, axis=-1, keepdims=True)


def attend_block(heads, block, rows_ref, scales, gain_ref, turn_ref, column, row, kept_ref, out_ref):
    width = out_ref.shape[2]
    size = width // heads
    allowed = allowed_pairs(column, row)
    cosine, sine = turn_ref[0], turn_ref[1]
    for h in range(heads):
        parts = []
        for part in range(3):
            columns = pl.ds(part * width + h * size, size)
            values = rows_ref[block, :, columns]
            if part < 2:
                values = values * scales[part]
                values = values * gain_ref[part : part + 1, h * size : (h + 1) * size]
                values = turn(values, cosine, sine)
            parts.append(values.astype(LOW))
            kept_ref[block, :, columns] = parts[-1]
        query, key, value = parts
        probs = softmax(query, key, allowed).astype(LOW)
        out_ref[block, :, pl.ds(h * size, size)] = jnp.dot(
            probs, value, preferred_element_type=FULL
        ).astype(LOW)


def attention_kernel(size, dp_count, heads, *refs):
    x_ref, w_ref, gain_ref, gains_ref, turn_ref, column_ref, row_ref, sheet_ref, dy_ref = refs[:9]
    h_out, rows_out, scale_ref, kept_ref, out_ref, own_out, sheet_out, dy_out = refs[9:17]
    x_held, h_held, rows, sums, squares, got = refs[17:23]
    x_sem, h_sem, rows_sem, send_sem, recv_sem, stay_sem = refs[23:29]
    square_sems, line_sems, sheet_sems = refs[29:32], refs[32:37], refs[37:]
    line = LineGather(size // 2, GATHER_CUTS, [dy_ref], [dy_out], *line_sems)
    sheets = Sheets(size, dp_count, sheet_ref, sheet_out, *sheet_sems)
    small = Exchange("expert", size, (True,), (1,), [squares], [got], *square_sems)
    place, model_dim = sheets.place, x_ref.shape[2]
    width = out_ref.shape[2]

    def loading(g):
        return pltpu.make_async_copy(x_ref.at[g], x_held.at[g], x_sem.at[g])

    def leaving(g):
        return (
            pltpu.make_async_copy(h_held.at[g], h_out.at[g], h_sem.at[g]),
            pltpu.make_async_copy(rows.at[g], rows_out.at[g], rows_sem.at[g]),
        )

    for g in range(size):
        loading(g).start()
    greet("expert", [(peer, None) for peer in small.peers])
    greet("dp", [(peer, None) for peer in sheets.peers])
    pl.semaphore_wait(pltpu.get_barrier_semaphore(), size + dp_count - 2)
    sheets.begin()
    line.begin()
    sums[...] = jnp.zeros_like(sums)
    lanes = lax.broadcasted_iota(jnp.int32, sums.shape, 1)

    @pl.loop(0, size)
    def _(g):
        loading(g).wait()
        values = x_held[g].astype(FULL)
        hidden = (values * rms_scale(values) * gain_ref[...]).astype(LOW)
        h_held[g] = hidden
        projected = jnp.dot(hidden, w_ref[...], preferred_element_type=FULL)
        rows[g] = projected
        for copy in leaving(g):
            copy.start()
        for part in range(2):
            half = projected[:, part * width : (part + 1) * width]
            total = jnp.sum(half * half, axis=-1, keepdims=True)
            sums[...] += jnp.where(lanes == part * size + g, total, 0.0)

    squares[...] = sums[...].T[: 2 * size]
    small.begin()
    sheets.forward(1)
    small.arrive()
    total = sum(got[i] for i in range(size))
    sums[:, : 2 * size] = lax.rsqrt(total / model_dim + NORM_EPS).T

    def sending(g, source):
        columns = pl.ds(pl.multiple_of(source * width, 128), width)
        target = own_out.at[:, columns]
        return remote(out_ref.at[g], target, send_sem.at[g], recv_sem.at[source], {"expert": g})

    own_columns = pl.ds(pl.multiple_of(place * width, 128), width)
    staying = pltpu.make_async_copy(out_ref.at[place], own_out.at[:, own_columns], stay_sem.at[0])

    @pl.loop(0, size)
    def _(i):
        g = lax.rem(place + 1 + i, size)
        scales = [
            jnp.sum(jnp.where(lanes == part * size + g, sums[...], 0.0), axis=-1, keepdims=True)
            for part in range(2)
        ]
        scale_ref[g] = jnp.concatenate(scales, axis=1)
        attend_block(
            heads, g, rows, scales, gains_ref, turn_ref, column_ref[g], row_ref[g], kept_ref, out_ref
        )
        pl.when(g != place)(lambda: sending(g, place).start())
        pl.when(lax.rem(i, 2) == 1)(lambda: line.turn(lax.div(i, 2)))

    staying.start()

    @pl.loop(size // 2, 2 * size)
    def _(i):
        for step in range(2, size // 2):
            pl.when(i == (step - 1) * (size // 2))(lambda: sheets.forward(step))
        line.turn(i)
        after = i - size - size // 2
        pl.when((after >= 0) & (after < size // 2))(lambda: sheets.cross(after))


    @pl.loop(1, size)
    def _(i):
        peer = lax.rem(place + i, size)
        sending(peer, peer).wait_recv()
        sending(peer, place).wait_send()

    @pl.loop(0, size)
    def _(g):
        for copy in leaving(g):
            copy.wait()

    staying.wait()
    small.finish()
    line.finish()
    sheets.finish()


def attention(size, dp_count, heads, arrays, number):
    x_all, w_here, sheet, dy = arrays[0], arrays[1], arrays[7], arrays[8]
    _, tokens, model_dim = x_all.shape
    columns = w_here.shape[1]
    width = columns // 3
    sems = pltpu.SemaphoreType.DMA
    seqs = (size, tokens)
    small = (2 * size, tokens)
    return pl.pallas_call(
        functools.partial(attention_kernel, size, dp_count, heads),
        out_shape=[
            jax.ShapeDtypeStruct(x_all.shape, LOW),
            jax.ShapeDtypeStruct(seqs + (columns,), FULL),
            jax.ShapeDtypeStruct(seqs + (2,), FULL),
            jax.ShapeDtypeStruct(seqs + (columns,), LOW),
            jax.ShapeDtypeStruct(seqs + (width,), LOW),
            jax.ShapeDtypeStruct((tokens, model_dim), LOW),
            jax.ShapeDtypeStruct((dp_count, size) + sheet.shape, LOW),
            jax.ShapeDtypeStruct((size,) + dy.shape, LOW),
        ],
        in_specs=[ANY] + [VMEM] * 6 + [ANY] * 2,
        out_specs=[ANY] * 2 + [VMEM] * 3 + [ANY] * 3,
        scratch_shapes=[
            pltpu.VMEM(x_all.shape, LOW),
            pltpu.VMEM(x_all.shape, LOW),
            pltpu.VMEM(seqs + (columns,), FULL),
            pltpu.VMEM((tokens, 128), FULL),
            pltpu.VMEM(small, FULL),
            pltpu.VMEM((size,) + small, FULL),
            sems((size,)),
            sems((size,)),
            sems((size,)),
            sems((size,)),
            sems((size,)),
            sems((1,)),
        ]
        + Exchange.scratch(size, (1,))
        + LineGather.scratch(size, GATHER_CUTS, 1)
        + Sheets.scratch(size, dp_count),
        compiler_params=pltpu.CompilerParams(
            collective_id=number, has_side_effects=True, vmem_limit_bytes=48 << 20
        ),
        cost_estimate=pl.CostEstimate(
            flops=2 * x_all.size * columns, transcendentals=0, bytes_accessed=100_000_000
        ),
        name="attention",
    )(*arrays)


def attend_back_block(heads, block, grad_ref, refs, back_ref, dots_ref, lanes, gains_ref, w_sum):
    w_ref, kept_ref, out_ref, rows_ref, scale_ref, gain_ref, turn_ref, column_ref, row_ref = refs
    width = out_ref.shape[2]
    size = width // heads
    scaling = 1.0 / math.sqrt(size)
    allowed = allowed_pairs(column_ref[block], row_ref[block])
    cosine, sine = turn_ref[0], turn_ref[1]
    grad_rows = grad_ref[block]
    grad_out = across_cols(grad_rows, w_ref[...]).astype(LOW)
    w_sum[...] += contract_rows(out_ref[block], grad_rows)
    dots = [0.0, 0.0]
    for h in range(heads):
        mine = slice(h * size, (h + 1) * size)
        query, key, value = (
            kept_ref[block, :, pl.ds(p * width + h * size, size)] for p in range(3)
        )
        probs = softmax(query, key, allowed)
        grad = grad_out[:, mine]
        grad_value = contract_rows(probs.astype(LOW), grad)
        grad_probs = across_cols(grad, value)
        delta = jnp.sum(grad_probs * probs, axis=-1, keepdims=True)
        grad_scores = (probs * (grad_probs - delta)).astype(LOW)
        grad_query = jnp.dot(grad_scores, key, preferred_element_type=FULL) * scaling
        grad_key = contract_rows(grad_scores, query) * scaling
        for part, grad_turned in enumerate((grad_query, grad_key)):
            columns = pl.ds(part * width + h * size, size)
            grad_normed = turn(grad_turned, cosine, -sine)
            normed = rows_ref[block, :, columns] * scale_ref[block, :, part : part + 1]
            gains_ref[part : part + 1, mine] += jnp.sum(grad_normed * normed, axis=0, keepdims=True)
            weighted = grad_normed * gain_ref[part : part + 1, mine]
            dots[part] += jnp.sum(weighted * normed, axis=-1, keepdims=True)
            back_ref[block, :, columns] = weighted
        back_ref[block, :, pl.ds(2 * width + h * size, size)] = grad_value
    groups = grad_ref.shape[0]
    for part in range(2):
        dots_ref[...] += jnp.where(lanes == part * groups + block, dots[part], 0.0)


def attend_back_kernel(levels, cuts, heads, grad_ref, *refs):
    w_ref, others, refs = refs[0], refs[1:9], refs[9:]
    proj_ref, gains_ref, w_grad_ref, w_sum, held, w_held, back, dots, squares, got, w_sem = refs[:11]
    reads = (w_held,) + tuple(others)
    rows_ref, scale_ref = others[2:4]
    size, model_dim = 2 * levels, grad_ref.shape[1]
    line = LineGather(levels, cuts, [grad_ref], [held], *refs[11:16])
    small = Exchange("expert", size, (True,), (1,), [squares], [got], *refs[16:])
    mine = pl.ds(pl.multiple_of(line.place * w_held.shape[0], 128), w_held.shape[0])
    loading = pltpu.make_async_copy(w_ref.at[mine], w_held, w_sem.at[0])
    loading.start()
    greet("expert", [(peer, None) for peer in small.peers])
    pl.semaphore_wait(pltpu.get_barrier_semaphore(), size - 1)
    line.begin()
    w_sum[...] = jnp.zeros_like(w_sum)
    gains_ref[...] = jnp.zeros_like(gains_ref)
    dots[...] = jnp.zeros_like(dots)
    lanes = lax.broadcasted_iota(jnp.int32, dots.shape, 1)
    loading.wait()
    line.staying(0).wait()

    def landed(block):
        attend_back_block(heads, block, held, reads, back, dots, lanes, gains_ref, w_sum)

    line.main(landed)
    squares[...] = dots[...].T[: 2 * size]
    small.begin()
    wide = w_grad_ref.shape[2]
    for copy in range(w_grad_ref.shape[0]):
        w_grad_ref[copy] = w_sum[:, copy * wide : (copy + 1) * wide].astype(LOW)
    small.arrive()
    dots[:, : 2 * size] = sum(got[i] for i in range(size)).T / model_dim
    width = w_held.shape[0]

    @pl.loop(0, size)
    def _(block):
        for part in range(2):
            columns = pl.ds(part * width, width)
            scale = scale_ref[block, :, part : part + 1]
            mean = jnp.where(lanes == part * size + block, dots[...], 0.0)
            mean = jnp.sum(mean, axis=-1, keepdims=True)
            normed = rows_ref[block, :, columns] * scale
            proj_ref[block, :, columns] = (scale * (back[block, :, columns] - normed * mean)).astype(LOW)
        columns = pl.ds(2 * width, width)
        proj_ref[block, :, columns] = back[block, :, columns].astype(LOW)

    line.finish(held=1)
    small.finish()


def attend_back(size, dp_count, heads, grad, arrays, number):
    _, _, out, rows = arrays[:4]
    width = out.shape[2]
    tokens, model_dim = grad.shape
    small = (2 * size, tokens)
    return pl.pallas_call(
        functools.partial(attend_back_kernel, size // 2, GATHER_CUTS, heads),
        out_shape=[
            jax.ShapeDtypeStruct(rows.shape, LOW),
            jax.ShapeDtypeStruct((2, width), FULL),
            jax.ShapeDtypeStruct((dp_count, width, model_dim // dp_count), LOW),
        ],
        in_specs=[ANY] * 2 + [VMEM] * (len(arrays) - 1),
        out_specs=[VMEM] * 3,
        scratch_shapes=[
            pltpu.VMEM((width, model_dim), FULL),
            pltpu.VMEM((size, tokens, model_dim), LOW),
            pltpu.VMEM((width, model_dim), LOW),
            pltpu.VMEM(rows.shape, FULL),
            pltpu.VMEM((tokens, 128), FULL),
            pltpu.VMEM(small, FULL),
            pltpu.VMEM((size,) + small, FULL),
            pltpu.SemaphoreType.DMA((1,)),
        ]
        + LineGather.scratch(size, GATHER_CUTS, 1)
        + Exchange.scratch(size, (1,)),
        compiler_params=pltpu.CompilerParams(
            collective_id=number, has_side_effects=True, vmem_limit_bytes=48 << 20
        ),
        cost_estimate=pl.CostEstimate(flops=0, transcendentals=0, bytes_accessed=150_000_000),
        name="attend_back",
    )(grad, *arrays)


def on_device(
    dp_count,
    line_count,
    layer_input,
    out_cotangent,
    segments,
    routes,
    w_qkv,
    w_out,
    w_router,
    attn_gain,
    mlp_gain,
    query_gain,
    key_gain,
    w_gate_up,
    w_down,
):
    row_count, model_dim = layer_input.shape
    top_count = routes.shape[1]
    expert_count = w_router.shape[1]
    local_count = w_gate_up.shape[0]
    head_size = model_dim // HEADS
    head_cols = model_dim // line_count
    heads_here = head_cols // head_size
    capacity = (row_count * top_count * 9 // 8 + expert_count - 1) // expert_count
    scaling = 1.0 / math.sqrt(head_size)
    place = lax.axis_index("expert")
    shard = w_qkv.shape[0]

    numbers = jnp.concatenate([routes.T, segments, jnp.zeros((7, row_count), jnp.int32)], axis=0)
    x_all, numbers_all, qkv_here, router_full, gains = opening(
        line_count,
        dp_count,
        [layer_input, numbers],
        GATHER_CUTS,
        w_qkv,
        [w_router, jnp.stack([attn_gain, mlp_gain, query_gain, key_gain])],
        1,
    )
    qkv_here = qkv_here.reshape(model_dim, 3 * head_cols)
    router_full = router_full.reshape(model_dim, expert_count)
    gains = gains.transpose(2, 0, 1, 3).reshape(4, model_dim).astype(FULL)
    gain_attn, gain_mlp = gains[0], gains[1]
    both_gains = lax.dynamic_slice_in_dim(gains[2:], place * head_cols, head_cols, axis=1)

    routes_all = numbers_all[:, :top_count]
    segments_all = numbers_all[:, top_count]
    turns = rotary_tables(row_count, head_size)
    column, row = segments_all[:, :, None], segments_all[:, None, :]
    arrays = [x_all, qkv_here, gain_attn[None], both_gains, turns, column, row, w_out, out_cotangent]
    hidden_one, projected, scales, kept, attended, own_attended, out_full, dy_all = attention(
        line_count, dp_count, heads_here, arrays, 4
    )
    out_full = out_full.reshape(model_dim, model_dim)
    inputs = layer_input.astype(FULL)
    scale_attn = rms_scale(inputs)
    normed_attn = inputs * scale_attn
    residual = inputs + jnp.dot(own_attended, out_full, preferred_element_type=FULL)
    scale_mlp = rms_scale(residual)
    normed_mlp = residual * scale_mlp
    hidden_two = (normed_mlp * gain_mlp).astype(LOW)

    logits = jnp.dot(hidden_two, router_full, preferred_element_type=FULL)
    chosen = jnp.any(routes[:, :, None] == jnp.arange(expert_count)[None, None, :], axis=1)
    masked = jnp.where(chosen, logits, -1e30)
    powers = jnp.where(chosen, jnp.exp(masked - jnp.max(masked, axis=-1, keepdims=True)), 0.0)
    gates = powers / jnp.sum(powers, axis=-1, keepdims=True)

    local = place * local_count + jnp.arange(local_count)
    used = jnp.any(routes_all[:, None] == local[None, :, None, None], axis=2)
    position = jnp.arange(row_count)
    lower = (position[:, None] < position[None, :]).astype(LOW)
    rank = einsum("gju,ut->gjt", used.astype(LOW), lower).astype(jnp.int32)
    rank = jnp.where(used, rank, -1)
    spots = jnp.arange(capacity)
    table = (rank[:, :, None, :] == spots[None, None, :, None]).astype(LOW)
    returns = [(rank[:, j, :, None] == spots[None, None, :]).astype(LOW) for j in range(local_count)]
    slots = line_count * capacity
    flat_table = table.reshape(line_count, local_count * capacity, row_count)
    expert_rows, dy_rows, gates_all = gather_place(
        line_count, hidden_two, gates.T, flat_table, dy_all, local_count, 6
    )
    local_gates = lax.dynamic_slice_in_dim(gates_all, place * local_count, local_count, axis=1)
    slot_gates = jnp.sum(table.astype(FULL) * local_gates[:, :, None, :], axis=-1)
    slot_gates = slot_gates.transpose(1, 0, 2).reshape(local_count, slots, 1)
    out_rows, back_rows, slot_grads, grad_sums = [], [], [], []
    both_rows = model_dim // dp_count + w_down.shape[1] // dp_count
    for first, count in ((0, 1), (1, local_count - 1)):
        grads, out_row, back_row, dots = expert(
            first, count, dp_count, expert_rows, dy_rows, slot_gates, w_gate_up, w_down
        )
        grads = grads.reshape(-1, model_dim)
        grads = lax.psum_scatter(grads, "dp", scatter_dimension=0, tiled=True)
        grad_sums.append(grads.reshape(count, both_rows, model_dim))
        for kept_list, rows in ((out_rows, out_row), (back_rows, back_row), (slot_grads, dots)):
            kept_list.append(rows.reshape(count, line_count, capacity, rows.shape[2]))
    gate_rows = model_dim // dp_count
    grad_two, grad_gates = collect_reduce(
        line_count, returns, back_rows, slot_grads, flat_table, 8
    )
    grad_gates = grad_gates.reshape(expert_count, row_count).T
    grad_two = grad_two.astype(FULL)

    grad_out_rows = out_cotangent.astype(FULL)
    grad_logits = gates * (grad_gates - jnp.sum(gates * grad_gates, axis=-1, keepdims=True))
    grad_logits = grad_logits.astype(LOW)
    grad_router = contract_rows(grad_logits, hidden_two)
    grad_two = grad_two + contract_cols(grad_logits, router_full)
    grad_gain_mlp = jnp.sum(grad_two * normed_mlp, axis=0)
    grad_resid = grad_out_rows + norm_back(grad_two * gain_mlp, normed_mlp, scale_mlp)
    grad_attn = grad_resid.astype(LOW)

    arrays = [out_full, kept, attended, projected, scales, both_gains, turns, column, row]
    grad_proj, gain_pair, out_parts = attend_back(
        line_count, dp_count, heads_here, grad_attn, arrays, 11
    )

    shared = jnp.concatenate([grad_router, grad_gain_mlp[None]], axis=0)
    tall = shared.shape[0] + -shared.shape[0] % 8
    shared = jnp.pad(shared, ((0, tall - shared.shape[0]), (0, 0)))
    shared = shared.reshape(tall, dp_count, line_count, shard).transpose(2, 1, 0, 3)
    shared = shared.reshape(line_count, dp_count * tall, shard)
    shared = jnp.pad(shared, ((0, 0), (0, 0), (0, 128 - shard)))
    arrays = [grad_proj, qkv_here, hidden_one, gain_attn[None]]
    grad_one, mixture, sum_qkv, sum_out, gain_pair, gain_sum, shared = closing(
        line_count, dp_count, returns, out_rows, arrays, [out_parts, gain_pair], shared, 14
    )
    here = (lax.axis_index("dp") * line_count + place) * shard
    grad_gain_attn = lax.dynamic_slice_in_dim(gain_sum[0], here, shard)
    output = (residual + mixture.astype(FULL)).astype(LOW)
    sum_qkv = sum_qkv.transpose(1, 0, 2)
    first_sums, mixture = lax.optimization_barrier((grad_sums[0], mixture))
    wide = widen(0, local_count, gate_rows, first_sums)
    sum_gate_up, sum_down = widen(1, local_count, gate_rows, grad_sums[1], wide)
    shared = shared[:, :shard]
    grad_one = grad_one.astype(FULL)
    grad_inputs = grad_resid + norm_back(grad_one * gain_attn, normed_attn, scale_attn)
    return (
        output,
        grad_inputs,
        sum_qkv,
        sum_out,
        shared[:expert_count].T,
        grad_gain_attn,
        shared[expert_count],
        gain_pair[0],
        gain_pair[1],
        sum_gate_up,
        sum_down,
    )


def solution(mesh):
    both = ("dp", "expert")
    rows, flat = P(both, None), P(both)
    placed = (rows,) * 7 + (flat,) * 4 + (P("expert", None, None),) * 2
    return jax.shard_map(
        functools.partial(on_device, mesh.shape["dp"], mesh.shape["expert"]),
        mesh=mesh,
        in_specs=placed,
        out_specs=(
            rows,
            rows,
            P("dp", None, "expert"),
            P("expert", "dp"),
            rows,
            flat,
            flat,
            P("expert"),
            P("expert"),
            P("expert", "dp", None),
            P("expert", "dp", None),
        ),
        check_vma=False,
    )
```

```python
import functools
import math

import jax
import jax.numpy as jnp
import numpy as np
from jax import lax
from jax.experimental import pallas as pl
from jax.experimental.pallas import tpu as pltpu
from jax.sharding import PartitionSpec as P

HEADS = 16
NORM_EPS = 1e-05
MESH = pl.DeviceIdType.MESH
ANY = pl.BlockSpec(memory_space=pl.ANY)
LOW = jnp.bfloat16
GATHER_CUTS, REDUCE_CUTS = 4, 3
FULL = jnp.float32


def line_place():
    place = lax.axis_index("expert")
    level, side = lax.div(place, 2), lax.rem(place, 2)
    return place, level, side, place + 1 - 2 * side


def greet(axis, targets):
    barrier = pltpu.get_barrier_semaphore()
    for target, there in targets:

        def signal(target=target):
            pl.semaphore_signal(barrier, inc=1, device_id={axis: target}, device_id_type=MESH)

        if there is None:
            signal()
        else:
            pl.when(there)(signal)


def line_barrier(levels):
    place, level, _, other = line_place()
    has_up, has_down = level < levels - 1, level > 0
    greet("expert", [(other, None), (place + 2, has_up), (place - 2, has_down)])
    count = 1 + has_up.astype(jnp.int32) + has_down.astype(jnp.int32)
    pl.semaphore_wait(pltpu.get_barrier_semaphore(), count)


def around(axis, size):
    place = lax.axis_index(axis)
    return [lax.rem(place + shift, size) for shift in range(1, size)]


def remote(source, target, send, recv, device):
    return pltpu.make_async_remote_copy(
        src_ref=source,
        dst_ref=target,
        send_sem=send,
        recv_sem=recv,
        device_id=device,
        device_id_type=MESH,
    )


class LineGather:
    def __init__(self, levels, cuts, ins, outs, up_sem, down_sem, side_sem, recv_sem, own_sem):
        self.levels, self.cuts, self.ins, self.outs = levels, cuts, ins, outs
        self.up_sem, self.down_sem, self.side_sem = up_sem, down_sem, side_sem
        self.recv_sem, self.own_sem = recv_sem, own_sem
        self.place, self.level, self.side, self.other = line_place()
        self.has_up, self.has_down = self.level < levels - 1, self.level > 0

    @staticmethod
    def scratch(size, cuts, count):
        levels, total = size // 2, cuts + count - 1
        shapes = ((levels, total), (levels, total), (2 * levels - 1, total), (size, total))
        return [pltpu.SemaphoreType.DMA(shape) for shape in shapes + ((count,),)]

    def pieces(self):
        return [(0, k) for k in range(self.cuts)] + [(i, 0) for i in range(1, len(self.ins))]

    def staying(self, i):
        target = self.outs[i].at[self.place]
        return pltpu.make_async_copy(self.ins[i], target, self.own_sem.at[i])

    def sending(self, piece, block, own, sem, target):
        i, k = piece
        landing, source, q = self.outs[i].at[block], self.ins[i], k
        if i:
            q = self.cuts + i - 1
        else:
            rows = source.shape[0] // self.cuts
            landing, source = landing.at[pl.ds(k * rows, rows)], source.at[pl.ds(k * rows, rows)]
        sems = sem.at[q], self.recv_sem.at[block, q]
        return remote(source if own else landing, landing, *sems, {"expert": target})

    def up(self, piece, step, own=False):
        block = self.place - 2 * step
        return self.sending(piece, block, own, self.up_sem.at[step], self.place + 2)

    def down(self, piece, step, own=False):
        block = self.place + 2 * step
        return self.sending(piece, block, own, self.down_sem.at[step], self.place - 2)

    def across(self, piece, step, own=False):
        sem = self.side_sem.at[step + self.levels - 1]
        return self.sending(piece, self.place - 2 * step, own, sem, self.other)

    def begin(self):
        for piece in self.pieces():
            pl.when(self.has_up)(self.up(piece, 0, True).start)
            pl.when(self.has_down)(self.down(piece, 0, True).start)
        for piece in self.pieces():
            self.across(piece, 0, True).start()
        for i in range(len(self.ins)):
            self.staying(i).start()

    def forward(self, step, piece):
        @pl.when(self.level >= step)
        def _():
            self.across(piece, step).wait_recv()
            pl.when(self.has_up)(self.up(piece, step).start)
            self.across(piece, step).start()

        @pl.when(self.level + step < self.levels)
        def _():
            self.across(piece, -step).wait_recv()
            pl.when(self.has_down)(self.down(piece, step).start)
            self.across(piece, -step).start()

    def land_across(self, block):
        for piece in self.pieces():
            self.sending(piece, block, False, self.side_sem.at[0], self.other).wait_recv()

    def turn(self, turn, landed=None):
        levels, cuts = self.levels, self.cuts
        step, k = lax.div(turn, 4) + 1, lax.rem(turn, 4)

        @pl.when((step < levels) & (k < cuts))
        def _():
            self.forward(step, (0, k))

            @pl.when(k == cuts - 1)
            def _():
                for i in range(1, len(self.ins)):
                    self.forward(step, (i, 0))

        group, sign, crossed = step - 1, 2 * lax.rem(k, 2) - 1, lax.div(k, 2)
        crossed = jnp.where(group == 0, k, crossed)
        far = jnp.where(group == 0, self.level, self.level + sign * group)

        @pl.when((far >= 0) & (far < levels) & ((group > 0) | (k < 2)))
        def _():
            block = 2 * far + self.side + crossed * (1 - 2 * self.side)

            @pl.when(crossed == 1)
            def _():
                self.land_across(block)

            if landed:
                landed(block)

    def main(self, landed=None):
        @pl.loop(0, 4 * self.levels)
        def _(turn):
            self.turn(turn, landed)

    def finish(self, held=0):
        for piece in self.pieces():
            self.across(piece, 0).wait_send()
            for step in range(self.levels):
                above, below = self.level >= step, self.level + step < self.levels
                pl.when(self.has_up & above)(self.up(piece, step).wait_send)
                pl.when(self.has_down & below)(self.down(piece, step).wait_send)
                if step:
                    pl.when(above)(self.across(piece, step).wait_send)
                    pl.when(below)(self.across(piece, -step).wait_send)
        for i in range(held, len(self.ins)):
            self.staying(i).wait()


def call(kernel, name, number, outs, scratch, arrays, moved):
    return pl.pallas_call(
        kernel,
        out_shape=outs,
        in_specs=[ANY] * len(arrays),
        out_specs=[ANY] * len(outs),
        scratch_shapes=scratch,
        compiler_params=pltpu.CompilerParams(
            collective_id=number, has_side_effects=True, vmem_limit_bytes=48 << 20
        ),
        cost_estimate=pl.CostEstimate(flops=0, transcendentals=0, bytes_accessed=moved),
        name=name,
    )(*arrays)


class LineReduce:
    def __init__(self, levels, cuts, parts, total, own, beside, rising, falling, *sems):
        self.levels, self.cuts, self.parts, self.total = levels, cuts, parts, total
        self.made = parts.shape[0] == levels
        self.own, self.beside, self.rising, self.falling = own, beside, rising, falling
        self.load_sem, self.side_send, self.side_recv = sems[:3]
        self.up_send, self.up_recv, self.down_send, self.down_recv, self.out_sem = sems[3:]
        self.place, self.level, self.side, self.other = line_place()
        self.has_up, self.has_down = self.level < levels - 1, self.level > 0
        self.rows = parts.shape[1] // cuts

    @staticmethod
    def scratch(size, block, dtype, cuts):
        levels = size // 2
        return (
            [pltpu.VMEM((levels,) + block, dtype)] * 2
            + [pltpu.VMEM((levels - 1,) + block, dtype)] * 2
            + [pltpu.SemaphoreType.DMA((levels, cuts))] * 7
            + [pltpu.SemaphoreType.DMA((cuts,))]
        )

    def cut(self, ref, block, k):
        return ref.at[block, pl.ds(k * self.rows, self.rows)]

    def loading(self, far, k):
        source = self.cut(self.parts, 2 * far + self.side, k)
        return pltpu.make_async_copy(source, self.cut(self.own, far, k), self.load_sem.at[far, k])

    def across(self, far, k):
        source = self.cut(self.parts, far if self.made else 2 * far + 1 - self.side, k)
        sems = self.side_send.at[far, k], self.side_recv.at[far, k]
        return remote(source, self.cut(self.beside, far, k), *sems, {"expert": self.other})

    def up(self, far, k):
        sems = self.up_send.at[far, k], self.up_recv.at[far, k]
        target = {"expert": self.place + 2}
        return remote(self.cut(self.own, far, k), self.cut(self.rising, far - 1, k), *sems, target)

    def down(self, far, k):
        sems = self.down_send.at[far, k], self.down_recv.at[far, k]
        target = {"expert": self.place - 2}
        return remote(self.cut(self.own, far, k), self.cut(self.falling, far, k), *sems, target)

    def value(self, ref, block, k):
        return self.cut(ref, block, k)[...].astype(FULL)

    def load(self):
        for i in range(self.levels):
            for k in range(self.cuts):
                self.loading(self.far(i), k).start()

    def begin(self):
        for i in range(self.levels):
            for k in range(self.cuts):
                self.across(self.far(i), k).start()

    def far(self, i):
        return jnp.where(lax.rem(i, 2) == 0, self.levels - 1 - lax.div(i, 2), lax.div(i, 2))

    def prepare(self, turn, make):
        far = self.far(lax.div(turn, 2))

        @pl.when(lax.rem(turn, 2) == 0)
        def _():
            make(2 * far + 1 - self.side, self.parts.at[far])
            for k in range(self.cuts):
                self.across(far, k).start()

        @pl.when(lax.rem(turn, 2) == 1)
        def _():
            make(2 * far + self.side, self.own.at[far])

    def pair(self, far, k):
        if not self.made:
            self.loading(far, k).wait()
        self.across(far, k).wait_recv()
        return self.value(self.own, far, k) + self.value(self.beside, far, k)

    def store(self, far, k, total):
        self.cut(self.own, far, k)[...] = total.astype(self.own.dtype)

    def toward(self, far, k, ahead, behind, move, arrived, shift):
        @pl.when(ahead & behind)
        def _():
            both = self.pair(far, k)
            move(far, k).wait_recv()
            self.store(far, k, both + self.value(arrived, far - shift, k))

        @pl.when(ahead & jnp.logical_not(behind))
        def _():
            self.store(far, k, self.pair(far, k))

        pl.when(ahead)(move(far, k).start)

    def main(self, beside=None):
        levels, cuts = self.levels, self.cuts
        lower = self.level < levels // 2

        def rise(far, k):
            self.toward(far, k, self.level < far, self.has_down, self.up, self.rising, 1)

        def fall(far, k):
            self.toward(far, k, self.level > far, self.has_up, self.down, self.falling, 0)

        @pl.loop(0, 2 * cuts)
        def _(turn):
            near, k = turn < cuts, lax.rem(turn, cuts)
            if beside:
                beside(turn)
            upward = (near & lower) | jnp.logical_not(near | lower)
            pl.when(upward)(lambda: rise(levels - 1, k))
            pl.when(jnp.logical_not(upward))(lambda: fall(0, k))

        @pl.loop(2 * cuts, levels * cuts)
        def _(turn):
            step, k = lax.div(turn, cuts) - 1, lax.rem(turn, cuts)
            if beside:
                beside(turn)
            rise(levels - 1 - step, k)
            fall(step, k)

    def settle(self):
        @pl.loop(0, self.cuts)
        def _(k):
            self.store(self.level, k, self.pair(self.level, k))
            for there, move, arrived, shift in (
                (self.has_down, self.up, self.rising, 1),
                (self.has_up, self.down, self.falling, 0),
            ):

                @pl.when(there)
                def _():
                    move(self.level, k).wait_recv()
                    total = self.value(self.own, self.level, k)
                    total += self.value(arrived, self.level - shift, k)
                    self.store(self.level, k, total)

            self.leaving(k).start()

    def leaving(self, k):
        target = self.total.at[pl.ds(k * self.rows, self.rows)]
        return pltpu.make_async_copy(self.cut(self.own, self.level, k), target, self.out_sem.at[k])

    def finish(self):
        for k in range(self.cuts):
            self.leaving(k).wait()
            for far in range(self.levels):
                self.across(far, k).wait_send()
                pl.when(self.level < far)(self.up(far, k).wait_send)
                pl.when(self.level > far)(self.down(far, k).wait_send)


class Exchange:
    def __init__(self, axis, size, spread, cuts, ins, outs, send_sem, recv_sem, own_sem):
        self.axis, self.spread, self.ins, self.outs = axis, spread, ins, outs
        self.send_sem, self.recv_sem, self.own_sem = send_sem, recv_sem, own_sem
        self.cuts = cuts
        self.firsts = [sum(cuts[:i]) for i in range(len(cuts))]
        self.pieces = [(i, k) for i in range(len(cuts)) for k in range(cuts[i])]
        self.place, self.peers = lax.axis_index(axis), around(axis, size)

    @staticmethod
    def scratch(size, cuts):
        sems = pltpu.SemaphoreType.DMA
        return [sems((sum(cuts), size)), sems((sum(cuts), size)), sems((len(cuts),))]

    def source(self, i, block):
        return self.ins[i] if self.spread[i] else self.ins[i].at[block]

    def staying(self, i):
        target = self.outs[i].at[self.place]
        return pltpu.make_async_copy(self.source(i, self.place), target, self.own_sem.at[i])

    def sending(self, i, k, shift, landing):
        peer = self.peers[shift]
        source, target, q = self.source(i, peer), self.outs[i].at[landing], self.firsts[i] + k
        if self.cuts[i] > 1:
            rows = target.shape[0] // self.cuts[i]
            source, target = source.at[pl.ds(k * rows, rows)], target.at[pl.ds(k * rows, rows)]
        sems = self.send_sem.at[q, shift], self.recv_sem.at[q, landing]
        return remote(source, target, *sems, {self.axis: peer})

    def send(self, i, k):
        for shift in range(len(self.peers)):
            self.sending(i, k, shift, self.place).start()

    def stay(self):
        for i in range(len(self.spread)):
            self.staying(i).start()

    def begin(self):
        for i, k in self.pieces:
            self.send(i, k)
        self.stay()

    def land(self):
        for shift, peer in enumerate(self.peers):
            for i, k in self.pieces:
                self.sending(i, k, shift, peer).wait_recv()

    def arrive(self):
        self.land()
        for i in range(len(self.spread)):
            self.staying(i).wait()

    def finish(self):
        for shift in range(len(self.peers)):
            for i, k in self.pieces:
                self.sending(i, k, shift, self.place).wait_send()


def exchange_kernel(axis, size, spread, *refs):
    count = len(spread)
    ins, outs, sems = refs[:count], refs[count : 2 * count], refs[2 * count :]
    moves = Exchange(axis, size, spread, (1,) * count, ins, outs, *sems)
    greet(axis, [(peer, None) for peer in moves.peers])
    pl.semaphore_wait(pltpu.get_barrier_semaphore(), size - 1)
    moves.begin()
    moves.arrive()
    moves.finish()


def exchange_outs(size, arrays, spread):
    return [
        jax.ShapeDtypeStruct((size,) + a.shape if flat else a.shape, a.dtype)
        for a, flat in zip(arrays, spread)
    ]


def exchange(axis, size, arrays, spread, number):
    return call(
        functools.partial(exchange_kernel, axis, size, tuple(spread)),
        "exchange_" + axis,
        number,
        exchange_outs(size, arrays, spread),
        Exchange.scratch(size, (1,) * len(arrays)),
        arrays,
        30_000_000,
    )


def opening_kernel(size, dp_count, count, cuts, *refs):
    ins, (w_ref, *small_refs) = refs[:count], refs[count : count + 3]
    outs, rest = refs[count + 3 : 2 * count + 3], refs[2 * count + 6 :]
    w_out, *small_outs = refs[2 * count + 3 : 2 * count + 6]
    line = LineGather(size // 2, cuts, ins, outs, *rest[:5])
    send_sem, recv_sem, own_sem = rest[5:8]
    place, mine = line.place, lax.axis_index("dp")
    peers = around("expert", size)
    width = w_out.shape[3] // 3
    lands = [w_out] + small_outs
    across = Exchange(
        "dp", dp_count, (True,) * 3, (size,) * 3, [a.at[mine] for a in lands], lands, *rest[8:]
    )
    greet("expert", [(peer, None) for peer in peers])
    greet("dp", [(peer, None) for peer in across.peers])
    pl.semaphore_wait(pltpu.get_barrier_semaphore(), size + dp_count - 2)

    def ends(peer, landing, j):
        if j >= 3:
            return small_refs[j - 3], small_outs[j - 3].at[mine, landing]
        start = pl.multiple_of(j * width * size + peer * width, 128)
        target = w_out.at[mine, landing, :, pl.ds(j * width, width)]
        return w_ref.at[:, pl.ds(start, width)], target

    def sending(shift, landing, j):
        source, target = ends(peers[shift], landing, j)
        sems = send_sem.at[shift, j], recv_sem.at[landing, j]
        return remote(source, target, *sems, {"expert": peers[shift]})

    own = [pltpu.make_async_copy(*ends(place, place, j), own_sem.at[j]) for j in range(5)]
    for shift in range(size - 1):
        for j in range(5):
            sending(shift, place, j).start()
    for copy in own:
        copy.start()
    line.begin()
    for copy in own:
        copy.wait()
    for i in range(3):
        across.send(i, place)
    for shift, peer in enumerate(peers):
        for j in range(5):
            sending(shift, peer, j).wait_recv()
        for i in range(3):
            across.send(i, peer)
    line.main()
    line.finish()
    for shift in range(size - 1):
        for j in range(5):
            sending(shift, place, j).wait_send()
    across.land()
    across.finish()


def opening(size, dp_count, arrays, cuts, weights, small, number):
    sems = pltpu.SemaphoreType.DMA
    outs = [jax.ShapeDtypeStruct((size,) + a.shape, a.dtype) for a in arrays]
    rows, columns = weights.shape
    whole = (dp_count, size, rows)
    outs.append(jax.ShapeDtypeStruct(whole + (columns // size,), weights.dtype))
    outs += [jax.ShapeDtypeStruct((dp_count, size) + a.shape, a.dtype) for a in small]
    return call(
        functools.partial(opening_kernel, size, dp_count, len(arrays), cuts),
        "opening",
        number,
        outs,
        LineGather.scratch(size, cuts, len(arrays))
        + [sems((size, 5)), sems((size, 5)), sems((5,))]
        + Exchange.scratch(dp_count, (size,) * 3),
        list(arrays) + [weights] + small,
        200_000_000,
    )


class Sheets:
    def __init__(self, size, dp_count, source, target, *sems):
        self.levels, self.dp_count, self.ins, self.out = size // 2, dp_count, source, target
        self.up_send, self.down_send, self.line_recv, self.dp_send, self.dp_recv = sems[:5]
        self.side_send, self.side_recv, self.own_sem = sems[5:]
        self.place, self.level, self.side, self.other = line_place()
        self.has_up, self.has_down = self.level < self.levels - 1, self.level > 0
        self.mine, self.peers = lax.axis_index("dp"), around("dp", dp_count)

    @staticmethod
    def scratch(size, dp_count):
        sems, levels = pltpu.SemaphoreType.DMA, size // 2
        return [sems((levels,))] * 3 + [sems((dp_count, levels))] * 4 + [sems((1,))]

    def along(self, far, own, send, target):
        landing = self.out.at[self.mine, 2 * far + self.side]
        source = self.ins if own else landing
        return remote(source, landing, send.at[far], self.line_recv.at[far], {"expert": target})

    def up(self, far, own=False):
        return self.along(far, own, self.up_send, self.place + 2)

    def down(self, far, own=False):
        return self.along(far, own, self.down_send, self.place - 2)

    def over(self, far, shift, copy, own=False):
        landing = self.out.at[copy, 2 * far + self.side]
        source = self.ins if own else landing
        sems = self.dp_send.at[shift, far], self.dp_recv.at[copy, far]
        return remote(source, landing, *sems, {"dp": self.peers[shift]})

    def across(self, far, copy, whose, own=False):
        landing = self.out.at[copy, 2 * far + whose]
        source = self.ins if own else landing
        sems = self.side_send.at[copy, far], self.side_recv.at[copy, far]
        return remote(source, landing, *sems, {"expert": self.other})

    def spread(self, far, own=False):
        for shift in range(self.dp_count - 1):
            self.over(far, shift, self.mine, own).start()
        self.across(far, self.mine, self.side, own).start()

    def staying(self):
        target = self.out.at[self.mine, self.place]
        return pltpu.make_async_copy(self.ins, target, self.own_sem.at[0])

    def begin(self):
        pl.when(self.has_up)(self.up(self.level, True).start)
        pl.when(self.has_down)(self.down(self.level, True).start)
        self.spread(self.level, True)
        self.staying().start()

    def forward(self, step):
        @pl.when(self.level >= step)
        def _():
            self.up(self.level - step).wait_recv()
            pl.when(self.has_up)(self.up(self.level - step).start)
            self.spread(self.level - step)

        @pl.when(self.level + step < self.levels)
        def _():
            self.down(self.level + step).wait_recv()
            pl.when(self.has_down)(self.down(self.level + step).start)
            self.spread(self.level + step)

    def cross(self, far):
        for shift, peer in enumerate(self.peers):
            self.over(far, shift, peer).wait_recv()
            self.across(far, peer, self.side).start()

    def finish(self):
        @pl.loop(0, self.levels)
        def _(far):
            pl.when(self.has_up & (self.level >= far))(self.up(far).wait_send)
            pl.when(self.has_down & (self.level <= far))(self.down(far).wait_send)
            for shift in range(self.dp_count - 1):
                self.over(far, shift, self.mine).wait_send()
            for copy in range(self.dp_count):
                self.across(far, copy, 1 - self.side).wait_recv()
                self.across(far, copy, self.side).wait_send()

        self.staying().wait()


VMEM = pl.BlockSpec(memory_space=pltpu.VMEM)
COLUMNS = 512


def gather_place_kernel(levels, cuts, *refs):
    rows_ref, gates_ref, table_ref, dy_ref, x_out, dy_out, gates_out = refs[:7]
    held, dy_held, x_stage, dy_stage = refs[7:11]
    line_sems, (dy_sem, x_sems, dy_sems) = refs[11:16], refs[16:]
    line = LineGather(levels, cuts, [rows_ref, gates_ref], [held, gates_out], *line_sems)
    size, width = 2 * levels, held.shape[2]
    _, local_count, capacity, _ = x_stage.shape

    def leaving(block, stage, out, sems):
        target = out.at[:, pl.ds(pl.multiple_of(block * capacity, 8), capacity)]
        return pltpu.make_async_copy(stage.at[block], target, sems.at[block])

    def place(block, rows, stage, out, sems):
        table = table_ref[block]

        @pl.loop(0, width // COLUMNS)
        def _(n):
            columns = pl.ds(pl.multiple_of(n * COLUMNS, COLUMNS), COLUMNS)
            placed = jnp.dot(table, rows[block, :, columns], preferred_element_type=FULL)
            for j in range(local_count):
                part = placed[j * capacity : (j + 1) * capacity]
                stage[block, j, :, columns] = part.astype(stage.dtype)

        leaving(block, stage, out, sems).start()

    def place_x(block):
        place(block, held, x_stage, x_out, x_sems)

    loading = pltpu.make_async_copy(dy_ref, dy_held, dy_sem.at[0])
    loading.start()
    line_barrier(levels)
    line.begin()
    loading.wait()

    @pl.loop(0, size)
    def _(block):
        place(block, dy_held, dy_stage, dy_out, dy_sems)

    line.staying(0).wait()
    line.main(place_x)
    line.finish(held=1)

    @pl.loop(0, size)
    def _(block):
        leaving(block, x_stage, x_out, x_sems).wait()
        leaving(block, dy_stage, dy_out, dy_sems).wait()


def gather_place(size, rows, gates, table, dy, local_count, number):
    cuts = GATHER_CUTS
    tokens, width = rows.shape
    capacity = table.shape[1] // local_count
    placed = jax.ShapeDtypeStruct((local_count, size * capacity, width), rows.dtype)
    sems = pltpu.SemaphoreType.DMA
    return pl.pallas_call(
        functools.partial(gather_place_kernel, size // 2, cuts),
        out_shape=[placed, placed, jax.ShapeDtypeStruct((size,) + gates.shape, gates.dtype)],
        in_specs=[ANY, ANY, VMEM, ANY],
        out_specs=[ANY] * 3,
        scratch_shapes=[pltpu.VMEM((size, tokens, width), rows.dtype)] * 2
        + [pltpu.VMEM((size, local_count, capacity, width), rows.dtype)] * 2
        + LineGather.scratch(size, cuts, 2)
        + [sems((1,)), sems((size,)), sems((size,))],
        compiler_params=pltpu.CompilerParams(
            collective_id=number, has_side_effects=True, vmem_limit_bytes=48 << 20
        ),
        cost_estimate=pl.CostEstimate(
            flops=4 * table.size * width, transcendentals=0, bytes_accessed=150_000_000
        ),
        name="gather_place",
    )(rows, gates, table, dy)


def several(index, turns, count, work):
    share = -(-count // turns)
    for i in range(share):
        item = share * index + i
        pl.when((index >= 0) & (item < count))(lambda item=item: work(item))


def split_at(arrays, j, block):
    for array in arrays:
        if j < array.shape[0]:
            return array.at[j, block]
        j -= array.shape[0]


def collect_block(tables, slots, block, target):
    @pl.loop(0, target.shape[1] // COLUMNS)
    def _(n):
        columns = pl.ds(pl.multiple_of(n * COLUMNS, COLUMNS), COLUMNS)
        total = 0.0
        for j, table in enumerate(tables):
            rows = split_at(slots, j, block)[:, columns]
            total += jnp.dot(table[block], rows, preferred_element_type=FULL)
        target[:, columns] = total.astype(target.dtype)


def collect_reduce_kernel(levels, cuts, local_count, *refs):
    tables, refs = refs[:local_count], refs[local_count:]
    slots, dots, (table_ref, total_ref, gates_out, away) = refs[:2], refs[2:4], refs[4:8]
    rest, (gates, *sems) = refs[8:20], refs[20:]
    line = LineReduce(levels, cuts, away, total_ref, *rest)
    small = Exchange("expert", 2 * levels, (False,), (1,), [gates], [gates_out], *sems)
    greet("expert", [(peer, None) for peer in small.peers])
    pl.semaphore_wait(pltpu.get_barrier_semaphore(), 2 * levels - 1)
    make = functools.partial(collect_block, tables, slots)

    @pl.loop(0, 4)
    def _(turn):
        line.prepare(turn, make)

    def gate_block(block):
        table = table_ref[block].astype(FULL)
        capacity = table.shape[0] // local_count
        for j in range(local_count):
            part = table[j * capacity : (j + 1) * capacity] * split_at(dots, j, block)[...]
            gates[block, j : j + 1] = jnp.sum(part, axis=0, keepdims=True)

    def beside(turn):
        pl.when(turn + 4 < 2 * levels)(lambda: line.prepare(turn + 4, make))
        turns = levels * cuts - levels
        several(turn - levels, turns, 2 * levels, gate_block)
        pl.when(turn == levels * cuts - 1)(small.begin)

    line.main(beside)
    line.settle()
    small.arrive()
    line.finish()
    small.finish()


def collect_reduce(size, tables, slots, dots, table, number):
    levels, cuts = size // 2, REDUCE_CUTS
    block = (tables[0].shape[1], slots[0].shape[3])
    kind = slots[0].dtype
    gates = (size, len(tables), block[0])
    return pl.pallas_call(
        functools.partial(collect_reduce_kernel, levels, cuts, len(tables)),
        out_shape=[jax.ShapeDtypeStruct(block, kind), jax.ShapeDtypeStruct(gates, FULL)],
        in_specs=[VMEM] * (len(tables) + 5),
        out_specs=[ANY, ANY],
        scratch_shapes=[pltpu.VMEM((levels,) + block, kind)]
        + LineReduce.scratch(size, block, kind, cuts)
        + [pltpu.VMEM(gates, FULL)]
        + Exchange.scratch(size, (1,)),
        compiler_params=pltpu.CompilerParams(
            collective_id=number, has_side_effects=True, vmem_limit_bytes=48 << 20
        ),
        cost_estimate=pl.CostEstimate(flops=0, transcendentals=0, bytes_accessed=150_000_000),
        name="collect_reduce",
    )(*tables, *slots, *dots, table)


class SquareSum:
    def __init__(self, cuts, parts, near, far, send_sem, recv_sem, last_send, last_recv):
        self.cuts, self.parts, self.near, self.far = cuts, parts, near, far
        self.send_sem, self.recv_sem, self.last_send, self.last_recv = send_sem, recv_sem, last_send, last_recv
        self.mine = lax.axis_index("dp")
        slow, fast = lax.div(self.mine, 2), lax.rem(self.mine, 2)
        self.along = 2 * slow + 1 - fast, 2 * (1 - slow) + fast
        self.across = 2 * (1 - slow) + 1 - fast
        self.step = parts.shape[1] // cuts

    @staticmethod
    def scratch(cuts, shape, dtype):
        sems = pltpu.SemaphoreType.DMA
        buffers = [pltpu.VMEM((2,) + shape[1:], dtype), pltpu.VMEM(shape[1:], dtype)]
        return buffers + [sems((cuts, 2)), sems((cuts, 2)), sems((cuts,)), sems((cuts,))]

    def rows(self, k):
        return pl.ds(pl.multiple_of(k * self.step, self.step), self.step)

    def peer(self, k, later):
        half = lax.div(k, self.cuts // 2)
        return jnp.where(half == later, self.along[0], self.along[1])

    def first(self, k, kind):
        peer, rows = self.peer(k, 0), self.rows(k)
        source = self.parts.at[self.across if kind else peer, rows]
        sems = self.send_sem.at[k, kind], self.recv_sem.at[k, kind]
        return remote(source, self.near.at[kind, rows], *sems, {"dp": peer})

    def second(self, k):
        peer, rows = self.peer(k, 1), self.rows(k)
        sems = self.last_send.at[k], self.last_recv.at[k]
        return remote(self.parts.at[peer, rows], self.far.at[rows], *sems, {"dp": peer})

    def begin(self, k):
        self.first(k, 0).start()
        self.first(k, 1).start()

    def turn(self, k):
        self.first(k, 1).wait_recv()
        peer, rows = self.peer(k, 1), self.rows(k)
        total = self.parts[peer, rows].astype(FULL) + self.near[1, rows].astype(FULL)
        self.parts[peer, rows] = total.astype(self.parts.dtype)
        self.second(k).start()

    def arrive(self):
        for k in range(self.cuts):
            self.first(k, 0).wait_recv()
            self.second(k).wait_recv()

    def total(self, columns):
        own = self.parts[self.mine, :, columns].astype(FULL)
        return own + self.near[0, :, columns].astype(FULL) + self.far[:, columns].astype(FULL)

    def finish(self):
        for k in range(self.cuts):
            self.first(k, 0).wait_send()
            self.first(k, 1).wait_send()
            self.second(k).wait_send()


def closing_kernel(size, dp_count, local_count, cuts, sum_cuts, *refs):
    refs, levels = list(refs), size // 2

    def take(count):
        taken = refs[:count]
        del refs[:count]
        return taken

    tables, slots = take(local_count), take(2)
    proj_ref, w_ref, h_ref, gain_ref, out_parts, gain_pair, shared_ref = take(7)
    back_out, mixed_out, qkv_out, w_out, gains_out, gain_out, shared_out = take(7)
    back = LineReduce(levels, cuts, *take(1), back_out, *take(12))
    mixed = LineReduce(levels, cuts, *take(1), mixed_out, *take(12))
    square = dp_count == 4
    if square:
        qkv_parts, gains_got = take(2)
        qkv_sum = SquareSum(sum_cuts[0], qkv_parts, *take(6))
        (out_own,) = take(1)
        out_sum = SquareSum(sum_cuts[1], out_own, *take(6))
        out_own[...] = out_parts[...]
    else:
        qkv_parts, gains_got, qkv_got, out_got = take(4)
    got, half, last, gain_sum, gain_got, gain_half, gain_last = take(7)
    parts, lands, spread, some = [gain_pair], [gains_got], (True,), (1,)
    if not square:
        parts, lands = parts + [qkv_parts, out_parts], lands + [qkv_got, out_got]
        spread, some = (True, False, False), (1,) + sum_cuts
    sums = Exchange("dp", dp_count, spread, some, parts, lands, *take(3))
    first = Exchange("expert", size, (False,), (1,), [shared_ref], [got], *take(3))
    second = Exchange("dp", dp_count, (False,), (1,), [half], [last], *take(3))
    gain_first = Exchange("expert", size, (True,), (1,), [gain_sum], [gain_got], *take(3))
    gain_second = Exchange("dp", dp_count, (True,), (1,), [gain_half], [gain_last], *take(3))
    greet("expert", [(peer, None) for peer in first.peers])
    greet("dp", [(peer, None) for peer in sums.peers])
    pl.semaphore_wait(pltpu.get_barrier_semaphore(), size + dp_count - 2)
    first.begin()
    sums.staying(0).start()
    if not square:
        sums.staying(2).start()
    gain_sum[...] = jnp.zeros_like(gain_sum)
    groups, tokens, model_dim = h_ref.shape
    tall, high = half.shape[1], model_dim // dp_count

    def make_back(block, target):
        @pl.loop(0, model_dim // COLUMNS)
        def _(n):
            columns = pl.ds(pl.multiple_of(n * COLUMNS, COLUMNS), COLUMNS)
            grad = across_cols(proj_ref[block], w_ref[columns, :])
            target[:, columns] = grad.astype(target.dtype)
            weighted = grad * h_ref[block, :, columns].astype(FULL)
            gain_sum[:, columns] += jnp.sum(weighted, axis=0, keepdims=True)

    def piece(turn):
        k, copy = lax.div(turn, dp_count), lax.rem(turn, dp_count)
        columns = pl.ds(pl.multiple_of(copy * high + k * 128, 128), 128)
        rows = h_ref[:, :, columns].reshape(groups * tokens, 128)
        grads = proj_ref[...].reshape(groups * tokens, proj_ref.shape[2])
        products = contract_rows(rows, grads).astype(LOW)
        qkv_parts[copy, pl.ds(pl.multiple_of(k * 128, 128), 128)] = products
        if square:
            pl.when(copy == dp_count - 1)(lambda: qkv_sum.begin(k))
        else:
            pl.when(copy == dp_count - 1)(lambda: sums.send(1, k))
            pl.when(turn == count - 1)(lambda: sums.staying(1).start())

    make_mixed = functools.partial(collect_block, tables, slots)
    ahead = levels

    @pl.loop(0, ahead)
    def _(turn):
        back.prepare(turn, make_back)

    rest, count = levels * cuts - ahead, sum_cuts[0] * dp_count

    def beside(turn):
        later = turn - ahead
        pl.when(turn + ahead < 2 * levels)(lambda: back.prepare(turn + ahead, make_back))
        send = out_sum.begin if square else functools.partial(sums.send, 2)
        pl.when(turn < sum_cuts[1])(lambda: send(turn))
        pl.when(turn == sum_cuts[1])(lambda: sums.send(0, 0))
        pl.when(later == 0)(gain_first.begin)
        several(later, rest, 2 * levels, lambda i: mixed.prepare(i, make_mixed))
        several(later, 2 * rest, count, piece)

        @pl.when(later == rest - 1)
        def _():
            first.arrive()
            for copy in range(dp_count):
                rows = pl.ds(copy * tall, tall)
                half[copy] = sum(got[i, rows, :] for i in range(size))
            second.begin()
            gain_first.arrive()
            gain_half[...] = sum(gain_got[i] for i in range(size))
            gain_second.begin()

    back.main(beside)
    wait = 2 * dp_count

    def beside_mixed(turn):
        several(rest + turn, 2 * rest, count, piece)
        if square:
            pl.when(turn < sum_cuts[1])(lambda: out_sum.turn(turn))
            after = rest + turn - wait
            here = (after >= 0) & (lax.rem(after, dp_count) == 0) & (after < count - dp_count)
            pl.when(here)(lambda: qkv_sum.turn(lax.div(after, dp_count)))

    mixed.main(beside_mixed)
    if square:
        qkv_sum.turn(sum_cuts[0] - 1)
    back.settle()
    mixed.settle()
    second.arrive()
    shared_out[...] = sum(last[i] for i in range(dp_count))
    gain_second.arrive()
    gain_out[...] = sum(gain_last[i] for i in range(dp_count)) / gain_ref[...]
    sums.arrive()
    wide = qkv_out.shape[2]
    if square:
        qkv_sum.arrive()
        out_sum.arrive()
    for j in range(3):
        columns = slice(j * wide, (j + 1) * wide)
        if square:
            qkv_out[j] = qkv_sum.total(columns)
        else:
            qkv_out[j] = sum(qkv_got[copy, :, columns].astype(FULL) for copy in range(dp_count))
    if square:
        w_out[...] = out_sum.total(slice(None))
    else:
        w_out[...] = sum(out_got[copy].astype(FULL) for copy in range(dp_count))
    gains_out[...] = sum(gains_got[copy] for copy in range(dp_count))
    moved = [back, mixed, first, second, sums, gain_first, gain_second]
    for moves in moved + ([qkv_sum, out_sum] if square else []):
        moves.finish()


def closing(size, dp_count, tables, slots, arrays, sums, shared, number):
    proj, _, hidden, gain = arrays
    levels, cuts = size // 2, REDUCE_CUTS
    _, tokens, model_dim = hidden.shape
    columns, high = proj.shape[2], model_dim // dp_count
    block = (tokens, model_dim)
    tall = shared.shape[1] // dp_count
    wide = shared.shape[2]
    sum_cuts = (high // 128, 2)
    parts = (dp_count, high, columns)
    out, pair = exchange_outs(dp_count, sums, (False, True))
    shapes = [(3, high, columns // 3), out.shape[1:], pair.shape[1:], gain.shape, (tall, wide)]
    outs = [jax.ShapeDtypeStruct(block, LOW)] * 2
    outs += [jax.ShapeDtypeStruct(shape, FULL) for shape in shapes]
    if dp_count == 4:
        landing, some = SquareSum.scratch(sum_cuts[0], parts, LOW), (1,)
        landing += [pltpu.VMEM(out.shape, LOW)] + SquareSum.scratch(sum_cuts[1], out.shape, LOW)
    else:
        landing, some = [pltpu.VMEM(parts, LOW), pltpu.VMEM(out.shape, LOW)], (1,) + sum_cuts
    line = [pltpu.VMEM((levels,) + block, LOW)] + LineReduce.scratch(size, block, LOW, cuts)
    return pl.pallas_call(
        functools.partial(closing_kernel, size, dp_count, len(tables), cuts, sum_cuts),
        out_shape=outs,
        in_specs=[VMEM] * (len(tables) + 7) + [ANY] * 2,
        out_specs=[ANY] * 2 + [VMEM] * 5,
        scratch_shapes=line
        + line
        + [pltpu.VMEM(parts, LOW), pltpu.VMEM(pair.shape, FULL)]
        + landing
        + [pltpu.VMEM((size,) + shared.shape[1:], FULL)]
        + [pltpu.VMEM((dp_count, tall, wide), FULL)] * 2
        + [
            pltpu.VMEM(gain.shape, FULL),
            pltpu.VMEM((size,) + gain.shape, FULL),
            pltpu.VMEM(gain.shape, FULL),
            pltpu.VMEM((dp_count,) + gain.shape, FULL),
        ]
        + Exchange.scratch(dp_count, some)
        + Exchange.scratch(size, (1,))
        + Exchange.scratch(dp_count, (1,))
        + Exchange.scratch(size, (1,))
        + Exchange.scratch(dp_count, (1,)),
        compiler_params=pltpu.CompilerParams(
            collective_id=number, has_side_effects=True, vmem_limit_bytes=62 << 20
        ),
        cost_estimate=pl.CostEstimate(flops=0, transcendentals=0, bytes_accessed=200_000_000),
        name="closing",
    )(*tables, *slots, *arrays, *sums, shared)


def across_cols(left_side, right_side):
    return lax.dot_general(
        left_side, right_side, (((1,), (1,)), ((), ())), preferred_element_type=FULL
    )


def expert_kernel(first, count, tiles, x_ref, dy_ref, scale_ref, side_ref, down_ref, grads_ref, out_ref, back_ref, dots_ref,
                  side_w, down_w, turned, turned_act, act, grad_side, side_buf, down_buf, w_sems, sems):
    e, step = pl.program_id(0), pl.program_id(1)
    slot = lax.rem(e, 2)
    hidden, model = down_w.shape[1], down_w.shape[2]
    width, wide = hidden // tiles, model // tiles
    copies = grads_ref.shape[0]
    high, low = model // copies, hidden // copies
    part = side_buf.shape[1]

    def loads(e, tile):
        slot = lax.rem(e, 2)
        out = []
        for half in range(2):
            columns = pl.ds(pl.multiple_of(half * hidden + tile * width, 128), width)
            out.append(pltpu.make_async_copy(side_ref.at[first + e, :, columns], side_w.at[slot, :, columns], w_sems.at[slot, tile, half]))
        rows = pl.ds(pl.multiple_of(tile * width, 128), width)
        out.append(pltpu.make_async_copy(down_ref.at[first + e, rows], down_w.at[slot, rows], w_sems.at[slot, tile, 2]))
        return out

    def leaving(at):
        e, chunk = lax.div(at, tiles), lax.rem(at, tiles)
        slot = lax.rem(at, 2)
        base = e * (high + low)
        columns = pl.ds(pl.multiple_of(chunk * wide, 128), wide)
        if wide >= high:
            target = grads_ref.at[pl.ds(chunk * part, part), pl.ds(base, high)]
        else:
            target = grads_ref.at[pl.ds(lax.div(chunk * wide, high), 1), pl.ds(base + lax.rem(chunk * wide, high), wide)]
        return (pltpu.make_async_copy(side_buf.at[slot], target, sems.at[slot, 0]),
                pltpu.make_async_copy(down_buf.at[slot], grads_ref.at[:, pl.ds(base + high, low), columns], sems.at[slot, 1]))

    @pl.when((e == 0) & (step == 0))
    def _():
        for tile in range(tiles):
            for copy in loads(e, tile): copy.start()

    @pl.when((e + 1 < count) & (step == 0))
    def _():
        for tile in range(tiles):
            for copy in loads(e + 1, tile): copy.start()

    @pl.when(step == 0)
    def _():
        turned[...] = x_ref[0].T
        dots_ref[...] = jnp.zeros_like(dots_ref)

    @pl.when(step < tiles)
    def _():
        for copy in loads(e, step): copy.wait()
        rows, grads, scale = x_ref[0], dy_ref[0], scale_ref[0]
        columns = pl.ds(pl.multiple_of(step * width, 128), width)
        others = pl.ds(pl.multiple_of(hidden + step * width, 128), width)
        gate = jnp.dot(rows, side_w[slot, :, columns], preferred_element_type=FULL)
        up = jnp.dot(rows, side_w[slot, :, others], preferred_element_type=FULL)
        grad_act = across_cols(grads, down_w[slot, columns, :])
        sigmoid = jax.nn.sigmoid(gate)
        silu = gate * sigmoid
        raw = silu * up
        dots_ref[0] += jnp.sum(raw * grad_act, axis=-1, keepdims=True)
        weighted = (scale * raw).astype(LOW)
        act[:, columns] = weighted
        turned_act[columns, :] = weighted.T
        grad_act = grad_act * scale
        grad_side[:, columns] = (grad_act * up * sigmoid * (1.0 + gate * (1.0 - sigmoid))).astype(LOW)
        grad_side[:, others] = (grad_act * silu).astype(LOW)

    @pl.when(step >= tiles)
    def _():
        chunk = step - tiles
        at = e * tiles + chunk
        spot = lax.rem(at, 2)
        columns = pl.ds(pl.multiple_of(chunk * wide, 128), wide)

        @pl.when(at >= 2)
        def _():
            for copy in leaving(at - 2): copy.wait()
        total = jnp.dot(turned[columns, :], grad_side[...], preferred_element_type=FULL)
        side_buf[spot] = total.astype(LOW).reshape(side_buf.shape[1:])
        leaving(at)[0].start()
        total = jnp.dot(turned_act[...], dy_ref[0, :, columns], preferred_element_type=FULL)
        down_buf[spot] = total.astype(LOW).reshape(down_buf.shape[1:])
        leaving(at)[1].start()
        back_ref[0, :, columns] = across_cols(grad_side[...], side_w[slot, columns, :]).astype(LOW)
        out_ref[0, :, columns] = jnp.dot(act[...], down_w[slot, :, columns], preferred_element_type=FULL).astype(LOW)

        @pl.when(at == count * tiles - 1)
        def _():
            for copy in leaving(at - 1) + leaving(at): copy.wait()

def expert(first, count, dp_count, x_rows, dy_rows, scales, w_gate_up, w_down, tiles=4):
    _, slots, width = x_rows.shape
    hidden = w_down.shape[1]
    high, low = width // dp_count, hidden // dp_count
    wide = width // tiles
    part = max(1, wide // high)
    rs = pl.BlockSpec((1, slots, width), lambda e, f: (first + e, 0, 0))
    os = pl.BlockSpec((1, slots, width), lambda e, f: (e, 0, 0))
    sems = pltpu.SemaphoreType.DMA
    return pl.pallas_call(
        functools.partial(expert_kernel, first, count, tiles),
        out_shape=[jax.ShapeDtypeStruct((dp_count, count * (high + low), width), LOW),
                   jax.ShapeDtypeStruct((count, slots, width), LOW), jax.ShapeDtypeStruct((count, slots, width), LOW),
                   jax.ShapeDtypeStruct((count, slots, 1), FULL)],
        grid=(count, 2 * tiles),
        in_specs=[rs, rs, pl.BlockSpec((1, slots, 1), lambda e, f: (first + e, 0, 0)), ANY, ANY],
        out_specs=[ANY, os, os, pl.BlockSpec((1, slots, 1), lambda e, f: (e, 0, 0))],
        scratch_shapes=[pltpu.VMEM((min(2, count), width, 2 * hidden), LOW), pltpu.VMEM((min(2, count), hidden, width), LOW),
                        pltpu.VMEM((width, slots), LOW), pltpu.VMEM((hidden, slots), LOW), pltpu.VMEM((slots, hidden), LOW), pltpu.VMEM((slots, 2 * hidden), LOW),
                        pltpu.VMEM((2, part, min(wide, high), 2 * hidden), LOW), pltpu.VMEM((2, dp_count, low, wide), LOW),
                        sems((min(2, count), tiles, 3)), sems((2, 2))],
        compiler_params=pltpu.CompilerParams(vmem_limit_bytes=62 << 20),
        cost_estimate=pl.CostEstimate(
            flops=18 * count * slots * width * hidden,
            transcendentals=count * slots * hidden,
            bytes_accessed=12 * count * width * hidden,
        ),
        name="expert",
    )(x_rows, dy_rows, scales, w_gate_up, w_down)


def rms_scale(values):
    return lax.rsqrt(jnp.mean(values * values, axis=-1, keepdims=True) + NORM_EPS)


def rotary_tables(length, size):
    index = np.arange(size // 2, dtype=np.float32)
    frequency = np.exp(index * np.float32(-2.0 * math.log(10000.0) / size))
    angles = np.arange(length, dtype=np.float32)[:, None] * frequency[None, :]
    cosine, sine = np.cos(angles), np.sin(angles)
    halves = [np.concatenate([cosine, cosine], axis=1), np.concatenate([-sine, sine], axis=1)]
    return jnp.asarray(np.stack(halves).astype(np.float32))


def norm_back(grad_normed, normed, scale_rows):
    return scale_rows * (
        grad_normed - normed * jnp.mean(grad_normed * normed, axis=-1, keepdims=True)
    )


def contract_rows(left_side, right_side):
    return lax.dot_general(
        left_side, right_side, (((0,), (0,)), ((), ())), preferred_element_type=FULL
    )


def contract_cols(left_side, right_side):
    return lax.dot_general(
        left_side, right_side, (((1,), (1,)), ((), ())), preferred_element_type=FULL
    )


def einsum(spec, left_side, right_side):
    return jnp.einsum(spec, left_side, right_side, preferred_element_type=FULL)


def widen_kernel(steps, *refs):
    low_ref, high_ref, down_ref = refs[0], refs[-2], refs[-1]
    step = pl.program_id(1)

    @pl.when(step < steps)
    def _():
        high_ref[...] = low_ref[...].astype(FULL)

    @pl.when(step >= steps)
    def _():
        down_ref[...] = low_ref[...].astype(FULL)


def widen(first, total, high, grads, held=()):
    count, both, width = grads.shape
    low = both - high
    rows = low
    steps = high // rows
    block = (1, rows, width)
    return pl.pallas_call(
        functools.partial(widen_kernel, steps),
        out_shape=[
            jax.ShapeDtypeStruct((total, high, width), FULL),
            jax.ShapeDtypeStruct((total, low, width), FULL),
        ],
        grid=(count, steps + 1),
        in_specs=[pl.BlockSpec(block, lambda e, r: (e, r, 0))] + [ANY] * len(held),
        out_specs=[
            pl.BlockSpec(block, lambda e, r: (first + e, jnp.minimum(r, steps - 1), 0)),
            pl.BlockSpec(block, lambda e, r: (first + e, jnp.maximum(r - steps, 0), 0)),
        ],
        input_output_aliases={1: 0, 2: 1} if held else {},
        cost_estimate=pl.CostEstimate(
            flops=grads.size, transcendentals=0, bytes_accessed=6 * grads.size
        ),
        name="widen",
    )(grads, *held)


def turn(values, cosine, sine):
    return values * cosine + pltpu.roll(values, values.shape[1] // 2, 1) * sine


def allowed_pairs(column, row):
    shape = (column.shape[0], row.shape[1])
    later = lax.broadcasted_iota(jnp.int32, shape, 0) >= lax.broadcasted_iota(jnp.int32, shape, 1)
    return later & (column == row)


def softmax(query, key, allowed):
    scores = across_cols(query, key) * (1.0 / math.sqrt(query.shape[1]))
    scores = jnp.where(allowed, scores, -1e30)
    powers = jnp.exp(scores - jnp.max(scores, axis=-1, keepdims=True))
    return powers / jnp.sum(powers, axis=-1, keepdims=True)


def attend_block(heads, block, rows_ref, scales, gain_ref, turn_ref, column, row, kept_ref, out_ref):
    width = out_ref.shape[2]
    size = width // heads
    allowed = allowed_pairs(column, row)
    cosine, sine = turn_ref[0], turn_ref[1]
    for h in range(heads):
        parts = []
        for part in range(3):
            columns = pl.ds(part * width + h * size, size)
            values = rows_ref[block, :, columns]
            if part < 2:
                values = values * scales[part]
                values = values * gain_ref[part : part + 1, h * size : (h + 1) * size]
                values = turn(values, cosine, sine)
            parts.append(values.astype(LOW))
            kept_ref[block, :, columns] = parts[-1]
        query, key, value = parts
        probs = softmax(query, key, allowed).astype(LOW)
        out_ref[block, :, pl.ds(h * size, size)] = jnp.dot(
            probs, value, preferred_element_type=FULL
        ).astype(LOW)


def attention_kernel(size, dp_count, heads, *refs):
    x_ref, w_ref, gain_ref, gains_ref, turn_ref, column_ref, row_ref, sheet_ref, dy_ref = refs[:9]
    h_out, rows_out, scale_ref, kept_ref, out_ref, own_out, sheet_out, dy_out = refs[9:17]
    x_held, h_held, rows, sums, squares, got = refs[17:23]
    x_sem, h_sem, rows_sem, send_sem, recv_sem, stay_sem = refs[23:29]
    square_sems, line_sems, sheet_sems = refs[29:32], refs[32:37], refs[37:]
    line = LineGather(size // 2, GATHER_CUTS, [dy_ref], [dy_out], *line_sems)
    sheets = Sheets(size, dp_count, sheet_ref, sheet_out, *sheet_sems)
    small = Exchange("expert", size, (True,), (1,), [squares], [got], *square_sems)
    place, model_dim = sheets.place, x_ref.shape[2]
    width = out_ref.shape[2]

    def loading(g):
        return pltpu.make_async_copy(x_ref.at[g], x_held.at[g], x_sem.at[g])

    def leaving(g):
        return (
            pltpu.make_async_copy(h_held.at[g], h_out.at[g], h_sem.at[g]),
            pltpu.make_async_copy(rows.at[g], rows_out.at[g], rows_sem.at[g]),
        )

    for g in range(size):
        loading(g).start()
    greet("expert", [(peer, None) for peer in small.peers])
    greet("dp", [(peer, None) for peer in sheets.peers])
    pl.semaphore_wait(pltpu.get_barrier_semaphore(), size + dp_count - 2)
    sheets.begin()
    line.begin()
    sums[...] = jnp.zeros_like(sums)
    lanes = lax.broadcasted_iota(jnp.int32, sums.shape, 1)

    @pl.loop(0, size)
    def _(g):
        loading(g).wait()
        values = x_held[g].astype(FULL)
        hidden = (values * rms_scale(values) * gain_ref[...]).astype(LOW)
        h_held[g] = hidden
        projected = jnp.dot(hidden, w_ref[...], preferred_element_type=FULL)
        rows[g] = projected
        for copy in leaving(g):
            copy.start()
        for part in range(2):
            half = projected[:, part * width : (part + 1) * width]
            total = jnp.sum(half * half, axis=-1, keepdims=True)
            sums[...] += jnp.where(lanes == part * size + g, total, 0.0)

    squares[...] = sums[...].T[: 2 * size]
    small.begin()
    sheets.forward(1)
    small.arrive()
    total = sum(got[i] for i in range(size))
    sums[:, : 2 * size] = lax.rsqrt(total / model_dim + NORM_EPS).T

    def sending(g, source):
        columns = pl.ds(pl.multiple_of(source * width, 128), width)
        target = own_out.at[:, columns]
        return remote(out_ref.at[g], target, send_sem.at[g], recv_sem.at[source], {"expert": g})

    own_columns = pl.ds(pl.multiple_of(place * width, 128), width)
    staying = pltpu.make_async_copy(out_ref.at[place], own_out.at[:, own_columns], stay_sem.at[0])

    @pl.loop(0, size)
    def _(i):
        g = lax.rem(place + 1 + i, size)
        scales = [
            jnp.sum(jnp.where(lanes == part * size + g, sums[...], 0.0), axis=-1, keepdims=True)
            for part in range(2)
        ]
        scale_ref[g] = jnp.concatenate(scales, axis=1)
        attend_block(
            heads, g, rows, scales, gains_ref, turn_ref, column_ref[g], row_ref[g], kept_ref, out_ref
        )
        pl.when(g != place)(lambda: sending(g, place).start())
        pl.when(lax.rem(i, 2) == 1)(lambda: line.turn(lax.div(i, 2)))

    staying.start()

    @pl.loop(size // 2, 2 * size)
    def _(i):
        for step in range(2, size // 2):
            pl.when(i == (step - 1) * (size // 2))(lambda: sheets.forward(step))
        line.turn(i)
        after = i - size - size // 2
        pl.when((after >= 0) & (after < size // 2))(lambda: sheets.cross(after))


    @pl.loop(1, size)
    def _(i):
        peer = lax.rem(place + i, size)
        sending(peer, peer).wait_recv()
        sending(peer, place).wait_send()

    @pl.loop(0, size)
    def _(g):
        for copy in leaving(g):
            copy.wait()

    staying.wait()
    small.finish()
    line.finish()
    sheets.finish()


def attention(size, dp_count, heads, arrays, number):
    x_all, w_here, sheet, dy = arrays[0], arrays[1], arrays[7], arrays[8]
    _, tokens, model_dim = x_all.shape
    columns = w_here.shape[1]
    width = columns // 3
    sems = pltpu.SemaphoreType.DMA
    seqs = (size, tokens)
    small = (2 * size, tokens)
    return pl.pallas_call(
        functools.partial(attention_kernel, size, dp_count, heads),
        out_shape=[
            jax.ShapeDtypeStruct(x_all.shape, LOW),
            jax.ShapeDtypeStruct(seqs + (columns,), FULL),
            jax.ShapeDtypeStruct(seqs + (2,), FULL),
            jax.ShapeDtypeStruct(seqs + (columns,), LOW),
            jax.ShapeDtypeStruct(seqs + (width,), LOW),
            jax.ShapeDtypeStruct((tokens, model_dim), LOW),
            jax.ShapeDtypeStruct((dp_count, size) + sheet.shape, LOW),
            jax.ShapeDtypeStruct((size,) + dy.shape, LOW),
        ],
        in_specs=[ANY] + [VMEM] * 6 + [ANY] * 2,
        out_specs=[ANY] * 2 + [VMEM] * 3 + [ANY] * 3,
        scratch_shapes=[
            pltpu.VMEM(x_all.shape, LOW),
            pltpu.VMEM(x_all.shape, LOW),
            pltpu.VMEM(seqs + (columns,), FULL),
            pltpu.VMEM((tokens, 128), FULL),
            pltpu.VMEM(small, FULL),
            pltpu.VMEM((size,) + small, FULL),
            sems((size,)),
            sems((size,)),
            sems((size,)),
            sems((size,)),
            sems((size,)),
            sems((1,)),
        ]
        + Exchange.scratch(size, (1,))
        + LineGather.scratch(size, GATHER_CUTS, 1)
        + Sheets.scratch(size, dp_count),
        compiler_params=pltpu.CompilerParams(
            collective_id=number, has_side_effects=True, vmem_limit_bytes=48 << 20
        ),
        cost_estimate=pl.CostEstimate(
            flops=2 * x_all.size * columns, transcendentals=0, bytes_accessed=100_000_000
        ),
        name="attention",
    )(*arrays)


def attend_back_block(heads, block, grad_ref, refs, back_ref, dots_ref, lanes, gains_ref, w_sum):
    w_ref, kept_ref, out_ref, rows_ref, scale_ref, gain_ref, turn_ref, column_ref, row_ref = refs
    width = out_ref.shape[2]
    size = width // heads
    scaling = 1.0 / math.sqrt(size)
    allowed = allowed_pairs(column_ref[block], row_ref[block])
    cosine, sine = turn_ref[0], turn_ref[1]
    grad_rows = grad_ref[block]
    grad_out = across_cols(grad_rows, w_ref[...]).astype(LOW)
    w_sum[...] += contract_rows(out_ref[block], grad_rows)
    dots = [0.0, 0.0]
    for h in range(heads):
        mine = slice(h * size, (h + 1) * size)
        query, key, value = (
            kept_ref[block, :, pl.ds(p * width + h * size, size)] for p in range(3)
        )
        probs = softmax(query, key, allowed)
        grad = grad_out[:, mine]
        grad_value = contract_rows(probs.astype(LOW), grad)
        grad_probs = across_cols(grad, value)
        delta = jnp.sum(grad_probs * probs, axis=-1, keepdims=True)
        grad_scores = (probs * (grad_probs - delta)).astype(LOW)
        grad_query = jnp.dot(grad_scores, key, preferred_element_type=FULL) * scaling
        grad_key = contract_rows(grad_scores, query) * scaling
        for part, grad_turned in enumerate((grad_query, grad_key)):
            columns = pl.ds(part * width + h * size, size)
            grad_normed = turn(grad_turned, cosine, -sine)
            normed = rows_ref[block, :, columns] * scale_ref[block, :, part : part + 1]
            gains_ref[part : part + 1, mine] += jnp.sum(grad_normed * normed, axis=0, keepdims=True)
            weighted = grad_normed * gain_ref[part : part + 1, mine]
            dots[part] += jnp.sum(weighted * normed, axis=-1, keepdims=True)
            back_ref[block, :, columns] = weighted
        back_ref[block, :, pl.ds(2 * width + h * size, size)] = grad_value
    groups = grad_ref.shape[0]
    for part in range(2):
        dots_ref[...] += jnp.where(lanes == part * groups + block, dots[part], 0.0)


def attend_back_kernel(levels, cuts, heads, grad_ref, *refs):
    w_ref, others, refs = refs[0], refs[1:9], refs[9:]
    proj_ref, gains_ref, w_grad_ref, w_sum, held, w_held, back, dots, squares, got, w_sem = refs[:11]
    reads = (w_held,) + tuple(others)
    rows_ref, scale_ref = others[2:4]
    size, model_dim = 2 * levels, grad_ref.shape[1]
    line = LineGather(levels, cuts, [grad_ref], [held], *refs[11:16])
    small = Exchange("expert", size, (True,), (1,), [squares], [got], *refs[16:])
    mine = pl.ds(pl.multiple_of(line.place * w_held.shape[0], 128), w_held.shape[0])
    loading = pltpu.make_async_copy(w_ref.at[mine], w_held, w_sem.at[0])
    loading.start()
    greet("expert", [(peer, None) for peer in small.peers])
    pl.semaphore_wait(pltpu.get_barrier_semaphore(), size - 1)
    line.begin()
    w_sum[...] = jnp.zeros_like(w_sum)
    gains_ref[...] = jnp.zeros_like(gains_ref)
    dots[...] = jnp.zeros_like(dots)
    lanes = lax.broadcasted_iota(jnp.int32, dots.shape, 1)
    loading.wait()
    line.staying(0).wait()

    def landed(block):
        attend_back_block(heads, block, held, reads, back, dots, lanes, gains_ref, w_sum)

    line.main(landed)
    squares[...] = dots[...].T[: 2 * size]
    small.begin()
    wide = w_grad_ref.shape[2]
    for copy in range(w_grad_ref.shape[0]):
        w_grad_ref[copy] = w_sum[:, copy * wide : (copy + 1) * wide].astype(LOW)
    small.arrive()
    dots[:, : 2 * size] = sum(got[i] for i in range(size)).T / model_dim
    width = w_held.shape[0]

    @pl.loop(0, size)
    def _(block):
        for part in range(2):
            columns = pl.ds(part * width, width)
            scale = scale_ref[block, :, part : part + 1]
            mean = jnp.where(lanes == part * size + block, dots[...], 0.0)
            mean = jnp.sum(mean, axis=-1, keepdims=True)
            normed = rows_ref[block, :, columns] * scale
            proj_ref[block, :, columns] = (scale * (back[block, :, columns] - normed * mean)).astype(LOW)
        columns = pl.ds(2 * width, width)
        proj_ref[block, :, columns] = back[block, :, columns].astype(LOW)

    line.finish(held=1)
    small.finish()


def attend_back(size, dp_count, heads, grad, arrays, number):
    _, _, out, rows = arrays[:4]
    width = out.shape[2]
    tokens, model_dim = grad.shape
    small = (2 * size, tokens)
    return pl.pallas_call(
        functools.partial(attend_back_kernel, size // 2, GATHER_CUTS, heads),
        out_shape=[
            jax.ShapeDtypeStruct(rows.shape, LOW),
            jax.ShapeDtypeStruct((2, width), FULL),
            jax.ShapeDtypeStruct((dp_count, width, model_dim // dp_count), LOW),
        ],
        in_specs=[ANY] * 2 + [VMEM] * (len(arrays) - 1),
        out_specs=[VMEM] * 3,
        scratch_shapes=[
            pltpu.VMEM((width, model_dim), FULL),
            pltpu.VMEM((size, tokens, model_dim), LOW),
            pltpu.VMEM((width, model_dim), LOW),
            pltpu.VMEM(rows.shape, FULL),
            pltpu.VMEM((tokens, 128), FULL),
            pltpu.VMEM(small, FULL),
            pltpu.VMEM((size,) + small, FULL),
            pltpu.SemaphoreType.DMA((1,)),
        ]
        + LineGather.scratch(size, GATHER_CUTS, 1)
        + Exchange.scratch(size, (1,)),
        compiler_params=pltpu.CompilerParams(
            collective_id=number, has_side_effects=True, vmem_limit_bytes=48 << 20
        ),
        cost_estimate=pl.CostEstimate(flops=0, transcendentals=0, bytes_accessed=150_000_000),
        name="attend_back",
    )(grad, *arrays)


def on_device(
    dp_count,
    line_count,
    layer_input,
    out_cotangent,
    segments,
    routes,
    w_qkv,
    w_out,
    w_router,
    attn_gain,
    mlp_gain,
    query_gain,
    key_gain,
    w_gate_up,
    w_down,
):
    row_count, model_dim = layer_input.shape
    top_count = routes.shape[1]
    expert_count = w_router.shape[1]
    local_count = w_gate_up.shape[0]
    head_size = model_dim // HEADS
    head_cols = model_dim // line_count
    heads_here = head_cols // head_size
    capacity = (row_count * top_count * 9 // 8 + expert_count - 1) // expert_count
    scaling = 1.0 / math.sqrt(head_size)
    place = lax.axis_index("expert")
    shard = w_qkv.shape[0]

    numbers = jnp.concatenate([routes.T, segments, jnp.zeros((7, row_count), jnp.int32)], axis=0)
    x_all, numbers_all, qkv_here, router_full, gains = opening(
        line_count,
        dp_count,
        [layer_input, numbers],
        GATHER_CUTS,
        w_qkv,
        [w_router, jnp.stack([attn_gain, mlp_gain, query_gain, key_gain])],
        1,
    )
    qkv_here = qkv_here.reshape(model_dim, 3 * head_cols)
    router_full = router_full.reshape(model_dim, expert_count)
    gains = gains.transpose(2, 0, 1, 3).reshape(4, model_dim).astype(FULL)
    gain_attn, gain_mlp = gains[0], gains[1]
    both_gains = lax.dynamic_slice_in_dim(gains[2:], place * head_cols, head_cols, axis=1)

    routes_all = numbers_all[:, :top_count]
    segments_all = numbers_all[:, top_count]
    turns = rotary_tables(row_count, head_size)
    column, row = segments_all[:, :, None], segments_all[:, None, :]
    arrays = [x_all, qkv_here, gain_attn[None], both_gains, turns, column, row, w_out, out_cotangent]
    hidden_one, projected, scales, kept, attended, own_attended, out_full, dy_all = attention(
        line_count, dp_count, heads_here, arrays, 4
    )
    out_full = out_full.reshape(model_dim, model_dim)
    inputs = layer_input.astype(FULL)
    scale_attn = rms_scale(inputs)
    normed_attn = inputs * scale_attn
    residual = inputs + jnp.dot(own_attended, out_full, preferred_element_type=FULL)
    scale_mlp = rms_scale(residual)
    normed_mlp = residual * scale_mlp
    hidden_two = (normed_mlp * gain_mlp).astype(LOW)

    logits = jnp.dot(hidden_two, router_full, preferred_element_type=FULL)
    chosen = jnp.any(routes[:, :, None] == jnp.arange(expert_count)[None, None, :], axis=1)
    masked = jnp.where(chosen, logits, -1e30)
    powers = jnp.where(chosen, jnp.exp(masked - jnp.max(masked, axis=-1, keepdims=True)), 0.0)
    gates = powers / jnp.sum(powers, axis=-1, keepdims=True)

    local = place * local_count + jnp.arange(local_count)
    used = jnp.any(routes_all[:, None] == local[None, :, None, None], axis=2)
    position = jnp.arange(row_count)
    lower = (position[:, None] < position[None, :]).astype(LOW)
    rank = einsum("gju,ut->gjt", used.astype(LOW), lower).astype(jnp.int32)
    rank = jnp.where(used, rank, -1)
    spots = jnp.arange(capacity)
    table = (rank[:, :, None, :] == spots[None, None, :, None]).astype(LOW)
    returns = [(rank[:, j, :, None] == spots[None, None, :]).astype(LOW) for j in range(local_count)]
    slots = line_count * capacity
    flat_table = table.reshape(line_count, local_count * capacity, row_count)
    expert_rows, dy_rows, gates_all = gather_place(
        line_count, hidden_two, gates.T, flat_table, dy_all, local_count, 6
    )
    local_gates = lax.dynamic_slice_in_dim(gates_all, place * local_count, local_count, axis=1)
    slot_gates = jnp.sum(table.astype(FULL) * local_gates[:, :, None, :], axis=-1)
    slot_gates = slot_gates.transpose(1, 0, 2).reshape(local_count, slots, 1)
    out_rows, back_rows, slot_grads, grad_sums = [], [], [], []
    both_rows = model_dim // dp_count + w_down.shape[1] // dp_count
    for first, count in ((0, 1), (1, local_count - 1)):
        grads, out_row, back_row, dots = expert(
            first, count, dp_count, expert_rows, dy_rows, slot_gates, w_gate_up, w_down
        )
        grads = grads.reshape(-1, model_dim)
        grads = lax.psum_scatter(grads, "dp", scatter_dimension=0, tiled=True)
        grad_sums.append(grads.reshape(count, both_rows, model_dim))
        for kept_list, rows in ((out_rows, out_row), (back_rows, back_row), (slot_grads, dots)):
            kept_list.append(rows.reshape(count, line_count, capacity, rows.shape[2]))
    gate_rows = model_dim // dp_count
    grad_two, grad_gates = collect_reduce(
        line_count, returns, back_rows, slot_grads, flat_table, 8
    )
    grad_gates = grad_gates.reshape(expert_count, row_count).T
    grad_two = grad_two.astype(FULL)

    grad_out_rows = out_cotangent.astype(FULL)
    grad_logits = gates * (grad_gates - jnp.sum(gates * grad_gates, axis=-1, keepdims=True))
    grad_logits = grad_logits.astype(LOW)
    grad_router = contract_rows(grad_logits, hidden_two)
    grad_two = grad_two + contract_cols(grad_logits, router_full)
    grad_gain_mlp = jnp.sum(grad_two * normed_mlp, axis=0)
    grad_resid = grad_out_rows + norm_back(grad_two * gain_mlp, normed_mlp, scale_mlp)
    grad_attn = grad_resid.astype(LOW)

    arrays = [out_full, kept, attended, projected, scales, both_gains, turns, column, row]
    grad_proj, gain_pair, out_parts = attend_back(
        line_count, dp_count, heads_here, grad_attn, arrays, 11
    )

    shared = jnp.concatenate([grad_router, grad_gain_mlp[None]], axis=0)
    tall = shared.shape[0] + -shared.shape[0] % 8
    shared = jnp.pad(shared, ((0, tall - shared.shape[0]), (0, 0)))
    shared = shared.reshape(tall, dp_count, line_count, shard).transpose(2, 1, 0, 3)
    shared = shared.reshape(line_count, dp_count * tall, shard)
    shared = jnp.pad(shared, ((0, 0), (0, 0), (0, 128 - shard)))
    arrays = [grad_proj, qkv_here, hidden_one, gain_attn[None]]
    grad_one, mixture, sum_qkv, sum_out, gain_pair, gain_sum, shared = closing(
        line_count, dp_count, returns, out_rows, arrays, [out_parts, gain_pair], shared, 14
    )
    here = (lax.axis_index("dp") * line_count + place) * shard
    grad_gain_attn = lax.dynamic_slice_in_dim(gain_sum[0], here, shard)
    output = (residual + mixture.astype(FULL)).astype(LOW)
    sum_qkv = sum_qkv.transpose(1, 0, 2)
    first_sums, mixture = lax.optimization_barrier((grad_sums[0], mixture))
    wide = widen(0, local_count, gate_rows, first_sums)
    sum_gate_up, sum_down = widen(1, local_count, gate_rows, grad_sums[1], wide)
    shared = shared[:, :shard]
    grad_one = grad_one.astype(FULL)
    grad_inputs = grad_resid + norm_back(grad_one * gain_attn, normed_attn, scale_attn)
    return (
        output,
        grad_inputs,
        sum_qkv,
        sum_out,
        shared[:expert_count].T,
        grad_gain_attn,
        shared[expert_count],
        gain_pair[0],
        gain_pair[1],
        sum_gate_up,
        sum_down,
    )


def solution(mesh):
    both = ("dp", "expert")
    rows, flat = P(both, None), P(both)
    placed = (rows,) * 7 + (flat,) * 4 + (P("expert", None, None),) * 2
    return jax.shard_map(
        functools.partial(on_device, mesh.shape["dp"], mesh.shape["expert"]),
        mesh=mesh,
        in_specs=placed,
        out_specs=(
            rows,
            rows,
            P("dp", None, "expert"),
            P("expert", "dp"),
            rows,
            flat,
            flat,
            P("expert"),
            P("expert"),
            P("expert", "dp", None),
            P("expert", "dp", None),
        ),
        check_vma=False,
    )
```

```python
import functools
import math

import jax
import jax.numpy as jnp
import numpy as np
from jax import lax
from jax.experimental import pallas as pl
from jax.experimental.pallas import tpu as pltpu
from jax.sharding import PartitionSpec as P

HEADS = 16
NORM_EPS = 1e-05
MESH = pl.DeviceIdType.MESH
ANY = pl.BlockSpec(memory_space=pl.ANY)
LOW = jnp.bfloat16
GATHER_CUTS, REDUCE_CUTS = 4, 3
FULL = jnp.float32


def line_place():
    place = lax.axis_index("expert")
    level, side = lax.div(place, 2), lax.rem(place, 2)
    return place, level, side, place + 1 - 2 * side


def greet(axis, targets):
    barrier = pltpu.get_barrier_semaphore()
    for target, there in targets:

        def signal(target=target):
            pl.semaphore_signal(barrier, inc=1, device_id={axis: target}, device_id_type=MESH)

        if there is None:
            signal()
        else:
            pl.when(there)(signal)


def line_barrier(levels):
    place, level, _, other = line_place()
    has_up, has_down = level < levels - 1, level > 0
    greet("expert", [(other, None), (place + 2, has_up), (place - 2, has_down)])
    count = 1 + has_up.astype(jnp.int32) + has_down.astype(jnp.int32)
    pl.semaphore_wait(pltpu.get_barrier_semaphore(), count)


def around(axis, size):
    place = lax.axis_index(axis)
    return [lax.rem(place + shift, size) for shift in range(1, size)]


def remote(source, target, send, recv, device):
    return pltpu.make_async_remote_copy(
        src_ref=source,
        dst_ref=target,
        send_sem=send,
        recv_sem=recv,
        device_id=device,
        device_id_type=MESH,
    )


class LineGather:
    def __init__(self, levels, cuts, ins, outs, up_sem, down_sem, side_sem, recv_sem, own_sem):
        self.levels, self.cuts, self.ins, self.outs = levels, cuts, ins, outs
        self.up_sem, self.down_sem, self.side_sem = up_sem, down_sem, side_sem
        self.recv_sem, self.own_sem = recv_sem, own_sem
        self.place, self.level, self.side, self.other = line_place()
        self.has_up, self.has_down = self.level < levels - 1, self.level > 0

    @staticmethod
    def scratch(size, cuts, count):
        levels, total = size // 2, cuts + count - 1
        shapes = ((levels, total), (levels, total), (2 * levels - 1, total), (size, total))
        return [pltpu.SemaphoreType.DMA(shape) for shape in shapes + ((count,),)]

    def pieces(self):
        return [(0, k) for k in range(self.cuts)] + [(i, 0) for i in range(1, len(self.ins))]

    def staying(self, i):
        target = self.outs[i].at[self.place]
        return pltpu.make_async_copy(self.ins[i], target, self.own_sem.at[i])

    def sending(self, piece, block, own, sem, target):
        i, k = piece
        landing, source, q = self.outs[i].at[block], self.ins[i], k
        if i:
            q = self.cuts + i - 1
        else:
            rows = source.shape[0] // self.cuts
            landing, source = landing.at[pl.ds(k * rows, rows)], source.at[pl.ds(k * rows, rows)]
        sems = sem.at[q], self.recv_sem.at[block, q]
        return remote(source if own else landing, landing, *sems, {"expert": target})

    def up(self, piece, step, own=False):
        block = self.place - 2 * step
        return self.sending(piece, block, own, self.up_sem.at[step], self.place + 2)

    def down(self, piece, step, own=False):
        block = self.place + 2 * step
        return self.sending(piece, block, own, self.down_sem.at[step], self.place - 2)

    def across(self, piece, step, own=False):
        sem = self.side_sem.at[step + self.levels - 1]
        return self.sending(piece, self.place - 2 * step, own, sem, self.other)

    def begin(self):
        for piece in self.pieces():
            pl.when(self.has_up)(self.up(piece, 0, True).start)
            pl.when(self.has_down)(self.down(piece, 0, True).start)
        for piece in self.pieces():
            self.across(piece, 0, True).start()
        for i in range(len(self.ins)):
            self.staying(i).start()

    def forward(self, step, piece):
        @pl.when(self.level >= step)
        def _():
            self.across(piece, step).wait_recv()
            pl.when(self.has_up)(self.up(piece, step).start)
            self.across(piece, step).start()

        @pl.when(self.level + step < self.levels)
        def _():
            self.across(piece, -step).wait_recv()
            pl.when(self.has_down)(self.down(piece, step).start)
            self.across(piece, -step).start()

    def land_across(self, block):
        for piece in self.pieces():
            self.sending(piece, block, False, self.side_sem.at[0], self.other).wait_recv()

    def turn(self, turn, landed=None):
        levels, cuts = self.levels, self.cuts
        step, k = lax.div(turn, 4) + 1, lax.rem(turn, 4)

        @pl.when((step < levels) & (k < cuts))
        def _():
            self.forward(step, (0, k))

            @pl.when(k == cuts - 1)
            def _():
                for i in range(1, len(self.ins)):
                    self.forward(step, (i, 0))

        group, sign, crossed = step - 1, 2 * lax.rem(k, 2) - 1, lax.div(k, 2)
        crossed = jnp.where(group == 0, k, crossed)
        far = jnp.where(group == 0, self.level, self.level + sign * group)

        @pl.when((far >= 0) & (far < levels) & ((group > 0) | (k < 2)))
        def _():
            block = 2 * far + self.side + crossed * (1 - 2 * self.side)

            @pl.when(crossed == 1)
            def _():
                self.land_across(block)

            if landed:
                landed(block)

    def main(self, landed=None):
        @pl.loop(0, 4 * self.levels)
        def _(turn):
            self.turn(turn, landed)

    def finish(self, held=0):
        for piece in self.pieces():
            self.across(piece, 0).wait_send()
            for step in range(self.levels):
                above, below = self.level >= step, self.level + step < self.levels
                pl.when(self.has_up & above)(self.up(piece, step).wait_send)
                pl.when(self.has_down & below)(self.down(piece, step).wait_send)
                if step:
                    pl.when(above)(self.across(piece, step).wait_send)
                    pl.when(below)(self.across(piece, -step).wait_send)
        for i in range(held, len(self.ins)):
            self.staying(i).wait()


def call(kernel, name, number, outs, scratch, arrays, moved):
    return pl.pallas_call(
        kernel,
        out_shape=outs,
        in_specs=[ANY] * len(arrays),
        out_specs=[ANY] * len(outs),
        scratch_shapes=scratch,
        compiler_params=pltpu.CompilerParams(
            collective_id=number, has_side_effects=True, vmem_limit_bytes=48 << 20
        ),
        cost_estimate=pl.CostEstimate(flops=0, transcendentals=0, bytes_accessed=moved),
        name=name,
    )(*arrays)


class LineReduce:
    def __init__(self, levels, cuts, parts, total, own, beside, rising, falling, *sems):
        self.levels, self.cuts, self.parts, self.total = levels, cuts, parts, total
        self.made = parts.shape[0] == levels
        self.own, self.beside, self.rising, self.falling = own, beside, rising, falling
        self.load_sem, self.side_send, self.side_recv = sems[:3]
        self.up_send, self.up_recv, self.down_send, self.down_recv, self.out_sem = sems[3:]
        self.place, self.level, self.side, self.other = line_place()
        self.has_up, self.has_down = self.level < levels - 1, self.level > 0
        self.rows = parts.shape[1] // cuts

    @staticmethod
    def scratch(size, block, dtype, cuts):
        levels = size // 2
        return (
            [pltpu.VMEM((levels,) + block, dtype)] * 2
            + [pltpu.VMEM((levels - 1,) + block, dtype)] * 2
            + [pltpu.SemaphoreType.DMA((levels, cuts))] * 7
            + [pltpu.SemaphoreType.DMA((cuts,))]
        )

    def cut(self, ref, block, k):
        return ref.at[block, pl.ds(k * self.rows, self.rows)]

    def loading(self, far, k):
        source = self.cut(self.parts, 2 * far + self.side, k)
        return pltpu.make_async_copy(source, self.cut(self.own, far, k), self.load_sem.at[far, k])

    def across(self, far, k):
        source = self.cut(self.parts, far if self.made else 2 * far + 1 - self.side, k)
        sems = self.side_send.at[far, k], self.side_recv.at[far, k]
        return remote(source, self.cut(self.beside, far, k), *sems, {"expert": self.other})

    def up(self, far, k):
        sems = self.up_send.at[far, k], self.up_recv.at[far, k]
        target = {"expert": self.place + 2}
        return remote(self.cut(self.own, far, k), self.cut(self.rising, far - 1, k), *sems, target)

    def down(self, far, k):
        sems = self.down_send.at[far, k], self.down_recv.at[far, k]
        target = {"expert": self.place - 2}
        return remote(self.cut(self.own, far, k), self.cut(self.falling, far, k), *sems, target)

    def value(self, ref, block, k):
        return self.cut(ref, block, k)[...].astype(FULL)

    def load(self):
        for i in range(self.levels):
            for k in range(self.cuts):
                self.loading(self.far(i), k).start()

    def begin(self):
        for i in range(self.levels):
            for k in range(self.cuts):
                self.across(self.far(i), k).start()

    def far(self, i):
        return jnp.where(lax.rem(i, 2) == 0, self.levels - 1 - lax.div(i, 2), lax.div(i, 2))

    def prepare(self, turn, make):
        far = self.far(lax.div(turn, 2))

        @pl.when(lax.rem(turn, 2) == 0)
        def _():
            make(2 * far + 1 - self.side, self.parts.at[far])
            for k in range(self.cuts):
                self.across(far, k).start()

        @pl.when(lax.rem(turn, 2) == 1)
        def _():
            make(2 * far + self.side, self.own.at[far])

    def pair(self, far, k):
        if not self.made:
            self.loading(far, k).wait()
        self.across(far, k).wait_recv()
        return self.value(self.own, far, k) + self.value(self.beside, far, k)

    def store(self, far, k, total):
        self.cut(self.own, far, k)[...] = total.astype(self.own.dtype)

    def toward(self, far, k, ahead, behind, move, arrived, shift):
        @pl.when(ahead & behind)
        def _():
            both = self.pair(far, k)
            move(far, k).wait_recv()
            self.store(far, k, both + self.value(arrived, far - shift, k))

        @pl.when(ahead & jnp.logical_not(behind))
        def _():
            self.store(far, k, self.pair(far, k))

        pl.when(ahead)(move(far, k).start)

    def main(self, beside=None):
        levels, cuts = self.levels, self.cuts
        lower = self.level < levels // 2

        def rise(far, k):
            self.toward(far, k, self.level < far, self.has_down, self.up, self.rising, 1)

        def fall(far, k):
            self.toward(far, k, self.level > far, self.has_up, self.down, self.falling, 0)

        @pl.loop(0, 2 * cuts)
        def _(turn):
            near, k = turn < cuts, lax.rem(turn, cuts)
            if beside:
                beside(turn)
            upward = (near & lower) | jnp.logical_not(near | lower)
            pl.when(upward)(lambda: rise(levels - 1, k))
            pl.when(jnp.logical_not(upward))(lambda: fall(0, k))

        @pl.loop(2 * cuts, levels * cuts)
        def _(turn):
            step, k = lax.div(turn, cuts) - 1, lax.rem(turn, cuts)
            if beside:
                beside(turn)
            rise(levels - 1 - step, k)
            fall(step, k)

    def settle(self):
        @pl.loop(0, self.cuts)
        def _(k):
            self.store(self.level, k, self.pair(self.level, k))
            for there, move, arrived, shift in (
                (self.has_down, self.up, self.rising, 1),
                (self.has_up, self.down, self.falling, 0),
            ):

                @pl.when(there)
                def _():
                    move(self.level, k).wait_recv()
                    total = self.value(self.own, self.level, k)
                    total += self.value(arrived, self.level - shift, k)
                    self.store(self.level, k, total)

            self.leaving(k).start()

    def leaving(self, k):
        target = self.total.at[pl.ds(k * self.rows, self.rows)]
        return pltpu.make_async_copy(self.cut(self.own, self.level, k), target, self.out_sem.at[k])

    def finish(self):
        for k in range(self.cuts):
            self.leaving(k).wait()
            for far in range(self.levels):
                self.across(far, k).wait_send()
                pl.when(self.level < far)(self.up(far, k).wait_send)
                pl.when(self.level > far)(self.down(far, k).wait_send)


class Exchange:
    def __init__(self, axis, size, spread, cuts, ins, outs, send_sem, recv_sem, own_sem):
        self.axis, self.spread, self.ins, self.outs = axis, spread, ins, outs
        self.send_sem, self.recv_sem, self.own_sem = send_sem, recv_sem, own_sem
        self.cuts = cuts
        self.firsts = [sum(cuts[:i]) for i in range(len(cuts))]
        self.pieces = [(i, k) for i in range(len(cuts)) for k in range(cuts[i])]
        self.place, self.peers = lax.axis_index(axis), around(axis, size)

    @staticmethod
    def scratch(size, cuts):
        sems = pltpu.SemaphoreType.DMA
        return [sems((sum(cuts), size)), sems((sum(cuts), size)), sems((len(cuts),))]

    def source(self, i, block):
        return self.ins[i] if self.spread[i] else self.ins[i].at[block]

    def staying(self, i):
        target = self.outs[i].at[self.place]
        return pltpu.make_async_copy(self.source(i, self.place), target, self.own_sem.at[i])

    def sending(self, i, k, shift, landing):
        peer = self.peers[shift]
        source, target, q = self.source(i, peer), self.outs[i].at[landing], self.firsts[i] + k
        if self.cuts[i] > 1:
            rows = target.shape[0] // self.cuts[i]
            source, target = source.at[pl.ds(k * rows, rows)], target.at[pl.ds(k * rows, rows)]
        sems = self.send_sem.at[q, shift], self.recv_sem.at[q, landing]
        return remote(source, target, *sems, {self.axis: peer})

    def send(self, i, k):
        for shift in range(len(self.peers)):
            self.sending(i, k, shift, self.place).start()

    def stay(self):
        for i in range(len(self.spread)):
            self.staying(i).start()

    def begin(self):
        for i, k in self.pieces:
            self.send(i, k)
        self.stay()

    def land(self):
        for shift, peer in enumerate(self.peers):
            for i, k in self.pieces:
                self.sending(i, k, shift, peer).wait_recv()

    def arrive(self):
        self.land()
        for i in range(len(self.spread)):
            self.staying(i).wait()

    def finish(self):
        for shift in range(len(self.peers)):
            for i, k in self.pieces:
                self.sending(i, k, shift, self.place).wait_send()


def exchange_kernel(axis, size, spread, *refs):
    count = len(spread)
    ins, outs, sems = refs[:count], refs[count : 2 * count], refs[2 * count :]
    moves = Exchange(axis, size, spread, (1,) * count, ins, outs, *sems)
    greet(axis, [(peer, None) for peer in moves.peers])
    pl.semaphore_wait(pltpu.get_barrier_semaphore(), size - 1)
    moves.begin()
    moves.arrive()
    moves.finish()


def exchange_outs(size, arrays, spread):
    return [
        jax.ShapeDtypeStruct((size,) + a.shape if flat else a.shape, a.dtype)
        for a, flat in zip(arrays, spread)
    ]


def exchange(axis, size, arrays, spread, number):
    return call(
        functools.partial(exchange_kernel, axis, size, tuple(spread)),
        "exchange_" + axis,
        number,
        exchange_outs(size, arrays, spread),
        Exchange.scratch(size, (1,) * len(arrays)),
        arrays,
        30_000_000,
    )


def opening_kernel(size, dp_count, count, cuts, *refs):
    ins, (w_ref, *small_refs) = refs[:count], refs[count : count + 3]
    outs, rest = refs[count + 3 : 2 * count + 3], refs[2 * count + 6 :]
    w_out, *small_outs = refs[2 * count + 3 : 2 * count + 6]
    line = LineGather(size // 2, cuts, ins, outs, *rest[:5])
    send_sem, recv_sem, own_sem = rest[5:8]
    place, mine = line.place, lax.axis_index("dp")
    peers = around("expert", size)
    width = w_out.shape[3] // 3
    lands = [w_out] + small_outs
    across = Exchange(
        "dp", dp_count, (True,) * 3, (size,) * 3, [a.at[mine] for a in lands], lands, *rest[8:]
    )
    greet("expert", [(peer, None) for peer in peers])
    greet("dp", [(peer, None) for peer in across.peers])
    pl.semaphore_wait(pltpu.get_barrier_semaphore(), size + dp_count - 2)

    def ends(peer, landing, j):
        if j >= 3:
            return small_refs[j - 3], small_outs[j - 3].at[mine, landing]
        start = pl.multiple_of(j * width * size + peer * width, 128)
        target = w_out.at[mine, landing, :, pl.ds(j * width, width)]
        return w_ref.at[:, pl.ds(start, width)], target

    def sending(shift, landing, j):
        source, target = ends(peers[shift], landing, j)
        sems = send_sem.at[shift, j], recv_sem.at[landing, j]
        return remote(source, target, *sems, {"expert": peers[shift]})

    own = [pltpu.make_async_copy(*ends(place, place, j), own_sem.at[j]) for j in range(5)]
    for shift in range(size - 1):
        for j in range(5):
            sending(shift, place, j).start()
    for copy in own:
        copy.start()
    line.begin()
    for copy in own:
        copy.wait()
    for i in range(3):
        across.send(i, place)
    for shift, peer in enumerate(peers):
        for j in range(5):
            sending(shift, peer, j).wait_recv()
        for i in range(3):
            across.send(i, peer)
    line.main()
    line.finish()
    for shift in range(size - 1):
        for j in range(5):
            sending(shift, place, j).wait_send()
    across.land()
    across.finish()


def opening(size, dp_count, arrays, cuts, weights, small, number):
    sems = pltpu.SemaphoreType.DMA
    outs = [jax.ShapeDtypeStruct((size,) + a.shape, a.dtype) for a in arrays]
    rows, columns = weights.shape
    whole = (dp_count, size, rows)
    outs.append(jax.ShapeDtypeStruct(whole + (columns // size,), weights.dtype))
    outs += [jax.ShapeDtypeStruct((dp_count, size) + a.shape, a.dtype) for a in small]
    return call(
        functools.partial(opening_kernel, size, dp_count, len(arrays), cuts),
        "opening",
        number,
        outs,
        LineGather.scratch(size, cuts, len(arrays))
        + [sems((size, 5)), sems((size, 5)), sems((5,))]
        + Exchange.scratch(dp_count, (size,) * 3),
        list(arrays) + [weights] + small,
        200_000_000,
    )


class Sheets:
    def __init__(self, size, dp_count, source, target, *sems):
        self.levels, self.dp_count, self.ins, self.out = size // 2, dp_count, source, target
        self.up_send, self.down_send, self.line_recv, self.dp_send, self.dp_recv = sems[:5]
        self.side_send, self.side_recv, self.own_sem = sems[5:]
        self.place, self.level, self.side, self.other = line_place()
        self.has_up, self.has_down = self.level < self.levels - 1, self.level > 0
        self.mine, self.peers = lax.axis_index("dp"), around("dp", dp_count)

    @staticmethod
    def scratch(size, dp_count):
        sems, levels = pltpu.SemaphoreType.DMA, size // 2
        return [sems((levels,))] * 3 + [sems((dp_count, levels))] * 4 + [sems((1,))]

    def along(self, far, own, send, target):
        landing = self.out.at[self.mine, 2 * far + self.side]
        source = self.ins if own else landing
        return remote(source, landing, send.at[far], self.line_recv.at[far], {"expert": target})

    def up(self, far, own=False):
        return self.along(far, own, self.up_send, self.place + 2)

    def down(self, far, own=False):
        return self.along(far, own, self.down_send, self.place - 2)

    def over(self, far, shift, copy, own=False):
        landing = self.out.at[copy, 2 * far + self.side]
        source = self.ins if own else landing
        sems = self.dp_send.at[shift, far], self.dp_recv.at[copy, far]
        return remote(source, landing, *sems, {"dp": self.peers[shift]})

    def across(self, far, copy, whose, own=False):
        landing = self.out.at[copy, 2 * far + whose]
        source = self.ins if own else landing
        sems = self.side_send.at[copy, far], self.side_recv.at[copy, far]
        return remote(source, landing, *sems, {"expert": self.other})

    def spread(self, far, own=False):
        for shift in range(self.dp_count - 1):
            self.over(far, shift, self.mine, own).start()
        self.across(far, self.mine, self.side, own).start()

    def staying(self):
        target = self.out.at[self.mine, self.place]
        return pltpu.make_async_copy(self.ins, target, self.own_sem.at[0])

    def begin(self):
        pl.when(self.has_up)(self.up(self.level, True).start)
        pl.when(self.has_down)(self.down(self.level, True).start)
        self.spread(self.level, True)
        self.staying().start()

    def forward(self, step):
        @pl.when(self.level >= step)
        def _():
            self.up(self.level - step).wait_recv()
            pl.when(self.has_up)(self.up(self.level - step).start)
            self.spread(self.level - step)

        @pl.when(self.level + step < self.levels)
        def _():
            self.down(self.level + step).wait_recv()
            pl.when(self.has_down)(self.down(self.level + step).start)
            self.spread(self.level + step)

    def cross(self, far):
        for shift, peer in enumerate(self.peers):
            self.over(far, shift, peer).wait_recv()
            self.across(far, peer, self.side).start()

    def finish(self):
        @pl.loop(0, self.levels)
        def _(far):
            pl.when(self.has_up & (self.level >= far))(self.up(far).wait_send)
            pl.when(self.has_down & (self.level <= far))(self.down(far).wait_send)
            for shift in range(self.dp_count - 1):
                self.over(far, shift, self.mine).wait_send()
            for copy in range(self.dp_count):
                self.across(far, copy, 1 - self.side).wait_recv()
                self.across(far, copy, self.side).wait_send()

        self.staying().wait()


VMEM = pl.BlockSpec(memory_space=pltpu.VMEM)
COLUMNS = 512


def gather_place_kernel(levels, cuts, *refs):
    rows_ref, gates_ref, table_ref, dy_ref, x_out, dy_out, gates_out = refs[:7]
    held, dy_held, x_stage, dy_stage = refs[7:11]
    line_sems, (dy_sem, x_sems, dy_sems) = refs[11:16], refs[16:]
    line = LineGather(levels, cuts, [rows_ref, gates_ref], [held, gates_out], *line_sems)
    size, width = 2 * levels, held.shape[2]
    _, local_count, capacity, _ = x_stage.shape

    def leaving(block, stage, out, sems):
        target = out.at[:, pl.ds(pl.multiple_of(block * capacity, 8), capacity)]
        return pltpu.make_async_copy(stage.at[block], target, sems.at[block])

    def place(block, rows, stage, out, sems):
        table = table_ref[block]

        @pl.loop(0, width // COLUMNS)
        def _(n):
            columns = pl.ds(pl.multiple_of(n * COLUMNS, COLUMNS), COLUMNS)
            placed = jnp.dot(table, rows[block, :, columns], preferred_element_type=FULL)
            for j in range(local_count):
                part = placed[j * capacity : (j + 1) * capacity]
                stage[block, j, :, columns] = part.astype(stage.dtype)

        leaving(block, stage, out, sems).start()

    def place_x(block):
        place(block, held, x_stage, x_out, x_sems)

    loading = pltpu.make_async_copy(dy_ref, dy_held, dy_sem.at[0])
    loading.start()
    line_barrier(levels)
    line.begin()
    loading.wait()

    @pl.loop(0, size)
    def _(block):
        place(block, dy_held, dy_stage, dy_out, dy_sems)

    line.staying(0).wait()
    line.main(place_x)
    line.finish(held=1)

    @pl.loop(0, size)
    def _(block):
        leaving(block, x_stage, x_out, x_sems).wait()
        leaving(block, dy_stage, dy_out, dy_sems).wait()


def gather_place(size, rows, gates, table, dy, local_count, number):
    cuts = GATHER_CUTS
    tokens, width = rows.shape
    capacity = table.shape[1] // local_count
    placed = jax.ShapeDtypeStruct((local_count, size * capacity, width), rows.dtype)
    sems = pltpu.SemaphoreType.DMA
    return pl.pallas_call(
        functools.partial(gather_place_kernel, size // 2, cuts),
        out_shape=[placed, placed, jax.ShapeDtypeStruct((size,) + gates.shape, gates.dtype)],
        in_specs=[ANY, ANY, VMEM, ANY],
        out_specs=[ANY] * 3,
        scratch_shapes=[pltpu.VMEM((size, tokens, width), rows.dtype)] * 2
        + [pltpu.VMEM((size, local_count, capacity, width), rows.dtype)] * 2
        + LineGather.scratch(size, cuts, 2)
        + [sems((1,)), sems((size,)), sems((size,))],
        compiler_params=pltpu.CompilerParams(
            collective_id=number, has_side_effects=True, vmem_limit_bytes=48 << 20
        ),
        cost_estimate=pl.CostEstimate(
            flops=4 * table.size * width, transcendentals=0, bytes_accessed=150_000_000
        ),
        name="gather_place",
    )(rows, gates, table, dy)


def several(index, turns, count, work):
    share = -(-count // turns)
    for i in range(share):
        item = share * index + i
        pl.when((index >= 0) & (item < count))(lambda item=item: work(item))


def split_at(arrays, j, block):
    for array in arrays:
        if j < array.shape[0]:
            return array.at[j, block]
        j -= array.shape[0]


def collect_block(tables, slots, block, target):
    @pl.loop(0, target.shape[1] // COLUMNS)
    def _(n):
        columns = pl.ds(pl.multiple_of(n * COLUMNS, COLUMNS), COLUMNS)
        total = 0.0
        for j, table in enumerate(tables):
            rows = split_at(slots, j, block)[:, columns]
            total += jnp.dot(table[block], rows, preferred_element_type=FULL)
        target[:, columns] = total.astype(target.dtype)


def collect_reduce_kernel(levels, cuts, local_count, *refs):
    tables, refs = refs[:local_count], refs[local_count:]
    slots, dots, (table_ref, total_ref, gates_out, away) = refs[:2], refs[2:4], refs[4:8]
    rest, (gates, *sems) = refs[8:20], refs[20:]
    line = LineReduce(levels, cuts, away, total_ref, *rest)
    small = Exchange("expert", 2 * levels, (False,), (1,), [gates], [gates_out], *sems)
    greet("expert", [(peer, None) for peer in small.peers])
    pl.semaphore_wait(pltpu.get_barrier_semaphore(), 2 * levels - 1)
    make = functools.partial(collect_block, tables, slots)

    @pl.loop(0, 4)
    def _(turn):
        line.prepare(turn, make)

    def gate_block(block):
        table = table_ref[block].astype(FULL)
        capacity = table.shape[0] // local_count
        for j in range(local_count):
            part = table[j * capacity : (j + 1) * capacity] * split_at(dots, j, block)[...]
            gates[block, j : j + 1] = jnp.sum(part, axis=0, keepdims=True)

    def beside(turn):
        pl.when(turn + 4 < 2 * levels)(lambda: line.prepare(turn + 4, make))
        turns = levels * cuts - levels
        several(turn - levels, turns, 2 * levels, gate_block)
        pl.when(turn == levels * cuts - 1)(small.begin)

    line.main(beside)
    line.settle()
    small.arrive()
    line.finish()
    small.finish()


def collect_reduce(size, tables, slots, dots, table, number):
    levels, cuts = size // 2, REDUCE_CUTS
    block = (tables[0].shape[1], slots[0].shape[3])
    kind = slots[0].dtype
    gates = (size, len(tables), block[0])
    return pl.pallas_call(
        functools.partial(collect_reduce_kernel, levels, cuts, len(tables)),
        out_shape=[jax.ShapeDtypeStruct(block, kind), jax.ShapeDtypeStruct(gates, FULL)],
        in_specs=[VMEM] * (len(tables) + 5),
        out_specs=[ANY, ANY],
        scratch_shapes=[pltpu.VMEM((levels,) + block, kind)]
        + LineReduce.scratch(size, block, kind, cuts)
        + [pltpu.VMEM(gates, FULL)]
        + Exchange.scratch(size, (1,)),
        compiler_params=pltpu.CompilerParams(
            collective_id=number, has_side_effects=True, vmem_limit_bytes=48 << 20
        ),
        cost_estimate=pl.CostEstimate(flops=0, transcendentals=0, bytes_accessed=150_000_000),
        name="collect_reduce",
    )(*tables, *slots, *dots, table)


class SquareSum:
    def __init__(self, cuts, parts, near, far, send_sem, recv_sem, last_send, last_recv):
        self.cuts, self.parts, self.near, self.far = cuts, parts, near, far
        self.send_sem, self.recv_sem, self.last_send, self.last_recv = send_sem, recv_sem, last_send, last_recv
        self.mine = lax.axis_index("dp")
        slow, fast = lax.div(self.mine, 2), lax.rem(self.mine, 2)
        self.along = 2 * slow + 1 - fast, 2 * (1 - slow) + fast
        self.across = 2 * (1 - slow) + 1 - fast
        self.step = parts.shape[1] // cuts

    @staticmethod
    def scratch(cuts, shape, dtype):
        sems = pltpu.SemaphoreType.DMA
        buffers = [pltpu.VMEM((2,) + shape[1:], dtype), pltpu.VMEM(shape[1:], dtype)]
        return buffers + [sems((cuts, 2)), sems((cuts, 2)), sems((cuts,)), sems((cuts,))]

    def rows(self, k):
        return pl.ds(pl.multiple_of(k * self.step, self.step), self.step)

    def peer(self, k, later):
        half = lax.div(k, self.cuts // 2)
        return jnp.where(half == later, self.along[0], self.along[1])

    def first(self, k, kind):
        peer, rows = self.peer(k, 0), self.rows(k)
        source = self.parts.at[self.across if kind else peer, rows]
        sems = self.send_sem.at[k, kind], self.recv_sem.at[k, kind]
        return remote(source, self.near.at[kind, rows], *sems, {"dp": peer})

    def second(self, k):
        peer, rows = self.peer(k, 1), self.rows(k)
        sems = self.last_send.at[k], self.last_recv.at[k]
        return remote(self.parts.at[peer, rows], self.far.at[rows], *sems, {"dp": peer})

    def begin(self, k):
        self.first(k, 0).start()
        self.first(k, 1).start()

    def turn(self, k):
        self.first(k, 1).wait_recv()
        peer, rows = self.peer(k, 1), self.rows(k)
        total = self.parts[peer, rows].astype(FULL) + self.near[1, rows].astype(FULL)
        self.parts[peer, rows] = total.astype(self.parts.dtype)
        self.second(k).start()

    def arrive(self):
        for k in range(self.cuts):
            self.first(k, 0).wait_recv()
            self.second(k).wait_recv()

    def total(self, columns):
        own = self.parts[self.mine, :, columns].astype(FULL)
        return own + self.near[0, :, columns].astype(FULL) + self.far[:, columns].astype(FULL)

    def finish(self):
        for k in range(self.cuts):
            self.first(k, 0).wait_send()
            self.first(k, 1).wait_send()
            self.second(k).wait_send()


def closing_kernel(size, dp_count, local_count, cuts, sum_cuts, *refs):
    refs, levels = list(refs), size // 2

    def take(count):
        taken = refs[:count]
        del refs[:count]
        return taken

    tables, slots = take(local_count), take(2)
    proj_ref, w_ref, h_ref, gain_ref, out_parts, gain_pair, shared_ref = take(7)
    back_out, mixed_out, qkv_out, w_out, gains_out, gain_out, shared_out = take(7)
    back = LineReduce(levels, cuts, *take(1), back_out, *take(12))
    mixed = LineReduce(levels, cuts, *take(1), mixed_out, *take(12))
    square = dp_count == 4
    if square:
        qkv_parts, gains_got = take(2)
        qkv_sum = SquareSum(sum_cuts[0], qkv_parts, *take(6))
        (out_own,) = take(1)
        out_sum = SquareSum(sum_cuts[1], out_own, *take(6))
        out_own[...] = out_parts[...]
    else:
        qkv_parts, gains_got, qkv_got, out_got = take(4)
    got, half, last, gain_sum, gain_got, gain_half, gain_last = take(7)
    parts, lands, spread, some = [gain_pair], [gains_got], (True,), (1,)
    if not square:
        parts, lands = parts + [qkv_parts, out_parts], lands + [qkv_got, out_got]
        spread, some = (True, False, False), (1,) + sum_cuts
    sums = Exchange("dp", dp_count, spread, some, parts, lands, *take(3))
    first = Exchange("expert", size, (False,), (1,), [shared_ref], [got], *take(3))
    second = Exchange("dp", dp_count, (False,), (1,), [half], [last], *take(3))
    gain_first = Exchange("expert", size, (True,), (1,), [gain_sum], [gain_got], *take(3))
    gain_second = Exchange("dp", dp_count, (True,), (1,), [gain_half], [gain_last], *take(3))
    greet("expert", [(peer, None) for peer in first.peers])
    greet("dp", [(peer, None) for peer in sums.peers])
    pl.semaphore_wait(pltpu.get_barrier_semaphore(), size + dp_count - 2)
    first.begin()
    sums.staying(0).start()
    if not square:
        sums.staying(2).start()
    gain_sum[...] = jnp.zeros_like(gain_sum)
    groups, tokens, model_dim = h_ref.shape
    tall, high = half.shape[1], model_dim // dp_count

    def make_back(block, target):
        @pl.loop(0, model_dim // COLUMNS)
        def _(n):
            columns = pl.ds(pl.multiple_of(n * COLUMNS, COLUMNS), COLUMNS)
            grad = across_cols(proj_ref[block], w_ref[columns, :])
            target[:, columns] = grad.astype(target.dtype)
            weighted = grad * h_ref[block, :, columns].astype(FULL)
            gain_sum[:, columns] += jnp.sum(weighted, axis=0, keepdims=True)

    def piece(turn):
        k, copy = lax.div(turn, dp_count), lax.rem(turn, dp_count)
        columns = pl.ds(pl.multiple_of(copy * high + k * 128, 128), 128)
        rows = h_ref[:, :, columns].reshape(groups * tokens, 128)
        grads = proj_ref[...].reshape(groups * tokens, proj_ref.shape[2])
        products = contract_rows(rows, grads).astype(LOW)
        qkv_parts[copy, pl.ds(pl.multiple_of(k * 128, 128), 128)] = products
        if square:
            pl.when(copy == dp_count - 1)(lambda: qkv_sum.begin(k))
        else:
            pl.when(copy == dp_count - 1)(lambda: sums.send(1, k))
            pl.when(turn == count - 1)(lambda: sums.staying(1).start())

    make_mixed = functools.partial(collect_block, tables, slots)
    ahead = levels

    @pl.loop(0, ahead)
    def _(turn):
        back.prepare(turn, make_back)

    rest, count = levels * cuts - ahead, sum_cuts[0] * dp_count

    def beside(turn):
        later = turn - ahead
        pl.when(turn + ahead < 2 * levels)(lambda: back.prepare(turn + ahead, make_back))
        send = out_sum.begin if square else functools.partial(sums.send, 2)
        pl.when(turn < sum_cuts[1])(lambda: send(turn))
        pl.when(turn == sum_cuts[1])(lambda: sums.send(0, 0))
        pl.when(later == 0)(gain_first.begin)
        several(later, rest, 2 * levels, lambda i: mixed.prepare(i, make_mixed))
        several(later, 2 * rest, count, piece)

        @pl.when(later == rest - 1)
        def _():
            first.arrive()
            for copy in range(dp_count):
                rows = pl.ds(copy * tall, tall)
                half[copy] = sum(got[i, rows, :] for i in range(size))
            second.begin()
            gain_first.arrive()
            gain_half[...] = sum(gain_got[i] for i in range(size))
            gain_second.begin()

    back.main(beside)
    settled = 2

    def beside_mixed(turn):
        several(rest + turn, 2 * rest, count, piece)
        if square:
            pl.when((turn >= 4) & (turn < 4 + sum_cuts[1]))(lambda: out_sum.turn(turn - 4))
            pl.when(turn == 7)(lambda: qkv_sum.turn(0))
            pl.when(turn == 11)(lambda: qkv_sum.turn(1))

    mixed.main(beside_mixed)
    if square:
        for k in range(settled, sum_cuts[0]):
            qkv_sum.turn(k)
    back.settle()
    mixed.settle()
    second.arrive()
    shared_out[...] = sum(last[i] for i in range(dp_count))
    gain_second.arrive()
    gain_out[...] = sum(gain_last[i] for i in range(dp_count)) / gain_ref[...]
    sums.arrive()
    wide = qkv_out.shape[2]
    if square:
        qkv_sum.arrive()
        out_sum.arrive()
    for j in range(3):
        columns = slice(j * wide, (j + 1) * wide)
        if square:
            qkv_out[j] = qkv_sum.total(columns)
        else:
            qkv_out[j] = sum(qkv_got[copy, :, columns].astype(FULL) for copy in range(dp_count))
    if square:
        w_out[...] = out_sum.total(slice(None))
    else:
        w_out[...] = sum(out_got[copy].astype(FULL) for copy in range(dp_count))
    gains_out[...] = sum(gains_got[copy] for copy in range(dp_count))
    moved = [back, mixed, first, second, sums, gain_first, gain_second]
    for moves in moved + ([qkv_sum, out_sum] if square else []):
        moves.finish()


def closing(size, dp_count, tables, slots, arrays, sums, shared, number):
    proj, _, hidden, gain = arrays
    levels, cuts = size // 2, REDUCE_CUTS
    _, tokens, model_dim = hidden.shape
    columns, high = proj.shape[2], model_dim // dp_count
    block = (tokens, model_dim)
    tall = shared.shape[1] // dp_count
    wide = shared.shape[2]
    sum_cuts = (high // 128, 2)
    parts = (dp_count, high, columns)
    out, pair = exchange_outs(dp_count, sums, (False, True))
    shapes = [(3, high, columns // 3), out.shape[1:], pair.shape[1:], gain.shape, (tall, wide)]
    outs = [jax.ShapeDtypeStruct(block, LOW)] * 2
    outs += [jax.ShapeDtypeStruct(shape, FULL) for shape in shapes]
    if dp_count == 4:
        landing, some = SquareSum.scratch(sum_cuts[0], parts, LOW), (1,)
        landing += [pltpu.VMEM(out.shape, LOW)] + SquareSum.scratch(sum_cuts[1], out.shape, LOW)
    else:
        landing, some = [pltpu.VMEM(parts, LOW), pltpu.VMEM(out.shape, LOW)], (1,) + sum_cuts
    line = [pltpu.VMEM((levels,) + block, LOW)] + LineReduce.scratch(size, block, LOW, cuts)
    return pl.pallas_call(
        functools.partial(closing_kernel, size, dp_count, len(tables), cuts, sum_cuts),
        out_shape=outs,
        in_specs=[VMEM] * (len(tables) + 7) + [ANY] * 2,
        out_specs=[ANY] * 2 + [VMEM] * 5,
        scratch_shapes=line
        + line
        + [pltpu.VMEM(parts, LOW), pltpu.VMEM(pair.shape, FULL)]
        + landing
        + [pltpu.VMEM((size,) + shared.shape[1:], FULL)]
        + [pltpu.VMEM((dp_count, tall, wide), FULL)] * 2
        + [
            pltpu.VMEM(gain.shape, FULL),
            pltpu.VMEM((size,) + gain.shape, FULL),
            pltpu.VMEM(gain.shape, FULL),
            pltpu.VMEM((dp_count,) + gain.shape, FULL),
        ]
        + Exchange.scratch(dp_count, some)
        + Exchange.scratch(size, (1,))
        + Exchange.scratch(dp_count, (1,))
        + Exchange.scratch(size, (1,))
        + Exchange.scratch(dp_count, (1,)),
        compiler_params=pltpu.CompilerParams(
            collective_id=number, has_side_effects=True, vmem_limit_bytes=62 << 20
        ),
        cost_estimate=pl.CostEstimate(flops=0, transcendentals=0, bytes_accessed=200_000_000),
        name="closing",
    )(*tables, *slots, *arrays, *sums, shared)


def across_cols(left_side, right_side):
    return lax.dot_general(
        left_side, right_side, (((1,), (1,)), ((), ())), preferred_element_type=FULL
    )


def expert_kernel(first, count, tiles, x_ref, dy_ref, scale_ref, side_ref, down_ref, grads_ref, out_ref, back_ref, dots_ref,
                  side_w, down_w, turned, turned_act, act, grad_side, side_buf, down_buf, w_sems, sems):
    e, step = pl.program_id(0), pl.program_id(1)
    slot = lax.rem(e, 2)
    hidden, model = down_w.shape[1], down_w.shape[2]
    width, wide = hidden // tiles, model // tiles
    copies = grads_ref.shape[0]
    high, low = model // copies, hidden // copies
    part = side_buf.shape[1]

    def loads(e, tile):
        slot = lax.rem(e, 2)
        out = []
        for half in range(2):
            columns = pl.ds(pl.multiple_of(half * hidden + tile * width, 128), width)
            out.append(pltpu.make_async_copy(side_ref.at[first + e, :, columns], side_w.at[slot, :, columns], w_sems.at[slot, tile, half]))
        rows = pl.ds(pl.multiple_of(tile * width, 128), width)
        out.append(pltpu.make_async_copy(down_ref.at[first + e, rows], down_w.at[slot, rows], w_sems.at[slot, tile, 2]))
        return out

    def leaving(at):
        e, chunk = lax.div(at, tiles), lax.rem(at, tiles)
        slot = lax.rem(at, 2)
        base = e * (high + low)
        columns = pl.ds(pl.multiple_of(chunk * wide, 128), wide)
        if wide >= high:
            target = grads_ref.at[pl.ds(chunk * part, part), pl.ds(base, high)]
        else:
            target = grads_ref.at[pl.ds(lax.div(chunk * wide, high), 1), pl.ds(base + lax.rem(chunk * wide, high), wide)]
        return (pltpu.make_async_copy(side_buf.at[slot], target, sems.at[slot, 0]),
                pltpu.make_async_copy(down_buf.at[slot], grads_ref.at[:, pl.ds(base + high, low), columns], sems.at[slot, 1]))

    @pl.when((e == 0) & (step == 0))
    def _():
        for tile in range(tiles):
            for copy in loads(e, tile): copy.start()

    @pl.when((e + 1 < count) & (step == 0))
    def _():
        for tile in range(tiles):
            for copy in loads(e + 1, tile): copy.start()

    @pl.when(step == 0)
    def _():
        turned[...] = x_ref[0].T
        dots_ref[...] = jnp.zeros_like(dots_ref)

    @pl.when(step < tiles)
    def _():
        for copy in loads(e, step): copy.wait()
        rows, grads, scale = x_ref[0], dy_ref[0], scale_ref[0]
        columns = pl.ds(pl.multiple_of(step * width, 128), width)
        others = pl.ds(pl.multiple_of(hidden + step * width, 128), width)
        gate = jnp.dot(rows, side_w[slot, :, columns], preferred_element_type=FULL)
        up = jnp.dot(rows, side_w[slot, :, others], preferred_element_type=FULL)
        grad_act = across_cols(grads, down_w[slot, columns, :])
        sigmoid = jax.nn.sigmoid(gate)
        silu = gate * sigmoid
        raw = silu * up
        dots_ref[0] += jnp.sum(raw * grad_act, axis=-1, keepdims=True)
        weighted = (scale * raw).astype(LOW)
        act[:, columns] = weighted
        turned_act[columns, :] = weighted.T
        grad_act = grad_act * scale
        grad_side[:, columns] = (grad_act * up * sigmoid * (1.0 + gate * (1.0 - sigmoid))).astype(LOW)
        grad_side[:, others] = (grad_act * silu).astype(LOW)

    @pl.when(step >= tiles)
    def _():
        chunk = step - tiles
        at = e * tiles + chunk
        spot = lax.rem(at, 2)
        columns = pl.ds(pl.multiple_of(chunk * wide, 128), wide)

        @pl.when(at >= 2)
        def _():
            for copy in leaving(at - 2): copy.wait()
        total = jnp.dot(turned[columns, :], grad_side[...], preferred_element_type=FULL)
        side_buf[spot] = total.astype(LOW).reshape(side_buf.shape[1:])
        leaving(at)[0].start()
        total = jnp.dot(turned_act[...], dy_ref[0, :, columns], preferred_element_type=FULL)
        down_buf[spot] = total.astype(LOW).reshape(down_buf.shape[1:])
        leaving(at)[1].start()
        back_ref[0, :, columns] = across_cols(grad_side[...], side_w[slot, columns, :]).astype(LOW)
        out_ref[0, :, columns] = jnp.dot(act[...], down_w[slot, :, columns], preferred_element_type=FULL).astype(LOW)

        @pl.when(at == count * tiles - 1)
        def _():
            for copy in leaving(at - 1) + leaving(at): copy.wait()

def expert(first, count, dp_count, x_rows, dy_rows, scales, w_gate_up, w_down, tiles=4):
    _, slots, width = x_rows.shape
    hidden = w_down.shape[1]
    high, low = width // dp_count, hidden // dp_count
    wide = width // tiles
    part = max(1, wide // high)
    rs = pl.BlockSpec((1, slots, width), lambda e, f: (first + e, 0, 0))
    os = pl.BlockSpec((1, slots, width), lambda e, f: (e, 0, 0))
    sems = pltpu.SemaphoreType.DMA
    return pl.pallas_call(
        functools.partial(expert_kernel, first, count, tiles),
        out_shape=[jax.ShapeDtypeStruct((dp_count, count * (high + low), width), LOW),
                   jax.ShapeDtypeStruct((count, slots, width), LOW), jax.ShapeDtypeStruct((count, slots, width), LOW),
                   jax.ShapeDtypeStruct((count, slots, 1), FULL)],
        grid=(count, 2 * tiles),
        in_specs=[rs, rs, pl.BlockSpec((1, slots, 1), lambda e, f: (first + e, 0, 0)), ANY, ANY],
        out_specs=[ANY, os, os, pl.BlockSpec((1, slots, 1), lambda e, f: (e, 0, 0))],
        scratch_shapes=[pltpu.VMEM((min(2, count), width, 2 * hidden), LOW), pltpu.VMEM((min(2, count), hidden, width), LOW),
                        pltpu.VMEM((width, slots), LOW), pltpu.VMEM((hidden, slots), LOW), pltpu.VMEM((slots, hidden), LOW), pltpu.VMEM((slots, 2 * hidden), LOW),
                        pltpu.VMEM((2, part, min(wide, high), 2 * hidden), LOW), pltpu.VMEM((2, dp_count, low, wide), LOW),
                        sems((min(2, count), tiles, 3)), sems((2, 2))],
        compiler_params=pltpu.CompilerParams(vmem_limit_bytes=62 << 20),
        cost_estimate=pl.CostEstimate(
            flops=18 * count * slots * width * hidden,
            transcendentals=count * slots * hidden,
            bytes_accessed=12 * count * width * hidden,
        ),
        name="expert",
    )(x_rows, dy_rows, scales, w_gate_up, w_down)


def rms_scale(values):
    return lax.rsqrt(jnp.mean(values * values, axis=-1, keepdims=True) + NORM_EPS)


def rotary_tables(length, size):
    index = np.arange(size // 2, dtype=np.float32)
    frequency = np.exp(index * np.float32(-2.0 * math.log(10000.0) / size))
    angles = np.arange(length, dtype=np.float32)[:, None] * frequency[None, :]
    cosine, sine = np.cos(angles), np.sin(angles)
    halves = [np.concatenate([cosine, cosine], axis=1), np.concatenate([-sine, sine], axis=1)]
    return jnp.asarray(np.stack(halves).astype(np.float32))


def norm_back(grad_normed, normed, scale_rows):
    return scale_rows * (
        grad_normed - normed * jnp.mean(grad_normed * normed, axis=-1, keepdims=True)
    )


def contract_rows(left_side, right_side):
    return lax.dot_general(
        left_side, right_side, (((0,), (0,)), ((), ())), preferred_element_type=FULL
    )


def contract_cols(left_side, right_side):
    return lax.dot_general(
        left_side, right_side, (((1,), (1,)), ((), ())), preferred_element_type=FULL
    )


def einsum(spec, left_side, right_side):
    return jnp.einsum(spec, left_side, right_side, preferred_element_type=FULL)


def widen_kernel(steps, *refs):
    low_ref, high_ref, down_ref = refs[0], refs[-2], refs[-1]
    step = pl.program_id(1)

    @pl.when(step < steps)
    def _():
        high_ref[...] = low_ref[...].astype(FULL)

    @pl.when(step >= steps)
    def _():
        down_ref[...] = low_ref[...].astype(FULL)


def widen(first, total, high, grads, held=()):
    count, both, width = grads.shape
    low = both - high
    rows = low
    steps = high // rows
    block = (1, rows, width)
    return pl.pallas_call(
        functools.partial(widen_kernel, steps),
        out_shape=[
            jax.ShapeDtypeStruct((total, high, width), FULL),
            jax.ShapeDtypeStruct((total, low, width), FULL),
        ],
        grid=(count, steps + 1),
        in_specs=[pl.BlockSpec(block, lambda e, r: (e, r, 0))] + [ANY] * len(held),
        out_specs=[
            pl.BlockSpec(block, lambda e, r: (first + e, jnp.minimum(r, steps - 1), 0)),
            pl.BlockSpec(block, lambda e, r: (first + e, jnp.maximum(r - steps, 0), 0)),
        ],
        input_output_aliases={1: 0, 2: 1} if held else {},
        cost_estimate=pl.CostEstimate(
            flops=grads.size, transcendentals=0, bytes_accessed=6 * grads.size
        ),
        name="widen",
    )(grads, *held)


def turn(values, cosine, sine):
    return values * cosine + pltpu.roll(values, values.shape[1] // 2, 1) * sine


def allowed_pairs(column, row):
    shape = (column.shape[0], row.shape[1])
    later = lax.broadcasted_iota(jnp.int32, shape, 0) >= lax.broadcasted_iota(jnp.int32, shape, 1)
    return later & (column == row)


def softmax(query, key, allowed):
    scores = across_cols(query, key) * (1.0 / math.sqrt(query.shape[1]))
    scores = jnp.where(allowed, scores, -1e30)
    powers = jnp.exp(scores - jnp.max(scores, axis=-1, keepdims=True))
    return powers / jnp.sum(powers, axis=-1, keepdims=True)


def attend_block(heads, block, rows_ref, scales, gain_ref, turn_ref, column, row, kept_ref, out_ref):
    width = out_ref.shape[2]
    size = width // heads
    allowed = allowed_pairs(column, row)
    cosine, sine = turn_ref[0], turn_ref[1]
    for h in range(heads):
        parts = []
        for part in range(3):
            columns = pl.ds(part * width + h * size, size)
            values = rows_ref[block, :, columns]
            if part < 2:
                values = values * scales[part]
                values = values * gain_ref[part : part + 1, h * size : (h + 1) * size]
                values = turn(values, cosine, sine)
            parts.append(values.astype(LOW))
            kept_ref[block, :, columns] = parts[-1]
        query, key, value = parts
        probs = softmax(query, key, allowed).astype(LOW)
        out_ref[block, :, pl.ds(h * size, size)] = jnp.dot(
            probs, value, preferred_element_type=FULL
        ).astype(LOW)


def attention_kernel(size, dp_count, heads, *refs):
    x_ref, w_ref, gain_ref, gains_ref, turn_ref, column_ref, row_ref, sheet_ref, dy_ref = refs[:9]
    h_out, rows_out, scale_ref, kept_ref, out_ref, own_out, sheet_out, dy_out = refs[9:17]
    x_held, h_held, rows, sums, squares, got = refs[17:23]
    x_sem, h_sem, rows_sem, send_sem, recv_sem, stay_sem = refs[23:29]
    square_sems, line_sems, sheet_sems = refs[29:32], refs[32:37], refs[37:]
    line = LineGather(size // 2, GATHER_CUTS, [dy_ref], [dy_out], *line_sems)
    sheets = Sheets(size, dp_count, sheet_ref, sheet_out, *sheet_sems)
    small = Exchange("expert", size, (True,), (1,), [squares], [got], *square_sems)
    place, model_dim = sheets.place, x_ref.shape[2]
    width = out_ref.shape[2]

    def loading(g):
        return pltpu.make_async_copy(x_ref.at[g], x_held.at[g], x_sem.at[g])

    def leaving(g):
        return (
            pltpu.make_async_copy(h_held.at[g], h_out.at[g], h_sem.at[g]),
            pltpu.make_async_copy(rows.at[g], rows_out.at[g], rows_sem.at[g]),
        )

    for g in range(size):
        loading(g).start()
    greet("expert", [(peer, None) for peer in small.peers])
    greet("dp", [(peer, None) for peer in sheets.peers])
    pl.semaphore_wait(pltpu.get_barrier_semaphore(), size + dp_count - 2)
    sheets.begin()
    line.begin()
    sums[...] = jnp.zeros_like(sums)
    lanes = lax.broadcasted_iota(jnp.int32, sums.shape, 1)

    @pl.loop(0, size)
    def _(g):
        loading(g).wait()
        values = x_held[g].astype(FULL)
        hidden = (values * rms_scale(values) * gain_ref[...]).astype(LOW)
        h_held[g] = hidden
        projected = jnp.dot(hidden, w_ref[...], preferred_element_type=FULL)
        rows[g] = projected
        for copy in leaving(g):
            copy.start()
        for part in range(2):
            half = projected[:, part * width : (part + 1) * width]
            total = jnp.sum(half * half, axis=-1, keepdims=True)
            sums[...] += jnp.where(lanes == part * size + g, total, 0.0)

    squares[...] = sums[...].T[: 2 * size]
    small.begin()
    sheets.forward(1)
    small.arrive()
    total = sum(got[i] for i in range(size))
    sums[:, : 2 * size] = lax.rsqrt(total / model_dim + NORM_EPS).T

    def sending(g, source):
        columns = pl.ds(pl.multiple_of(source * width, 128), width)
        target = own_out.at[:, columns]
        return remote(out_ref.at[g], target, send_sem.at[g], recv_sem.at[source], {"expert": g})

    own_columns = pl.ds(pl.multiple_of(place * width, 128), width)
    staying = pltpu.make_async_copy(out_ref.at[place], own_out.at[:, own_columns], stay_sem.at[0])

    @pl.loop(0, size)
    def _(i):
        g = lax.rem(place + 1 + i, size)
        scales = [
            jnp.sum(jnp.where(lanes == part * size + g, sums[...], 0.0), axis=-1, keepdims=True)
            for part in range(2)
        ]
        scale_ref[g] = jnp.concatenate(scales, axis=1)
        attend_block(
            heads, g, rows, scales, gains_ref, turn_ref, column_ref[g], row_ref[g], kept_ref, out_ref
        )
        pl.when(g != place)(lambda: sending(g, place).start())
        pl.when(lax.rem(i, 2) == 1)(lambda: line.turn(lax.div(i, 2)))

    staying.start()

    @pl.loop(size // 2, 2 * size)
    def _(i):
        for step in range(2, size // 2):
            pl.when(i == (step - 1) * (size // 2))(lambda: sheets.forward(step))
        line.turn(i)
        after = i - size - size // 2
        pl.when((after >= 0) & (after < size // 2))(lambda: sheets.cross(after))


    @pl.loop(1, size)
    def _(i):
        peer = lax.rem(place + i, size)
        sending(peer, peer).wait_recv()
        sending(peer, place).wait_send()

    @pl.loop(0, size)
    def _(g):
        for copy in leaving(g):
            copy.wait()

    staying.wait()
    small.finish()
    line.finish()
    sheets.finish()


def attention(size, dp_count, heads, arrays, number):
    x_all, w_here, sheet, dy = arrays[0], arrays[1], arrays[7], arrays[8]
    _, tokens, model_dim = x_all.shape
    columns = w_here.shape[1]
    width = columns // 3
    sems = pltpu.SemaphoreType.DMA
    seqs = (size, tokens)
    small = (2 * size, tokens)
    return pl.pallas_call(
        functools.partial(attention_kernel, size, dp_count, heads),
        out_shape=[
            jax.ShapeDtypeStruct(x_all.shape, LOW),
            jax.ShapeDtypeStruct(seqs + (columns,), FULL),
            jax.ShapeDtypeStruct(seqs + (2,), FULL),
            jax.ShapeDtypeStruct(seqs + (columns,), LOW),
            jax.ShapeDtypeStruct(seqs + (width,), LOW),
            jax.ShapeDtypeStruct((tokens, model_dim), LOW),
            jax.ShapeDtypeStruct((dp_count, size) + sheet.shape, LOW),
            jax.ShapeDtypeStruct((size,) + dy.shape, LOW),
        ],
        in_specs=[ANY] + [VMEM] * 6 + [ANY] * 2,
        out_specs=[ANY] * 2 + [VMEM] * 3 + [ANY] * 3,
        scratch_shapes=[
            pltpu.VMEM(x_all.shape, LOW),
            pltpu.VMEM(x_all.shape, LOW),
            pltpu.VMEM(seqs + (columns,), FULL),
            pltpu.VMEM((tokens, 128), FULL),
            pltpu.VMEM(small, FULL),
            pltpu.VMEM((size,) + small, FULL),
            sems((size,)),
            sems((size,)),
            sems((size,)),
            sems((size,)),
            sems((size,)),
            sems((1,)),
        ]
        + Exchange.scratch(size, (1,))
        + LineGather.scratch(size, GATHER_CUTS, 1)
        + Sheets.scratch(size, dp_count),
        compiler_params=pltpu.CompilerParams(
            collective_id=number, has_side_effects=True, vmem_limit_bytes=48 << 20
        ),
        cost_estimate=pl.CostEstimate(
            flops=2 * x_all.size * columns, transcendentals=0, bytes_accessed=100_000_000
        ),
        name="attention",
    )(*arrays)


def attend_back_block(heads, block, grad_ref, refs, back_ref, dots_ref, lanes, gains_ref, w_sum):
    w_ref, kept_ref, out_ref, rows_ref, scale_ref, gain_ref, turn_ref, column_ref, row_ref = refs
    width = out_ref.shape[2]
    size = width // heads
    scaling = 1.0 / math.sqrt(size)
    allowed = allowed_pairs(column_ref[block], row_ref[block])
    cosine, sine = turn_ref[0], turn_ref[1]
    grad_rows = grad_ref[block]
    grad_out = across_cols(grad_rows, w_ref[...]).astype(LOW)
    w_sum[...] += contract_rows(out_ref[block], grad_rows)
    dots = [0.0, 0.0]
    for h in range(heads):
        mine = slice(h * size, (h + 1) * size)
        query, key, value = (
            kept_ref[block, :, pl.ds(p * width + h * size, size)] for p in range(3)
        )
        probs = softmax(query, key, allowed)
        grad = grad_out[:, mine]
        grad_value = contract_rows(probs.astype(LOW), grad)
        grad_probs = across_cols(grad, value)
        delta = jnp.sum(grad_probs * probs, axis=-1, keepdims=True)
        grad_scores = (probs * (grad_probs - delta)).astype(LOW)
        grad_query = jnp.dot(grad_scores, key, preferred_element_type=FULL) * scaling
        grad_key = contract_rows(grad_scores, query) * scaling
        for part, grad_turned in enumerate((grad_query, grad_key)):
            columns = pl.ds(part * width + h * size, size)
            grad_normed = turn(grad_turned, cosine, -sine)
            normed = rows_ref[block, :, columns] * scale_ref[block, :, part : part + 1]
            gains_ref[part : part + 1, mine] += jnp.sum(grad_normed * normed, axis=0, keepdims=True)
            weighted = grad_normed * gain_ref[part : part + 1, mine]
            dots[part] += jnp.sum(weighted * normed, axis=-1, keepdims=True)
            back_ref[block, :, columns] = weighted
        back_ref[block, :, pl.ds(2 * width + h * size, size)] = grad_value
    groups = grad_ref.shape[0]
    for part in range(2):
        dots_ref[...] += jnp.where(lanes == part * groups + block, dots[part], 0.0)


def attend_back_kernel(levels, cuts, heads, grad_ref, *refs):
    w_ref, others, refs = refs[0], refs[1:9], refs[9:]
    proj_ref, gains_ref, w_grad_ref, w_sum, held, w_held, back, dots, squares, got, w_sem = refs[:11]
    reads = (w_held,) + tuple(others)
    rows_ref, scale_ref = others[2:4]
    size, model_dim = 2 * levels, grad_ref.shape[1]
    line = LineGather(levels, cuts, [grad_ref], [held], *refs[11:16])
    small = Exchange("expert", size, (True,), (1,), [squares], [got], *refs[16:])
    mine = pl.ds(pl.multiple_of(line.place * w_held.shape[0], 128), w_held.shape[0])
    loading = pltpu.make_async_copy(w_ref.at[mine], w_held, w_sem.at[0])
    loading.start()
    greet("expert", [(peer, None) for peer in small.peers])
    pl.semaphore_wait(pltpu.get_barrier_semaphore(), size - 1)
    line.begin()
    w_sum[...] = jnp.zeros_like(w_sum)
    gains_ref[...] = jnp.zeros_like(gains_ref)
    dots[...] = jnp.zeros_like(dots)
    lanes = lax.broadcasted_iota(jnp.int32, dots.shape, 1)
    loading.wait()
    line.staying(0).wait()

    def landed(block):
        attend_back_block(heads, block, held, reads, back, dots, lanes, gains_ref, w_sum)

    line.main(landed)
    squares[...] = dots[...].T[: 2 * size]
    small.begin()
    wide = w_grad_ref.shape[2]
    for copy in range(w_grad_ref.shape[0]):
        w_grad_ref[copy] = w_sum[:, copy * wide : (copy + 1) * wide].astype(LOW)
    small.arrive()
    dots[:, : 2 * size] = sum(got[i] for i in range(size)).T / model_dim
    width = w_held.shape[0]

    @pl.loop(0, size)
    def _(block):
        for part in range(2):
            columns = pl.ds(part * width, width)
            scale = scale_ref[block, :, part : part + 1]
            mean = jnp.where(lanes == part * size + block, dots[...], 0.0)
            mean = jnp.sum(mean, axis=-1, keepdims=True)
            normed = rows_ref[block, :, columns] * scale
            proj_ref[block, :, columns] = (scale * (back[block, :, columns] - normed * mean)).astype(LOW)
        columns = pl.ds(2 * width, width)
        proj_ref[block, :, columns] = back[block, :, columns].astype(LOW)

    line.finish(held=1)
    small.finish()


def attend_back(size, dp_count, heads, grad, arrays, number):
    _, _, out, rows = arrays[:4]
    width = out.shape[2]
    tokens, model_dim = grad.shape
    small = (2 * size, tokens)
    return pl.pallas_call(
        functools.partial(attend_back_kernel, size // 2, GATHER_CUTS, heads),
        out_shape=[
            jax.ShapeDtypeStruct(rows.shape, LOW),
            jax.ShapeDtypeStruct((2, width), FULL),
            jax.ShapeDtypeStruct((dp_count, width, model_dim // dp_count), LOW),
        ],
        in_specs=[ANY] * 2 + [VMEM] * (len(arrays) - 1),
        out_specs=[VMEM] * 3,
        scratch_shapes=[
            pltpu.VMEM((width, model_dim), FULL),
            pltpu.VMEM((size, tokens, model_dim), LOW),
            pltpu.VMEM((width, model_dim), LOW),
            pltpu.VMEM(rows.shape, FULL),
            pltpu.VMEM((tokens, 128), FULL),
            pltpu.VMEM(small, FULL),
            pltpu.VMEM((size,) + small, FULL),
            pltpu.SemaphoreType.DMA((1,)),
        ]
        + LineGather.scratch(size, GATHER_CUTS, 1)
        + Exchange.scratch(size, (1,)),
        compiler_params=pltpu.CompilerParams(
            collective_id=number, has_side_effects=True, vmem_limit_bytes=48 << 20
        ),
        cost_estimate=pl.CostEstimate(flops=0, transcendentals=0, bytes_accessed=150_000_000),
        name="attend_back",
    )(grad, *arrays)


def on_device(
    dp_count,
    line_count,
    layer_input,
    out_cotangent,
    segments,
    routes,
    w_qkv,
    w_out,
    w_router,
    attn_gain,
    mlp_gain,
    query_gain,
    key_gain,
    w_gate_up,
    w_down,
):
    row_count, model_dim = layer_input.shape
    top_count = routes.shape[1]
    expert_count = w_router.shape[1]
    local_count = w_gate_up.shape[0]
    head_size = model_dim // HEADS
    head_cols = model_dim // line_count
    heads_here = head_cols // head_size
    capacity = (row_count * top_count * 9 // 8 + expert_count - 1) // expert_count
    scaling = 1.0 / math.sqrt(head_size)
    place = lax.axis_index("expert")
    shard = w_qkv.shape[0]

    numbers = jnp.concatenate([routes.T, segments, jnp.zeros((7, row_count), jnp.int32)], axis=0)
    x_all, numbers_all, qkv_here, router_full, gains = opening(
        line_count,
        dp_count,
        [layer_input, numbers],
        GATHER_CUTS,
        w_qkv,
        [w_router, jnp.stack([attn_gain, mlp_gain, query_gain, key_gain])],
        1,
    )
    qkv_here = qkv_here.reshape(model_dim, 3 * head_cols)
    router_full = router_full.reshape(model_dim, expert_count)
    gains = gains.transpose(2, 0, 1, 3).reshape(4, model_dim).astype(FULL)
    gain_attn, gain_mlp = gains[0], gains[1]
    both_gains = lax.dynamic_slice_in_dim(gains[2:], place * head_cols, head_cols, axis=1)

    routes_all = numbers_all[:, :top_count]
    segments_all = numbers_all[:, top_count]
    turns = rotary_tables(row_count, head_size)
    column, row = segments_all[:, :, None], segments_all[:, None, :]
    arrays = [x_all, qkv_here, gain_attn[None], both_gains, turns, column, row, w_out, out_cotangent]
    hidden_one, projected, scales, kept, attended, own_attended, out_full, dy_all = attention(
        line_count, dp_count, heads_here, arrays, 4
    )
    out_full = out_full.reshape(model_dim, model_dim)
    inputs = layer_input.astype(FULL)
    scale_attn = rms_scale(inputs)
    normed_attn = inputs * scale_attn
    residual = inputs + jnp.dot(own_attended, out_full, preferred_element_type=FULL)
    scale_mlp = rms_scale(residual)
    normed_mlp = residual * scale_mlp
    hidden_two = (normed_mlp * gain_mlp).astype(LOW)

    logits = jnp.dot(hidden_two, router_full, preferred_element_type=FULL)
    chosen = jnp.any(routes[:, :, None] == jnp.arange(expert_count)[None, None, :], axis=1)
    masked = jnp.where(chosen, logits, -1e30)
    powers = jnp.where(chosen, jnp.exp(masked - jnp.max(masked, axis=-1, keepdims=True)), 0.0)
    gates = powers / jnp.sum(powers, axis=-1, keepdims=True)

    local = place * local_count + jnp.arange(local_count)
    used = jnp.any(routes_all[:, None] == local[None, :, None, None], axis=2)
    position = jnp.arange(row_count)
    lower = (position[:, None] < position[None, :]).astype(LOW)
    rank = einsum("gju,ut->gjt", used.astype(LOW), lower).astype(jnp.int32)
    rank = jnp.where(used, rank, -1)
    spots = jnp.arange(capacity)
    table = (rank[:, :, None, :] == spots[None, None, :, None]).astype(LOW)
    returns = [(rank[:, j, :, None] == spots[None, None, :]).astype(LOW) for j in range(local_count)]
    slots = line_count * capacity
    flat_table = table.reshape(line_count, local_count * capacity, row_count)
    expert_rows, dy_rows, gates_all = gather_place(
        line_count, hidden_two, gates.T, flat_table, dy_all, local_count, 6
    )
    local_gates = lax.dynamic_slice_in_dim(gates_all, place * local_count, local_count, axis=1)
    slot_gates = jnp.sum(table.astype(FULL) * local_gates[:, :, None, :], axis=-1)
    slot_gates = slot_gates.transpose(1, 0, 2).reshape(local_count, slots, 1)
    out_rows, back_rows, slot_grads, grad_sums = [], [], [], []
    both_rows = model_dim // dp_count + w_down.shape[1] // dp_count
    for first, count in ((0, 1), (1, local_count - 1)):
        grads, out_row, back_row, dots = expert(
            first, count, dp_count, expert_rows, dy_rows, slot_gates, w_gate_up, w_down
        )
        grads = grads.reshape(-1, model_dim)
        grads = lax.psum_scatter(grads, "dp", scatter_dimension=0, tiled=True)
        grad_sums.append(grads.reshape(count, both_rows, model_dim))
        for kept_list, rows in ((out_rows, out_row), (back_rows, back_row), (slot_grads, dots)):
            kept_list.append(rows.reshape(count, line_count, capacity, rows.shape[2]))
    gate_rows = model_dim // dp_count
    grad_two, grad_gates = collect_reduce(
        line_count, returns, back_rows, slot_grads, flat_table, 8
    )
    grad_gates = grad_gates.reshape(expert_count, row_count).T
    grad_two = grad_two.astype(FULL)

    grad_out_rows = out_cotangent.astype(FULL)
    grad_logits = gates * (grad_gates - jnp.sum(gates * grad_gates, axis=-1, keepdims=True))
    grad_logits = grad_logits.astype(LOW)
    grad_router = contract_rows(grad_logits, hidden_two)
    grad_two = grad_two + contract_cols(grad_logits, router_full)
    grad_gain_mlp = jnp.sum(grad_two * normed_mlp, axis=0)
    grad_resid = grad_out_rows + norm_back(grad_two * gain_mlp, normed_mlp, scale_mlp)
    grad_attn = grad_resid.astype(LOW)

    arrays = [out_full, kept, attended, projected, scales, both_gains, turns, column, row]
    grad_proj, gain_pair, out_parts = attend_back(
        line_count, dp_count, heads_here, grad_attn, arrays, 11
    )

    shared = jnp.concatenate([grad_router, grad_gain_mlp[None]], axis=0)
    tall = shared.shape[0] + -shared.shape[0] % 8
    shared = jnp.pad(shared, ((0, tall - shared.shape[0]), (0, 0)))
    shared = shared.reshape(tall, dp_count, line_count, shard).transpose(2, 1, 0, 3)
    shared = shared.reshape(line_count, dp_count * tall, shard)
    shared = jnp.pad(shared, ((0, 0), (0, 0), (0, 128 - shard)))
    arrays = [grad_proj, qkv_here, hidden_one, gain_attn[None]]
    grad_one, mixture, sum_qkv, sum_out, gain_pair, gain_sum, shared = closing(
        line_count, dp_count, returns, out_rows, arrays, [out_parts, gain_pair], shared, 14
    )
    here = (lax.axis_index("dp") * line_count + place) * shard
    grad_gain_attn = lax.dynamic_slice_in_dim(gain_sum[0], here, shard)
    output = (residual + mixture.astype(FULL)).astype(LOW)
    sum_qkv = sum_qkv.transpose(1, 0, 2)
    first_sums, mixture = lax.optimization_barrier((grad_sums[0], mixture))
    wide = widen(0, local_count, gate_rows, first_sums)
    sum_gate_up, sum_down = widen(1, local_count, gate_rows, grad_sums[1], wide)
    shared = shared[:, :shard]
    grad_one = grad_one.astype(FULL)
    grad_inputs = grad_resid + norm_back(grad_one * gain_attn, normed_attn, scale_attn)
    return (
        output,
        grad_inputs,
        sum_qkv,
        sum_out,
        shared[:expert_count].T,
        grad_gain_attn,
        shared[expert_count],
        gain_pair[0],
        gain_pair[1],
        sum_gate_up,
        sum_down,
    )


def solution(mesh):
    both = ("dp", "expert")
    rows, flat = P(both, None), P(both)
    placed = (rows,) * 7 + (flat,) * 4 + (P("expert", None, None),) * 2
    return jax.shard_map(
        functools.partial(on_device, mesh.shape["dp"], mesh.shape["expert"]),
        mesh=mesh,
        in_specs=placed,
        out_specs=(
            rows,
            rows,
            P("dp", None, "expert"),
            P("expert", "dp"),
            rows,
            flat,
            flat,
            P("expert"),
            P("expert"),
            P("expert", "dp", None),
            P("expert", "dp", None),
        ),
        check_vma=False,
    )
```

```python
import functools
import math

import jax
import jax.numpy as jnp
import numpy as np
from jax import lax
from jax.experimental import pallas as pl
from jax.experimental.pallas import tpu as pltpu
from jax.sharding import PartitionSpec as P

HEADS = 16
NORM_EPS = 1e-05
MESH = pl.DeviceIdType.MESH
ANY = pl.BlockSpec(memory_space=pl.ANY)
LOW = jnp.bfloat16
GATHER_CUTS, REDUCE_CUTS = 4, 3
FULL = jnp.float32


def line_place():
    place = lax.axis_index("expert")
    level, side = lax.div(place, 2), lax.rem(place, 2)
    return place, level, side, place + 1 - 2 * side


def greet(axis, targets):
    barrier = pltpu.get_barrier_semaphore()
    for target, there in targets:

        def signal(target=target):
            pl.semaphore_signal(barrier, inc=1, device_id={axis: target}, device_id_type=MESH)

        if there is None:
            signal()
        else:
            pl.when(there)(signal)


def line_barrier(levels):
    place, level, _, other = line_place()
    has_up, has_down = level < levels - 1, level > 0
    greet("expert", [(other, None), (place + 2, has_up), (place - 2, has_down)])
    count = 1 + has_up.astype(jnp.int32) + has_down.astype(jnp.int32)
    pl.semaphore_wait(pltpu.get_barrier_semaphore(), count)


def around(axis, size):
    place = lax.axis_index(axis)
    return [lax.rem(place + shift, size) for shift in range(1, size)]


def remote(source, target, send, recv, device):
    return pltpu.make_async_remote_copy(
        src_ref=source,
        dst_ref=target,
        send_sem=send,
        recv_sem=recv,
        device_id=device,
        device_id_type=MESH,
    )


class LineGather:
    def __init__(self, levels, cuts, ins, outs, up_sem, down_sem, side_sem, recv_sem, own_sem):
        self.levels, self.cuts, self.ins, self.outs = levels, cuts, ins, outs
        self.up_sem, self.down_sem, self.side_sem = up_sem, down_sem, side_sem
        self.recv_sem, self.own_sem = recv_sem, own_sem
        self.place, self.level, self.side, self.other = line_place()
        self.has_up, self.has_down = self.level < levels - 1, self.level > 0

    @staticmethod
    def scratch(size, cuts, count):
        levels, total = size // 2, cuts + count - 1
        shapes = ((levels, total), (levels, total), (2 * levels - 1, total), (size, total))
        return [pltpu.SemaphoreType.DMA(shape) for shape in shapes + ((count,),)]

    def pieces(self):
        return [(0, k) for k in range(self.cuts)] + [(i, 0) for i in range(1, len(self.ins))]

    def staying(self, i):
        target = self.outs[i].at[self.place]
        return pltpu.make_async_copy(self.ins[i], target, self.own_sem.at[i])

    def sending(self, piece, block, own, sem, target):
        i, k = piece
        landing, source, q = self.outs[i].at[block], self.ins[i], k
        if i:
            q = self.cuts + i - 1
        else:
            rows = source.shape[0] // self.cuts
            landing, source = landing.at[pl.ds(k * rows, rows)], source.at[pl.ds(k * rows, rows)]
        sems = sem.at[q], self.recv_sem.at[block, q]
        return remote(source if own else landing, landing, *sems, {"expert": target})

    def up(self, piece, step, own=False):
        block = self.place - 2 * step
        return self.sending(piece, block, own, self.up_sem.at[step], self.place + 2)

    def down(self, piece, step, own=False):
        block = self.place + 2 * step
        return self.sending(piece, block, own, self.down_sem.at[step], self.place - 2)

    def across(self, piece, step, own=False):
        sem = self.side_sem.at[step + self.levels - 1]
        return self.sending(piece, self.place - 2 * step, own, sem, self.other)

    def begin(self):
        for piece in self.pieces():
            pl.when(self.has_up)(self.up(piece, 0, True).start)
            pl.when(self.has_down)(self.down(piece, 0, True).start)
        for piece in self.pieces():
            self.across(piece, 0, True).start()
        for i in range(len(self.ins)):
            self.staying(i).start()

    def forward(self, step, piece):
        @pl.when(self.level >= step)
        def _():
            self.across(piece, step).wait_recv()
            pl.when(self.has_up)(self.up(piece, step).start)
            self.across(piece, step).start()

        @pl.when(self.level + step < self.levels)
        def _():
            self.across(piece, -step).wait_recv()
            pl.when(self.has_down)(self.down(piece, step).start)
            self.across(piece, -step).start()

    def land_across(self, block):
        for piece in self.pieces():
            self.sending(piece, block, False, self.side_sem.at[0], self.other).wait_recv()

    def turn(self, turn, landed=None):
        levels, cuts = self.levels, self.cuts
        step, k = lax.div(turn, 4) + 1, lax.rem(turn, 4)

        @pl.when((step < levels) & (k < cuts))
        def _():
            self.forward(step, (0, k))

            @pl.when(k == cuts - 1)
            def _():
                for i in range(1, len(self.ins)):
                    self.forward(step, (i, 0))

        group, sign, crossed = step - 1, 2 * lax.rem(k, 2) - 1, lax.div(k, 2)
        crossed = jnp.where(group == 0, k, crossed)
        far = jnp.where(group == 0, self.level, self.level + sign * group)

        @pl.when((far >= 0) & (far < levels) & ((group > 0) | (k < 2)))
        def _():
            block = 2 * far + self.side + crossed * (1 - 2 * self.side)

            @pl.when(crossed == 1)
            def _():
                self.land_across(block)

            if landed:
                landed(block)

    def main(self, landed=None):
        @pl.loop(0, 4 * self.levels)
        def _(turn):
            self.turn(turn, landed)

    def finish(self, held=0):
        for piece in self.pieces():
            self.across(piece, 0).wait_send()
            for step in range(self.levels):
                above, below = self.level >= step, self.level + step < self.levels
                pl.when(self.has_up & above)(self.up(piece, step).wait_send)
                pl.when(self.has_down & below)(self.down(piece, step).wait_send)
                if step:
                    pl.when(above)(self.across(piece, step).wait_send)
                    pl.when(below)(self.across(piece, -step).wait_send)
        for i in range(held, len(self.ins)):
            self.staying(i).wait()


def call(kernel, name, number, outs, scratch, arrays, moved):
    return pl.pallas_call(
        kernel,
        out_shape=outs,
        in_specs=[ANY] * len(arrays),
        out_specs=[ANY] * len(outs),
        scratch_shapes=scratch,
        compiler_params=pltpu.CompilerParams(
            collective_id=number, has_side_effects=True, vmem_limit_bytes=48 << 20
        ),
        cost_estimate=pl.CostEstimate(flops=0, transcendentals=0, bytes_accessed=moved),
        name=name,
    )(*arrays)


class LineReduce:
    def __init__(self, levels, cuts, parts, total, own, beside, rising, falling, *sems):
        self.levels, self.cuts, self.parts, self.total = levels, cuts, parts, total
        self.made = parts.shape[0] == levels
        self.own, self.beside, self.rising, self.falling = own, beside, rising, falling
        self.load_sem, self.side_send, self.side_recv = sems[:3]
        self.up_send, self.up_recv, self.down_send, self.down_recv, self.out_sem = sems[3:]
        self.place, self.level, self.side, self.other = line_place()
        self.has_up, self.has_down = self.level < levels - 1, self.level > 0
        self.rows = parts.shape[1] // cuts

    @staticmethod
    def scratch(size, block, dtype, cuts):
        levels = size // 2
        return (
            [pltpu.VMEM((levels,) + block, dtype)] * 2
            + [pltpu.VMEM((levels - 1,) + block, dtype)] * 2
            + [pltpu.SemaphoreType.DMA((levels, cuts))] * 7
            + [pltpu.SemaphoreType.DMA((cuts,))]
        )

    def cut(self, ref, block, k):
        return ref.at[block, pl.ds(k * self.rows, self.rows)]

    def loading(self, far, k):
        source = self.cut(self.parts, 2 * far + self.side, k)
        return pltpu.make_async_copy(source, self.cut(self.own, far, k), self.load_sem.at[far, k])

    def across(self, far, k):
        source = self.cut(self.parts, far if self.made else 2 * far + 1 - self.side, k)
        sems = self.side_send.at[far, k], self.side_recv.at[far, k]
        return remote(source, self.cut(self.beside, far, k), *sems, {"expert": self.other})

    def up(self, far, k):
        sems = self.up_send.at[far, k], self.up_recv.at[far, k]
        target = {"expert": self.place + 2}
        return remote(self.cut(self.own, far, k), self.cut(self.rising, far - 1, k), *sems, target)

    def down(self, far, k):
        sems = self.down_send.at[far, k], self.down_recv.at[far, k]
        target = {"expert": self.place - 2}
        return remote(self.cut(self.own, far, k), self.cut(self.falling, far, k), *sems, target)

    def value(self, ref, block, k):
        return self.cut(ref, block, k)[...].astype(FULL)

    def load(self):
        for i in range(self.levels):
            for k in range(self.cuts):
                self.loading(self.far(i), k).start()

    def begin(self):
        for i in range(self.levels):
            for k in range(self.cuts):
                self.across(self.far(i), k).start()

    def far(self, i):
        return jnp.where(lax.rem(i, 2) == 0, self.levels - 1 - lax.div(i, 2), lax.div(i, 2))

    def prepare(self, turn, make):
        far = self.far(lax.div(turn, 2))

        @pl.when(lax.rem(turn, 2) == 0)
        def _():
            make(2 * far + 1 - self.side, self.parts.at[far])
            for k in range(self.cuts):
                self.across(far, k).start()

        @pl.when(lax.rem(turn, 2) == 1)
        def _():
            make(2 * far + self.side, self.own.at[far])

    def pair(self, far, k):
        if not self.made:
            self.loading(far, k).wait()
        self.across(far, k).wait_recv()
        return self.value(self.own, far, k) + self.value(self.beside, far, k)

    def store(self, far, k, total):
        self.cut(self.own, far, k)[...] = total.astype(self.own.dtype)

    def toward(self, far, k, ahead, behind, move, arrived, shift):
        @pl.when(ahead & behind)
        def _():
            both = self.pair(far, k)
            move(far, k).wait_recv()
            self.store(far, k, both + self.value(arrived, far - shift, k))

        @pl.when(ahead & jnp.logical_not(behind))
        def _():
            self.store(far, k, self.pair(far, k))

        pl.when(ahead)(move(far, k).start)

    def main(self, beside=None):
        levels, cuts = self.levels, self.cuts
        lower = self.level < levels // 2

        def rise(far, k):
            self.toward(far, k, self.level < far, self.has_down, self.up, self.rising, 1)

        def fall(far, k):
            self.toward(far, k, self.level > far, self.has_up, self.down, self.falling, 0)

        @pl.loop(0, 2 * cuts)
        def _(turn):
            near, k = turn < cuts, lax.rem(turn, cuts)
            if beside:
                beside(turn)
            upward = (near & lower) | jnp.logical_not(near | lower)
            pl.when(upward)(lambda: rise(levels - 1, k))
            pl.when(jnp.logical_not(upward))(lambda: fall(0, k))

        @pl.loop(2 * cuts, levels * cuts)
        def _(turn):
            step, k = lax.div(turn, cuts) - 1, lax.rem(turn, cuts)
            if beside:
                beside(turn)
            rise(levels - 1 - step, k)
            fall(step, k)

    def settle(self):
        @pl.loop(0, self.cuts)
        def _(k):
            self.store(self.level, k, self.pair(self.level, k))
            for there, move, arrived, shift in (
                (self.has_down, self.up, self.rising, 1),
                (self.has_up, self.down, self.falling, 0),
            ):

                @pl.when(there)
                def _():
                    move(self.level, k).wait_recv()
                    total = self.value(self.own, self.level, k)
                    total += self.value(arrived, self.level - shift, k)
                    self.store(self.level, k, total)

            self.leaving(k).start()

    def leaving(self, k):
        target = self.total.at[pl.ds(k * self.rows, self.rows)]
        return pltpu.make_async_copy(self.cut(self.own, self.level, k), target, self.out_sem.at[k])

    def finish(self):
        for k in range(self.cuts):
            self.leaving(k).wait()
            for far in range(self.levels):
                self.across(far, k).wait_send()
                pl.when(self.level < far)(self.up(far, k).wait_send)
                pl.when(self.level > far)(self.down(far, k).wait_send)


class Exchange:
    def __init__(self, axis, size, spread, cuts, ins, outs, send_sem, recv_sem, own_sem):
        self.axis, self.spread, self.ins, self.outs = axis, spread, ins, outs
        self.send_sem, self.recv_sem, self.own_sem = send_sem, recv_sem, own_sem
        self.cuts = cuts
        self.firsts = [sum(cuts[:i]) for i in range(len(cuts))]
        self.pieces = [(i, k) for i in range(len(cuts)) for k in range(cuts[i])]
        self.place, self.peers = lax.axis_index(axis), around(axis, size)

    @staticmethod
    def scratch(size, cuts):
        sems = pltpu.SemaphoreType.DMA
        return [sems((sum(cuts), size)), sems((sum(cuts), size)), sems((len(cuts),))]

    def source(self, i, block):
        return self.ins[i] if self.spread[i] else self.ins[i].at[block]

    def staying(self, i):
        target = self.outs[i].at[self.place]
        return pltpu.make_async_copy(self.source(i, self.place), target, self.own_sem.at[i])

    def sending(self, i, k, shift, landing):
        peer = self.peers[shift]
        source, target, q = self.source(i, peer), self.outs[i].at[landing], self.firsts[i] + k
        if self.cuts[i] > 1:
            rows = target.shape[0] // self.cuts[i]
            source, target = source.at[pl.ds(k * rows, rows)], target.at[pl.ds(k * rows, rows)]
        sems = self.send_sem.at[q, shift], self.recv_sem.at[q, landing]
        return remote(source, target, *sems, {self.axis: peer})

    def send(self, i, k):
        for shift in range(len(self.peers)):
            self.sending(i, k, shift, self.place).start()

    def stay(self):
        for i in range(len(self.spread)):
            self.staying(i).start()

    def begin(self):
        for i, k in self.pieces:
            self.send(i, k)
        self.stay()

    def land(self):
        for shift, peer in enumerate(self.peers):
            for i, k in self.pieces:
                self.sending(i, k, shift, peer).wait_recv()

    def arrive(self):
        self.land()
        for i in range(len(self.spread)):
            self.staying(i).wait()

    def finish(self):
        for shift in range(len(self.peers)):
            for i, k in self.pieces:
                self.sending(i, k, shift, self.place).wait_send()


def exchange_kernel(axis, size, spread, *refs):
    count = len(spread)
    ins, outs, sems = refs[:count], refs[count : 2 * count], refs[2 * count :]
    moves = Exchange(axis, size, spread, (1,) * count, ins, outs, *sems)
    greet(axis, [(peer, None) for peer in moves.peers])
    pl.semaphore_wait(pltpu.get_barrier_semaphore(), size - 1)
    moves.begin()
    moves.arrive()
    moves.finish()


def exchange_outs(size, arrays, spread):
    return [
        jax.ShapeDtypeStruct((size,) + a.shape if flat else a.shape, a.dtype)
        for a, flat in zip(arrays, spread)
    ]


def exchange(axis, size, arrays, spread, number):
    return call(
        functools.partial(exchange_kernel, axis, size, tuple(spread)),
        "exchange_" + axis,
        number,
        exchange_outs(size, arrays, spread),
        Exchange.scratch(size, (1,) * len(arrays)),
        arrays,
        30_000_000,
    )


def opening_kernel(size, dp_count, count, cuts, *refs):
    ins, (w_ref, *small_refs) = refs[:count], refs[count : count + 3]
    outs, rest = refs[count + 3 : 2 * count + 3], refs[2 * count + 6 :]
    w_out, *small_outs = refs[2 * count + 3 : 2 * count + 6]
    line = LineGather(size // 2, cuts, ins, outs, *rest[:5])
    send_sem, recv_sem, own_sem = rest[5:8]
    place, mine = line.place, lax.axis_index("dp")
    peers = around("expert", size)
    width = w_out.shape[3] // 3
    lands = [w_out] + small_outs
    across = Exchange(
        "dp", dp_count, (True,) * 3, (size,) * 3, [a.at[mine] for a in lands], lands, *rest[8:]
    )
    greet("expert", [(peer, None) for peer in peers])
    greet("dp", [(peer, None) for peer in across.peers])
    pl.semaphore_wait(pltpu.get_barrier_semaphore(), size + dp_count - 2)

    def ends(peer, landing, j):
        if j >= 3:
            return small_refs[j - 3], small_outs[j - 3].at[mine, landing]
        start = pl.multiple_of(j * width * size + peer * width, 128)
        target = w_out.at[mine, landing, :, pl.ds(j * width, width)]
        return w_ref.at[:, pl.ds(start, width)], target

    def sending(shift, landing, j):
        source, target = ends(peers[shift], landing, j)
        sems = send_sem.at[shift, j], recv_sem.at[landing, j]
        return remote(source, target, *sems, {"expert": peers[shift]})

    own = [pltpu.make_async_copy(*ends(place, place, j), own_sem.at[j]) for j in range(5)]
    for shift in range(size - 1):
        for j in range(5):
            sending(shift, place, j).start()
    for copy in own:
        copy.start()
    line.begin()
    for copy in own:
        copy.wait()
    for i in range(3):
        across.send(i, place)
    for shift, peer in enumerate(peers):
        for j in range(5):
            sending(shift, peer, j).wait_recv()
        for i in range(3):
            across.send(i, peer)
    line.main()
    line.finish()
    for shift in range(size - 1):
        for j in range(5):
            sending(shift, place, j).wait_send()
    across.land()
    across.finish()


def opening(size, dp_count, arrays, cuts, weights, small, number):
    sems = pltpu.SemaphoreType.DMA
    outs = [jax.ShapeDtypeStruct((size,) + a.shape, a.dtype) for a in arrays]
    rows, columns = weights.shape
    whole = (dp_count, size, rows)
    outs.append(jax.ShapeDtypeStruct(whole + (columns // size,), weights.dtype))
    outs += [jax.ShapeDtypeStruct((dp_count, size) + a.shape, a.dtype) for a in small]
    return call(
        functools.partial(opening_kernel, size, dp_count, len(arrays), cuts),
        "opening",
        number,
        outs,
        LineGather.scratch(size, cuts, len(arrays))
        + [sems((size, 5)), sems((size, 5)), sems((5,))]
        + Exchange.scratch(dp_count, (size,) * 3),
        list(arrays) + [weights] + small,
        200_000_000,
    )


class Sheets:
    def __init__(self, size, dp_count, source, target, *sems):
        self.levels, self.dp_count, self.ins, self.out = size // 2, dp_count, source, target
        self.up_send, self.down_send, self.line_recv, self.dp_send, self.dp_recv = sems[:5]
        self.side_send, self.side_recv, self.own_sem = sems[5:]
        self.place, self.level, self.side, self.other = line_place()
        self.has_up, self.has_down = self.level < self.levels - 1, self.level > 0
        self.mine, self.peers = lax.axis_index("dp"), around("dp", dp_count)

    @staticmethod
    def scratch(size, dp_count):
        sems, levels = pltpu.SemaphoreType.DMA, size // 2
        return [sems((levels,))] * 3 + [sems((dp_count, levels))] * 4 + [sems((1,))]

    def along(self, far, own, send, target):
        landing = self.out.at[self.mine, 2 * far + self.side]
        source = self.ins if own else landing
        return remote(source, landing, send.at[far], self.line_recv.at[far], {"expert": target})

    def up(self, far, own=False):
        return self.along(far, own, self.up_send, self.place + 2)

    def down(self, far, own=False):
        return self.along(far, own, self.down_send, self.place - 2)

    def over(self, far, shift, copy, own=False):
        landing = self.out.at[copy, 2 * far + self.side]
        source = self.ins if own else landing
        sems = self.dp_send.at[shift, far], self.dp_recv.at[copy, far]
        return remote(source, landing, *sems, {"dp": self.peers[shift]})

    def across(self, far, copy, whose, own=False):
        landing = self.out.at[copy, 2 * far + whose]
        source = self.ins if own else landing
        sems = self.side_send.at[copy, far], self.side_recv.at[copy, far]
        return remote(source, landing, *sems, {"expert": self.other})

    def spread(self, far, own=False):
        for shift in range(self.dp_count - 1):
            self.over(far, shift, self.mine, own).start()
        self.across(far, self.mine, self.side, own).start()

    def staying(self):
        target = self.out.at[self.mine, self.place]
        return pltpu.make_async_copy(self.ins, target, self.own_sem.at[0])

    def begin(self):
        pl.when(self.has_up)(self.up(self.level, True).start)
        pl.when(self.has_down)(self.down(self.level, True).start)
        self.spread(self.level, True)
        self.staying().start()

    def forward(self, step):
        @pl.when(self.level >= step)
        def _():
            self.up(self.level - step).wait_recv()
            pl.when(self.has_up)(self.up(self.level - step).start)
            self.spread(self.level - step)

        @pl.when(self.level + step < self.levels)
        def _():
            self.down(self.level + step).wait_recv()
            pl.when(self.has_down)(self.down(self.level + step).start)
            self.spread(self.level + step)

    def cross(self, far):
        for shift, peer in enumerate(self.peers):
            self.over(far, shift, peer).wait_recv()
            self.across(far, peer, self.side).start()

    def finish(self):
        @pl.loop(0, self.levels)
        def _(far):
            pl.when(self.has_up & (self.level >= far))(self.up(far).wait_send)
            pl.when(self.has_down & (self.level <= far))(self.down(far).wait_send)
            for shift in range(self.dp_count - 1):
                self.over(far, shift, self.mine).wait_send()
            for copy in range(self.dp_count):
                self.across(far, copy, 1 - self.side).wait_recv()
                self.across(far, copy, self.side).wait_send()

        self.staying().wait()


VMEM = pl.BlockSpec(memory_space=pltpu.VMEM)
COLUMNS = 512


def gather_place_kernel(levels, cuts, *refs):
    rows_ref, gates_ref, table_ref, dy_ref, x_out, dy_out, gates_out = refs[:7]
    held, dy_held, x_stage, dy_stage = refs[7:11]
    line_sems, (dy_sem, x_sems, dy_sems) = refs[11:16], refs[16:]
    line = LineGather(levels, cuts, [rows_ref, gates_ref], [held, gates_out], *line_sems)
    size, width = 2 * levels, held.shape[2]
    _, local_count, capacity, _ = x_stage.shape

    def leaving(block, stage, out, sems):
        target = out.at[:, pl.ds(pl.multiple_of(block * capacity, 8), capacity)]
        return pltpu.make_async_copy(stage.at[block], target, sems.at[block])

    def place(block, rows, stage, out, sems):
        table = table_ref[block]

        @pl.loop(0, width // COLUMNS)
        def _(n):
            columns = pl.ds(pl.multiple_of(n * COLUMNS, COLUMNS), COLUMNS)
            placed = jnp.dot(table, rows[block, :, columns], preferred_element_type=FULL)
            for j in range(local_count):
                part = placed[j * capacity : (j + 1) * capacity]
                stage[block, j, :, columns] = part.astype(stage.dtype)

        leaving(block, stage, out, sems).start()

    def place_x(block):
        place(block, held, x_stage, x_out, x_sems)

    loading = pltpu.make_async_copy(dy_ref, dy_held, dy_sem.at[0])
    loading.start()
    line_barrier(levels)
    line.begin()
    loading.wait()

    @pl.loop(0, size)
    def _(block):
        place(block, dy_held, dy_stage, dy_out, dy_sems)

    line.staying(0).wait()
    line.main(place_x)
    line.finish(held=1)

    @pl.loop(0, size)
    def _(block):
        leaving(block, x_stage, x_out, x_sems).wait()
        leaving(block, dy_stage, dy_out, dy_sems).wait()


def gather_place(size, rows, gates, table, dy, local_count, number):
    cuts = GATHER_CUTS
    tokens, width = rows.shape
    capacity = table.shape[1] // local_count
    placed = jax.ShapeDtypeStruct((local_count, size * capacity, width), rows.dtype)
    sems = pltpu.SemaphoreType.DMA
    return pl.pallas_call(
        functools.partial(gather_place_kernel, size // 2, cuts),
        out_shape=[placed, placed, jax.ShapeDtypeStruct((size,) + gates.shape, gates.dtype)],
        in_specs=[ANY, ANY, VMEM, ANY],
        out_specs=[ANY] * 3,
        scratch_shapes=[pltpu.VMEM((size, tokens, width), rows.dtype)] * 2
        + [pltpu.VMEM((size, local_count, capacity, width), rows.dtype)] * 2
        + LineGather.scratch(size, cuts, 2)
        + [sems((1,)), sems((size,)), sems((size,))],
        compiler_params=pltpu.CompilerParams(
            collective_id=number, has_side_effects=True, vmem_limit_bytes=48 << 20
        ),
        cost_estimate=pl.CostEstimate(
            flops=4 * table.size * width, transcendentals=0, bytes_accessed=150_000_000
        ),
        name="gather_place",
    )(rows, gates, table, dy)


def several(index, turns, count, work):
    share = -(-count // turns)
    for i in range(share):
        item = share * index + i
        pl.when((index >= 0) & (item < count))(lambda item=item: work(item))


def split_at(arrays, j, block):
    for array in arrays:
        if j < array.shape[0]:
            return array.at[j, block]
        j -= array.shape[0]


def collect_block(tables, slots, block, target):
    @pl.loop(0, target.shape[1] // COLUMNS)
    def _(n):
        columns = pl.ds(pl.multiple_of(n * COLUMNS, COLUMNS), COLUMNS)
        total = 0.0
        for j, table in enumerate(tables):
            rows = split_at(slots, j, block)[:, columns]
            total += jnp.dot(table[block], rows, preferred_element_type=FULL)
        target[:, columns] = total.astype(target.dtype)


def collect_reduce_kernel(levels, cuts, local_count, *refs):
    tables, refs = refs[:local_count], refs[local_count:]
    slots, dots, (table_ref, total_ref, gates_out, away) = refs[:2], refs[2:4], refs[4:8]
    rest, (gates, *sems) = refs[8:20], refs[20:]
    line = LineReduce(levels, cuts, away, total_ref, *rest)
    small = Exchange("expert", 2 * levels, (False,), (1,), [gates], [gates_out], *sems)
    greet("expert", [(peer, None) for peer in small.peers])
    pl.semaphore_wait(pltpu.get_barrier_semaphore(), 2 * levels - 1)
    make = functools.partial(collect_block, tables, slots)

    @pl.loop(0, 4)
    def _(turn):
        line.prepare(turn, make)

    def gate_block(block):
        table = table_ref[block].astype(FULL)
        capacity = table.shape[0] // local_count
        for j in range(local_count):
            part = table[j * capacity : (j + 1) * capacity] * split_at(dots, j, block)[...]
            gates[block, j : j + 1] = jnp.sum(part, axis=0, keepdims=True)

    def beside(turn):
        pl.when(turn + 4 < 2 * levels)(lambda: line.prepare(turn + 4, make))
        turns = levels * cuts - levels
        several(turn - levels, turns, 2 * levels, gate_block)
        pl.when(turn == levels * cuts - 1)(small.begin)

    line.main(beside)
    line.settle()
    small.arrive()
    line.finish()
    small.finish()


def collect_reduce(size, tables, slots, dots, table, number):
    levels, cuts = size // 2, REDUCE_CUTS
    block = (tables[0].shape[1], slots[0].shape[3])
    kind = slots[0].dtype
    gates = (size, len(tables), block[0])
    return pl.pallas_call(
        functools.partial(collect_reduce_kernel, levels, cuts, len(tables)),
        out_shape=[jax.ShapeDtypeStruct(block, kind), jax.ShapeDtypeStruct(gates, FULL)],
        in_specs=[VMEM] * (len(tables) + 5),
        out_specs=[ANY, ANY],
        scratch_shapes=[pltpu.VMEM((levels,) + block, kind)]
        + LineReduce.scratch(size, block, kind, cuts)
        + [pltpu.VMEM(gates, FULL)]
        + Exchange.scratch(size, (1,)),
        compiler_params=pltpu.CompilerParams(
            collective_id=number, has_side_effects=True, vmem_limit_bytes=48 << 20
        ),
        cost_estimate=pl.CostEstimate(flops=0, transcendentals=0, bytes_accessed=150_000_000),
        name="collect_reduce",
    )(*tables, *slots, *dots, table)


class SquareSum:
    def __init__(self, cuts, parts, near, far, send_sem, recv_sem, last_send, last_recv):
        self.cuts, self.parts, self.near, self.far = cuts, parts, near, far
        self.send_sem, self.recv_sem, self.last_send, self.last_recv = send_sem, recv_sem, last_send, last_recv
        self.mine = lax.axis_index("dp")
        slow, fast = lax.div(self.mine, 2), lax.rem(self.mine, 2)
        self.along = 2 * slow + 1 - fast, 2 * (1 - slow) + fast
        self.across = 2 * (1 - slow) + 1 - fast
        self.step = parts.shape[1] // cuts

    @staticmethod
    def scratch(cuts, shape, dtype):
        sems = pltpu.SemaphoreType.DMA
        buffers = [pltpu.VMEM((2,) + shape[1:], dtype), pltpu.VMEM(shape[1:], dtype)]
        return buffers + [sems((cuts, 2)), sems((cuts, 2)), sems((cuts,)), sems((cuts,))]

    def rows(self, k):
        return pl.ds(pl.multiple_of(k * self.step, self.step), self.step)

    def peer(self, k, later):
        half = lax.div(k, self.cuts // 2)
        return jnp.where(half == later, self.along[0], self.along[1])

    def first(self, k, kind):
        peer, rows = self.peer(k, 0), self.rows(k)
        source = self.parts.at[self.across if kind else peer, rows]
        sems = self.send_sem.at[k, kind], self.recv_sem.at[k, kind]
        return remote(source, self.near.at[kind, rows], *sems, {"dp": peer})

    def second(self, k):
        peer, rows = self.peer(k, 1), self.rows(k)
        sems = self.last_send.at[k], self.last_recv.at[k]
        return remote(self.parts.at[peer, rows], self.far.at[rows], *sems, {"dp": peer})

    def begin(self, k):
        self.first(k, 0).start()
        self.first(k, 1).start()

    def turn(self, k):
        self.first(k, 1).wait_recv()
        peer, rows = self.peer(k, 1), self.rows(k)
        total = self.parts[peer, rows].astype(FULL) + self.near[1, rows].astype(FULL)
        self.parts[peer, rows] = total.astype(self.parts.dtype)
        self.second(k).start()

    def arrive(self):
        for k in range(self.cuts):
            self.first(k, 0).wait_recv()
            self.second(k).wait_recv()

    def total(self, columns):
        own = self.parts[self.mine, :, columns].astype(FULL)
        return own + self.near[0, :, columns].astype(FULL) + self.far[:, columns].astype(FULL)

    def finish(self):
        for k in range(self.cuts):
            self.first(k, 0).wait_send()
            self.first(k, 1).wait_send()
            self.second(k).wait_send()


def closing_kernel(size, dp_count, local_count, cuts, sum_cuts, *refs):
    refs, levels = list(refs), size // 2

    def take(count):
        taken = refs[:count]
        del refs[:count]
        return taken

    tables, slots = take(local_count), take(2)
    proj_ref, w_ref, h_ref, gain_ref, out_parts, gain_pair, shared_ref = take(7)
    back_out, mixed_out, qkv_out, w_out, gains_out, gain_out, shared_out = take(7)
    back = LineReduce(levels, cuts, *take(1), back_out, *take(12))
    mixed = LineReduce(levels, cuts, *take(1), mixed_out, *take(12))
    square = dp_count == 4
    if square:
        qkv_parts, gains_got = take(2)
        qkv_sum = SquareSum(sum_cuts[0], qkv_parts, *take(6))
        (out_own,) = take(1)
        out_sum = SquareSum(sum_cuts[1], out_own, *take(6))
        out_own[...] = out_parts[...]
    else:
        qkv_parts, gains_got, qkv_got, out_got = take(4)
    got, half, last, gain_sum, gain_got, gain_half, gain_last = take(7)
    parts, lands, spread, some = [gain_pair], [gains_got], (True,), (1,)
    if not square:
        parts, lands = parts + [qkv_parts, out_parts], lands + [qkv_got, out_got]
        spread, some = (True, False, False), (1,) + sum_cuts
    sums = Exchange("dp", dp_count, spread, some, parts, lands, *take(3))
    first = Exchange("expert", size, (False,), (1,), [shared_ref], [got], *take(3))
    second = Exchange("dp", dp_count, (False,), (1,), [half], [last], *take(3))
    gain_first = Exchange("expert", size, (True,), (1,), [gain_sum], [gain_got], *take(3))
    gain_second = Exchange("dp", dp_count, (True,), (1,), [gain_half], [gain_last], *take(3))
    greet("expert", [(peer, None) for peer in first.peers])
    greet("dp", [(peer, None) for peer in sums.peers])
    pl.semaphore_wait(pltpu.get_barrier_semaphore(), size + dp_count - 2)
    first.begin()
    sums.staying(0).start()
    if not square:
        sums.staying(2).start()
    gain_sum[...] = jnp.zeros_like(gain_sum)
    groups, tokens, model_dim = h_ref.shape
    tall, high = half.shape[1], model_dim // dp_count

    def make_back(block, target):
        @pl.loop(0, model_dim // COLUMNS)
        def _(n):
            columns = pl.ds(pl.multiple_of(n * COLUMNS, COLUMNS), COLUMNS)
            grad = across_cols(proj_ref[block], w_ref[columns, :])
            target[:, columns] = grad.astype(target.dtype)
            weighted = grad * h_ref[block, :, columns].astype(FULL)
            gain_sum[:, columns] += jnp.sum(weighted, axis=0, keepdims=True)

    def piece(turn):
        k, copy = lax.div(turn, dp_count), lax.rem(turn, dp_count)
        columns = pl.ds(pl.multiple_of(copy * high + k * 128, 128), 128)
        rows = h_ref[:, :, columns].reshape(groups * tokens, 128)
        grads = proj_ref[...].reshape(groups * tokens, proj_ref.shape[2])
        products = contract_rows(rows, grads).astype(LOW)
        qkv_parts[copy, pl.ds(pl.multiple_of(k * 128, 128), 128)] = products
        if square:
            pl.when(copy == dp_count - 1)(lambda: qkv_sum.begin(k))
        else:
            pl.when(copy == dp_count - 1)(lambda: sums.send(1, k))
            pl.when(turn == count - 1)(lambda: sums.staying(1).start())

    make_mixed = functools.partial(collect_block, tables, slots)
    ahead = levels

    @pl.loop(0, ahead)
    def _(turn):
        back.prepare(turn, make_back)

    rest, count = levels * cuts - ahead, sum_cuts[0] * dp_count

    def beside(turn):
        later = turn - ahead
        pl.when(turn + ahead < 2 * levels)(lambda: back.prepare(turn + ahead, make_back))
        send = out_sum.begin if square else functools.partial(sums.send, 2)
        pl.when(turn < sum_cuts[1])(lambda: send(turn))
        pl.when(turn == sum_cuts[1])(lambda: sums.send(0, 0))
        pl.when(later == 0)(gain_first.begin)
        several(later, rest, 2 * levels, lambda i: mixed.prepare(i, make_mixed))
        several(later, rest, count, piece)

        @pl.when(later == rest - 1)
        def _():
            first.arrive()
            for copy in range(dp_count):
                rows = pl.ds(copy * tall, tall)
                half[copy] = sum(got[i, rows, :] for i in range(size))
            second.begin()
            gain_first.arrive()
            gain_half[...] = sum(gain_got[i] for i in range(size))
            gain_second.begin()

    back.main(beside)
    def beside_mixed(turn):
        if square:
            pl.when(turn < sum_cuts[1])(lambda: out_sum.turn(turn))
            after = turn - 1
            here = (after >= 0) & (lax.rem(after, 3) == 0) & (after < 3 * sum_cuts[0])
            pl.when(here)(lambda: qkv_sum.turn(lax.div(after, 3)))

    mixed.main(beside_mixed)
    back.settle()
    mixed.settle()
    second.arrive()
    shared_out[...] = sum(last[i] for i in range(dp_count))
    gain_second.arrive()
    gain_out[...] = sum(gain_last[i] for i in range(dp_count)) / gain_ref[...]
    sums.arrive()
    wide = qkv_out.shape[2]
    if square:
        qkv_sum.arrive()
        out_sum.arrive()
    for j in range(3):
        columns = slice(j * wide, (j + 1) * wide)
        if square:
            qkv_out[j] = qkv_sum.total(columns)
        else:
            qkv_out[j] = sum(qkv_got[copy, :, columns].astype(FULL) for copy in range(dp_count))
    if square:
        w_out[...] = out_sum.total(slice(None))
    else:
        w_out[...] = sum(out_got[copy].astype(FULL) for copy in range(dp_count))
    gains_out[...] = sum(gains_got[copy] for copy in range(dp_count))
    moved = [back, mixed, first, second, sums, gain_first, gain_second]
    for moves in moved + ([qkv_sum, out_sum] if square else []):
        moves.finish()


def closing(size, dp_count, tables, slots, arrays, sums, shared, number):
    proj, _, hidden, gain = arrays
    levels, cuts = size // 2, REDUCE_CUTS
    _, tokens, model_dim = hidden.shape
    columns, high = proj.shape[2], model_dim // dp_count
    block = (tokens, model_dim)
    tall = shared.shape[1] // dp_count
    wide = shared.shape[2]
    sum_cuts = (high // 128, 2)
    parts = (dp_count, high, columns)
    out, pair = exchange_outs(dp_count, sums, (False, True))
    shapes = [(3, high, columns // 3), out.shape[1:], pair.shape[1:], gain.shape, (tall, wide)]
    outs = [jax.ShapeDtypeStruct(block, LOW)] * 2
    outs += [jax.ShapeDtypeStruct(shape, FULL) for shape in shapes]
    if dp_count == 4:
        landing, some = SquareSum.scratch(sum_cuts[0], parts, LOW), (1,)
        landing += [pltpu.VMEM(out.shape, LOW)] + SquareSum.scratch(sum_cuts[1], out.shape, LOW)
    else:
        landing, some = [pltpu.VMEM(parts, LOW), pltpu.VMEM(out.shape, LOW)], (1,) + sum_cuts
    line = [pltpu.VMEM((levels,) + block, LOW)] + LineReduce.scratch(size, block, LOW, cuts)
    return pl.pallas_call(
        functools.partial(closing_kernel, size, dp_count, len(tables), cuts, sum_cuts),
        out_shape=outs,
        in_specs=[VMEM] * (len(tables) + 7) + [ANY] * 2,
        out_specs=[ANY] * 2 + [VMEM] * 5,
        scratch_shapes=line
        + line
        + [pltpu.VMEM(parts, LOW), pltpu.VMEM(pair.shape, FULL)]
        + landing
        + [pltpu.VMEM((size,) + shared.shape[1:], FULL)]
        + [pltpu.VMEM((dp_count, tall, wide), FULL)] * 2
        + [
            pltpu.VMEM(gain.shape, FULL),
            pltpu.VMEM((size,) + gain.shape, FULL),
            pltpu.VMEM(gain.shape, FULL),
            pltpu.VMEM((dp_count,) + gain.shape, FULL),
        ]
        + Exchange.scratch(dp_count, some)
        + Exchange.scratch(size, (1,))
        + Exchange.scratch(dp_count, (1,))
        + Exchange.scratch(size, (1,))
        + Exchange.scratch(dp_count, (1,)),
        compiler_params=pltpu.CompilerParams(
            collective_id=number, has_side_effects=True, vmem_limit_bytes=62 << 20
        ),
        cost_estimate=pl.CostEstimate(flops=0, transcendentals=0, bytes_accessed=200_000_000),
        name="closing",
    )(*tables, *slots, *arrays, *sums, shared)


def across_cols(left_side, right_side):
    return lax.dot_general(
        left_side, right_side, (((1,), (1,)), ((), ())), preferred_element_type=FULL
    )


def expert_kernel(first, count, tiles, x_ref, dy_ref, scale_ref, side_ref, down_ref, grads_ref, out_ref, back_ref, dots_ref,
                  side_w, down_w, turned, turned_act, act, grad_side, side_buf, down_buf, w_sems, sems):
    e, step = pl.program_id(0), pl.program_id(1)
    slot = lax.rem(e, 2)
    hidden, model = down_w.shape[1], down_w.shape[2]
    width, wide = hidden // tiles, model // tiles
    copies = grads_ref.shape[0]
    high, low = model // copies, hidden // copies
    part = side_buf.shape[1]

    def loads(e, tile):
        slot = lax.rem(e, 2)
        out = []
        for half in range(2):
            columns = pl.ds(pl.multiple_of(half * hidden + tile * width, 128), width)
            out.append(pltpu.make_async_copy(side_ref.at[first + e, :, columns], side_w.at[slot, :, columns], w_sems.at[slot, tile, half]))
        rows = pl.ds(pl.multiple_of(tile * width, 128), width)
        out.append(pltpu.make_async_copy(down_ref.at[first + e, rows], down_w.at[slot, rows], w_sems.at[slot, tile, 2]))
        return out

    def leaving(at):
        e, chunk = lax.div(at, tiles), lax.rem(at, tiles)
        slot = lax.rem(at, 2)
        base = e * (high + low)
        columns = pl.ds(pl.multiple_of(chunk * wide, 128), wide)
        if wide >= high:
            target = grads_ref.at[pl.ds(chunk * part, part), pl.ds(base, high)]
        else:
            target = grads_ref.at[pl.ds(lax.div(chunk * wide, high), 1), pl.ds(base + lax.rem(chunk * wide, high), wide)]
        return (pltpu.make_async_copy(side_buf.at[slot], target, sems.at[slot, 0]),
                pltpu.make_async_copy(down_buf.at[slot], grads_ref.at[:, pl.ds(base + high, low), columns], sems.at[slot, 1]))

    @pl.when((e == 0) & (step == 0))
    def _():
        for tile in range(tiles):
            for copy in loads(e, tile): copy.start()

    @pl.when((e + 1 < count) & (step == 0))
    def _():
        for tile in range(tiles):
            for copy in loads(e + 1, tile): copy.start()

    @pl.when(step == 0)
    def _():
        turned[...] = x_ref[0].T
        dots_ref[...] = jnp.zeros_like(dots_ref)

    @pl.when(step < tiles)
    def _():
        for copy in loads(e, step): copy.wait()
        rows, grads, scale = x_ref[0], dy_ref[0], scale_ref[0]
        columns = pl.ds(pl.multiple_of(step * width, 128), width)
        others = pl.ds(pl.multiple_of(hidden + step * width, 128), width)
        gate = jnp.dot(rows, side_w[slot, :, columns], preferred_element_type=FULL)
        up = jnp.dot(rows, side_w[slot, :, others], preferred_element_type=FULL)
        grad_act = across_cols(grads, down_w[slot, columns, :])
        sigmoid = jax.nn.sigmoid(gate)
        silu = gate * sigmoid
        raw = silu * up
        dots_ref[0] += jnp.sum(raw * grad_act, axis=-1, keepdims=True)
        weighted = (scale * raw).astype(LOW)
        act[:, columns] = weighted
        turned_act[columns, :] = weighted.T
        grad_act = grad_act * scale
        grad_side[:, columns] = (grad_act * up * sigmoid * (1.0 + gate * (1.0 - sigmoid))).astype(LOW)
        grad_side[:, others] = (grad_act * silu).astype(LOW)

    @pl.when(step >= tiles)
    def _():
        chunk = step - tiles
        at = e * tiles + chunk
        spot = lax.rem(at, 2)
        columns = pl.ds(pl.multiple_of(chunk * wide, 128), wide)

        @pl.when(at >= 2)
        def _():
            for copy in leaving(at - 2): copy.wait()
        total = jnp.dot(turned[columns, :], grad_side[...], preferred_element_type=FULL)
        side_buf[spot] = total.astype(LOW).reshape(side_buf.shape[1:])
        leaving(at)[0].start()
        total = jnp.dot(turned_act[...], dy_ref[0, :, columns], preferred_element_type=FULL)
        down_buf[spot] = total.astype(LOW).reshape(down_buf.shape[1:])
        leaving(at)[1].start()
        back_ref[0, :, columns] = across_cols(grad_side[...], side_w[slot, columns, :]).astype(LOW)
        out_ref[0, :, columns] = jnp.dot(act[...], down_w[slot, :, columns], preferred_element_type=FULL).astype(LOW)

        @pl.when(at == count * tiles - 1)
        def _():
            for copy in leaving(at - 1) + leaving(at): copy.wait()

def expert(first, count, dp_count, x_rows, dy_rows, scales, w_gate_up, w_down, tiles=4):
    _, slots, width = x_rows.shape
    hidden = w_down.shape[1]
    high, low = width // dp_count, hidden // dp_count
    wide = width // tiles
    part = max(1, wide // high)
    rs = pl.BlockSpec((1, slots, width), lambda e, f: (first + e, 0, 0))
    os = pl.BlockSpec((1, slots, width), lambda e, f: (e, 0, 0))
    sems = pltpu.SemaphoreType.DMA
    return pl.pallas_call(
        functools.partial(expert_kernel, first, count, tiles),
        out_shape=[jax.ShapeDtypeStruct((dp_count, count * (high + low), width), LOW),
                   jax.ShapeDtypeStruct((count, slots, width), LOW), jax.ShapeDtypeStruct((count, slots, width), LOW),
                   jax.ShapeDtypeStruct((count, slots, 1), FULL)],
        grid=(count, 2 * tiles),
        in_specs=[rs, rs, pl.BlockSpec((1, slots, 1), lambda e, f: (first + e, 0, 0)), ANY, ANY],
        out_specs=[ANY, os, os, pl.BlockSpec((1, slots, 1), lambda e, f: (e, 0, 0))],
        scratch_shapes=[pltpu.VMEM((min(2, count), width, 2 * hidden), LOW), pltpu.VMEM((min(2, count), hidden, width), LOW),
                        pltpu.VMEM((width, slots), LOW), pltpu.VMEM((hidden, slots), LOW), pltpu.VMEM((slots, hidden), LOW), pltpu.VMEM((slots, 2 * hidden), LOW),
                        pltpu.VMEM((2, part, min(wide, high), 2 * hidden), LOW), pltpu.VMEM((2, dp_count, low, wide), LOW),
                        sems((min(2, count), tiles, 3)), sems((2, 2))],
        compiler_params=pltpu.CompilerParams(vmem_limit_bytes=62 << 20),
        cost_estimate=pl.CostEstimate(
            flops=18 * count * slots * width * hidden,
            transcendentals=count * slots * hidden,
            bytes_accessed=12 * count * width * hidden,
        ),
        name="expert",
    )(x_rows, dy_rows, scales, w_gate_up, w_down)


def rms_scale(values):
    return lax.rsqrt(jnp.mean(values * values, axis=-1, keepdims=True) + NORM_EPS)


def rotary_tables(length, size):
    index = np.arange(size // 2, dtype=np.float32)
    frequency = np.exp(index * np.float32(-2.0 * math.log(10000.0) / size))
    angles = np.arange(length, dtype=np.float32)[:, None] * frequency[None, :]
    cosine, sine = np.cos(angles), np.sin(angles)
    halves = [np.concatenate([cosine, cosine], axis=1), np.concatenate([-sine, sine], axis=1)]
    return jnp.asarray(np.stack(halves).astype(np.float32))


def norm_back(grad_normed, normed, scale_rows):
    return scale_rows * (
        grad_normed - normed * jnp.mean(grad_normed * normed, axis=-1, keepdims=True)
    )


def contract_rows(left_side, right_side):
    return lax.dot_general(
        left_side, right_side, (((0,), (0,)), ((), ())), preferred_element_type=FULL
    )


def contract_cols(left_side, right_side):
    return lax.dot_general(
        left_side, right_side, (((1,), (1,)), ((), ())), preferred_element_type=FULL
    )


def einsum(spec, left_side, right_side):
    return jnp.einsum(spec, left_side, right_side, preferred_element_type=FULL)


def widen_kernel(steps, *refs):
    low_ref, high_ref, down_ref = refs[0], refs[-2], refs[-1]
    step = pl.program_id(1)

    @pl.when(step < steps)
    def _():
        high_ref[...] = low_ref[...].astype(FULL)

    @pl.when(step >= steps)
    def _():
        down_ref[...] = low_ref[...].astype(FULL)


def widen(first, total, high, grads, held=()):
    count, both, width = grads.shape
    low = both - high
    rows = low
    steps = high // rows
    block = (1, rows, width)
    return pl.pallas_call(
        functools.partial(widen_kernel, steps),
        out_shape=[
            jax.ShapeDtypeStruct((total, high, width), FULL),
            jax.ShapeDtypeStruct((total, low, width), FULL),
        ],
        grid=(count, steps + 1),
        in_specs=[pl.BlockSpec(block, lambda e, r: (e, r, 0))] + [ANY] * len(held),
        out_specs=[
            pl.BlockSpec(block, lambda e, r: (first + e, jnp.minimum(r, steps - 1), 0)),
            pl.BlockSpec(block, lambda e, r: (first + e, jnp.maximum(r - steps, 0), 0)),
        ],
        input_output_aliases={1: 0, 2: 1} if held else {},
        cost_estimate=pl.CostEstimate(
            flops=grads.size, transcendentals=0, bytes_accessed=6 * grads.size
        ),
        name="widen",
    )(grads, *held)


def turn(values, cosine, sine):
    return values * cosine + pltpu.roll(values, values.shape[1] // 2, 1) * sine


def allowed_pairs(column, row):
    shape = (column.shape[0], row.shape[1])
    later = lax.broadcasted_iota(jnp.int32, shape, 0) >= lax.broadcasted_iota(jnp.int32, shape, 1)
    return later & (column == row)


def softmax(query, key, allowed):
    scores = across_cols(query, key) * (1.0 / math.sqrt(query.shape[1]))
    scores = jnp.where(allowed, scores, -1e30)
    powers = jnp.exp(scores - jnp.max(scores, axis=-1, keepdims=True))
    return powers / jnp.sum(powers, axis=-1, keepdims=True)


def attend_block(heads, block, rows_ref, scales, gain_ref, turn_ref, column, row, kept_ref, out_ref):
    width = out_ref.shape[2]
    size = width // heads
    allowed = allowed_pairs(column, row)
    cosine, sine = turn_ref[0], turn_ref[1]
    for h in range(heads):
        parts = []
        for part in range(3):
            columns = pl.ds(part * width + h * size, size)
            values = rows_ref[block, :, columns]
            if part < 2:
                values = values * scales[part]
                values = values * gain_ref[part : part + 1, h * size : (h + 1) * size]
                values = turn(values, cosine, sine)
            parts.append(values.astype(LOW))
            kept_ref[block, :, columns] = parts[-1]
        query, key, value = parts
        probs = softmax(query, key, allowed).astype(LOW)
        out_ref[block, :, pl.ds(h * size, size)] = jnp.dot(
            probs, value, preferred_element_type=FULL
        ).astype(LOW)


def attention_kernel(size, dp_count, heads, *refs):
    x_ref, w_ref, gain_ref, gains_ref, turn_ref, column_ref, row_ref, sheet_ref, dy_ref = refs[:9]
    h_out, rows_out, scale_ref, kept_ref, out_ref, own_out, sheet_out, dy_out = refs[9:17]
    x_held, h_held, rows, sums, squares, got = refs[17:23]
    x_sem, h_sem, rows_sem, send_sem, recv_sem, stay_sem = refs[23:29]
    square_sems, line_sems, sheet_sems = refs[29:32], refs[32:37], refs[37:]
    line = LineGather(size // 2, GATHER_CUTS, [dy_ref], [dy_out], *line_sems)
    sheets = Sheets(size, dp_count, sheet_ref, sheet_out, *sheet_sems)
    small = Exchange("expert", size, (True,), (1,), [squares], [got], *square_sems)
    place, model_dim = sheets.place, x_ref.shape[2]
    width = out_ref.shape[2]

    def loading(g):
        return pltpu.make_async_copy(x_ref.at[g], x_held.at[g], x_sem.at[g])

    def leaving(g):
        return (
            pltpu.make_async_copy(h_held.at[g], h_out.at[g], h_sem.at[g]),
            pltpu.make_async_copy(rows.at[g], rows_out.at[g], rows_sem.at[g]),
        )

    for g in range(size):
        loading(g).start()
    greet("expert", [(peer, None) for peer in small.peers])
    greet("dp", [(peer, None) for peer in sheets.peers])
    pl.semaphore_wait(pltpu.get_barrier_semaphore(), size + dp_count - 2)
    sheets.begin()
    line.begin()
    sums[...] = jnp.zeros_like(sums)
    lanes = lax.broadcasted_iota(jnp.int32, sums.shape, 1)

    @pl.loop(0, size)
    def _(g):
        loading(g).wait()
        values = x_held[g].astype(FULL)
        hidden = (values * rms_scale(values) * gain_ref[...]).astype(LOW)
        h_held[g] = hidden
        projected = jnp.dot(hidden, w_ref[...], preferred_element_type=FULL)
        rows[g] = projected
        for copy in leaving(g):
            copy.start()
        for part in range(2):
            half = projected[:, part * width : (part + 1) * width]
            total = jnp.sum(half * half, axis=-1, keepdims=True)
            sums[...] += jnp.where(lanes == part * size + g, total, 0.0)

    squares[...] = sums[...].T[: 2 * size]
    small.begin()
    sheets.forward(1)
    small.arrive()
    total = sum(got[i] for i in range(size))
    sums[:, : 2 * size] = lax.rsqrt(total / model_dim + NORM_EPS).T

    def sending(g, source):
        columns = pl.ds(pl.multiple_of(source * width, 128), width)
        target = own_out.at[:, columns]
        return remote(out_ref.at[g], target, send_sem.at[g], recv_sem.at[source], {"expert": g})

    own_columns = pl.ds(pl.multiple_of(place * width, 128), width)
    staying = pltpu.make_async_copy(out_ref.at[place], own_out.at[:, own_columns], stay_sem.at[0])

    @pl.loop(0, size)
    def _(i):
        g = lax.rem(place + 1 + i, size)
        scales = [
            jnp.sum(jnp.where(lanes == part * size + g, sums[...], 0.0), axis=-1, keepdims=True)
            for part in range(2)
        ]
        scale_ref[g] = jnp.concatenate(scales, axis=1)
        attend_block(
            heads, g, rows, scales, gains_ref, turn_ref, column_ref[g], row_ref[g], kept_ref, out_ref
        )
        pl.when(g != place)(lambda: sending(g, place).start())
        pl.when(lax.rem(i, 2) == 1)(lambda: line.turn(lax.div(i, 2)))

    staying.start()

    @pl.loop(size // 2, 2 * size)
    def _(i):
        for step in range(2, size // 2):
            pl.when(i == (step - 1) * (size // 2))(lambda: sheets.forward(step))
        line.turn(i)
        after = i - size - size // 2
        pl.when((after >= 0) & (after < size // 2))(lambda: sheets.cross(after))


    @pl.loop(1, size)
    def _(i):
        peer = lax.rem(place + i, size)
        sending(peer, peer).wait_recv()
        sending(peer, place).wait_send()

    @pl.loop(0, size)
    def _(g):
        for copy in leaving(g):
            copy.wait()

    staying.wait()
    small.finish()
    line.finish()
    sheets.finish()


def attention(size, dp_count, heads, arrays, number):
    x_all, w_here, sheet, dy = arrays[0], arrays[1], arrays[7], arrays[8]
    _, tokens, model_dim = x_all.shape
    columns = w_here.shape[1]
    width = columns // 3
    sems = pltpu.SemaphoreType.DMA
    seqs = (size, tokens)
    small = (2 * size, tokens)
    return pl.pallas_call(
        functools.partial(attention_kernel, size, dp_count, heads),
        out_shape=[
            jax.ShapeDtypeStruct(x_all.shape, LOW),
            jax.ShapeDtypeStruct(seqs + (columns,), FULL),
            jax.ShapeDtypeStruct(seqs + (2,), FULL),
            jax.ShapeDtypeStruct(seqs + (columns,), LOW),
            jax.ShapeDtypeStruct(seqs + (width,), LOW),
            jax.ShapeDtypeStruct((tokens, model_dim), LOW),
            jax.ShapeDtypeStruct((dp_count, size) + sheet.shape, LOW),
            jax.ShapeDtypeStruct((size,) + dy.shape, LOW),
        ],
        in_specs=[ANY] + [VMEM] * 6 + [ANY] * 2,
        out_specs=[ANY] * 2 + [VMEM] * 3 + [ANY] * 3,
        scratch_shapes=[
            pltpu.VMEM(x_all.shape, LOW),
            pltpu.VMEM(x_all.shape, LOW),
            pltpu.VMEM(seqs + (columns,), FULL),
            pltpu.VMEM((tokens, 128), FULL),
            pltpu.VMEM(small, FULL),
            pltpu.VMEM((size,) + small, FULL),
            sems((size,)),
            sems((size,)),
            sems((size,)),
            sems((size,)),
            sems((size,)),
            sems((1,)),
        ]
        + Exchange.scratch(size, (1,))
        + LineGather.scratch(size, GATHER_CUTS, 1)
        + Sheets.scratch(size, dp_count),
        compiler_params=pltpu.CompilerParams(
            collective_id=number, has_side_effects=True, vmem_limit_bytes=48 << 20
        ),
        cost_estimate=pl.CostEstimate(
            flops=2 * x_all.size * columns, transcendentals=0, bytes_accessed=100_000_000
        ),
        name="attention",
    )(*arrays)


def attend_back_block(heads, block, grad_ref, refs, back_ref, dots_ref, lanes, gains_ref, w_sum):
    w_ref, kept_ref, out_ref, rows_ref, scale_ref, gain_ref, turn_ref, column_ref, row_ref = refs
    width = out_ref.shape[2]
    size = width // heads
    scaling = 1.0 / math.sqrt(size)
    allowed = allowed_pairs(column_ref[block], row_ref[block])
    cosine, sine = turn_ref[0], turn_ref[1]
    grad_rows = grad_ref[block]
    grad_out = across_cols(grad_rows, w_ref[...]).astype(LOW)
    w_sum[...] += contract_rows(out_ref[block], grad_rows)
    dots = [0.0, 0.0]
    for h in range(heads):
        mine = slice(h * size, (h + 1) * size)
        query, key, value = (
            kept_ref[block, :, pl.ds(p * width + h * size, size)] for p in range(3)
        )
        probs = softmax(query, key, allowed)
        grad = grad_out[:, mine]
        grad_value = contract_rows(probs.astype(LOW), grad)
        grad_probs = across_cols(grad, value)
        delta = jnp.sum(grad_probs * probs, axis=-1, keepdims=True)
        grad_scores = (probs * (grad_probs - delta)).astype(LOW)
        grad_query = jnp.dot(grad_scores, key, preferred_element_type=FULL) * scaling
        grad_key = contract_rows(grad_scores, query) * scaling
        for part, grad_turned in enumerate((grad_query, grad_key)):
            columns = pl.ds(part * width + h * size, size)
            grad_normed = turn(grad_turned, cosine, -sine)
            normed = rows_ref[block, :, columns] * scale_ref[block, :, part : part + 1]
            gains_ref[part : part + 1, mine] += jnp.sum(grad_normed * normed, axis=0, keepdims=True)
            weighted = grad_normed * gain_ref[part : part + 1, mine]
            dots[part] += jnp.sum(weighted * normed, axis=-1, keepdims=True)
            back_ref[block, :, columns] = weighted
        back_ref[block, :, pl.ds(2 * width + h * size, size)] = grad_value
    groups = grad_ref.shape[0]
    for part in range(2):
        dots_ref[...] += jnp.where(lanes == part * groups + block, dots[part], 0.0)


def attend_back_kernel(levels, cuts, heads, grad_ref, *refs):
    w_ref, others, refs = refs[0], refs[1:9], refs[9:]
    proj_ref, gains_ref, w_grad_ref, w_sum, held, w_held, back, dots, squares, got, w_sem = refs[:11]
    reads = (w_held,) + tuple(others)
    rows_ref, scale_ref = others[2:4]
    size, model_dim = 2 * levels, grad_ref.shape[1]
    line = LineGather(levels, cuts, [grad_ref], [held], *refs[11:16])
    small = Exchange("expert", size, (True,), (1,), [squares], [got], *refs[16:])
    mine = pl.ds(pl.multiple_of(line.place * w_held.shape[0], 128), w_held.shape[0])
    loading = pltpu.make_async_copy(w_ref.at[mine], w_held, w_sem.at[0])
    loading.start()
    greet("expert", [(peer, None) for peer in small.peers])
    pl.semaphore_wait(pltpu.get_barrier_semaphore(), size - 1)
    line.begin()
    w_sum[...] = jnp.zeros_like(w_sum)
    gains_ref[...] = jnp.zeros_like(gains_ref)
    dots[...] = jnp.zeros_like(dots)
    lanes = lax.broadcasted_iota(jnp.int32, dots.shape, 1)
    loading.wait()
    line.staying(0).wait()

    def landed(block):
        attend_back_block(heads, block, held, reads, back, dots, lanes, gains_ref, w_sum)

    line.main(landed)
    squares[...] = dots[...].T[: 2 * size]
    small.begin()
    wide = w_grad_ref.shape[2]
    for copy in range(w_grad_ref.shape[0]):
        w_grad_ref[copy] = w_sum[:, copy * wide : (copy + 1) * wide].astype(LOW)
    small.arrive()
    dots[:, : 2 * size] = sum(got[i] for i in range(size)).T / model_dim
    width = w_held.shape[0]

    @pl.loop(0, size)
    def _(block):
        for part in range(2):
            columns = pl.ds(part * width, width)
            scale = scale_ref[block, :, part : part + 1]
            mean = jnp.where(lanes == part * size + block, dots[...], 0.0)
            mean = jnp.sum(mean, axis=-1, keepdims=True)
            normed = rows_ref[block, :, columns] * scale
            proj_ref[block, :, columns] = (scale * (back[block, :, columns] - normed * mean)).astype(LOW)
        columns = pl.ds(2 * width, width)
        proj_ref[block, :, columns] = back[block, :, columns].astype(LOW)

    line.finish(held=1)
    small.finish()


def attend_back(size, dp_count, heads, grad, arrays, number):
    _, _, out, rows = arrays[:4]
    width = out.shape[2]
    tokens, model_dim = grad.shape
    small = (2 * size, tokens)
    return pl.pallas_call(
        functools.partial(attend_back_kernel, size // 2, GATHER_CUTS, heads),
        out_shape=[
            jax.ShapeDtypeStruct(rows.shape, LOW),
            jax.ShapeDtypeStruct((2, width), FULL),
            jax.ShapeDtypeStruct((dp_count, width, model_dim // dp_count), LOW),
        ],
        in_specs=[ANY] * 2 + [VMEM] * (len(arrays) - 1),
        out_specs=[VMEM] * 3,
        scratch_shapes=[
            pltpu.VMEM((width, model_dim), FULL),
            pltpu.VMEM((size, tokens, model_dim), LOW),
            pltpu.VMEM((width, model_dim), LOW),
            pltpu.VMEM(rows.shape, FULL),
            pltpu.VMEM((tokens, 128), FULL),
            pltpu.VMEM(small, FULL),
            pltpu.VMEM((size,) + small, FULL),
            pltpu.SemaphoreType.DMA((1,)),
        ]
        + LineGather.scratch(size, GATHER_CUTS, 1)
        + Exchange.scratch(size, (1,)),
        compiler_params=pltpu.CompilerParams(
            collective_id=number, has_side_effects=True, vmem_limit_bytes=48 << 20
        ),
        cost_estimate=pl.CostEstimate(flops=0, transcendentals=0, bytes_accessed=150_000_000),
        name="attend_back",
    )(grad, *arrays)


def on_device(
    dp_count,
    line_count,
    layer_input,
    out_cotangent,
    segments,
    routes,
    w_qkv,
    w_out,
    w_router,
    attn_gain,
    mlp_gain,
    query_gain,
    key_gain,
    w_gate_up,
    w_down,
):
    row_count, model_dim = layer_input.shape
    top_count = routes.shape[1]
    expert_count = w_router.shape[1]
    local_count = w_gate_up.shape[0]
    head_size = model_dim // HEADS
    head_cols = model_dim // line_count
    heads_here = head_cols // head_size
    capacity = (row_count * top_count * 9 // 8 + expert_count - 1) // expert_count
    scaling = 1.0 / math.sqrt(head_size)
    place = lax.axis_index("expert")
    shard = w_qkv.shape[0]

    numbers = jnp.concatenate([routes.T, segments, jnp.zeros((7, row_count), jnp.int32)], axis=0)
    x_all, numbers_all, qkv_here, router_full, gains = opening(
        line_count,
        dp_count,
        [layer_input, numbers],
        GATHER_CUTS,
        w_qkv,
        [w_router, jnp.stack([attn_gain, mlp_gain, query_gain, key_gain])],
        1,
    )
    qkv_here = qkv_here.reshape(model_dim, 3 * head_cols)
    router_full = router_full.reshape(model_dim, expert_count)
    gains = gains.transpose(2, 0, 1, 3).reshape(4, model_dim).astype(FULL)
    gain_attn, gain_mlp = gains[0], gains[1]
    both_gains = lax.dynamic_slice_in_dim(gains[2:], place * head_cols, head_cols, axis=1)

    routes_all = numbers_all[:, :top_count]
    segments_all = numbers_all[:, top_count]
    turns = rotary_tables(row_count, head_size)
    column, row = segments_all[:, :, None], segments_all[:, None, :]
    arrays = [x_all, qkv_here, gain_attn[None], both_gains, turns, column, row, w_out, out_cotangent]
    hidden_one, projected, scales, kept, attended, own_attended, out_full, dy_all = attention(
        line_count, dp_count, heads_here, arrays, 4
    )
    out_full = out_full.reshape(model_dim, model_dim)
    inputs = layer_input.astype(FULL)
    scale_attn = rms_scale(inputs)
    normed_attn = inputs * scale_attn
    residual = inputs + jnp.dot(own_attended, out_full, preferred_element_type=FULL)
    scale_mlp = rms_scale(residual)
    normed_mlp = residual * scale_mlp
    hidden_two = (normed_mlp * gain_mlp).astype(LOW)

    logits = jnp.dot(hidden_two, router_full, preferred_element_type=FULL)
    chosen = jnp.any(routes[:, :, None] == jnp.arange(expert_count)[None, None, :], axis=1)
    masked = jnp.where(chosen, logits, -1e30)
    powers = jnp.where(chosen, jnp.exp(masked - jnp.max(masked, axis=-1, keepdims=True)), 0.0)
    gates = powers / jnp.sum(powers, axis=-1, keepdims=True)

    local = place * local_count + jnp.arange(local_count)
    used = jnp.any(routes_all[:, None] == local[None, :, None, None], axis=2)
    position = jnp.arange(row_count)
    lower = (position[:, None] < position[None, :]).astype(LOW)
    rank = einsum("gju,ut->gjt", used.astype(LOW), lower).astype(jnp.int32)
    rank = jnp.where(used, rank, -1)
    spots = jnp.arange(capacity)
    table = (rank[:, :, None, :] == spots[None, None, :, None]).astype(LOW)
    returns = [(rank[:, j, :, None] == spots[None, None, :]).astype(LOW) for j in range(local_count)]
    slots = line_count * capacity
    flat_table = table.reshape(line_count, local_count * capacity, row_count)
    expert_rows, dy_rows, gates_all = gather_place(
        line_count, hidden_two, gates.T, flat_table, dy_all, local_count, 6
    )
    local_gates = lax.dynamic_slice_in_dim(gates_all, place * local_count, local_count, axis=1)
    slot_gates = jnp.sum(table.astype(FULL) * local_gates[:, :, None, :], axis=-1)
    slot_gates = slot_gates.transpose(1, 0, 2).reshape(local_count, slots, 1)
    out_rows, back_rows, slot_grads, grad_sums = [], [], [], []
    both_rows = model_dim // dp_count + w_down.shape[1] // dp_count
    for first, count in ((0, 1), (1, local_count - 1)):
        grads, out_row, back_row, dots = expert(
            first, count, dp_count, expert_rows, dy_rows, slot_gates, w_gate_up, w_down
        )
        grads = grads.reshape(-1, model_dim)
        grads = lax.psum_scatter(grads, "dp", scatter_dimension=0, tiled=True)
        grad_sums.append(grads.reshape(count, both_rows, model_dim))
        for kept_list, rows in ((out_rows, out_row), (back_rows, back_row), (slot_grads, dots)):
            kept_list.append(rows.reshape(count, line_count, capacity, rows.shape[2]))
    gate_rows = model_dim // dp_count
    grad_two, grad_gates = collect_reduce(
        line_count, returns, back_rows, slot_grads, flat_table, 8
    )
    grad_gates = grad_gates.reshape(expert_count, row_count).T
    grad_two = grad_two.astype(FULL)

    grad_out_rows = out_cotangent.astype(FULL)
    grad_logits = gates * (grad_gates - jnp.sum(gates * grad_gates, axis=-1, keepdims=True))
    grad_logits = grad_logits.astype(LOW)
    grad_router = contract_rows(grad_logits, hidden_two)
    grad_two = grad_two + contract_cols(grad_logits, router_full)
    grad_gain_mlp = jnp.sum(grad_two * normed_mlp, axis=0)
    grad_resid = grad_out_rows + norm_back(grad_two * gain_mlp, normed_mlp, scale_mlp)
    grad_attn = grad_resid.astype(LOW)

    arrays = [out_full, kept, attended, projected, scales, both_gains, turns, column, row]
    grad_proj, gain_pair, out_parts = attend_back(
        line_count, dp_count, heads_here, grad_attn, arrays, 11
    )

    shared = jnp.concatenate([grad_router, grad_gain_mlp[None]], axis=0)
    tall = shared.shape[0] + -shared.shape[0] % 8
    shared = jnp.pad(shared, ((0, tall - shared.shape[0]), (0, 0)))
    shared = shared.reshape(tall, dp_count, line_count, shard).transpose(2, 1, 0, 3)
    shared = shared.reshape(line_count, dp_count * tall, shard)
    shared = jnp.pad(shared, ((0, 0), (0, 0), (0, 128 - shard)))
    arrays = [grad_proj, qkv_here, hidden_one, gain_attn[None]]
    grad_one, mixture, sum_qkv, sum_out, gain_pair, gain_sum, shared = closing(
        line_count, dp_count, returns, out_rows, arrays, [out_parts, gain_pair], shared, 14
    )
    here = (lax.axis_index("dp") * line_count + place) * shard
    grad_gain_attn = lax.dynamic_slice_in_dim(gain_sum[0], here, shard)
    output = (residual + mixture.astype(FULL)).astype(LOW)
    sum_qkv = sum_qkv.transpose(1, 0, 2)
    first_sums, mixture = lax.optimization_barrier((grad_sums[0], mixture))
    wide = widen(0, local_count, gate_rows, first_sums)
    sum_gate_up, sum_down = widen(1, local_count, gate_rows, grad_sums[1], wide)
    shared = shared[:, :shard]
    grad_one = grad_one.astype(FULL)
    grad_inputs = grad_resid + norm_back(grad_one * gain_attn, normed_attn, scale_attn)
    return (
        output,
        grad_inputs,
        sum_qkv,
        sum_out,
        shared[:expert_count].T,
        grad_gain_attn,
        shared[expert_count],
        gain_pair[0],
        gain_pair[1],
        sum_gate_up,
        sum_down,
    )


def solution(mesh):
    both = ("dp", "expert")
    rows, flat = P(both, None), P(both)
    placed = (rows,) * 7 + (flat,) * 4 + (P("expert", None, None),) * 2
    return jax.shard_map(
        functools.partial(on_device, mesh.shape["dp"], mesh.shape["expert"]),
        mesh=mesh,
        in_specs=placed,
        out_specs=(
            rows,
            rows,
            P("dp", None, "expert"),
            P("expert", "dp"),
            rows,
            flat,
            flat,
            P("expert"),
            P("expert"),
            P("expert", "dp", None),
            P("expert", "dp", None),
        ),
        check_vma=False,
    )
```
